32 devices in a mesh: fsdp: 4 (over z), ctx: 2 (over x), tp: 4 (over y, core).
Axes of the slice: x: 2, y: 2, z: 4, core: 2. Of those that a mesh axis runs over, the one named last changes fastest.
Arguments:
- layer_in: bfloat16 [8, 1024, 1024], P('fsdp', ('ctx', 'tp')), may hold values from -6 to 6
- attn_gain: bfloat16 [1024], replicated, may hold values from 0.5 to 1.5
- ffn_gain: bfloat16 [1024], replicated, may hold values from 0.5 to 1.5
- query_weight: bfloat16 [1024, 1024], P(('fsdp', 'ctx'), 'tp'), may hold values from -0.1875 to 0.1875
- key_weight: bfloat16 [1024, 1024], P(('fsdp', 'ctx'), 'tp'), may hold values from -0.1875 to 0.1875
- value_weight: bfloat16 [1024, 1024], P(('fsdp', 'ctx'), 'tp'), may hold values from -0.1875 to 0.1875
- out_weight: bfloat16 [1024, 1024], P(('fsdp', 'ctx'), 'tp'), may hold values from -0.75 to 0.75
- variate_bias: float32 [2, 16], P(None, 'tp'), may hold values from -4 to 4
- gate_weight: bfloat16 [1024, 4096], P(('fsdp', 'ctx'), 'tp'), may hold values from -0.1875 to 0.1875
- up_weight: bfloat16 [1024, 4096], P(('fsdp', 'ctx'), 'tp'), may hold values from -0.1875 to 0.1875
- down_weight: bfloat16 [1024, 4096], P(('fsdp', 'ctx'), 'tp'), may hold values from -0.09375 to 0.09375
- segment_ids: int32 [8, 1024], P('fsdp'), may hold values from 0 to 15, never falling along the last dimension, each value on 1 to 512 neighbouring positions
- variate_ids: int32 [8, 1024], P('fsdp'), may hold values from 0 to 3
- time_ids: int32 [8, 1024], P('fsdp'), may hold values from 0 to 1023
- out_grad: bfloat16 [8, 1024, 1024], P('fsdp', ('ctx', 'tp')), may hold values from -6 to 6
Outputs:
- layer_out: bfloat16 [8, 1024, 1024], P('fsdp', ('ctx', 'tp'))
- in_grad: bfloat16 [8, 1024, 1024], P('fsdp', ('ctx', 'tp'))
- attn_gain_grad: float32 [1024], replicated
- ffn_gain_grad: float32 [1024], replicated
- query_grad: float32 [1024, 1024], P(('fsdp', 'ctx'), 'tp')
- key_grad: float32 [1024, 1024], P(('fsdp', 'ctx'), 'tp')
- value_grad: float32 [1024, 1024], P(('fsdp', 'ctx'), 'tp')
- out_weight_grad: float32 [1024, 1024], P(('fsdp', 'ctx'), 'tp')
- bias_grad: float32 [2, 16], P(None, 'tp')
- gate_grad: float32 [1024, 4096], P(('fsdp', 'ctx'), 'tp')
- up_grad: float32 [1024, 4096], P(('fsdp', 'ctx'), 'tp')
- down_grad: float32 [1024, 4096], P(('fsdp', 'ctx'), 'tp')
The draws below stay inside these ranges and needn't reach their ends.
All inputs are finite; a program needn't handle non-finite values.
Results may differ from the reference program's by a relative error of at most 0.019.
Values may be sent and summed in bfloat16 or wider, within the bound.
No kernel may reach another device: no remote copies, remote signals or barrier semaphores. Data moves between devices by JAX's collectives and lax.ppermute only.
A program may use at most 128 MiB of HBM per device.

```python
import math
from functools import partial
import jax
import jax.numpy as jnp
import numpy as np
from jax import lax

D = 1024
HEADS = 16
HEAD = 64
FF = 4096
LENGTH = 1024
SEQS = 8


def place_ends(array, rng, least, high):
    longest = array.shape.index(max(array.shape))
    spots = []
    for shift in (0, 1):
        where = [jax.random.randint(jax.random.fold_in(rng, axis), (), 0, length) for axis, length in enumerate(array.shape)]
        where[longest] = (where[longest] + shift) % array.shape[longest]
        spots.append(tuple(where))
    return array.at[spots[0]].set(least).at[spots[1]].set(high)


def level_of(key, dims, split, least, largest):
    factor_of, own = 1.0, jax.random.fold_in(key, 6)
    for position, blocks in split:
        steps = jnp.exp(jax.random.uniform(jax.random.fold_in(own, position), (blocks,), jnp.float32, least / len(split), largest / len(split)))
        factor_of = factor_of * jnp.repeat(steps, dims[position] // blocks).reshape([-1 if axis == position else 1 for axis in range(len(dims))])
    return factor_of


def profile(amount, total, bound, lean):
    weights = [(1 << 20) // math.isqrt(standing ** lean) + 1 for standing in range(2, amount + 1)]
    surplus, counts = total - bound - (amount - 1), [1] * (amount - 1)
    while surplus > 0:
        movable = [i for i in range(amount - 1) if counts[i] < bound]
        mass, remaining = sum([weights[i] for i in movable]), surplus
        for i in movable:
            addition = min(bound - counts[i], max(1, remaining * weights[i] // mass), surplus)
            counts[i] = counts[i] + addition
            surplus = surplus - addition
    return np.array([bound] + counts)


def uneven_parts(rng, amount, total, reach, skew):
    if amount == 2:
        one = jax.random.randint(rng, (), max(1, total - reach), min(reach, total - 1) + 1)
        return jnp.stack([one, total - one])
    tallies = jnp.asarray(profile(amount, total, reach, skew), jnp.int32)
    twos = (amount - 1) // 2
    source_of, sink = tallies[1:1 + 2 * twos:2], tallies[2:2 + 2 * twos:2]
    slack = jnp.minimum(source_of - 1, reach - sink)
    passed = jax.random.randint(jax.random.fold_in(rng, 1), (twos,), 0, 1 << 20) % (slack + 1)
    tallies = tallies.at[1:1 + 2 * twos:2].set(source_of - passed).at[2:2 + 2 * twos:2].set(sink + passed)
    return tallies[jax.random.permutation(jax.random.fold_in(rng, 2), amount)]


def gaussian(rng, shape, deviation, limit, pieces=(), kind=jnp.bfloat16):
    drawn = jax.random.normal(rng, shape, jnp.float32) * deviation
    if len(pieces) > 0:
        drawn = level_of(rng, shape, pieces, -0.22, 0.18) * drawn
    return jnp.clip(drawn, min=-limit, max=limit).astype(kind)


def setup_inputs(seed: int = 0) -> dict:
    splits = jax.random.split(jax.random.key(seed), 16)
    return {
        "layer_in": gaussian(splits[0], (SEQS, LENGTH, D), 1.0, 6.0, ((0, 4), (1, 8))),
        "attn_gain": jnp.clip(1.0 + 0.1 * jax.random.normal(splits[1], (D,), jnp.float32), 0.5, 1.5).astype(jnp.bfloat16),
        "ffn_gain": jnp.clip(1.0 + 0.1 * jax.random.normal(splits[2], (D,), jnp.float32), 0.5, 1.5).astype(jnp.bfloat16),
        "query_weight": gaussian(splits[3], (D, HEADS * HEAD), D ** -0.5, 0.1875, ((0, 8), (1, 4))),
        "key_weight": gaussian(splits[4], (D, HEADS * HEAD), D ** -0.5, 0.1875, ((0, 8), (1, 4))),
        "value_weight": gaussian(splits[5], (D, HEADS * HEAD), D ** -0.5, 0.1875, ((0, 8), (1, 4))),
        "out_weight": gaussian(splits[6], (D, HEADS * HEAD), (HEADS * HEAD // 16) ** -0.5, 0.75, ((0, 8), (1, 4))),
        "variate_bias": gaussian(splits[7], (2, HEADS), 1.0, 4.0, ((1, 4),), jnp.float32),
        "gate_weight": gaussian(splits[8], (D, FF), D ** -0.5, 0.1875, ((0, 8), (1, 4))),
        "up_weight": gaussian(splits[9], (D, FF), D ** -0.5, 0.1875, ((0, 8), (1, 4))),
        "down_weight": gaussian(splits[10], (D, FF), FF ** -0.5, 0.09375, ((0, 8), (1, 4))),
        "segment_ids": jax.vmap(lambda own: jnp.searchsorted(jnp.cumsum(uneven_parts(own, 16, LENGTH, LENGTH // 2, 2)), jnp.arange(LENGTH), side="right"))(jax.random.split(splits[11], SEQS)).reshape((SEQS, LENGTH)).astype(jnp.int32),
        "variate_ids": place_ends(jax.random.randint(splits[12], (SEQS, LENGTH), 0, 4), jax.random.fold_in(splits[12], 1), 0, 3).astype(jnp.int32),
        "time_ids": place_ends(jax.random.randint(splits[13], (SEQS, LENGTH), 0, LENGTH), jax.random.fold_in(splits[13], 1), 0, LENGTH - 1).astype(jnp.int32),
        "out_grad": gaussian(splits[14], (SEQS, LENGTH, D), 1.0, 6.0, ((0, 4), (1, 8))),
    }


@jax.custom_vjp
def low(v):
    return lax.optimization_barrier(v.astype(jnp.bfloat16)).astype(jnp.float32)

@jax.custom_vjp
def low_back(v):
    return v

def low_keep(v):
    return (low(v), None)

def low_pass(kept, grad):
    return (grad,)

def back_keep(v):
    return (v, None)

def back_low(kept, grad):
    return (low(grad),)
low.defvjp(low_keep, low_pass)
low_back.defvjp(back_keep, back_low)
EPS = 1e-05
NEG = -1e+30

def matmul(left, right):
    return jnp.dot(left, right, precision=lax.Precision.HIGHEST, preferred_element_type=jnp.float32)

def rms_norm(values, gain):
    return values * lax.rsqrt(lax.optimization_barrier(jnp.mean(values * values, axis=-1, keepdims=True)) + EPS) * gain

def rotate(values, time_rows):
    half_dim = values.shape[-1] // 2
    frequency = 10000.0 ** (-2.0 * jnp.arange(half_dim, dtype=jnp.float32) / values.shape[-1])
    angles = time_rows.astype(jnp.float32)[..., None, None] * frequency
    cosine = jnp.cos(angles)
    sine_part = jnp.sin(angles)
    first_half = values[..., :half_dim]
    second = values[..., half_dim:]
    return jnp.concatenate([first_half * cosine - second * sine_part, second * cosine + first_half * sine_part], axis=-1)

def head_attention(parts, segments, variates):
    query, key_rows, value_rows, same_bias, diff_bias = parts
    raw = matmul(query, key_rows.T) * HEAD ** (-0.5)
    raw = raw + jnp.where(variates[:, None] == variates[None, :], same_bias, diff_bias)
    scores = low_back(raw)
    scores = jnp.where(segments[:, None] == segments[None, :], scores, NEG)
    probs = jax.nn.softmax(scores, axis=-1)
    return low(low_back(matmul(low(probs), value_rows)))

def layer(inputs, gain_one, gain_two, query_w, key_w, value_w, out_w, bias_table, gate_w, up_w, down_w, segments, variates, time_rows):
    seq_len = inputs.shape[0]
    normed_one = low(rms_norm(inputs, gain_one))
    queries = low_back(matmul(normed_one, query_w)).reshape(seq_len, HEADS, HEAD)
    keys_raw = low_back(matmul(normed_one, key_w)).reshape(seq_len, HEADS, HEAD)
    values = low(low_back(matmul(normed_one, value_w))).reshape(seq_len, HEADS, HEAD)
    queries = low(rotate(queries, time_rows))
    keys_rot = low(rotate(keys_raw, time_rows))
    per_head = lax.map(jax.checkpoint(partial(head_attention, segments=segments, variates=variates)), (queries.transpose(1, 0, 2), keys_rot.transpose(1, 0, 2), values.transpose(1, 0, 2), bias_table[0], bias_table[1]))
    mixed = per_head.transpose(1, 0, 2).reshape(seq_len, HEADS * HEAD)
    hidden = inputs + low_back(matmul(mixed, out_w.T))
    normed_two = low(rms_norm(hidden, gain_two))
    gate = low_back(matmul(normed_two, gate_w))
    up_vals = low_back(matmul(normed_two, up_w))
    act = low(jax.nn.silu(gate) * up_vals)
    return hidden + low_back(matmul(act, down_w.T))

def reference(layer_in, attn_gain, ffn_gain, query_weight, key_weight, value_weight, out_weight, variate_bias, gate_weight, up_weight, down_weight, segment_ids, variate_ids, time_ids, out_grad):
    weights = (attn_gain.astype(jnp.float32), ffn_gain.astype(jnp.float32), query_weight.astype(jnp.float32), key_weight.astype(jnp.float32), value_weight.astype(jnp.float32), out_weight.astype(jnp.float32), variate_bias.astype(jnp.float32), gate_weight.astype(jnp.float32), up_weight.astype(jnp.float32), down_weight.astype(jnp.float32))

    def one_seq(carry, item):
        seq_in, seq_grad, segments, variates, time_rows = item

        def forward(inputs, *params):
            return layer(inputs, *params, segments, variates, time_rows)
        result, pull = jax.vjp(forward, seq_in.astype(jnp.float32), *weights)
        grads = pull(seq_grad.astype(jnp.float32))
        summed = tuple((total + part for total, part in zip(carry, grads[1:])))
        return (summed, (result.astype(jnp.bfloat16), grads[0].astype(jnp.bfloat16)))
    zeros = tuple((jnp.zeros(w.shape, jnp.float32) for w in weights))
    sums, (outputs, in_grads) = lax.scan(one_seq, zeros, (layer_in, out_grad, segment_ids, variate_ids, time_ids))
    return (outputs, in_grads, sums[0], sums[1], sums[2], sums[3], sums[4], sums[5], sums[6], sums[7], sums[8], sums[9])
```

```python
import jax
import jax.numpy as jnp
from jax import lax
from jax.sharding import PartitionSpec as P

HEADS = 16
HEAD = 64
EPS = 1e-05
NEG = -1e30
F32 = jnp.float32
BF16 = jnp.bfloat16


def hop(values, axis, flip):
    size = lax.axis_size(axis)
    return lax.ppermute(values, axis, [(i, i ^ flip) for i in range(size)])


def swap_blocks(values, axis, index, size):
    shape = values.shape
    bit = 1
    while bit < size:
        split = shape[:axis] + (size // (2 * bit), 2, bit) + shape[axis + 1 :]
        cut = values.reshape(split)
        cut = jnp.where((index & bit) != 0, jnp.flip(cut, axis + 1), cut)
        values = cut.reshape(shape)
        bit *= 2
    return values


def gather_weight(block):
    nz = lax.axis_size("fsdp")
    across = hop(block, "ctx", 1)
    mine = [block] + [hop(block, "fsdp", k) for k in range(1, nz)]
    rest = [hop(piece, "ctx", 1) for piece in mine[1:]]
    return jnp.concatenate(mine + [across] + rest, axis=0)


def scatter_weight(partial):
    nz = lax.axis_size("fsdp")
    half = partial.shape[0] // 2
    rows = half // nz
    other = hop(partial[half:], "ctx", 1)
    total = partial[:half].astype(F32) + other.astype(F32)
    low = total.astype(BF16)
    out = total[:rows]
    for k in range(1, nz):
        out = out + hop(low[k * rows : (k + 1) * rows], "fsdp", k).astype(F32)
    return out


def gather_rows(block):
    nt = lax.axis_size("tp")
    mine = [block] + [hop(block, "tp", 2 * k) for k in range(1, nt // 2)]
    twin = [hop(piece, "tp", 1) for piece in mine]
    return jnp.concatenate(mine + twin, axis=0)


def scatter_rows(partial):
    nt = lax.axis_size("tp")
    half = partial.shape[0] // 2
    rows = 2 * half // nt
    total = partial[:half].astype(F32) + hop(partial[half:].astype(BF16), "tp", 1).astype(F32)
    low = total.astype(BF16)
    out = total[:rows]
    for k in range(1, nt // 2):
        out = out + hop(low[k * rows : (k + 1) * rows], "tp", 2 * k).astype(F32)
    return out


def heads_to_rows(values):
    nt = lax.axis_size("tp")
    rows = values.shape[0] // nt
    parts = []
    for flip in range(nt):
        slot = (flip & 1) * (nt // 2) + (flip >> 1)
        piece = values[slot * rows : (slot + 1) * rows]
        parts.append(piece if flip == 0 else hop(piece, "tp", flip))
    return jnp.concatenate(parts, axis=1)


def gather_heads(block):
    nt = lax.axis_size("tp")
    mine = [block] + [hop(block, "tp", 2 * k) for k in range(1, nt // 2)]
    twin = [hop(piece, "tp", 1) for piece in mine]
    parts = [None] * nt
    for k in range(nt // 2):
        parts[2 * k] = mine[k]
        parts[2 * k + 1] = twin[k]
    return jnp.concatenate(parts, axis=1)


def psum_all(values):
    nz = lax.axis_size("fsdp")
    nt = lax.axis_size("tp")
    for axis, size in (("tp", nt), ("ctx", 2), ("fsdp", nz)):
        bit = 1
        while bit < size:
            values = values + hop(values, axis, bit)
            bit *= 2
    return values


def psum_rows(values):
    nz = lax.axis_size("fsdp")
    for axis, size in (("ctx", 2), ("fsdp", nz)):
        bit = 1
        while bit < size:
            values = values + hop(values, axis, bit)
            bit *= 2
    return values


def inverse_rms(values):
    return lax.rsqrt(jnp.mean(values * values, axis=-1, keepdims=True) + EPS)


def norm_back(values, inv, gain, grad):
    scaled = grad * gain
    normed = values * inv
    d_gain = jnp.sum(grad * normed, axis=0)
    d_values = inv * (scaled - normed * jnp.mean(scaled * normed, axis=-1, keepdims=True))
    return d_values, d_gain


def angles_of(times):
    half = HEAD // 2
    frequency = 10000.0 ** (-2.0 * jnp.arange(half, dtype=F32) / HEAD)
    angles = times.astype(F32)[:, None, None] * frequency
    return jnp.cos(angles), jnp.sin(angles)


def rotate(values, cosine, sine):
    half = HEAD // 2
    first, second = values[..., :half], values[..., half:]
    return jnp.concatenate([first * cosine - second * sine, second * cosine + first * sine], axis=-1)


def dot(left, right, left_dim, right_dim):
    return lax.dot_general(
        left, right, (((left_dim,), (right_dim,)), ((), ())), preferred_element_type=F32
    )


def shards(
    layer_in,
    attn_gain,
    ffn_gain,
    query_weight,
    key_weight,
    value_weight,
    out_weight,
    variate_bias,
    gate_weight,
    up_weight,
    down_weight,
    segment_ids,
    variate_ids,
    time_ids,
    out_grad,
):
    seq_count, share, width = layer_in.shape
    nz, nx, nt = lax.axis_size("fsdp"), lax.axis_size("ctx"), lax.axis_size("tp")
    iz, ix, it = lax.axis_index("fsdp"), lax.axis_index("ctx"), lax.axis_index("tp")
    assert nx == 2 and seq_count == nx
    length = segment_ids.shape[1]
    local_heads = variate_bias.shape[1]
    proj = local_heads * HEAD
    scale = HEAD ** (-0.5)

    def to_slots(values):
        cut = values.reshape(values.shape[0], nz, nx, width // (nz * nx))
        cut = swap_blocks(swap_blocks(cut, 1, iz, nz), 2, ix, nx)
        return cut.transpose(0, 2, 1, 3).reshape(values.shape)

    def from_slots(values):
        cut = values.reshape(values.shape[0], nx, nz, width // (nz * nx)).transpose(0, 2, 1, 3)
        return swap_blocks(swap_blocks(cut, 1, iz, nz), 2, ix, nx).reshape(values.shape)

    def own_sequence(values):
        mine = lax.dynamic_index_in_dim(values, ix, 0, keepdims=False)
        other = lax.dynamic_index_in_dim(values, 1 - ix, 0, keepdims=False)
        return jnp.concatenate([mine, hop(other, "ctx", 1)], axis=0)

    def both_sequences(values):
        mine, other = values[:share], hop(values[share:], "ctx", 1)
        first = jnp.where(ix == 0, mine, other)
        second = jnp.where(ix == 0, other, mine)
        return jnp.stack([first, second])

    def ids_of(table):
        ids = lax.dynamic_index_in_dim(table, ix, 0, keepdims=False)
        cut = ids.reshape(nx, nt // 2, 2, share)
        cut = swap_blocks(cut, 0, ix, nx)
        cut = swap_blocks(cut, 1, it // 2, nt // 2)
        cut = swap_blocks(cut, 2, it % 2, 2)
        return cut.transpose(2, 1, 0, 3).reshape(length)

    gain_one = attn_gain.astype(F32)
    gain_two = ffn_gain.astype(F32)
    inputs = own_sequence(layer_in).astype(F32)
    grads = own_sequence(out_grad)
    inv_one = inverse_rms(inputs)
    rows_one = gather_rows(to_slots((inputs * inv_one * gain_one).astype(BF16)))
    qkv_full = gather_weight(jnp.concatenate([query_weight, key_weight, value_weight], axis=1))
    out_full = gather_weight(out_weight)
    gate_full = gather_weight(gate_weight)
    up_full = gather_weight(up_weight)
    down_full = gather_weight(down_weight)
    out_all = gather_heads(out_full)
    grad_rows = gather_rows(to_slots(grads))

    times, variates, segments = ids_of(time_ids), ids_of(variate_ids), ids_of(segment_ids)
    cosine, sine = angles_of(times)
    qkv = dot(rows_one, qkv_full, 1, 0)
    queries_raw = qkv[:, :proj].reshape(length, local_heads, HEAD)
    keys_raw = qkv[:, proj : 2 * proj].reshape(length, local_heads, HEAD)
    values = qkv[:, 2 * proj :].astype(BF16).reshape(length, local_heads, HEAD)
    queries = rotate(queries_raw, cosine, sine).astype(BF16)
    keys = rotate(keys_raw, cosine, sine).astype(BF16)

    def scores_of():
        raw = jnp.einsum("qhd,khd->hqk", queries, keys, preferred_element_type=F32) * scale
        same = (variates[:, None] == variates[None, :])[None]
        raw = raw + jnp.where(same, variate_bias[0][:, None, None], variate_bias[1][:, None, None])
        return jnp.where((segments[:, None] == segments[None, :])[None], raw, NEG), same

    scores, same = scores_of()
    top = jnp.max(scores, axis=-1, keepdims=True)
    expo = jnp.exp(scores - top)
    total = jnp.sum(expo, axis=-1, keepdims=True)
    probs = (expo / total).astype(BF16)
    mixed = jnp.einsum("hqk,khd->qhd", probs, values, preferred_element_type=F32)
    mixed = mixed.astype(BF16).reshape(length, proj)
    lse = top + jnp.log(total)

    attn = dot(heads_to_rows(mixed), out_all, 1, 1)
    hidden = inputs + from_slots(attn)
    inv_two = inverse_rms(hidden)
    rows_two = gather_rows(to_slots((hidden * inv_two * gain_two).astype(BF16)))
    gate = dot(rows_two, gate_full, 1, 0)
    up_vals = dot(rows_two, up_full, 1, 0)
    sig = jax.nn.sigmoid(gate)
    silu = gate * sig
    act = (silu * up_vals).astype(BF16)
    d_act = dot(grad_rows, down_full, 1, 0)
    d_gate = (d_act * up_vals * (sig + silu * (1.0 - sig))).astype(BF16)
    d_up = (d_act * silu).astype(BF16)
    d_normed_two = dot(d_gate, gate_full, 1, 1) + dot(d_up, up_full, 1, 1)
    d_normed_two = from_slots(scatter_rows(d_normed_two))

    ffn = scatter_rows(dot(act, down_full, 1, 1))
    layer_out = both_sequences((hidden + from_slots(ffn)).astype(BF16))

    down_grad = scatter_weight(dot(grad_rows, act, 0, 0).astype(BF16))
    gate_grad = scatter_weight(dot(rows_two, d_gate, 0, 0).astype(BF16))
    up_grad = scatter_weight(dot(rows_two, d_up, 0, 0).astype(BF16))

    d_hidden_norm, d_gain_two = norm_back(hidden, inv_two, gain_two, d_normed_two)
    d_hidden = grads.astype(F32) + d_hidden_norm
    branch_rows = gather_rows(to_slots(d_hidden.astype(BF16)))
    d_mixed = dot(branch_rows, out_full, 1, 0).astype(BF16).reshape(length, local_heads, HEAD)
    out_weight_grad = scatter_weight(dot(branch_rows, mixed, 0, 0).astype(BF16))

    scores, same = scores_of()
    probs = jnp.exp(scores - lse)
    probs_low = probs.astype(BF16)
    d_probs = jnp.einsum("qhd,khd->hqk", d_mixed, values, preferred_element_type=F32)
    delta = jnp.sum(probs * d_probs, axis=-1, keepdims=True)
    d_scores = (probs * (d_probs - delta)).astype(BF16)
    d_queries = jnp.einsum("hqk,khd->qhd", d_scores, keys, preferred_element_type=F32) * scale
    d_keys = jnp.einsum("hqk,qhd->khd", d_scores, queries, preferred_element_type=F32) * scale
    d_values = jnp.einsum("hqk,qhd->khd", probs_low, d_mixed, preferred_element_type=F32)
    wide = d_scores.astype(F32)
    same_sum = jnp.sum(jnp.where(same, wide, 0.0), axis=(1, 2))
    diff_sum = jnp.sum(jnp.where(same, 0.0, wide), axis=(1, 2))
    bias_grad = psum_rows(jnp.stack([same_sum, diff_sum]))

    d_query_raw = rotate(d_queries, cosine, -sine).astype(BF16).reshape(length, proj)
    d_key_raw = rotate(d_keys, cosine, -sine).astype(BF16).reshape(length, proj)
    d_qkv = jnp.concatenate([d_query_raw, d_key_raw, d_values.astype(BF16).reshape(length, proj)], axis=1)
    d_normed_one = from_slots(scatter_rows(dot(d_qkv, qkv_full, 1, 1)))
    qkv_grad = scatter_weight(dot(rows_one, d_qkv, 0, 0).astype(BF16))
    d_input_norm, d_gain_one = norm_back(inputs, inv_one, gain_one, d_normed_one)
    in_grad = both_sequences((d_hidden + d_input_norm).astype(BF16))
    gain_grads = psum_all(jnp.stack([d_gain_one, d_gain_two]))
    return (
        layer_out,
        in_grad,
        gain_grads[0],
        gain_grads[1],
        qkv_grad[:, :proj],
        qkv_grad[:, proj : 2 * proj],
        qkv_grad[:, 2 * proj :],
        out_weight_grad,
        bias_grad,
        gate_grad,
        up_grad,
        down_grad,
    )


def solution(mesh):
    rows = P("fsdp", ("ctx", "tp"), None)
    weight = P(("fsdp", "ctx"), "tp")
    ids = P("fsdp", None)
    bias = P(None, "tp")
    in_specs = (rows, P(), P()) + (weight,) * 4 + (bias,) + (weight,) * 3 + (ids,) * 3 + (rows,)
    out_specs = (rows, rows, P(), P()) + (weight,) * 4 + (bias,) + (weight,) * 3
    return jax.shard_map(shards, mesh=mesh, in_specs=in_specs, out_specs=out_specs, check_vma=False)
```

```python
import functools
import jax
import jax.numpy as jnp
from jax import lax
from jax.sharding import PartitionSpec as P
from jax.experimental import pallas as pl
from jax.experimental.pallas import tpu as pltpu

HEADS = 16
HEAD = 64
EPS = 1e-05
NEG = -1e30
F32 = jnp.float32
BF16 = jnp.bfloat16
LANES = 128
QUERIES = 256
STEP = 128
VMEM_LIMIT = 56 * 1024 * 1024


def nt_dot(left, right):
    return lax.dot_general(left, right, (((1,), (1,)), ((), ())), preferred_element_type=F32)


def nn_dot(left, right):
    return lax.dot_general(left, right, (((1,), (0,)), ((), ())), preferred_element_type=F32)


def tn_dot(left, right):
    return lax.dot_general(left, right, (((0,), (0,)), ((), ())), preferred_element_type=F32)


def lane_of(shape):
    return lax.broadcasted_iota(jnp.int32, shape, len(shape) - 1)


def half_swap(values):
    lane = lane_of(values.shape)
    forward = pltpu.roll(values, LANES - HEAD // 2, 1)
    back = pltpu.roll(values, HEAD // 2, 1)
    return jnp.where(lane % HEAD < HEAD // 2, forward, back)


def fwd_kernel(row_parts, weight_parts, heads, *refs):
    tables, refs = refs[0], refs[1:]
    rows, refs = refs[:row_parts], refs[row_parts:]
    weights, refs = refs[:weight_parts], refs[weight_parts:]
    outs_w, refs = refs[:weight_parts], refs[weight_parts:]
    cosine, sine, seg_row, seg_wide, feature, coef = refs[:6]
    q_aug, k_aug, v_out, mixed_out, lse_out, keep_out, send_out = refs[6:13]
    full, out_full, mixed_wide, v_turn = refs[13:]
    pairs = heads // 2
    proj = heads * HEAD
    length = q_aug.shape[1]
    block = weights[0].shape[0]
    part = rows[0].shape[0]
    share = part // 2
    for i in range(weight_parts):
        full[i * block : (i + 1) * block, :] = weights[i][...]
        out_full[i * block : (i + 1) * block, :] = outs_w[i][...]
    for p in range(row_parts):
        raw = nn_dot(rows[p][...], full[...])
        for k in range(2):
            piece = raw[k * share : (k + 1) * share]
            start = pl.multiple_of(tables[0, 2 * p + k] * share, share)
            at = pl.ds(start, share)
            cos_now, sin_now, feat = cosine[at, :], sine[at, :], feature[at, :].astype(F32)
            lane = lane_of((share, LANES))
            for pair in range(pairs):
                low = pair * LANES
                q = piece[:, low : low + LANES]
                q = (q * cos_now + half_swap(q) * sin_now).astype(BF16).astype(F32) * HEAD**-0.5
                kk = piece[:, proj + low : proj + low + LANES]
                kk = kk * cos_now + half_swap(kk) * sin_now
                v_out[pair, at, :] = piece[:, 2 * proj + low : 2 * proj + low + LANES].astype(BF16)
                for odd in range(2):
                    head = 2 * pair + odd
                    q_now = pltpu.roll(q, HEAD, 1) if odd else q
                    k_now = pltpu.roll(kk, HEAD, 1) if odd else kk
                    q_feat = feat * coef[head : head + 1, :]
                    q_aug[head, at, :] = jnp.where(lane < HEAD, q_now, q_feat).astype(BF16)
                    k_aug[head, at, :] = jnp.where(lane < HEAD, k_now, feat).astype(BF16)
    for pair in range(pairs):
        for b in range(length // LANES):
            tile = v_out[pair, b * LANES : (b + 1) * LANES, :].astype(F32)
            v_turn[pair, :, b * LANES : (b + 1) * LANES] = tile.T.astype(BF16)

    def query_block(b, carry):
        at = pl.ds(pl.multiple_of(b * QUERIES, QUERIES), QUERIES)
        seg_q = seg_row[pl.ds(b, 1), :]
        first = pl.multiple_of(tables[1, b] * LANES, LANES)
        for kind in range(1, length // STEP + 1):

            @pl.when(tables[2, b] == kind)
            def _(kind=kind):
                win = pl.ds(first, kind * STEP)
                keep = seg_wide[win, :] == seg_q
                scores = [nt_dot(k_aug[h, win, :], q_aug[h, at, :]) for h in range(heads)]
                probs, totals = [], []
                for head in range(heads):
                    s = jnp.where(keep, scores[head], NEG)
                    top = jnp.max(s, axis=0, keepdims=True)
                    p = jnp.exp(s - top)
                    total = jnp.sum(p, axis=0, keepdims=True)
                    probs.append(p.astype(BF16))
                    totals.append(total)
                    lse_out[head, pl.ds(b, 1), :] = top + jnp.log(total)
                for pair in range(pairs):
                    outs = []
                    for odd in range(2):
                        head = 2 * pair + odd
                        turn = v_turn[pair, odd * HEAD : (odd + 1) * HEAD, win]
                        outs.append(nn_dot(turn, probs[head]) / totals[head])
                    mixed = jnp.concatenate(outs, axis=0).T
                    mixed_wide[at, pair * LANES : (pair + 1) * LANES] = mixed

        return carry

    lax.fori_loop(0, length // QUERIES, query_block, 0)
    for slot in range(2 * row_parts):
        start = pl.multiple_of(tables[0, slot] * share, share)
        piece = mixed_wide[pl.ds(start, share), :]
        mixed_out[slot * share : (slot + 1) * share, :] = piece.astype(BF16)
    half = row_parts // 2
    for p in range(row_parts):
        back = nt_dot(mixed_out[p * part : (p + 1) * part, :], out_full[...])
        if p < half:
            keep_out[p * part : (p + 1) * part, :] = back
        else:
            send_out[(p - half) * part : (p - half + 1) * part, :] = back.astype(BF16)


def vmem():
    return pl.BlockSpec(memory_space=pltpu.VMEM)


def smem():
    return pl.BlockSpec(memory_space=pltpu.SMEM)


def attention_forward(tables, rows, weights, outs_w, cosine, sine, seg_row, seg_wide, feature, coef, heads):
    proj = heads * HEAD
    length = cosine.shape[0]
    width = rows[0].shape[1]
    shapes = (
        jax.ShapeDtypeStruct((heads, length, LANES), BF16),
        jax.ShapeDtypeStruct((heads, length, LANES), BF16),
        jax.ShapeDtypeStruct((heads // 2, length, LANES), BF16),
        jax.ShapeDtypeStruct((length, proj), BF16),
        jax.ShapeDtypeStruct((heads, length // QUERIES, QUERIES), F32),
        jax.ShapeDtypeStruct((length // 2, width), F32),
        jax.ShapeDtypeStruct((length // 2, width), BF16),
    )
    count = len(rows) + 2 * len(weights) + 6
    return pl.pallas_call(
        functools.partial(fwd_kernel, len(rows), len(weights), heads),
        out_shape=shapes,
        in_specs=[smem()] + [vmem()] * count,
        out_specs=[vmem()] * 7,
        scratch_shapes=[
            pltpu.VMEM((width, 3 * proj), BF16),
            pltpu.VMEM((width, proj), BF16),
            pltpu.VMEM((length, proj), F32),
            pltpu.VMEM((heads // 2, LANES, length), BF16),
        ],
        compiler_params=pltpu.CompilerParams(vmem_limit_bytes=VMEM_LIMIT),
        cost_estimate=pl.CostEstimate(
            flops=2 * length * width * 3 * proj, bytes_accessed=8 << 20, transcendentals=length * length * heads // 2
        ),
        name="attn_fwd",
    )(tables, *rows, *weights, *outs_w, cosine, sine, seg_row, seg_wide, feature, coef)


def bwd_kernel(row_parts, weight_parts, heads, *refs):
    tables, refs = refs[0], refs[1:]
    rows, refs = refs[:row_parts], refs[row_parts:]
    outs_w, refs = refs[:weight_parts], refs[weight_parts:]
    weights, refs = refs[:weight_parts], refs[weight_parts:]
    q_aug, k_aug, v_in, lse, cosine, sine, seg_row, seg_wide, hot_rows = refs[:9]
    keep_out, send_out, d_qkv_out, bias_out = refs[9:13]
    full, out_full, d_out, k_turn, dq_acc, dk_acc, dv_acc = refs[13:]
    pairs = heads // 2
    proj = heads * HEAD
    length = q_aug.shape[1]
    block = weights[0].shape[0]
    part = rows[0].shape[0]
    share = part // 2
    for i in range(weight_parts):
        full[i * block : (i + 1) * block, :] = weights[i][...]
        out_full[i * block : (i + 1) * block, :] = outs_w[i][...]
    for p in range(row_parts):
        raw = nn_dot(rows[p][...], out_full[...]).astype(BF16)
        for k in range(2):
            start = pl.multiple_of(tables[0, 2 * p + k] * share, share)
            d_out[pl.ds(start, share), :] = raw[k * share : (k + 1) * share]
    for head in range(heads):
        for b in range(length // LANES):
            tile = k_aug[head, b * LANES : (b + 1) * LANES, :].astype(F32)
            k_turn[head, :, b * LANES : (b + 1) * LANES] = tile.T.astype(BF16)
    dk_acc[...] = jnp.zeros(dk_acc.shape, F32)
    dv_acc[...] = jnp.zeros(dv_acc.shape, F32)
    bias_out[...] = jnp.zeros(bias_out.shape, F32)

    def query_block(b, carry):
        at = pl.ds(pl.multiple_of(b * QUERIES, QUERIES), QUERIES)
        seg_q = seg_row[pl.ds(b, 1), :]
        hot = hot_rows[:, at]
        first = pl.multiple_of(tables[1, b] * LANES, LANES)
        for kind in range(1, length // STEP + 1):

            @pl.when(tables[2, b] == kind)
            def _(kind=kind):
                win = pl.ds(first, kind * STEP)
                keep = seg_wide[win, :] == seg_q
                owns = []
                for head in range(heads):
                    chunk = slice(head // 2 * LANES, (head // 2 + 1) * LANES)
                    d_pair = d_out[at, chunk]
                    lane = lane_of(d_pair.shape)
                    owns.append(jnp.where((lane >= HEAD) == (head % 2 == 1), d_pair, jnp.zeros_like(d_pair)))
                turned = []
                for base in range(0, heads, 2):
                    group = range(base, base + 2)
                    s = [nt_dot(k_aug[h, win, :], q_aug[h, at, :]) for h in group]
                    dp = [nt_dot(v_in[h // 2, win, :], owns[h]) for h in group]
                    low, ds = [], []
                    for i, h in enumerate(group):
                        p = jnp.exp(jnp.where(keep, s[i] - lse[h, pl.ds(b, 1), :], NEG))
                        low.append(p.astype(BF16))
                        ds.append((p * (dp[i] - jnp.sum(p * dp[i], axis=0, keepdims=True))).astype(BF16))
                    for i, h in enumerate(group):
                        if i % 2 == 0:
                            both = jnp.concatenate(low[i : i + 2], axis=1)
                            dv_acc[h // 2, win, :] += nn_dot(both, jnp.concatenate(owns[h : h + 2], axis=0))
                        dk_acc[h, win, :] += nn_dot(ds[i], q_aug[h, at, :])
                        dq = nn_dot(k_turn[h, :, win], ds[i])
                        turned.append(dq[:HEAD])
                        sums = dq[HEAD : HEAD + 8]
                        bias_out[h] += jnp.concatenate([sums * hot[:8], sums * hot[8:]], axis=0)
                for pair in range(pairs):
                    chunk = slice(pair * LANES, (pair + 1) * LANES)
                    dq_acc[at, chunk] = jnp.concatenate(turned[2 * pair : 2 * pair + 2], axis=0).T * HEAD**-0.5

        return carry

    lax.fori_loop(0, length // QUERIES, query_block, 0)
    for p in range(row_parts):
        for k in range(2):
            slot = 2 * p + k
            at = pl.ds(pl.multiple_of(tables[0, slot] * share, share), share)
            to = slice(slot * share, (slot + 1) * share)
            cos_now, sin_now = cosine[at, :], sine[at, :]
            lane = lane_of((share, LANES))
            for pair in range(pairs):
                low = pair * LANES
                dq = dq_acc[at, low : low + LANES]
                dk = jnp.where(lane < HEAD, dk_acc[2 * pair, at, :], pltpu.roll(dk_acc[2 * pair + 1, at, :], HEAD, 1))
                d_qkv_out[to, low : low + LANES] = (dq * cos_now - half_swap(dq) * sin_now).astype(BF16)
                d_qkv_out[to, proj + low : proj + low + LANES] = (dk * cos_now - half_swap(dk) * sin_now).astype(BF16)
                d_qkv_out[to, 2 * proj + low : 2 * proj + low + LANES] = dv_acc[pair, at, :].astype(BF16)
        part_rows = d_qkv_out[p * part : (p + 1) * part, :]
        back = nt_dot(part_rows, full[...])
        half = row_parts // 2
        if p < half:
            keep_out[p * part : (p + 1) * part, :] = back
        else:
            send_out[(p - half) * part : (p - half + 1) * part, :] = back.astype(BF16)


def attention_backward(tables, rows, outs_w, weights, q_aug, k_aug, v_in, lse, cosine, sine, seg_row, seg_wide, hot_rows, heads):
    proj = heads * HEAD
    length = cosine.shape[0]
    width = rows[0].shape[1]
    shapes = (
        jax.ShapeDtypeStruct((length // 2, width), F32),
        jax.ShapeDtypeStruct((length // 2, width), BF16),
        jax.ShapeDtypeStruct((length, 3 * proj), BF16),
        jax.ShapeDtypeStruct((heads, 16, QUERIES), F32),
    )
    count = len(rows) + 2 * len(weights) + 9
    return pl.pallas_call(
        functools.partial(bwd_kernel, len(rows), len(weights), heads),
        out_shape=shapes,
        in_specs=[smem()] + [vmem()] * count,
        out_specs=[vmem()] * 4,
        scratch_shapes=[
            pltpu.VMEM((width, 3 * proj), BF16),
            pltpu.VMEM((width, proj), BF16),
            pltpu.VMEM((length, proj), BF16),
            pltpu.VMEM((heads, LANES, length), BF16),
            pltpu.VMEM((length, proj), F32),
            pltpu.VMEM((heads, length, LANES), F32),
            pltpu.VMEM((heads // 2, length, LANES), F32),
        ],
        compiler_params=pltpu.CompilerParams(vmem_limit_bytes=VMEM_LIMIT),
        cost_estimate=pl.CostEstimate(
            flops=2 * length * width * 4 * proj, bytes_accessed=12 << 20, transcendentals=length * length * heads // 2
        ),
        name="attn_bwd",
    )(tables, *rows, *outs_w, *weights, q_aug, k_aug, v_in, lse, cosine, sine, seg_row, seg_wide, hot_rows)


def attention_tables(segments, variates, times, variate_bias, order, share):
    length = segments.shape[0]
    heads = variate_bias.shape[1]
    count = length // QUERIES
    half = HEAD // 2
    frequency = 10000.0 ** (-2.0 * jnp.arange(half, dtype=F32) / HEAD)
    angles = times.astype(F32)[:, None] * frequency
    cos_half, sin_half = jnp.cos(angles), jnp.sin(angles)
    cosine = jnp.concatenate([cos_half] * 4, axis=1)
    sine = jnp.concatenate([-sin_half, sin_half] * 2, axis=1)
    seg_row = segments.reshape(count, QUERIES)
    seg_wide = jnp.broadcast_to(segments[:, None], (length, QUERIES))
    lane = jnp.arange(LANES)
    live = (lane >= HEAD) & (lane < HEAD + 12)
    feature = ((variates[:, None] == (lane % 4)[None, :]) & live[None, :]).astype(BF16)
    gap = variate_bias[0] - variate_bias[1]
    high = lax.reduce_precision(gap, 8, 7)
    mid = lax.reduce_precision(gap - high, 8, 7)
    low = lax.reduce_precision(gap - high - mid, 8, 7)
    parts = jnp.repeat(jnp.stack([high, mid, low], axis=1), 4, axis=1)
    coef = jnp.pad(parts, ((0, -heads % 8), (HEAD, LANES - HEAD - 12)))
    kinds = jnp.arange(4)
    same = (variates[None, :] == kinds[:, None]).astype(F32)
    zeros = jnp.zeros_like(same)
    hot_rows = jnp.concatenate([same, zeros, 1.0 - same, zeros], axis=0)
    ends = segments.reshape(count, QUERIES)
    start = jnp.sum(segments[None, :] < ends[:, :1], axis=1)
    stop = jnp.sum(segments[None, :] <= ends[:, -1:], axis=1)
    first = start // LANES
    kind = (stop - first * LANES + STEP - 1) // STEP
    first = jnp.minimum(first, (length - kind * STEP) // LANES)
    size = max(count, order.shape[0])
    pad = lambda a: jnp.pad(a.astype(jnp.int32), (0, size - a.shape[0]))
    tables = jnp.stack([pad(order), pad(first), pad(kind)])
    return tables, cosine, sine, seg_row, seg_wide, feature, coef, hot_rows

def ffn_kernel(row_parts, weight_parts, *refs):
    rows, refs = refs[:row_parts], refs[row_parts:]
    grads, refs = refs[:row_parts], refs[row_parts:]
    gates, refs = refs[:weight_parts], refs[weight_parts:]
    ups, refs = refs[:weight_parts], refs[weight_parts:]
    downs, refs = refs[:weight_parts], refs[weight_parts:]
    act_out, d_gate_out, d_up_out, keep_out, send_out, gate_full, up_full, down_full = refs
    block = gates[0].shape[0]
    part = rows[0].shape[0]
    for i in range(weight_parts):
        at = slice(i * block, (i + 1) * block)
        gate_full[at, :] = gates[i][...]
        up_full[at, :] = ups[i][...]
        down_full[at, :] = downs[i][...]
    half = row_parts // 2
    for p in list(range(half, row_parts)) + list(range(half)):
        at = slice(p * part, (p + 1) * part)
        gate = nn_dot(rows[p][...], gate_full[...])
        up = nn_dot(rows[p][...], up_full[...])
        d_act = nn_dot(grads[p][...], down_full[...])
        sig = 1.0 / (1.0 + jnp.exp(-gate))
        silu = gate * sig
        act_out[at, :] = (silu * up).astype(BF16)
        d_gate_out[at, :] = (d_act * up * (sig + silu * (1.0 - sig))).astype(BF16)
        d_up_out[at, :] = (d_act * silu).astype(BF16)
        back = nt_dot(d_gate_out[at, :], gate_full[...]) + nt_dot(d_up_out[at, :], up_full[...])
        if p < half:
            keep_out[at, :] = back
        else:
            send_out[(p - half) * part : (p - half + 1) * part, :] = back.astype(BF16)


def ffn_middle(rows, grads, gates, ups, downs):
    part, width = rows[0].shape
    length = part * len(rows)
    hidden = gates[0].shape[1]
    units = jax.ShapeDtypeStruct((length, hidden), BF16)
    return pl.pallas_call(
        functools.partial(ffn_kernel, len(rows), len(gates)),
        out_shape=(
            units,
            units,
            units,
            jax.ShapeDtypeStruct((length // 2, width), F32),
            jax.ShapeDtypeStruct((length // 2, width), BF16),
        ),
        in_specs=[vmem()] * (2 * len(rows) + 3 * len(gates)),
        out_specs=[vmem()] * 5,
        scratch_shapes=[pltpu.VMEM((width, hidden), BF16)] * 3,
        compiler_params=pltpu.CompilerParams(vmem_limit_bytes=VMEM_LIMIT),
        cost_estimate=pl.CostEstimate(
            flops=10 * length * width * hidden, bytes_accessed=20 << 20, transcendentals=length * hidden
        ),
        name="ffn_middle",
    )(*rows, *grads, *gates, *ups, *downs)


def grad_kernel(row_parts, blocks, *refs):
    rows, refs = refs[:row_parts], refs[row_parts:]
    right, refs = refs[0], refs[1:]
    keeps, send, left = refs[:blocks], refs[blocks], refs[blocks + 1]
    part, width = rows[0].shape
    for p in range(row_parts):
        for c in range(width // LANES):
            tile = rows[p][:, c * LANES : (c + 1) * LANES].astype(F32)
            left[c * LANES : (c + 1) * LANES, p * part : (p + 1) * part] = tile.T.astype(BF16)
    step = width // 4
    block = keeps[0].shape[0]
    send[: step, :] = nn_dot(left[2 * step : 3 * step, :], right[...]).astype(BF16)
    send[step :, :] = nn_dot(left[3 * step :, :], right[...]).astype(BF16)
    for s in range(2):
        both = nn_dot(left[s * step : (s + 1) * step, :], right[...])
        for k in range(step // block):
            keeps[s * step // block + k][...] = both[k * block : (k + 1) * block].astype(keeps[0].dtype)


def weight_partials(rows, right, blocks):
    part, width = rows[0].shape
    length, cols = right.shape
    block = width // (2 * blocks)
    return pl.pallas_call(
        functools.partial(grad_kernel, len(rows), blocks),
        out_shape=(jax.ShapeDtypeStruct((block, cols), BF16),) * blocks
        + (jax.ShapeDtypeStruct((width // 2, cols), BF16),),
        in_specs=[vmem()] * (len(rows) + 1),
        out_specs=[vmem()] * (blocks + 1),
        scratch_shapes=[pltpu.VMEM((width, length), BF16)],
        compiler_params=pltpu.CompilerParams(vmem_limit_bytes=VMEM_LIMIT),
        cost_estimate=pl.CostEstimate(
            flops=2 * length * width * cols, bytes_accessed=8 << 20, transcendentals=0
        ),
        name="weight_partials",
    )(*rows, right)


def hop(values, axis, flip):
    size = lax.axis_size(axis)
    return lax.ppermute(values, axis, [(i, i ^ flip) for i in range(size)])


def swap_blocks(values, axis, index, size):
    shape = values.shape
    bit = 1
    while bit < size:
        split = shape[:axis] + (size // (2 * bit), 2, bit) + shape[axis + 1 :]
        cut = values.reshape(split)
        cut = jnp.where((index & bit) != 0, jnp.flip(cut, axis + 1), cut)
        values = cut.reshape(shape)
        bit *= 2
    return values


def gather_weight(block):
    nz = lax.axis_size("fsdp")
    mine = [block] + [hop(block, "fsdp", k) for k in range(1, nz)]
    return mine + [hop(piece, "ctx", 1) for piece in mine]


def scatter_weight(partials):
    keeps, send = partials[:-1], partials[-1]
    rows = keeps[0].shape[0]
    other = hop(send, "ctx", 1)
    out = None
    for k, keep in enumerate(keeps):
        total = keep.astype(F32) + other[k * rows : (k + 1) * rows].astype(F32)
        if k == 0:
            out = total
        else:
            out = out + hop(total.astype(BF16), "fsdp", k).astype(F32)
    return out


def gather_rows(block):
    nt = lax.axis_size("tp")
    mine = [block] + [hop(block, "tp", 2 * k) for k in range(1, nt // 2)]
    return mine + [hop(piece, "tp", 1) for piece in mine]


def scatter_rows(keep, send):
    nt = lax.axis_size("tp")
    rows = 2 * keep.shape[0] // nt
    other = hop(send, "tp", 1)
    total = keep + other.astype(F32)
    out = total[:rows]
    for k in range(1, nt // 2):
        out = out + hop(total[k * rows : (k + 1) * rows].astype(BF16), "tp", 2 * k).astype(F32)
    return out


def psum_over(values, axes):
    for axis in axes:
        bit = 1
        while bit < lax.axis_size(axis):
            values = values + hop(values, axis, bit)
            bit *= 2
    return values


def inverse_rms(values):
    return lax.rsqrt(jnp.mean(values * values, axis=-1, keepdims=True) + EPS)


def norm_back(values, inv, gain, grad):
    scaled = grad * gain
    normed = values * inv
    d_gain = jnp.sum(grad * normed, axis=0, keepdims=True)
    d_values = inv * (scaled - normed * jnp.mean(scaled * normed, axis=-1, keepdims=True))
    return d_values, d_gain


def shards(
    layer_in,
    attn_gain,
    ffn_gain,
    query_weight,
    key_weight,
    value_weight,
    out_weight,
    variate_bias,
    gate_weight,
    up_weight,
    down_weight,
    segment_ids,
    variate_ids,
    time_ids,
    out_grad,
):
    seq_count, share, width = layer_in.shape
    nz, nx, nt = lax.axis_size("fsdp"), lax.axis_size("ctx"), lax.axis_size("tp")
    iz, ix, it = lax.axis_index("fsdp"), lax.axis_index("ctx"), lax.axis_index("tp")
    assert nx == 2 and seq_count == nx
    length = segment_ids.shape[1]
    heads = variate_bias.shape[1]
    proj = heads * HEAD

    def to_slots(values):
        cut = values.reshape(values.shape[0], nz, nx, width // (nz * nx))
        cut = swap_blocks(swap_blocks(cut, 1, iz, nz), 2, ix, nx)
        return cut.transpose(0, 2, 1, 3).reshape(values.shape)

    def from_slots(values):
        cut = values.reshape(values.shape[0], nx, nz, width // (nz * nx)).transpose(0, 2, 1, 3)
        return swap_blocks(swap_blocks(cut, 1, iz, nz), 2, ix, nx).reshape(values.shape)

    def own_sequence(values):
        mine = lax.dynamic_index_in_dim(values, ix, 0, keepdims=False)
        other = lax.dynamic_index_in_dim(values, 1 - ix, 0, keepdims=False)
        return to_slots(jnp.concatenate([mine, hop(other, "ctx", 1)], axis=0))

    def both_sequences(values):
        values = from_slots(values)
        mine, other = values[:share], hop(values[share:], "ctx", 1)
        first = jnp.where(ix == 0, mine, other)
        second = jnp.where(ix == 0, other, mine)
        return jnp.stack([first, second])

    def own_ids(table):
        return lax.dynamic_index_in_dim(table, ix, 0, keepdims=False)

    order = jnp.arange(nx * nt).reshape(nx, nt // 2, 2)
    order = swap_blocks(swap_blocks(swap_blocks(order, 0, ix, nx), 1, it // 2, nt // 2), 2, it % 2, 2)
    order = order.transpose(2, 1, 0).reshape(nx * nt)
    tables, cosine, sine, seg_row, seg_wide, feature, coef, hot_rows = attention_tables(
        own_ids(segment_ids), own_ids(variate_ids), own_ids(time_ids), variate_bias, order, share
    )
    gain_one = to_slots(attn_gain.astype(F32)[None])
    gain_two = to_slots(ffn_gain.astype(F32)[None])
    low_inputs = own_sequence(layer_in)
    inputs = low_inputs.astype(F32)
    inv_one = inverse_rms(inputs)
    rows_one = gather_rows((inputs * inv_one * gain_one).astype(BF16))
    qkv_w = gather_weight(jnp.concatenate([query_weight, key_weight, value_weight], axis=1))
    out_w = gather_weight(out_weight)
    gate_w = gather_weight(gate_weight)
    up_w = gather_weight(up_weight)
    down_w = gather_weight(down_weight)
    grads = own_sequence(out_grad)
    grad_rows = gather_rows(grads)

    q_aug, k_aug, v_rows, mixed, lse, keep, send = attention_forward(
        tables, rows_one, qkv_w, out_w, cosine, sine, seg_row, seg_wide, feature, coef, heads
    )
    hidden = inputs + scatter_rows(keep, send)
    inv_two = inverse_rms(hidden)
    rows_two = gather_rows((hidden * inv_two * gain_two).astype(BF16))
    act, d_gate, d_up, keep, send = ffn_middle(rows_two, grad_rows, gate_w, up_w, down_w)
    d_normed_two = scatter_rows(keep, send)
    down_grad = scatter_weight(weight_partials(grad_rows, act, nz))
    gate_grad = scatter_weight(weight_partials(rows_two, d_gate, nz))
    up_grad = scatter_weight(weight_partials(rows_two, d_up, nz))

    down_full = jnp.concatenate(down_w, axis=0)
    ffn = lax.dot_general(act, down_full, (((1,), (1,)), ((), ())), preferred_element_type=F32)
    ffn = scatter_rows(ffn[: length // 2], ffn[length // 2 :].astype(BF16))
    layer_out = both_sequences((hidden + ffn).astype(BF16))

    d_hidden_norm, d_gain_two = norm_back(hidden, inv_two, gain_two, d_normed_two)
    d_hidden = grads.astype(F32) + d_hidden_norm
    branch_rows = gather_rows(d_hidden.astype(BF16))
    keep, send, d_qkv, bias_parts = attention_backward(
        tables, branch_rows, out_w, qkv_w, q_aug, k_aug, v_rows, lse, cosine, sine, seg_row, seg_wide, hot_rows, heads
    )
    d_normed_one = scatter_rows(keep, send)
    out_weight_grad = scatter_weight(weight_partials(branch_rows, mixed, nz))
    qkv_grad = scatter_weight(weight_partials(rows_one, d_qkv, nz))
    sums = jnp.sum(bias_parts, axis=2)
    bias_grad = jnp.stack([jnp.sum(sums[:, :8], axis=1), jnp.sum(sums[:, 8:], axis=1)])
    bias_grad = psum_over(bias_grad, ("ctx", "fsdp"))

    d_input_norm, d_gain_one = norm_back(inputs, inv_one, gain_one, d_normed_one)
    in_grad = both_sequences((d_hidden + d_input_norm).astype(BF16))
    gain_grads = from_slots(jnp.concatenate([d_gain_one, d_gain_two], axis=0))
    gain_grads = psum_over(gain_grads, ("tp", "ctx", "fsdp"))
    return (
        layer_out,
        in_grad,
        gain_grads[0],
        gain_grads[1],
        qkv_grad[:, :proj],
        qkv_grad[:, proj : 2 * proj],
        qkv_grad[:, 2 * proj :],
        out_weight_grad,
        bias_grad,
        gate_grad,
        up_grad,
        down_grad,
    )


def solution(mesh):
    rows = P("fsdp", ("ctx", "tp"), None)
    weight = P(("fsdp", "ctx"), "tp")
    ids = P("fsdp", None)
    bias = P(None, "tp")
    in_specs = (rows, P(), P()) + (weight,) * 4 + (bias,) + (weight,) * 3 + (ids,) * 3 + (rows,)
    out_specs = (rows, rows, P(), P()) + (weight,) * 4 + (bias,) + (weight,) * 3
    return jax.shard_map(shards, mesh=mesh, in_specs=in_specs, out_specs=out_specs, check_vma=False)
```

```python
import functools
import jax
import jax.numpy as jnp
from jax import lax
from jax.sharding import PartitionSpec as P
from jax.experimental import pallas as pl
from jax.experimental.pallas import tpu as pltpu

HEADS = 16
HEAD = 64
EPS = 1e-05
NEG = -1e30
F32 = jnp.float32
BF16 = jnp.bfloat16
LANES = 128
QUERIES = 256
STEP = 128
VMEM_LIMIT = 56 * 1024 * 1024


def nt_dot(left, right):
    return lax.dot_general(left, right, (((1,), (1,)), ((), ())), preferred_element_type=F32)


def nn_dot(left, right):
    return lax.dot_general(left, right, (((1,), (0,)), ((), ())), preferred_element_type=F32)


def tn_dot(left, right):
    return lax.dot_general(left, right, (((0,), (0,)), ((), ())), preferred_element_type=F32)


def lane_of(shape):
    return lax.broadcasted_iota(jnp.int32, shape, len(shape) - 1)


def half_swap(values):
    lane = lane_of(values.shape)
    forward = pltpu.roll(values, LANES - HEAD // 2, 1)
    back = pltpu.roll(values, HEAD // 2, 1)
    return jnp.where(lane % HEAD < HEAD // 2, forward, back)


def fwd_kernel(row_parts, weight_parts, heads, *refs):
    tables, refs = refs[0], refs[1:]
    rows, refs = refs[:row_parts], refs[row_parts:]
    weights, refs = refs[:weight_parts], refs[weight_parts:]
    cosine, sine, seg_row, seg_wide, feature, coef = refs[:6]
    q_aug, k_aug, v_out, mixed_out, lse_out, keep_out, send_out = refs[6:13]
    full, out_full, mixed_wide, v_turn = refs[13:]
    pairs = heads // 2
    proj = heads * HEAD
    length = q_aug.shape[1]
    block = weights[0].shape[0]
    part = rows[0].shape[0]
    share = part // 2
    for i in range(weight_parts):
        at = pl.ds(pl.multiple_of(tables[3, i] * block, block), block)
        full[at, :] = weights[i][:, : 3 * proj]
        out_full[at, :] = weights[i][:, 3 * proj :]
    for p in range(row_parts):
        raw = nn_dot(rows[p][...], full[...])
        for k in range(2):
            piece = raw[k * share : (k + 1) * share]
            start = pl.multiple_of(tables[0, 2 * p + k] * share, share)
            at = pl.ds(start, share)
            cos_now, sin_now, feat = cosine[at, :], sine[at, :], feature[at, :].astype(F32)
            lane = lane_of((share, LANES))
            for pair in range(pairs):
                low = pair * LANES
                q = piece[:, low : low + LANES]
                q = (q * cos_now + half_swap(q) * sin_now).astype(BF16).astype(F32) * HEAD**-0.5
                kk = piece[:, proj + low : proj + low + LANES]
                kk = kk * cos_now + half_swap(kk) * sin_now
                v_out[pair, at, :] = piece[:, 2 * proj + low : 2 * proj + low + LANES].astype(BF16)
                for odd in range(2):
                    head = 2 * pair + odd
                    q_now = pltpu.roll(q, HEAD, 1) if odd else q
                    k_now = pltpu.roll(kk, HEAD, 1) if odd else kk
                    q_feat = feat * coef[head : head + 1, :]
                    q_aug[head, at, :] = jnp.where(lane < HEAD, q_now, q_feat).astype(BF16)
                    k_aug[head, at, :] = jnp.where(lane < HEAD, k_now, feat).astype(BF16)
    for pair in range(pairs):
        for b in range(length // LANES):
            tile = v_out[pair, b * LANES : (b + 1) * LANES, :].astype(F32)
            v_turn[pair, :, b * LANES : (b + 1) * LANES] = tile.T.astype(BF16)

    def query_block(b, carry):
        at = pl.ds(pl.multiple_of(b * QUERIES, QUERIES), QUERIES)
        seg_q = seg_row[pl.ds(b, 1), :]
        first = pl.multiple_of(tables[1, b] * LANES, LANES)
        for kind in range(1, length // STEP + 1):

            @pl.when(tables[2, b] == kind)
            def _(kind=kind):
                win = pl.ds(first, kind * STEP)
                keep = seg_wide[win, :] == seg_q
                scores = [nt_dot(k_aug[h, win, :], q_aug[h, at, :]) for h in range(heads)]
                probs, totals = [], []
                for head in range(heads):
                    s = jnp.where(keep, scores[head], NEG)
                    top = jnp.max(s, axis=0, keepdims=True)
                    p = jnp.exp(s - top)
                    total = jnp.sum(p, axis=0, keepdims=True)
                    probs.append(p.astype(BF16))
                    totals.append(total)
                    lse_out[head, pl.ds(b, 1), :] = top + jnp.log(total)
                for pair in range(pairs):
                    outs = []
                    for odd in range(2):
                        head = 2 * pair + odd
                        turn = v_turn[pair, odd * HEAD : (odd + 1) * HEAD, win]
                        outs.append(nn_dot(turn, probs[head]) / totals[head])
                    mixed = jnp.concatenate(outs, axis=0).T
                    mixed_wide[at, pair * LANES : (pair + 1) * LANES] = mixed

        return carry

    lax.fori_loop(0, length // QUERIES, query_block, 0)
    for slot in range(2 * row_parts):
        start = pl.multiple_of(tables[0, slot] * share, share)
        piece = mixed_wide[pl.ds(start, share), :]
        mixed_out[slot * share : (slot + 1) * share, :] = piece.astype(BF16)
    half = row_parts // 2
    for p in range(row_parts):
        back = nt_dot(mixed_out[p * part : (p + 1) * part, :], out_full[...])
        if p < half:
            keep_out[p * part : (p + 1) * part, :] = back
        else:
            send_out[(p - half) * part : (p - half + 1) * part, :] = back.astype(BF16)


def vmem():
    return pl.BlockSpec(memory_space=pltpu.VMEM)


def smem():
    return pl.BlockSpec(memory_space=pltpu.SMEM)


def attention_forward(tables, rows, weights, cosine, sine, seg_row, seg_wide, feature, coef, heads):
    proj = heads * HEAD
    length = cosine.shape[0]
    width = rows[0].shape[1]
    shapes = (
        jax.ShapeDtypeStruct((heads, length, LANES), BF16),
        jax.ShapeDtypeStruct((heads, length, LANES), BF16),
        jax.ShapeDtypeStruct((heads // 2, length, LANES), BF16),
        jax.ShapeDtypeStruct((length, proj), BF16),
        jax.ShapeDtypeStruct((heads, length // QUERIES, QUERIES), F32),
        jax.ShapeDtypeStruct((length // 2, width), F32),
        jax.ShapeDtypeStruct((length // 2, width), BF16),
    )
    count = len(rows) + len(weights) + 6
    return pl.pallas_call(
        functools.partial(fwd_kernel, len(rows), len(weights), heads),
        out_shape=shapes,
        in_specs=[smem()] + [vmem()] * count,
        out_specs=[vmem()] * 7,
        scratch_shapes=[
            pltpu.VMEM((width, 3 * proj), BF16),
            pltpu.VMEM((width, proj), BF16),
            pltpu.VMEM((length, proj), F32),
            pltpu.VMEM((heads // 2, LANES, length), BF16),
        ],
        compiler_params=pltpu.CompilerParams(vmem_limit_bytes=VMEM_LIMIT),
        cost_estimate=pl.CostEstimate(
            flops=2 * length * width * 3 * proj, bytes_accessed=8 << 20, transcendentals=length * length * heads // 2
        ),
        name="attn_fwd",
    )(tables, *rows, *weights, cosine, sine, seg_row, seg_wide, feature, coef)


def bwd_kernel(row_parts, weight_parts, heads, *refs):
    tables, refs = refs[0], refs[1:]
    rows, refs = refs[:row_parts], refs[row_parts:]
    weights, refs = refs[:weight_parts], refs[weight_parts:]
    q_aug, k_aug, v_in, lse, cosine, sine, seg_row, seg_wide, hot_rows = refs[:9]
    keep_out, send_out, d_qkv_out, bias_out = refs[9:13]
    full, out_full, d_out, k_turn, dq_acc, dk_acc, dv_acc = refs[13:]
    pairs = heads // 2
    proj = heads * HEAD
    length = q_aug.shape[1]
    block = weights[0].shape[0]
    part = rows[0].shape[0]
    share = part // 2
    for i in range(weight_parts):
        at = pl.ds(pl.multiple_of(tables[3, i] * block, block), block)
        full[at, :] = weights[i][:, : 3 * proj]
        out_full[at, :] = weights[i][:, 3 * proj :]
    for p in range(row_parts):
        raw = nn_dot(rows[p][...], out_full[...]).astype(BF16)
        for k in range(2):
            start = pl.multiple_of(tables[0, 2 * p + k] * share, share)
            d_out[pl.ds(start, share), :] = raw[k * share : (k + 1) * share]
    for head in range(heads):
        for b in range(length // LANES):
            tile = k_aug[head, b * LANES : (b + 1) * LANES, :].astype(F32)
            k_turn[head, :, b * LANES : (b + 1) * LANES] = tile.T.astype(BF16)
    dk_acc[...] = jnp.zeros(dk_acc.shape, F32)
    dv_acc[...] = jnp.zeros(dv_acc.shape, F32)
    bias_out[...] = jnp.zeros(bias_out.shape, F32)

    def query_block(b, carry):
        at = pl.ds(pl.multiple_of(b * QUERIES, QUERIES), QUERIES)
        seg_q = seg_row[pl.ds(b, 1), :]
        hot = hot_rows[:, at]
        first = pl.multiple_of(tables[1, b] * LANES, LANES)
        for kind in range(1, length // STEP + 1):

            @pl.when(tables[2, b] == kind)
            def _(kind=kind):
                win = pl.ds(first, kind * STEP)
                keep = seg_wide[win, :] == seg_q
                owns = []
                for head in range(heads):
                    chunk = slice(head // 2 * LANES, (head // 2 + 1) * LANES)
                    d_pair = d_out[at, chunk]
                    lane = lane_of(d_pair.shape)
                    owns.append(jnp.where((lane >= HEAD) == (head % 2 == 1), d_pair, jnp.zeros_like(d_pair)))
                turned = []
                for base in range(0, heads, 2):
                    group = range(base, base + 2)
                    s = [nt_dot(k_aug[h, win, :], q_aug[h, at, :]) for h in group]
                    dp = [nt_dot(v_in[h // 2, win, :], owns[h]) for h in group]
                    low, ds = [], []
                    for i, h in enumerate(group):
                        p = jnp.exp(jnp.where(keep, s[i] - lse[h, pl.ds(b, 1), :], NEG))
                        low.append(p.astype(BF16))
                        ds.append((p * (dp[i] - jnp.sum(p * dp[i], axis=0, keepdims=True))).astype(BF16))
                    for i, h in enumerate(group):
                        if i % 2 == 0:
                            both = jnp.concatenate(low[i : i + 2], axis=1)
                            dv_acc[h // 2, win, :] += nn_dot(both, jnp.concatenate(owns[h : h + 2], axis=0))
                        dk_acc[h, win, :] += nn_dot(ds[i], q_aug[h, at, :])
                        dq = nn_dot(k_turn[h, :, win], ds[i])
                        turned.append(dq[:HEAD])
                        sums = dq[HEAD : HEAD + 8]
                        bias_out[h] += jnp.concatenate([sums * hot[:8], sums * hot[8:]], axis=0)
                for pair in range(pairs):
                    chunk = slice(pair * LANES, (pair + 1) * LANES)
                    dq_acc[at, chunk] = jnp.concatenate(turned[2 * pair : 2 * pair + 2], axis=0).T * HEAD**-0.5

        return carry

    lax.fori_loop(0, length // QUERIES, query_block, 0)
    for p in range(row_parts):
        for k in range(2):
            slot = 2 * p + k
            at = pl.ds(pl.multiple_of(tables[0, slot] * share, share), share)
            to = slice(slot * share, (slot + 1) * share)
            cos_now, sin_now = cosine[at, :], sine[at, :]
            lane = lane_of((share, LANES))
            for pair in range(pairs):
                low = pair * LANES
                dq = dq_acc[at, low : low + LANES]
                dk = jnp.where(lane < HEAD, dk_acc[2 * pair, at, :], pltpu.roll(dk_acc[2 * pair + 1, at, :], HEAD, 1))
                d_qkv_out[to, low : low + LANES] = (dq * cos_now - half_swap(dq) * sin_now).astype(BF16)
                d_qkv_out[to, proj + low : proj + low + LANES] = (dk * cos_now - half_swap(dk) * sin_now).astype(BF16)
                d_qkv_out[to, 2 * proj + low : 2 * proj + low + LANES] = dv_acc[pair, at, :].astype(BF16)
        part_rows = d_qkv_out[p * part : (p + 1) * part, :]
        back = nt_dot(part_rows, full[...])
        half = row_parts // 2
        if p < half:
            keep_out[p * part : (p + 1) * part, :] = back
        else:
            send_out[(p - half) * part : (p - half + 1) * part, :] = back.astype(BF16)


def attention_backward(tables, rows, weights, q_aug, k_aug, v_in, lse, cosine, sine, seg_row, seg_wide, hot_rows, heads):
    proj = heads * HEAD
    length = cosine.shape[0]
    width = rows[0].shape[1]
    shapes = (
        jax.ShapeDtypeStruct((length // 2, width), F32),
        jax.ShapeDtypeStruct((length // 2, width), BF16),
        jax.ShapeDtypeStruct((length, 3 * proj), BF16),
        jax.ShapeDtypeStruct((heads, 16, QUERIES), F32),
    )
    count = len(rows) + len(weights) + 9
    return pl.pallas_call(
        functools.partial(bwd_kernel, len(rows), len(weights), heads),
        out_shape=shapes,
        in_specs=[smem()] + [vmem()] * count,
        out_specs=[vmem()] * 4,
        scratch_shapes=[
            pltpu.VMEM((width, 3 * proj), BF16),
            pltpu.VMEM((width, proj), BF16),
            pltpu.VMEM((length, proj), BF16),
            pltpu.VMEM((heads, LANES, length), BF16),
            pltpu.VMEM((length, proj), F32),
            pltpu.VMEM((heads, length, LANES), F32),
            pltpu.VMEM((heads // 2, length, LANES), F32),
        ],
        compiler_params=pltpu.CompilerParams(vmem_limit_bytes=VMEM_LIMIT),
        cost_estimate=pl.CostEstimate(
            flops=2 * length * width * 4 * proj, bytes_accessed=12 << 20, transcendentals=length * length * heads // 2
        ),
        name="attn_bwd",
    )(tables, *rows, *weights, q_aug, k_aug, v_in, lse, cosine, sine, seg_row, seg_wide, hot_rows)


def attention_tables(segments, variates, times, variate_bias, order, places):
    length = segments.shape[0]
    heads = variate_bias.shape[1]
    count = length // QUERIES
    half = HEAD // 2
    frequency = 10000.0 ** (-2.0 * jnp.arange(half, dtype=F32) / HEAD)
    angles = times.astype(F32)[:, None] * frequency
    cos_half, sin_half = jnp.cos(angles), jnp.sin(angles)
    cosine = jnp.concatenate([cos_half] * 4, axis=1)
    sine = jnp.concatenate([-sin_half, sin_half] * 2, axis=1)
    seg_row = segments.reshape(count, QUERIES)
    seg_wide = jnp.broadcast_to(segments[:, None], (length, QUERIES))
    lane = jnp.arange(LANES)
    live = (lane >= HEAD) & (lane < HEAD + 12)
    feature = ((variates[:, None] == (lane % 4)[None, :]) & live[None, :]).astype(BF16)
    gap = variate_bias[0] - variate_bias[1]
    high = lax.reduce_precision(gap, 8, 7)
    mid = lax.reduce_precision(gap - high, 8, 7)
    low = lax.reduce_precision(gap - high - mid, 8, 7)
    parts = jnp.repeat(jnp.stack([high, mid, low], axis=1), 4, axis=1)
    coef = jnp.pad(parts, ((0, -heads % 8), (HEAD, LANES - HEAD - 12)))
    kinds = jnp.arange(4)
    same = (variates[None, :] == kinds[:, None]).astype(F32)
    zeros = jnp.zeros_like(same)
    hot_rows = jnp.concatenate([same, zeros, 1.0 - same, zeros], axis=0)
    ends = segments.reshape(count, QUERIES)
    start = jnp.sum(segments[None, :] < ends[:, :1], axis=1)
    stop = jnp.sum(segments[None, :] <= ends[:, -1:], axis=1)
    first = start // LANES
    kind = (stop - first * LANES + STEP - 1) // STEP
    first = jnp.minimum(first, (length - kind * STEP) // LANES)
    size = max(count, order.shape[0], places.shape[0])
    pad = lambda a: jnp.pad(a.astype(jnp.int32), (0, size - a.shape[0]))
    tables = jnp.stack([pad(order), pad(first), pad(kind), pad(places)])
    return tables, cosine, sine, seg_row, seg_wide, feature, coef, hot_rows


def ffn_kernel(row_parts, seq, *refs):
    rows, refs = refs[:row_parts], refs[row_parts:]
    grads, refs = refs[:row_parts], refs[row_parts:]
    weight, act_out, d_both_out, keep_out, send_out = refs
    part = rows[0].shape[0]
    cols = act_out.shape[1]
    half = row_parts // 2
    for p in list(range(half, row_parts)) + list(range(half)):
        at = slice(p * part, (p + 1) * part)
        both = nn_dot(rows[p][...], weight[:, : 2 * cols])
        d_act = nn_dot(grads[p][seq * part : (seq + 1) * part, :], weight[:, 2 * cols :])
        gate, up = both[:, :cols], both[:, cols:]
        sig = 1.0 / (1.0 + jnp.exp(-gate))
        silu = gate * sig
        act_out[at, :] = (silu * up).astype(BF16)
        d_both_out[at, :cols] = (d_act * up * (sig + silu * (1.0 - sig))).astype(BF16)
        d_both_out[at, cols:] = (d_act * silu).astype(BF16)
        back = nt_dot(d_both_out[at, :], weight[:, : 2 * cols])
        if p < half:
            keep_out[at, :] = back
        else:
            send_out[(p - half) * part : (p - half + 1) * part, :] = back.astype(BF16)


def ffn_middle(seq, rows, grads, weight):
    part, width = rows[0].shape
    length = part * len(rows)
    cols = weight.shape[1] // 3
    return pl.pallas_call(
        functools.partial(ffn_kernel, len(rows), seq),
        out_shape=(
            jax.ShapeDtypeStruct((length, cols), BF16),
            jax.ShapeDtypeStruct((length, 2 * cols), BF16),
            jax.ShapeDtypeStruct((length // 2, width), F32),
            jax.ShapeDtypeStruct((length // 2, width), BF16),
        ),
        in_specs=[vmem()] * (2 * len(rows) + 1),
        out_specs=[vmem()] * 4,
        compiler_params=pltpu.CompilerParams(vmem_limit_bytes=VMEM_LIMIT),
        cost_estimate=pl.CostEstimate(
            flops=10 * length * width * cols, bytes_accessed=16 << 20, transcendentals=length * cols
        ),
        name="ffn_middle",
    )(*rows, *grads, weight)


def ffn_grad_kernel(row_parts, *refs):
    own, refs = refs[:row_parts], refs[row_parts:]
    other, refs = refs[:row_parts], refs[row_parts:]
    grads, refs = refs[:row_parts], refs[row_parts:]
    act_own, act_other, d_own, d_other, out, left = refs
    part, width = own[0].shape
    length = part * row_parts
    cols = act_own.shape[1]
    for what in range(2):
        for seq in range(2):
            for p in range(row_parts):
                for c in range(width // LANES):
                    lanes = slice(c * LANES, (c + 1) * LANES)
                    if what == 0:
                        tile = grads[p][seq * part : (seq + 1) * part, lanes]
                    else:
                        tile = (own, other)[seq][p][:, lanes]
                    at = seq * length + p * part
                    left[lanes, at : at + part] = tile.astype(F32).T.astype(BF16)
        first, second = ((act_own, act_other), (d_own, d_other))[what]
        to = slice(2 * cols, 3 * cols) if what == 0 else slice(0, 2 * cols)
        step = width // 4
        for s in range(4):
            at = slice(s * step, (s + 1) * step)
            total = nn_dot(left[at, :length], first[...]) + nn_dot(left[at, length:], second[...])
            out[at, to] = total.astype(BF16)


def ffn_partials(own, other, grads, act_own, act_other, d_own, d_other):
    part, width = own[0].shape
    length = part * len(own)
    cols = act_own.shape[1]
    return pl.pallas_call(
        functools.partial(ffn_grad_kernel, len(own)),
        out_shape=jax.ShapeDtypeStruct((width, 3 * cols), BF16),
        in_specs=[vmem()] * (3 * len(own) + 4),
        out_specs=vmem(),
        scratch_shapes=[pltpu.VMEM((width, 2 * length), BF16)],
        compiler_params=pltpu.CompilerParams(vmem_limit_bytes=VMEM_LIMIT),
        cost_estimate=pl.CostEstimate(
            flops=12 * length * width * cols, bytes_accessed=17 << 20, transcendentals=0
        ),
        name="ffn_partials",
    )(*own, *other, *grads, act_own, act_other, d_own, d_other)


def ffn_out_kernel(act_own, act_other, weight, keep_out, send_out):
    length, cols = act_own.shape
    half = length // 2
    down = weight[:, 2 * cols :]
    for seq, act in enumerate((act_own, act_other)):
        at = slice(seq * half, (seq + 1) * half)
        keep_out[at, :] = nt_dot(act[:half, :], down)
        send_out[at, :] = nt_dot(act[half:, :], down).astype(BF16)


def ffn_result(act_own, act_other, weight):
    length, cols = act_own.shape
    width = weight.shape[0]
    return pl.pallas_call(
        ffn_out_kernel,
        out_shape=(jax.ShapeDtypeStruct((length, width), F32), jax.ShapeDtypeStruct((length, width), BF16)),
        in_specs=[vmem()] * 3,
        out_specs=[vmem()] * 2,
        compiler_params=pltpu.CompilerParams(vmem_limit_bytes=VMEM_LIMIT),
        cost_estimate=pl.CostEstimate(
            flops=4 * length * width * cols, bytes_accessed=12 << 20, transcendentals=0
        ),
        name="ffn_result",
    )(act_own, act_other, weight)


def grad_kernel(row_parts, blocks, tables, *refs):
    rows, refs = refs[:row_parts], refs[row_parts:]
    right, refs = refs[0], refs[1:]
    keeps, send, left = refs[:blocks], refs[blocks], refs[blocks + 1]
    part, width = rows[0].shape
    block = keeps[0].shape[0]
    for p in range(row_parts):
        for c in range(width // LANES):
            tile = rows[p][:, c * LANES : (c + 1) * LANES].astype(F32)
            left[c * LANES : (c + 1) * LANES, p * part : (p + 1) * part] = tile.T.astype(BF16)
    for s in range(2 * blocks):
        at = pl.ds(pl.multiple_of(tables[3, s] * block, block), block)
        total = nn_dot(left[at, :], right[...]).astype(BF16)
        if s < blocks:
            keeps[s][...] = total
        else:
            send[(s - blocks) * block : (s - blocks + 1) * block, :] = total


def weight_partials(tables, rows, right, blocks):
    part, width = rows[0].shape
    length, cols = right.shape
    block = width // (2 * blocks)
    return pl.pallas_call(
        functools.partial(grad_kernel, len(rows), blocks),
        out_shape=(jax.ShapeDtypeStruct((block, cols), BF16),) * blocks
        + (jax.ShapeDtypeStruct((width // 2, cols), BF16),),
        in_specs=[smem()] + [vmem()] * (len(rows) + 1),
        out_specs=[vmem()] * (blocks + 1),
        scratch_shapes=[pltpu.VMEM((width, length), BF16)],
        compiler_params=pltpu.CompilerParams(vmem_limit_bytes=VMEM_LIMIT),
        cost_estimate=pl.CostEstimate(
            flops=2 * length * width * cols, bytes_accessed=8 << 20, transcendentals=0
        ),
        name="weight_partials",
    )(tables, *rows, right)


def hop(values, axis, flip):
    size = lax.axis_size(axis)
    return lax.ppermute(values, axis, [(i, i ^ flip) for i in range(size)])


def swap_blocks(values, axis, index, size):
    shape = values.shape
    bit = 1
    while bit < size:
        split = shape[:axis] + (size // (2 * bit), 2, bit) + shape[axis + 1 :]
        cut = values.reshape(split)
        cut = jnp.where((index & bit) != 0, jnp.flip(cut, axis + 1), cut)
        values = cut.reshape(shape)
        bit *= 2
    return values


def gather_weight(block):
    nz = lax.axis_size("fsdp")
    mine = [block] + [hop(block, "fsdp", k) for k in range(1, nz)]
    return mine + [hop(piece, "ctx", 1) for piece in mine]


def scatter_weight(partials):
    keeps, send = partials[:-1], partials[-1]
    rows = keeps[0].shape[0]
    other = hop(send, "ctx", 1)
    out = None
    for k, keep in enumerate(keeps):
        total = keep.astype(F32) + other[k * rows : (k + 1) * rows].astype(F32)
        if k == 0:
            out = total
        else:
            out = out + hop(total.astype(BF16), "fsdp", k).astype(F32)
    return out


def gather_chips(block):
    nt = lax.axis_size("tp")
    return [block] + [hop(block, "tp", 2 * k) for k in range(1, nt // 2)]


def with_twins(blocks):
    return blocks + [hop(block, "tp", 1) for block in blocks]


def gather_rows(block):
    return with_twins(gather_chips(block))


def scatter_rows(keep, send):
    nt = lax.axis_size("tp")
    rows = 2 * keep.shape[0] // nt
    other = hop(send, "tp", 1)
    total = keep + other.astype(F32)
    out = total[:rows]
    for k in range(1, nt // 2):
        out = out + hop(total[k * rows : (k + 1) * rows].astype(BF16), "tp", 2 * k).astype(F32)
    return out


def total_over(values):
    nt, nz = lax.axis_size("tp"), lax.axis_size("fsdp")
    values = values + hop(values, "tp", 1)
    across = hop(values, "ctx", 1)
    values = values + across
    values = sum([hop(values, "tp", 2 * k) for k in range(1, nt // 2)], values)
    return sum([hop(values, "fsdp", k) for k in range(1, nz)], values)


def inverse_rms(values):
    return lax.rsqrt(jnp.mean(values * values, axis=-1, keepdims=True) + EPS)


def norm_back(values, inv, gain, grad):
    scaled = grad * gain
    normed = values * inv
    d_gain = jnp.sum(grad * normed, axis=0, keepdims=True)
    d_values = inv * (scaled - normed * jnp.mean(scaled * normed, axis=-1, keepdims=True))
    return d_values, d_gain


def shards(
    layer_in,
    attn_gain,
    ffn_gain,
    query_weight,
    key_weight,
    value_weight,
    out_weight,
    variate_bias,
    gate_weight,
    up_weight,
    down_weight,
    segment_ids,
    variate_ids,
    time_ids,
    out_grad,
):
    seq_count, share, width = layer_in.shape
    nz, nx, nt = lax.axis_size("fsdp"), lax.axis_size("ctx"), lax.axis_size("tp")
    iz, ix, it = lax.axis_index("fsdp"), lax.axis_index("ctx"), lax.axis_index("tp")
    assert nx == 2 and seq_count == nx
    length = segment_ids.shape[1]
    heads = variate_bias.shape[1]
    proj = heads * HEAD

    def pick(table, which):
        return lax.dynamic_index_in_dim(table, which, 0, keepdims=False)

    def swap(mine, theirs):
        return jnp.where(ix == 0, mine, theirs), jnp.where(ix == 0, theirs, mine)

    order = jnp.arange(nx * nt).reshape(nx, nt // 2, 2)
    order = swap_blocks(swap_blocks(swap_blocks(order, 0, ix, nx), 1, it // 2, nt // 2), 2, it % 2, 2)
    order = order.transpose(2, 1, 0).reshape(nx * nt)
    places = jnp.arange(nz * nx).reshape(nz, nx)
    places = swap_blocks(swap_blocks(places, 0, iz, nz), 1, ix, nx).transpose(1, 0).reshape(nz * nx)
    tables, cosine, sine, seg_row, seg_wide, feature, coef, hot_rows = attention_tables(
        pick(segment_ids, ix), pick(variate_ids, ix), pick(time_ids, ix), variate_bias, order, places
    )
    gain_one = attn_gain.astype(F32)[None]
    gain_two = ffn_gain.astype(F32)[None]

    inputs = jnp.concatenate([pick(layer_in, ix), hop(pick(layer_in, 1 - ix), "ctx", 1)], axis=0).astype(F32)
    inv_one = inverse_rms(inputs)
    rows_one = gather_rows((inputs * inv_one * gain_one).astype(BF16))
    attn_w = gather_weight(jnp.concatenate([query_weight, key_weight, value_weight, out_weight], axis=1))

    cols = gate_weight.shape[1] // 2
    pieces = [w.reshape(w.shape[0], 2, cols) for w in (gate_weight, up_weight, down_weight)]
    mine = jnp.concatenate([lax.dynamic_index_in_dim(w, ix, 1, keepdims=False) for w in pieces], axis=1)
    theirs = jnp.concatenate([lax.dynamic_index_in_dim(w, 1 - ix, 1, keepdims=False) for w in pieces], axis=1)
    ffn_w = jnp.concatenate(swap(mine, hop(theirs, "ctx", 1)), axis=0)
    ffn_w = lax.all_gather(ffn_w, "fsdp", axis=0, tiled=True)

    other_grad = hop(out_grad, "ctx", 1)
    grads = jnp.concatenate([pick(out_grad, ix), pick(other_grad, ix)], axis=0)
    grads_next = jnp.concatenate([pick(other_grad, 1 - ix), pick(out_grad, 1 - ix)], axis=0)
    grad_rows = gather_rows(jnp.concatenate([grads, grads_next], axis=0))

    q_aug, k_aug, v_rows, mixed, lse, keep, send = attention_forward(
        tables, rows_one, attn_w, cosine, sine, seg_row, seg_wide, feature, coef, heads
    )
    hidden = inputs + scatter_rows(keep, send)
    inv_two = inverse_rms(hidden)
    chips_two = gather_chips((hidden * inv_two * gain_two).astype(BF16))
    rows_two = with_twins(chips_two)
    rows_next = with_twins([hop(block, "ctx", 1) for block in chips_two])
    act, d_both, keep, send = ffn_middle(0, rows_two, grad_rows, ffn_w)
    d_normed_two = scatter_rows(keep, send)
    act_next, d_both_next, keep, send = ffn_middle(1, rows_next, grad_rows, ffn_w)
    d_normed_two = d_normed_two + hop(scatter_rows(keep, send).astype(BF16), "ctx", 1).astype(F32)

    ffn_grad = ffn_partials(rows_two, rows_next, grad_rows, act, act_next, d_both, d_both_next)
    ffn_grad = lax.psum_scatter(ffn_grad, "fsdp", scatter_dimension=0, tiled=True)
    ffn_grad = ffn_grad.reshape(nx, ffn_grad.shape[0] // nx, ffn_grad.shape[1])
    low, high = swap(pick(ffn_grad, ix), hop(pick(ffn_grad, 1 - ix), "ctx", 1))
    gate_grad, up_grad, down_grad = [
        jnp.concatenate([low[:, k * cols : (k + 1) * cols], high[:, k * cols : (k + 1) * cols]], axis=1).astype(F32)
        for k in range(3)
    ]

    keep, send = ffn_result(act, act_next, ffn_w)
    other = hop(send, "tp", 1)
    total = (keep + other.astype(F32)).reshape(2, nt // 2, nx * share, width)
    ffn = total[:, 0]
    for k in range(1, nt // 2):
        ffn = ffn + hop(total[:, k].astype(BF16), "tp", 2 * k).astype(F32)
    mine, theirs = (ffn[0] + hidden).reshape(2, share, width), ffn[1].reshape(2, share, width)
    sent = hop(jnp.stack([mine[1], theirs[0]]).astype(BF16), "ctx", 1).astype(F32)
    layer_out = jnp.stack(swap(mine[0] + sent[1], theirs[1] + sent[0])).astype(BF16)

    d_hidden_norm, d_gain_two = norm_back(hidden, inv_two, gain_two, d_normed_two)
    d_hidden = grads.astype(F32) + d_hidden_norm
    branch_rows = gather_rows(d_hidden.astype(BF16))
    keep, send, d_qkv, bias_parts = attention_backward(
        tables, branch_rows, attn_w, q_aug, k_aug, v_rows, lse, cosine, sine, seg_row, seg_wide, hot_rows, heads
    )
    d_normed_one = scatter_rows(keep, send)
    out_weight_grad = scatter_weight(weight_partials(tables, branch_rows, mixed, nz))
    qkv_grad = scatter_weight(weight_partials(tables, rows_one, d_qkv, nz))

    d_input_norm, d_gain_one = norm_back(inputs, inv_one, gain_one, d_normed_one)
    d_inputs = (d_hidden + d_input_norm).astype(BF16)
    in_grad = jnp.stack(swap(d_inputs[:share], hop(d_inputs[share:], "ctx", 1)))
    sums = jnp.sum(bias_parts, axis=2)
    bias_sums = jnp.stack([jnp.sum(sums[:, :8], axis=1), jnp.sum(sums[:, 8:], axis=1)])
    spread = lax.dynamic_update_slice(jnp.zeros((2, width), F32), bias_sums, (0, it * heads))
    totals = total_over(jnp.concatenate([d_gain_one, d_gain_two, spread], axis=0))
    bias_grad = lax.dynamic_slice(totals, (2, it * heads), (2, heads))
    return (
        layer_out,
        in_grad,
        totals[0],
        totals[1],
        qkv_grad[:, :proj],
        qkv_grad[:, proj : 2 * proj],
        qkv_grad[:, 2 * proj :],
        out_weight_grad,
        bias_grad,
        gate_grad,
        up_grad,
        down_grad,
    )


def solution(mesh):
    rows = P("fsdp", ("ctx", "tp"), None)
    weight = P(("fsdp", "ctx"), "tp")
    ids = P("fsdp", None)
    bias = P(None, "tp")
    in_specs = (rows, P(), P()) + (weight,) * 4 + (bias,) + (weight,) * 3 + (ids,) * 3 + (rows,)
    out_specs = (rows, rows, P(), P()) + (weight,) * 4 + (bias,) + (weight,) * 3
    return jax.shard_map(shards, mesh=mesh, in_specs=in_specs, out_specs=out_specs, check_vma=False)
```

```python
import functools
import jax
import jax.numpy as jnp
from jax import lax
from jax.sharding import PartitionSpec as P
from jax.experimental import pallas as pl
from jax.experimental.pallas import tpu as pltpu

HEADS = 16
HEAD = 64
EPS = 1e-05
NEG = -1e30
F32 = jnp.float32
BF16 = jnp.bfloat16
LANES = 128
QUERIES = 256
STEP = 128
VMEM_LIMIT = 56 * 1024 * 1024


def nt_dot(left, right):
    return lax.dot_general(left, right, (((1,), (1,)), ((), ())), preferred_element_type=F32)


def nn_dot(left, right):
    return lax.dot_general(left, right, (((1,), (0,)), ((), ())), preferred_element_type=F32)


def tn_dot(left, right):
    return lax.dot_general(left, right, (((0,), (0,)), ((), ())), preferred_element_type=F32)


def lane_of(shape):
    return lax.broadcasted_iota(jnp.int32, shape, len(shape) - 1)


def half_swap(values):
    lane = lane_of(values.shape)
    forward = pltpu.roll(values, LANES - HEAD // 2, 1)
    back = pltpu.roll(values, HEAD // 2, 1)
    return jnp.where(lane % HEAD < HEAD // 2, forward, back)


def fwd_kernel(row_parts, weight_parts, heads, *refs):
    tables, refs = refs[0], refs[1:]
    rows, refs = refs[:row_parts], refs[row_parts:]
    weights, refs = refs[:weight_parts], refs[weight_parts:]
    cosine, sine, seg_row, seg_wide, feature, coef = refs[:6]
    q_aug, k_aug, v_out, mixed_out, lse_out, keep_out, rest_out, send_own, send_rest = refs[6:15]
    full, out_full, mixed_wide, v_turn = refs[15:]
    pairs = heads // 2
    proj = heads * HEAD
    length = q_aug.shape[1]
    block = weights[0].shape[0]
    part = rows[0].shape[0]
    share = part // 2
    for i in range(weight_parts):
        at = pl.ds(pl.multiple_of(tables[3, i] * block, block), block)
        full[at, :] = weights[i][:, : 3 * proj]
        out_full[at, :] = weights[i][:, 3 * proj :]
    for p in range(row_parts):
        raw = nn_dot(rows[p][...], full[...])
        for k in range(2):
            piece = raw[k * share : (k + 1) * share]
            start = pl.multiple_of(tables[0, 2 * p + k] * share, share)
            at = pl.ds(start, share)
            cos_now, sin_now, feat = cosine[at, :], sine[at, :], feature[at, :].astype(F32)
            lane = lane_of((share, LANES))
            for pair in range(pairs):
                low = pair * LANES
                q = piece[:, low : low + LANES]
                q = (q * cos_now + half_swap(q) * sin_now).astype(BF16).astype(F32) * HEAD**-0.5
                kk = piece[:, proj + low : proj + low + LANES]
                kk = kk * cos_now + half_swap(kk) * sin_now
                v_out[pair, at, :] = piece[:, 2 * proj + low : 2 * proj + low + LANES].astype(BF16)
                for odd in range(2):
                    head = 2 * pair + odd
                    q_now = pltpu.roll(q, HEAD, 1) if odd else q
                    k_now = pltpu.roll(kk, HEAD, 1) if odd else kk
                    q_feat = feat * coef[head : head + 1, :]
                    q_aug[head, at, :] = jnp.where(lane < HEAD, q_now, q_feat).astype(BF16)
                    k_aug[head, at, :] = jnp.where(lane < HEAD, k_now, feat).astype(BF16)
    for pair in range(pairs):
        for b in range(length // LANES):
            tile = v_out[pair, b * LANES : (b + 1) * LANES, :].astype(F32)
            v_turn[pair, :, b * LANES : (b + 1) * LANES] = tile.T.astype(BF16)

    def query_block(b, carry):
        at = pl.ds(pl.multiple_of(b * QUERIES, QUERIES), QUERIES)
        seg_q = seg_row[pl.ds(b, 1), :]
        first = pl.multiple_of(tables[1, b] * LANES, LANES)
        for kind in range(1, length // STEP + 1):

            @pl.when(tables[2, b] == kind)
            def _(kind=kind):
                win = pl.ds(first, kind * STEP)
                keep = seg_wide[win, :] == seg_q
                scores = [nt_dot(k_aug[h, win, :], q_aug[h, at, :]) for h in range(heads)]
                probs, totals = [], []
                for head in range(heads):
                    s = jnp.where(keep, scores[head], NEG)
                    top = jnp.max(s, axis=0, keepdims=True)
                    p = jnp.exp(s - top)
                    total = jnp.sum(p, axis=0, keepdims=True)
                    probs.append(p.astype(BF16))
                    totals.append(total)
                    lse_out[head, pl.ds(b, 1), :] = top + jnp.log(total)
                for pair in range(pairs):
                    outs = []
                    for odd in range(2):
                        head = 2 * pair + odd
                        turn = v_turn[pair, odd * HEAD : (odd + 1) * HEAD, win]
                        outs.append(nn_dot(turn, probs[head]) / totals[head])
                    mixed = jnp.concatenate(outs, axis=0).T
                    mixed_wide[at, pair * LANES : (pair + 1) * LANES] = mixed

        return carry

    lax.fori_loop(0, length // QUERIES, query_block, 0)
    for slot in range(2 * row_parts):
        start = pl.multiple_of(tables[0, slot] * share, share)
        piece = mixed_wide[pl.ds(start, share), :]
        mixed_out[slot * share : (slot + 1) * share, :] = piece.astype(BF16)
    half = row_parts // 2
    for p in range(row_parts):
        back = nt_dot(mixed_out[p * part : (p + 1) * part, :], out_full[...])
        if p == 0:
            keep_out[...] = back
        elif p < half:
            rest_out[(p - 1) * part : p * part, :] = back
        else:
            if p == half:
                send_own[...] = back.astype(BF16)
            else:
                send_rest[(p - half - 1) * part : (p - half) * part, :] = back.astype(BF16)


def vmem():
    return pl.BlockSpec(memory_space=pltpu.VMEM)


def anywhere():
    return pl.BlockSpec(memory_space=pl.ANY)


def smem():
    return pl.BlockSpec(memory_space=pltpu.SMEM)


def attention_forward(tables, rows, weights, cosine, sine, seg_row, seg_wide, feature, coef, heads, behind=()):
    proj = heads * HEAD
    length = cosine.shape[0]
    part, width = rows[0].shape
    shapes = (
        jax.ShapeDtypeStruct((heads, length, LANES), BF16),
        jax.ShapeDtypeStruct((heads, length, LANES), BF16),
        jax.ShapeDtypeStruct((heads // 2, length, LANES), BF16),
        jax.ShapeDtypeStruct((length, proj), BF16),
        jax.ShapeDtypeStruct((heads, length // QUERIES, QUERIES), F32),
        jax.ShapeDtypeStruct((part, width), F32),
        jax.ShapeDtypeStruct((length // 2 - part, width), F32),
        jax.ShapeDtypeStruct((part, width), BF16),
        jax.ShapeDtypeStruct((length // 2 - part, width), BF16),
    )
    count = len(rows) + len(weights) + 6
    operands = (tables, *rows, *weights, cosine, sine, seg_row, seg_wide, feature, coef)
    return pl.pallas_call(
        without(functools.partial(fwd_kernel, len(rows), len(weights), heads), len(operands), len(behind)),
        out_shape=shapes,
        in_specs=[smem()] + [vmem()] * count + [anywhere()] * len(behind),
        out_specs=[vmem()] * 9,
        scratch_shapes=[
            pltpu.VMEM((width, 3 * proj), BF16),
            pltpu.VMEM((width, proj), BF16),
            pltpu.VMEM((length, proj), F32),
            pltpu.VMEM((heads // 2, LANES, length), BF16),
        ],
        compiler_params=pltpu.CompilerParams(vmem_limit_bytes=VMEM_LIMIT),
        cost_estimate=pl.CostEstimate(
            flops=2 * length * width * 3 * proj, bytes_accessed=8 << 20, transcendentals=length * length * heads // 2
        ),
        name="attn_fwd",
    )(*operands, *behind)


def bwd_kernel(row_parts, weight_parts, heads, *refs):
    tables, refs = refs[0], refs[1:]
    rows, refs = refs[:row_parts], refs[row_parts:]
    weights, refs = refs[:weight_parts], refs[weight_parts:]
    q_aug, k_aug, v_in, lse, cosine, sine, seg_row, seg_wide, hot_rows = refs[:9]
    keep_out, rest_out, send_own, send_rest, d_qkv_out, bias_out = refs[9:15]
    full, out_full, d_out, k_turn, dq_acc, dk_acc, dv_acc = refs[15:]
    pairs = heads // 2
    proj = heads * HEAD
    length = q_aug.shape[1]
    block = weights[0].shape[0]
    part = rows[0].shape[0]
    share = part // 2
    for i in range(weight_parts):
        at = pl.ds(pl.multiple_of(tables[3, i] * block, block), block)
        full[at, :] = weights[i][:, : 3 * proj]
        out_full[at, :] = weights[i][:, 3 * proj :]
    for p in range(row_parts):
        raw = nn_dot(rows[p][...], out_full[...]).astype(BF16)
        for k in range(2):
            start = pl.multiple_of(tables[0, 2 * p + k] * share, share)
            d_out[pl.ds(start, share), :] = raw[k * share : (k + 1) * share]
    for head in range(heads):
        for b in range(length // LANES):
            tile = k_aug[head, b * LANES : (b + 1) * LANES, :].astype(F32)
            k_turn[head, :, b * LANES : (b + 1) * LANES] = tile.T.astype(BF16)
    dk_acc[...] = jnp.zeros(dk_acc.shape, F32)
    dv_acc[...] = jnp.zeros(dv_acc.shape, F32)
    bias_out[...] = jnp.zeros(bias_out.shape, F32)

    def query_block(b, carry):
        at = pl.ds(pl.multiple_of(b * QUERIES, QUERIES), QUERIES)
        seg_q = seg_row[pl.ds(b, 1), :]
        hot = hot_rows[:, at]
        first = pl.multiple_of(tables[1, b] * LANES, LANES)
        for kind in range(1, length // STEP + 1):

            @pl.when(tables[2, b] == kind)
            def _(kind=kind):
                win = pl.ds(first, kind * STEP)
                keep = seg_wide[win, :] == seg_q
                owns = []
                for head in range(heads):
                    chunk = slice(head // 2 * LANES, (head // 2 + 1) * LANES)
                    d_pair = d_out[at, chunk]
                    lane = lane_of(d_pair.shape)
                    owns.append(jnp.where((lane >= HEAD) == (head % 2 == 1), d_pair, jnp.zeros_like(d_pair)))
                turned = []
                for base in range(0, heads, 2):
                    group = range(base, base + 2)
                    s = [nt_dot(k_aug[h, win, :], q_aug[h, at, :]) for h in group]
                    dp = [nt_dot(v_in[h // 2, win, :], owns[h]) for h in group]
                    low, ds = [], []
                    for i, h in enumerate(group):
                        p = jnp.exp(jnp.where(keep, s[i] - lse[h, pl.ds(b, 1), :], NEG))
                        low.append(p.astype(BF16))
                        ds.append((p * (dp[i] - jnp.sum(p * dp[i], axis=0, keepdims=True))).astype(BF16))
                    for i, h in enumerate(group):
                        if i % 2 == 0:
                            both = jnp.concatenate(low[i : i + 2], axis=1)
                            dv_acc[h // 2, win, :] += nn_dot(both, jnp.concatenate(owns[h : h + 2], axis=0))
                        dk_acc[h, win, :] += nn_dot(ds[i], q_aug[h, at, :])
                        dq = nn_dot(k_turn[h, :, win], ds[i])
                        turned.append(dq[:HEAD])
                        sums = dq[HEAD : HEAD + 8]
                        bias_out[h] += jnp.concatenate([sums * hot[:8], sums * hot[8:]], axis=0)
                for pair in range(pairs):
                    chunk = slice(pair * LANES, (pair + 1) * LANES)
                    dq_acc[at, chunk] = jnp.concatenate(turned[2 * pair : 2 * pair + 2], axis=0).T * HEAD**-0.5

        return carry

    lax.fori_loop(0, length // QUERIES, query_block, 0)
    for p in range(row_parts):
        for k in range(2):
            slot = 2 * p + k
            at = pl.ds(pl.multiple_of(tables[0, slot] * share, share), share)
            to = slice(slot * share, (slot + 1) * share)
            cos_now, sin_now = cosine[at, :], sine[at, :]
            lane = lane_of((share, LANES))
            for pair in range(pairs):
                low = pair * LANES
                dq = dq_acc[at, low : low + LANES]
                dk = jnp.where(lane < HEAD, dk_acc[2 * pair, at, :], pltpu.roll(dk_acc[2 * pair + 1, at, :], HEAD, 1))
                d_qkv_out[to, low : low + LANES] = (dq * cos_now - half_swap(dq) * sin_now).astype(BF16)
                d_qkv_out[to, proj + low : proj + low + LANES] = (dk * cos_now - half_swap(dk) * sin_now).astype(BF16)
                d_qkv_out[to, 2 * proj + low : 2 * proj + low + LANES] = dv_acc[pair, at, :].astype(BF16)
        part_rows = d_qkv_out[p * part : (p + 1) * part, :]
        back = nt_dot(part_rows, full[...])
        half = row_parts // 2
        if p == 0:
            keep_out[...] = back
        elif p < half:
            rest_out[(p - 1) * part : p * part, :] = back
        else:
            if p == half:
                send_own[...] = back.astype(BF16)
            else:
                send_rest[(p - half - 1) * part : (p - half) * part, :] = back.astype(BF16)


def attention_backward(tables, rows, weights, q_aug, k_aug, v_in, lse, cosine, sine, seg_row, seg_wide, hot_rows, heads, behind=()):
    proj = heads * HEAD
    length = cosine.shape[0]
    part, width = rows[0].shape
    shapes = (
        jax.ShapeDtypeStruct((part, width), F32),
        jax.ShapeDtypeStruct((length // 2 - part, width), F32),
        jax.ShapeDtypeStruct((part, width), BF16),
        jax.ShapeDtypeStruct((length // 2 - part, width), BF16),
        jax.ShapeDtypeStruct((length, 3 * proj), BF16),
        jax.ShapeDtypeStruct((heads, 16, QUERIES), F32),
    )
    count = len(rows) + len(weights) + 9
    operands = (tables, *rows, *weights, q_aug, k_aug, v_in, lse, cosine, sine, seg_row, seg_wide, hot_rows)
    return pl.pallas_call(
        without(functools.partial(bwd_kernel, len(rows), len(weights), heads), len(operands), len(behind)),
        out_shape=shapes,
        in_specs=[smem()] + [vmem()] * count + [anywhere()] * len(behind),
        out_specs=[vmem()] * 6,
        scratch_shapes=[
            pltpu.VMEM((width, 3 * proj), BF16),
            pltpu.VMEM((width, proj), BF16),
            pltpu.VMEM((length, proj), BF16),
            pltpu.VMEM((heads, LANES, length), BF16),
            pltpu.VMEM((length, proj), F32),
            pltpu.VMEM((heads, length, LANES), F32),
            pltpu.VMEM((heads // 2, length, LANES), F32),
        ],
        compiler_params=pltpu.CompilerParams(vmem_limit_bytes=VMEM_LIMIT),
        cost_estimate=pl.CostEstimate(
            flops=2 * length * width * 4 * proj, bytes_accessed=12 << 20, transcendentals=length * length * heads // 2
        ),
        name="attn_bwd",
    )(*operands, *behind)


def attention_tables(segments, variates, times, variate_bias, order, places):
    length = segments.shape[0]
    heads = variate_bias.shape[1]
    count = length // QUERIES
    half = HEAD // 2
    frequency = 10000.0 ** (-2.0 * jnp.arange(half, dtype=F32) / HEAD)
    angles = times.astype(F32)[:, None] * frequency
    cos_half, sin_half = jnp.cos(angles), jnp.sin(angles)
    cosine = jnp.concatenate([cos_half] * 4, axis=1)
    sine = jnp.concatenate([-sin_half, sin_half] * 2, axis=1)
    seg_row = segments.reshape(count, QUERIES)
    seg_wide = jnp.broadcast_to(segments[:, None], (length, QUERIES))
    lane = jnp.arange(LANES)
    live = (lane >= HEAD) & (lane < HEAD + 12)
    feature = ((variates[:, None] == (lane % 4)[None, :]) & live[None, :]).astype(BF16)
    gap = variate_bias[0] - variate_bias[1]
    high = lax.reduce_precision(gap, 8, 7)
    mid = lax.reduce_precision(gap - high, 8, 7)
    low = lax.reduce_precision(gap - high - mid, 8, 7)
    parts = jnp.repeat(jnp.stack([high, mid, low], axis=1), 4, axis=1)
    coef = jnp.pad(parts, ((0, -heads % 8), (HEAD, LANES - HEAD - 12)))
    kinds = jnp.arange(4)
    same = (variates[None, :] == kinds[:, None]).astype(F32)
    zeros = jnp.zeros_like(same)
    hot_rows = jnp.concatenate([same, zeros, 1.0 - same, zeros], axis=0)
    ends = segments.reshape(count, QUERIES)
    start = jnp.sum(segments[None, :] < ends[:, :1], axis=1)
    stop = jnp.sum(segments[None, :] <= ends[:, -1:], axis=1)
    first = start // LANES
    kind = (stop - first * LANES + STEP - 1) // STEP
    first = jnp.minimum(first, (length - kind * STEP) // LANES)
    size = max(count, order.shape[0], places.shape[0])
    pad = lambda a: jnp.pad(a.astype(jnp.int32), (0, size - a.shape[0]))
    tables = jnp.stack([pad(order), pad(first), pad(kind), pad(places)])
    return tables, cosine, sine, seg_row, seg_wide, feature, coef, hot_rows


def ffn_kernel(row_parts, flipped, which, *refs):
    rows, refs = refs[:row_parts], refs[row_parts:]
    near, refs = refs[:row_parts], refs[row_parts:]
    far, refs = refs[:row_parts], refs[row_parts:]
    weight, act_out, d_both_out, keep_out, rest_out, send_own, send_rest, grads, sems = refs
    part = rows[0].shape[0]
    share = part // 2
    cols = act_out.shape[1]
    half = row_parts // 2
    copies = []
    for p in range(row_parts):
        pair = (far[p], near[p]) if flipped else (near[p], far[p])
        for k in range(2):
            copy = pltpu.make_async_copy(pair[k].at[which[0]], grads.at[p, pl.ds(k * share, share)], sems.at[p, k])
            copy.start()
            copies.append(copy)
    for p in list(range(half, row_parts)) + list(range(half)):
        at = slice(p * part, (p + 1) * part)
        both = nn_dot(rows[p][...], weight[:, : 2 * cols])
        copies[2 * p].wait()
        copies[2 * p + 1].wait()
        d_act = nn_dot(grads[p], weight[:, 2 * cols :])
        gate, up = both[:, :cols], both[:, cols:]
        sig = 1.0 / (1.0 + jnp.exp(-gate))
        silu = gate * sig
        act_out[at, :] = (silu * up).astype(BF16)
        d_both_out[at, :cols] = (d_act * up * (sig + silu * (1.0 - sig))).astype(BF16)
        d_both_out[at, cols:] = (d_act * silu).astype(BF16)
        back = nt_dot(d_both_out[at, :], weight[:, : 2 * cols])
        if p == 0:
            keep_out[...] = back
        elif p < half:
            rest_out[(p - 1) * part : p * part, :] = back
        else:
            if p == half:
                send_own[...] = back.astype(BF16)
            else:
                send_rest[(p - half - 1) * part : (p - half) * part, :] = back.astype(BF16)


def ffn_middle(flipped, which, rows, near, far, weight, behind=()):
    part, width = rows[0].shape
    count = len(rows)
    length = part * count
    cols = weight.shape[1] // 3
    operands = (which, *rows, *near, *far, weight)
    return pl.pallas_call(
        without(functools.partial(ffn_kernel, count, flipped), len(operands), len(behind)),
        out_shape=(
            jax.ShapeDtypeStruct((length, cols), BF16),
            jax.ShapeDtypeStruct((length, 2 * cols), BF16),
            jax.ShapeDtypeStruct((part, width), F32),
            jax.ShapeDtypeStruct((length // 2 - part, width), F32),
            jax.ShapeDtypeStruct((part, width), BF16),
            jax.ShapeDtypeStruct((length // 2 - part, width), BF16),
        ),
        in_specs=[smem()] + [vmem()] * count + [anywhere()] * (2 * count) + [vmem()] + [anywhere()] * len(behind),
        out_specs=[vmem()] * 6,
        scratch_shapes=[pltpu.VMEM((count, part, width), BF16), pltpu.SemaphoreType.DMA((count, 2))],
        compiler_params=pltpu.CompilerParams(vmem_limit_bytes=VMEM_LIMIT),
        cost_estimate=pl.CostEstimate(
            flops=10 * length * width * cols, bytes_accessed=16 << 20, transcendentals=length * cols
        ),
        name="ffn_middle",
    )(*operands, *behind)


def ffn_grad_kernel(row_parts, which, *refs):
    own, refs = refs[:row_parts], refs[row_parts:]
    other, refs = refs[:row_parts], refs[row_parts:]
    near, refs = refs[:row_parts], refs[row_parts:]
    far, refs = refs[:row_parts], refs[row_parts:]
    act_own, act_other, d_own, d_other, out, left = refs
    part, width = own[0].shape
    share = part // 2
    length = part * row_parts
    cols = act_own.shape[1]
    ix = which[0]
    for what in range(2):
        for seq in range(2):
            for p in range(row_parts):
                at = seq * length + p * part
                for c in range(width // LANES):
                    lanes = slice(c * LANES, (c + 1) * LANES)
                    if what == 0:
                        now = ix if seq == 0 else 1 - ix
                        pair = (near[p], far[p]) if seq == 0 else (far[p], near[p])
                        tile = jnp.concatenate([ref[now, :, lanes] for ref in pair], axis=0)
                    else:
                        tile = (own, other)[seq][p][:, lanes]
                    left[lanes, at : at + part] = tile.astype(F32).T.astype(BF16)
        first, second = ((act_own, act_other), (d_own, d_other))[what]
        to = slice(2 * cols, 3 * cols) if what == 0 else slice(0, 2 * cols)
        step = width // 4
        for s in range(4):
            at = slice(s * step, (s + 1) * step)
            total = nn_dot(left[at, :length], first[...]) + nn_dot(left[at, length:], second[...])
            out[at, to] = total.astype(BF16)


def ffn_partials(which, own, other, near, far, act_own, act_other, d_own, d_other, behind=()):
    part, width = own[0].shape
    length = part * len(own)
    cols = act_own.shape[1]
    operands = (which, *own, *other, *near, *far, act_own, act_other, d_own, d_other)
    return pl.pallas_call(
        without(functools.partial(ffn_grad_kernel, len(own)), len(operands), len(behind)),
        out_shape=jax.ShapeDtypeStruct((width, 3 * cols), BF16),
        in_specs=[smem()] + [vmem()] * (4 * len(own) + 4) + [anywhere()] * len(behind),
        out_specs=vmem(),
        scratch_shapes=[pltpu.VMEM((width, 2 * length), BF16)],
        compiler_params=pltpu.CompilerParams(vmem_limit_bytes=VMEM_LIMIT),
        cost_estimate=pl.CostEstimate(
            flops=12 * length * width * cols, bytes_accessed=17 << 20, transcendentals=0
        ),
        name="ffn_partials",
    )(*operands, *behind)


def ffn_out_kernel(act_own, act_other, weight, *outs):
    length, cols = act_own.shape
    part = outs[0].shape[0]
    half = length // 2
    down = weight[:, 2 * cols :]
    for seq, act in enumerate((act_own, act_other)):
        both = nt_dot(act[:half, :], down)
        outs[4 * seq][...] = both[:part]
        outs[4 * seq + 1][...] = both[part:]
        both = nt_dot(act[half:, :], down).astype(BF16)
        outs[4 * seq + 2][...] = both[:part]
        outs[4 * seq + 3][...] = both[part:]


def ffn_result(act_own, act_other, weight, part, behind=()):
    length, cols = act_own.shape
    width = weight.shape[0]
    shapes = (
        jax.ShapeDtypeStruct((part, width), F32),
        jax.ShapeDtypeStruct((length // 2 - part, width), F32),
        jax.ShapeDtypeStruct((part, width), BF16),
        jax.ShapeDtypeStruct((length // 2 - part, width), BF16),
    )
    operands = (act_own, act_other, weight)
    return pl.pallas_call(
        without(ffn_out_kernel, len(operands), len(behind)),
        out_shape=shapes * 2,
        in_specs=[vmem()] * 3 + [anywhere()] * len(behind),
        out_specs=[vmem()] * 8,
        compiler_params=pltpu.CompilerParams(vmem_limit_bytes=VMEM_LIMIT),
        cost_estimate=pl.CostEstimate(
            flops=4 * length * width * cols, bytes_accessed=12 << 20, transcendentals=0
        ),
        name="ffn_result",
    )(*operands, *behind)


def without(kernel, start, count):
    return lambda *refs: kernel(*refs[:start], *refs[start + count :])


def rows_call(kernel, name, shapes, *operands, scalars=(), behind=()):
    single = not isinstance(shapes, (list, tuple))
    count = len(scalars) + len(operands)
    return pl.pallas_call(
        without(kernel, count, len(behind)),
        out_shape=shapes,
        in_specs=[smem()] * len(scalars) + [vmem()] * len(operands) + [anywhere()] * len(behind),
        out_specs=vmem() if single else [vmem()] * len(shapes),
        compiler_params=pltpu.CompilerParams(vmem_limit_bytes=VMEM_LIMIT),
        cost_estimate=pl.CostEstimate(
            flops=16 * operands[0].size, bytes_accessed=sum(o.size * o.dtype.itemsize for o in operands), transcendentals=0
        ),
        name=name,
    )(*scalars, *operands, *behind)


def pack_kernel(*refs):
    out, start = refs[-1], 0
    for ref in refs[:-1]:
        stop = start + ref.shape[1]
        out[:, start:stop] = ref[...]
        start = stop


def split_kernel(which, gate, up, down, mine, theirs):
    cols = gate.shape[1] // 2
    for k, ref in enumerate((gate, up, down)):
        for own, out in ((0, mine), (1, theirs)):

            @pl.when(which[0] == 0)
            def _(ref=ref, out=out, k=k, own=own):
                out[:, k * cols : (k + 1) * cols] = ref[:, own * cols : (own + 1) * cols]

            @pl.when(which[0] == 1)
            def _(ref=ref, out=out, k=k, own=own):
                out[:, k * cols : (k + 1) * cols] = ref[:, (1 - own) * cols : (2 - own) * cols]


def stack_kernel(which, mine, theirs, out):
    block = mine.shape[0]
    first = pl.multiple_of(which[0] * block, block)
    second = pl.multiple_of((1 - which[0]) * block, block)
    out[pl.ds(first, block), :] = mine[...]
    out[pl.ds(second, block), :] = theirs[...]


def pair_kernel(*refs):
    blocks = (len(refs) - 1) // 2
    keeps, other, outs = refs[:blocks], refs[blocks], refs[blocks + 1 :]
    rows = keeps[0].shape[0]
    for k in range(blocks):
        total = keeps[k][...].astype(F32) + other[k * rows : (k + 1) * rows, :].astype(F32)
        outs[k][...] = total.astype(outs[k].dtype)


def finish_kernel(count, own, *refs):
    total = own[...]
    for ref in refs[:-count]:
        total = total + ref[...].astype(F32)
    start = 0
    for out in refs[-count:]:
        stop = start + out.shape[1]
        out[...] = total[:, start:stop]
        start = stop


def pair_sums(partials, other):
    shape = partials[0].shape
    blocks = len(partials) - 1
    shapes = [jax.ShapeDtypeStruct(shape, F32 if k == 0 else BF16) for k in range(blocks)]
    return rows_call(pair_kernel, "pair_sums", shapes, *partials[:-1], other)


def weight_sums(own, arrived, pieces):
    outs = [jax.ShapeDtypeStruct((own.shape[0], own.shape[1] // pieces), F32)] * pieces
    return rows_call(functools.partial(finish_kernel, pieces), "weight_sums", outs, own, *arrived)


def ffn_finish_kernel(which, grads, far, *outs):
    cols = far.shape[1] // 3
    rows = far.shape[0]
    mine = grads[pl.ds(pl.multiple_of(which[0] * rows, rows), rows), :].astype(F32)
    theirs = far[...].astype(F32)
    for own in range(2):

        @pl.when(which[0] == own)
        def _(own=own):
            for k, out in enumerate(outs):
                out[:, own * cols : (own + 1) * cols] = mine[:, k * cols : (k + 1) * cols]
                out[:, (1 - own) * cols : (2 - own) * cols] = theirs[:, k * cols : (k + 1) * cols]


def out_kernel(hidden, keep, twin, keep_next, twin_next, *refs):
    count = (len(refs) - 2) // 2
    mine = rows_sum(keep, twin, refs[:count]) + hidden[...]
    theirs = rows_sum(keep_next, twin_next, refs[count : 2 * count])
    held, sent = refs[-2:]
    share = held.shape[1]
    held[0] = mine[:share]
    held[1] = theirs[share:]
    sent[0] = theirs[:share].astype(BF16)
    sent[1] = mine[share:].astype(BF16)


def out_finish_kernel(which, held, arrived, out):
    for own in range(2):
        out[pl.ds(which[0] if own == 0 else 1 - which[0], 1)] = (held[own] + arrived[own].astype(F32)).astype(BF16)[None]


def inverse_rms(values):
    return lax.rsqrt(jnp.mean(values * values, axis=-1, keepdims=True) + EPS)


def both_halves(first, second):
    return jnp.concatenate([first[...], second[...]], axis=0).astype(F32)


def rows_sum(keep, twin, arrived):
    total = keep[...] + twin[...].astype(F32)
    for ref in arrived:
        total = total + ref[...].astype(F32)
    return total


def norm_kernel(near, far, gain, out):
    values = both_halves(near, far)
    out[...] = (values * inverse_rms(values) * gain[...].astype(F32)).astype(BF16)


def rest_kernel(rest, twin, out):
    out[...] = (rest[...] + twin[...].astype(F32)).astype(BF16)


def sum_kernel(keep, twin, *refs):
    refs[-1][...] = rows_sum(keep, twin, refs[:-1]).astype(BF16)


def middle_kernel(near, far, gain, keep, twin, *refs):
    arrived, (hidden, out) = refs[:-2], refs[-2:]
    values = both_halves(near, far) + rows_sum(keep, twin, arrived)
    hidden[...] = values
    out[...] = (values * inverse_rms(values) * gain[...].astype(F32)).astype(BF16)


def pull_norm(values, gain, grad):
    inv = inverse_rms(values)
    scaled = grad * gain
    normed = values * inv
    d_values = inv * (scaled - normed * jnp.mean(scaled * normed, axis=-1, keepdims=True))
    return d_values, jnp.sum(grad * normed, axis=0, keepdims=True)


def back_two_kernel(hidden, near, far, gain, across, keep, twin, *refs):
    arrived, (d_hidden, low, d_gain) = refs[:-3], refs[-3:]
    grad = rows_sum(keep, twin, arrived) + across[...].astype(F32)
    d_values, d_gain[...] = pull_norm(hidden[...], gain[...].astype(F32), grad)
    total = both_halves(near, far) + d_values
    d_hidden[...] = total
    low[...] = total.astype(BF16)


def back_one_kernel(near, far, gain, d_hidden, keep, twin, *refs):
    arrived, (first, second, d_gain) = refs[:-3], refs[-3:]
    grad = rows_sum(keep, twin, arrived)
    d_values, d_gain[...] = pull_norm(both_halves(near, far), gain[...].astype(F32), grad)
    total = (d_hidden[...] + d_values).astype(BF16)
    share = first.shape[0]
    first[...] = total[:share]
    second[...] = total[share:]


def grad_kernel(row_parts, blocks, tables, *refs):
    rows, refs = refs[:row_parts], refs[row_parts:]
    right, refs = refs[0], refs[1:]
    keeps, send, left = refs[:blocks], refs[blocks], refs[blocks + 1]
    part, width = rows[0].shape
    block = keeps[0].shape[0]
    for p in range(row_parts):
        for c in range(width // LANES):
            tile = rows[p][:, c * LANES : (c + 1) * LANES].astype(F32)
            left[c * LANES : (c + 1) * LANES, p * part : (p + 1) * part] = tile.T.astype(BF16)
    for s in range(2 * blocks):
        at = pl.ds(pl.multiple_of(tables[3, s] * block, block), block)
        total = nn_dot(left[at, :], right[...]).astype(BF16)
        if s < blocks:
            keeps[s][...] = total
        else:
            send[(s - blocks) * block : (s - blocks + 1) * block, :] = total


def weight_partials(tables, rows, right, blocks):
    part, width = rows[0].shape
    length, cols = right.shape
    block = width // (2 * blocks)
    return pl.pallas_call(
        functools.partial(grad_kernel, len(rows), blocks),
        out_shape=(jax.ShapeDtypeStruct((block, cols), BF16),) * blocks
        + (jax.ShapeDtypeStruct((width // 2, cols), BF16),),
        in_specs=[smem()] + [vmem()] * (len(rows) + 1),
        out_specs=[vmem()] * (blocks + 1),
        scratch_shapes=[pltpu.VMEM((width, length), BF16)],
        compiler_params=pltpu.CompilerParams(vmem_limit_bytes=VMEM_LIMIT),
        cost_estimate=pl.CostEstimate(
            flops=2 * length * width * cols, bytes_accessed=8 << 20, transcendentals=0
        ),
        name="weight_partials",
    )(tables, *rows, right)


def hop(values, axis, flip):
    size = lax.axis_size(axis)
    return lax.ppermute(values, axis, [(i, i ^ flip) for i in range(size)])


def swap_blocks(values, axis, index, size):
    shape = values.shape
    bit = 1
    while bit < size:
        split = shape[:axis] + (size // (2 * bit), 2, bit) + shape[axis + 1 :]
        cut = values.reshape(split)
        cut = jnp.where((index & bit) != 0, jnp.flip(cut, axis + 1), cut)
        values = cut.reshape(shape)
        bit *= 2
    return values


def gather_chips(block):
    nt = lax.axis_size("tp")
    return [block] + [hop(block, "tp", 2 * k) for k in range(1, nt // 2)]


def with_twins(blocks):
    return blocks + [hop(block, "tp", 1) for block in blocks]


def gather_rows(block):
    return with_twins(gather_chips(block))


def region(ready, run):
    shapes = jax.eval_shape(run)
    return lax.cond(ready, run, lambda: jax.tree.map(lambda a: jnp.zeros(a.shape, a.dtype), shapes))


def chips_low(rest, twin, *behind):
    return rows_call(
        rest_kernel, "rest_rows", jax.ShapeDtypeStruct(rest.shape, BF16), rest, twin, behind=behind
    )


def chips_hop(low, nt):
    if nt == 4:
        return [hop(low, "tp", 2)]
    rows = low.shape[0] // (nt // 2 - 1)
    return [hop(low[(k - 1) * rows : k * rows], "tp", 2 * k) for k in range(1, nt // 2)]


def total_over(values):
    nt, nz = lax.axis_size("tp"), lax.axis_size("fsdp")
    values = values + hop(values, "tp", 1)
    across = hop(values, "ctx", 1)
    values = values + across
    values = sum([hop(values, "tp", 2 * k) for k in range(1, nt // 2)], values)
    return sum([hop(values, "fsdp", k) for k in range(1, nz)], values)


def shards(
    layer_in,
    attn_gain,
    ffn_gain,
    query_weight,
    key_weight,
    value_weight,
    out_weight,
    variate_bias,
    gate_weight,
    up_weight,
    down_weight,
    segment_ids,
    variate_ids,
    time_ids,
    out_grad,
):
    seq_count, share, width = layer_in.shape
    nz, nx, nt = lax.axis_size("fsdp"), lax.axis_size("ctx"), lax.axis_size("tp")
    iz, ix, it = lax.axis_index("fsdp"), lax.axis_index("ctx"), lax.axis_index("tp")
    assert nx == 2 and seq_count == nx
    length = segment_ids.shape[1]
    heads = variate_bias.shape[1]
    proj = heads * HEAD

    def pick(table, which):
        return lax.dynamic_index_in_dim(table, which, 0, keepdims=False)

    def swap(mine, theirs):
        return jnp.where(ix == 0, mine, theirs), jnp.where(ix == 0, theirs, mine)

    gain_one, gain_two = attn_gain[None], ffn_gain[None]
    part = nx * share
    low_rows = jax.ShapeDtypeStruct((part, width), BF16)
    wide_rows = jax.ShapeDtypeStruct((part, width), F32)
    gain_row = jax.ShapeDtypeStruct((1, width), F32)
    half_rows = jax.ShapeDtypeStruct((share, width), BF16)
    which = ix.astype(jnp.int32).reshape(1)
    ready = ix >= 0
    cols = gate_weight.shape[1] // 2
    near, grad_own = pick(layer_in, ix), out_grad
    attn_shape = jax.ShapeDtypeStruct((query_weight.shape[0], 4 * proj), BF16)
    ffn_shape = jax.ShapeDtypeStruct((gate_weight.shape[0], 3 * cols), BF16)
    attn_own = rows_call(
        pack_kernel, "pack_weights", attn_shape, query_weight, key_weight, value_weight, out_weight
    )
    mine, theirs = rows_call(
        split_kernel, "split_weights", (ffn_shape, ffn_shape), gate_weight, up_weight, down_weight, scalars=(which,)
    )

    def twin(block):
        return hop(block, "tp", 1)

    def across(block):
        return hop(block, "ctx", 1)

    def first_transfers():
        far = across(pick(layer_in, 1 - ix))
        attn_z = [hop(attn_own, "fsdp", k) for k in range(1, nz)]
        attn_x = across(attn_own)
        ffn_x = across(theirs)
        grad_y = gather_chips(grad_own)[1:]
        order = jnp.arange(nx * nt).reshape(nx, nt // 2, 2)
        order = swap_blocks(swap_blocks(swap_blocks(order, 0, ix, nx), 1, it // 2, nt // 2), 2, it % 2, 2)
        order = order.transpose(2, 1, 0).reshape(nx * nt)
        places = jnp.arange(nz * nx).reshape(nz, nx)
        places = swap_blocks(swap_blocks(places, 0, iz, nz), 1, ix, nx).transpose(1, 0).reshape(nz * nx)
        tables = attention_tables(
            pick(segment_ids, ix), pick(variate_ids, ix), pick(time_ids, ix), variate_bias, order, places
        )
        return far, attn_z, attn_x, ffn_x, grad_y, tables

    far, attn_z, attn_x, ffn_x, grad_y, made = region(ready, first_transfers)
    tables, cosine, sine, seg_row, seg_wide, feature, coef, hot_rows = made
    ffn_w = rows_call(
        stack_kernel, "stack_weights", jax.ShapeDtypeStruct((2 * ffn_shape.shape[0], 3 * cols), BF16), mine, ffn_x,
        scalars=(which,),
    )
    ffn_w = lax.all_gather(ffn_w, "fsdp", axis=0, tiled=True)

    def gather_one():
        rows = rows_call(norm_kernel, "norm_rows", low_rows, near, far, gain_one)
        return gather_rows(rows), [across(piece) for piece in attn_z]

    rows_one, rest_x = region(ready, gather_one)
    attn_w = [attn_own] + attn_z + [attn_x] + rest_x

    def attend():
        return across(grad_own), attention_forward(
            tables, rows_one, attn_w, cosine, sine, seg_row, seg_wide, feature, coef, heads
        )

    grad_far, (q_aug, k_aug, v_rows, mixed, lse, keep, rest, send, send_rest) = region(ready, attend)

    def scatter_attn():
        low = chips_low(rest, twin(send_rest))
        return chips_hop(low, nt), twin(send), [across(piece) for piece in grad_y]

    chips, twins, grad_far_y = region(ready, scatter_attn)
    grad_near, grad_far = [grad_own] + grad_y, [grad_far] + grad_far_y
    hidden, rows_two = rows_call(
        middle_kernel, "middle_rows", (wide_rows, low_rows), near, far, gain_two, keep, twins, *chips
    )

    def gather_two():
        return gather_chips(rows_two), across(rows_two), with_twins(grad_near), with_twins(grad_far), twin(rows_two)

    chips_two, next_own, grad_near, grad_far, rows_twin = region(ready, gather_two)

    def ffn_own():
        rows = chips_two + [rows_twin] + [twin(block) for block in chips_two[1:]]
        return [across(block) for block in chips_two[1:]], rows, ffn_middle(
            False, which, rows, grad_near, grad_far, ffn_w
        )

    next_y, rows_two, (act, d_both, keep, rest, send, send_rest) = region(ready, ffn_own)

    def ffn_next():
        low = chips_low(rest, twin(send_rest))
        rows = with_twins([next_own] + next_y)
        return chips_hop(low, nt), twin(send), rows, ffn_middle(True, 1 - which, rows, grad_near, grad_far, ffn_w)

    chips, twins, rows_next, made = region(ready, ffn_next)
    act_next, d_both_next, keep_next, rest_next, send_next, send_rest = made
    low_next = chips_low(rest_next, twin(send_rest))

    def scatter_next():
        parts = ffn_result(act, act_next, ffn_w, part)
        return chips_hop(low_next, nt), twin(send_next), parts, [twin(parts[k]) for k in (2, 3, 6, 7)]

    chips_next, twins_next, ffn_parts, out_twins = region(ready, scatter_next)
    low_across = rows_call(sum_kernel, "sum_rows", low_rows, keep_next, twins_next, *chips_next)
    low_out = chips_low(ffn_parts[1], out_twins[1])

    def cross_next():
        return across(low_across), chips_hop(low_out, nt), ffn_partials(
            which, rows_two, rows_next, grad_near, grad_far, act, act_next, d_both, d_both_next
        )

    arrived, out_chips, ffn_grad = region(ready, cross_next)
    ffn_grad = lax.psum_scatter(ffn_grad, "fsdp", scatter_dimension=0, tiled=True)
    d_hidden, low, d_gain_two = rows_call(
        back_two_kernel,
        "back_two",
        (wide_rows, low_rows, gain_row),
        hidden,
        pick(grad_near[0], ix),
        pick(grad_far[0], ix),
        gain_two,
        arrived,
        keep,
        twins,
        *chips,
    )

    def gather_back():
        rows = gather_rows(low)
        return rows, chips_low(ffn_parts[5], out_twins[3])

    branch_rows, low_out = region(ready, gather_back)
    out_grads = weight_partials(tables, branch_rows, mixed, nz)

    def attend_back():
        return chips_hop(low_out, nt), across(out_grads[-1]), attention_backward(
            tables, branch_rows, attn_w, q_aug, k_aug, v_rows, lse, cosine, sine, seg_row, seg_wide, hot_rows, heads
        )

    out_chips_next, out_other, made = region(ready, attend_back)
    keep, rest, send, send_rest, d_qkv, bias_parts = made

    def scatter_one():
        low = chips_low(rest, twin(send_rest))
        grads = weight_partials(tables, rows_one, d_qkv, nz)
        sums = pair_sums(out_grads, out_other)
        arrived = [hop(piece, "fsdp", k) for k, piece in enumerate(sums) if k > 0]
        return chips_hop(low, nt), twin(send), grads, across(grads[-1]), sums[0], arrived

    chips, twins, qkv_grads, qkv_other, out_sum, out_arrived = region(ready, scatter_one)
    d_near, d_far, d_gain_one = rows_call(
        back_one_kernel,
        "back_one",
        (half_rows, half_rows, gain_row),
        near,
        far,
        gain_one,
        d_hidden,
        keep,
        twins,
        *chips,
    )
    qkv_sums = pair_sums(qkv_grads, qkv_other)
    bias_sums = jnp.sum(bias_parts, axis=2)
    bias_sums = jnp.stack([jnp.sum(bias_sums[:, :8], axis=1), jnp.sum(bias_sums[:, 8:], axis=1)])
    spread = lax.dynamic_update_slice(jnp.zeros((2, width), F32), bias_sums, (0, it * heads))
    gains = jnp.concatenate([d_gain_one, d_gain_two, spread], axis=0)

    def last_transfers():
        arrived = [hop(piece, "fsdp", k) for k, piece in enumerate(qkv_sums) if k > 0]
        ffn_half = ffn_grad.shape[0] // 2
        ffn_far = across(lax.dynamic_slice_in_dim(ffn_grad, (1 - ix) * ffn_half, ffn_half, 0))
        held, sent = rows_call(
            out_kernel,
            "out_rows",
            (jax.ShapeDtypeStruct(layer_in.shape, F32), jax.ShapeDtypeStruct(layer_in.shape, BF16)),
            hidden,
            ffn_parts[0],
            out_twins[0],
            ffn_parts[4],
            out_twins[2],
            *out_chips,
            *out_chips_next,
        )
        (out_weight_grad,) = weight_sums(out_sum, out_arrived, 1)
        return arrived, ffn_far, across(d_far), held, across(sent), total_over(gains), out_weight_grad

    arrived, ffn_far, d_cross, held, out_cross, totals, out_weight_grad = region(ready, last_transfers)
    query_grad, key_grad, value_grad = weight_sums(qkv_sums[0], arrived, 3)
    in_grad = jnp.stack(swap(d_near, d_cross))
    layer_out = rows_call(
        out_finish_kernel, "layer_out", jax.ShapeDtypeStruct(layer_in.shape, BF16), held, out_cross, scalars=(which,)
    )
    gate_grad, up_grad, down_grad = rows_call(
        ffn_finish_kernel, "ffn_sums", [jax.ShapeDtypeStruct(gate_weight.shape, F32)] * 3, ffn_grad, ffn_far,
        scalars=(which,),
    )
    bias_grad = lax.dynamic_slice(totals, (2, it * heads), (2, heads))
    return (
        layer_out,
        in_grad,
        totals[0],
        totals[1],
        query_grad,
        key_grad,
        value_grad,
        out_weight_grad,
        bias_grad,
        gate_grad,
        up_grad,
        down_grad,
    )


def solution(mesh):
    rows = P("fsdp", ("ctx", "tp"), None)
    weight = P(("fsdp", "ctx"), "tp")
    ids = P("fsdp", None)
    bias = P(None, "tp")
    in_specs = (rows, P(), P()) + (weight,) * 4 + (bias,) + (weight,) * 3 + (ids,) * 3 + (rows,)
    out_specs = (rows, rows, P(), P()) + (weight,) * 4 + (bias,) + (weight,) * 3
    return jax.shard_map(shards, mesh=mesh, in_specs=in_specs, out_specs=out_specs, check_vma=False)
```

```python
import functools
import jax
import jax.numpy as jnp
from jax import lax
from jax.sharding import PartitionSpec as P
from jax.experimental import pallas as pl
from jax.experimental.pallas import tpu as pltpu

HEADS = 16
HEAD = 64
EPS = 1e-05
NEG = -1e30
F32 = jnp.float32
BF16 = jnp.bfloat16
LANES = 128
QUERIES = 256
STEP = 128
VMEM_LIMIT = 56 * 1024 * 1024


def nt_dot(left, right):
    return lax.dot_general(left, right, (((1,), (1,)), ((), ())), preferred_element_type=F32)


def nn_dot(left, right):
    return lax.dot_general(left, right, (((1,), (0,)), ((), ())), preferred_element_type=F32)


def tn_dot(left, right):
    return lax.dot_general(left, right, (((0,), (0,)), ((), ())), preferred_element_type=F32)


def lane_of(shape):
    return lax.broadcasted_iota(jnp.int32, shape, len(shape) - 1)


def half_swap(values):
    lane = lane_of(values.shape)
    forward = pltpu.roll(values, LANES - HEAD // 2, 1)
    back = pltpu.roll(values, HEAD // 2, 1)
    return jnp.where(lane % HEAD < HEAD // 2, forward, back)


def fwd_kernel(row_parts, weight_parts, heads, *refs):
    tables, refs = refs[0], refs[1:]
    rows, refs = refs[:row_parts], refs[row_parts:]
    weights, refs = refs[:weight_parts], refs[weight_parts:]
    cosine, sine, seg_row, seg_wide, feature, coef = refs[:6]
    q_aug, k_aug, v_out, mixed_out, lse_out, keep_out, rest_out, send_own, send_rest = refs[6:15]
    full, out_full, mixed_wide, v_turn = refs[15:]
    pairs = heads // 2
    proj = heads * HEAD
    length = q_aug.shape[1]
    block = weights[0].shape[0]
    part = rows[0].shape[0]
    share = part // 2
    for i in range(weight_parts):
        at = pl.ds(pl.multiple_of(tables[3, i] * block, block), block)
        full[at, :] = weights[i][:block, : 3 * proj]
        out_full[at, :] = weights[i][:block, 3 * proj : 4 * proj]
    for p in range(row_parts):
        raw = nn_dot(rows[p][...], full[...])
        for k in range(2):
            piece = raw[k * share : (k + 1) * share]
            start = pl.multiple_of(tables[0, 2 * p + k] * share, share)
            at = pl.ds(start, share)
            cos_now, sin_now, feat = cosine[at, :], sine[at, :], feature[at, :].astype(F32)
            lane = lane_of((share, LANES))
            for pair in range(pairs):
                low = pair * LANES
                q = piece[:, low : low + LANES]
                q = (q * cos_now + half_swap(q) * sin_now).astype(BF16).astype(F32) * HEAD**-0.5
                kk = piece[:, proj + low : proj + low + LANES]
                kk = kk * cos_now + half_swap(kk) * sin_now
                v_out[pair, at, :] = piece[:, 2 * proj + low : 2 * proj + low + LANES].astype(BF16)
                for odd in range(2):
                    head = 2 * pair + odd
                    q_now = pltpu.roll(q, HEAD, 1) if odd else q
                    k_now = pltpu.roll(kk, HEAD, 1) if odd else kk
                    q_feat = feat * coef[head : head + 1, :]
                    q_aug[head, at, :] = jnp.where(lane < HEAD, q_now, q_feat).astype(BF16)
                    k_aug[head, at, :] = jnp.where(lane < HEAD, k_now, feat).astype(BF16)
    for pair in range(pairs):
        for b in range(length // LANES):
            tile = v_out[pair, b * LANES : (b + 1) * LANES, :].astype(F32)
            v_turn[pair, :, b * LANES : (b + 1) * LANES] = tile.T.astype(BF16)

    def query_block(b, carry):
        at = pl.ds(pl.multiple_of(b * QUERIES, QUERIES), QUERIES)
        seg_q = seg_row[pl.ds(b, 1), :]
        first = pl.multiple_of(tables[1, b] * LANES, LANES)
        for kind in range(1, length // STEP + 1):

            @pl.when(tables[2, b] == kind)
            def _(kind=kind):
                win = pl.ds(first, kind * STEP)
                keep = seg_wide[win, :] == seg_q
                scores = [nt_dot(k_aug[h, win, :], q_aug[h, at, :]) for h in range(heads)]
                probs, totals = [], []
                for head in range(heads):
                    s = jnp.where(keep, scores[head], NEG)
                    top = jnp.max(s, axis=0, keepdims=True)
                    p = jnp.exp(s - top)
                    total = jnp.sum(p, axis=0, keepdims=True)
                    probs.append(p.astype(BF16))
                    totals.append(total)
                    lse_out[head, pl.ds(b, 1), :] = top + jnp.log(total)
                for pair in range(pairs):
                    outs = []
                    for odd in range(2):
                        head = 2 * pair + odd
                        turn = v_turn[pair, odd * HEAD : (odd + 1) * HEAD, win]
                        outs.append(nn_dot(turn, probs[head]) / totals[head])
                    mixed = jnp.concatenate(outs, axis=0).T
                    mixed_wide[at, pair * LANES : (pair + 1) * LANES] = mixed

        return carry

    lax.fori_loop(0, length // QUERIES, query_block, 0)
    for slot in range(2 * row_parts):
        start = pl.multiple_of(tables[0, slot] * share, share)
        piece = mixed_wide[pl.ds(start, share), :]
        mixed_out[slot * share : (slot + 1) * share, :] = piece.astype(BF16)
    half = row_parts // 2
    for p in range(row_parts):
        back = nt_dot(mixed_out[p * part : (p + 1) * part, :], out_full[...])
        if p == 0:
            keep_out[...] = back
        elif p < half:
            rest_out[(p - 1) * part : p * part, :] = back
        else:
            if p == half:
                send_own[...] = back.astype(BF16)
            else:
                send_rest[(p - half - 1) * part : (p - half) * part, :] = back.astype(BF16)


def vmem():
    return pl.BlockSpec(memory_space=pltpu.VMEM)


def anywhere():
    return pl.BlockSpec(memory_space=pl.ANY)


def smem():
    return pl.BlockSpec(memory_space=pltpu.SMEM)


def attention_forward(tables, rows, weights, cosine, sine, seg_row, seg_wide, feature, coef, heads, behind=()):
    proj = heads * HEAD
    length = cosine.shape[0]
    part, width = rows[0].shape
    shapes = (
        jax.ShapeDtypeStruct((heads, length, LANES), BF16),
        jax.ShapeDtypeStruct((heads, length, LANES), BF16),
        jax.ShapeDtypeStruct((heads // 2, length, LANES), BF16),
        jax.ShapeDtypeStruct((length, proj), BF16),
        jax.ShapeDtypeStruct((heads, length // QUERIES, QUERIES), F32),
        jax.ShapeDtypeStruct((part, width), F32),
        jax.ShapeDtypeStruct((length // 2 - part, width), F32),
        jax.ShapeDtypeStruct((part, width), BF16),
        jax.ShapeDtypeStruct((length // 2 - part, width), BF16),
    )
    count = len(rows) + len(weights) + 6
    operands = (tables, *rows, *weights, cosine, sine, seg_row, seg_wide, feature, coef)
    return pl.pallas_call(
        without(functools.partial(fwd_kernel, len(rows), len(weights), heads), len(operands), len(behind)),
        out_shape=shapes,
        in_specs=[smem()] + [vmem()] * count + [anywhere()] * len(behind),
        out_specs=[vmem()] * 9,
        scratch_shapes=[
            pltpu.VMEM((width, 3 * proj), BF16),
            pltpu.VMEM((width, proj), BF16),
            pltpu.VMEM((length, proj), F32),
            pltpu.VMEM((heads // 2, LANES, length), BF16),
        ],
        compiler_params=pltpu.CompilerParams(vmem_limit_bytes=VMEM_LIMIT),
        cost_estimate=pl.CostEstimate(
            flops=2 * length * width * 3 * proj, bytes_accessed=8 << 20, transcendentals=length * length * heads // 2
        ),
        name="attn_fwd",
    )(*operands, *behind)


def bwd_kernel(row_parts, weight_parts, heads, *refs):
    tables, refs = refs[0], refs[1:]
    rows, refs = refs[:row_parts], refs[row_parts:]
    weights, refs = refs[:weight_parts], refs[weight_parts:]
    q_aug, k_aug, v_in, lse, cosine, sine, seg_row, seg_wide, hot_rows = refs[:9]
    keep_out, rest_out, send_own, send_rest, d_qkv_out, bias_out = refs[9:15]
    full, out_full, d_out, k_turn, dq_acc, dk_acc, dv_acc = refs[15:]
    pairs = heads // 2
    proj = heads * HEAD
    length = q_aug.shape[1]
    block = weights[0].shape[0]
    part = rows[0].shape[0]
    share = part // 2
    for i in range(weight_parts):
        at = pl.ds(pl.multiple_of(tables[3, i] * block, block), block)
        full[at, :] = weights[i][:block, : 3 * proj]
        out_full[at, :] = weights[i][:block, 3 * proj : 4 * proj]
    for p in range(row_parts):
        raw = nn_dot(rows[p][...], out_full[...]).astype(BF16)
        for k in range(2):
            start = pl.multiple_of(tables[0, 2 * p + k] * share, share)
            d_out[pl.ds(start, share), :] = raw[k * share : (k + 1) * share]
    for head in range(heads):
        for b in range(length // LANES):
            tile = k_aug[head, b * LANES : (b + 1) * LANES, :].astype(F32)
            k_turn[head, :, b * LANES : (b + 1) * LANES] = tile.T.astype(BF16)
    dk_acc[...] = jnp.zeros(dk_acc.shape, F32)
    dv_acc[...] = jnp.zeros(dv_acc.shape, F32)
    bias_out[...] = jnp.zeros(bias_out.shape, F32)

    def query_block(b, carry):
        at = pl.ds(pl.multiple_of(b * QUERIES, QUERIES), QUERIES)
        seg_q = seg_row[pl.ds(b, 1), :]
        hot = hot_rows[:, at]
        first = pl.multiple_of(tables[1, b] * LANES, LANES)
        for kind in range(1, length // STEP + 1):

            @pl.when(tables[2, b] == kind)
            def _(kind=kind):
                win = pl.ds(first, kind * STEP)
                keep = seg_wide[win, :] == seg_q
                owns = []
                for head in range(heads):
                    chunk = slice(head // 2 * LANES, (head // 2 + 1) * LANES)
                    d_pair = d_out[at, chunk]
                    lane = lane_of(d_pair.shape)
                    owns.append(jnp.where((lane >= HEAD) == (head % 2 == 1), d_pair, jnp.zeros_like(d_pair)))
                turned = []
                for base in range(0, heads, 2):
                    group = range(base, base + 2)
                    s = [nt_dot(k_aug[h, win, :], q_aug[h, at, :]) for h in group]
                    dp = [nt_dot(v_in[h // 2, win, :], owns[h]) for h in group]
                    low, ds = [], []
                    for i, h in enumerate(group):
                        p = jnp.exp(jnp.where(keep, s[i] - lse[h, pl.ds(b, 1), :], NEG))
                        low.append(p.astype(BF16))
                        ds.append((p * (dp[i] - jnp.sum(p * dp[i], axis=0, keepdims=True))).astype(BF16))
                    for i, h in enumerate(group):
                        if i % 2 == 0:
                            both = jnp.concatenate(low[i : i + 2], axis=1)
                            dv_acc[h // 2, win, :] += nn_dot(both, jnp.concatenate(owns[h : h + 2], axis=0))
                        dk_acc[h, win, :] += nn_dot(ds[i], q_aug[h, at, :])
                        dq = nn_dot(k_turn[h, :, win], ds[i])
                        turned.append(dq[:HEAD])
                        sums = dq[HEAD : HEAD + 8]
                        bias_out[h] += jnp.concatenate([sums * hot[:8], sums * hot[8:]], axis=0)
                for pair in range(pairs):
                    chunk = slice(pair * LANES, (pair + 1) * LANES)
                    dq_acc[at, chunk] = jnp.concatenate(turned[2 * pair : 2 * pair + 2], axis=0).T * HEAD**-0.5

        return carry

    lax.fori_loop(0, length // QUERIES, query_block, 0)
    for p in range(row_parts):
        for k in range(2):
            slot = 2 * p + k
            at = pl.ds(pl.multiple_of(tables[0, slot] * share, share), share)
            to = slice(slot * share, (slot + 1) * share)
            cos_now, sin_now = cosine[at, :], sine[at, :]
            lane = lane_of((share, LANES))
            for pair in range(pairs):
                low = pair * LANES
                dq = dq_acc[at, low : low + LANES]
                dk = jnp.where(lane < HEAD, dk_acc[2 * pair, at, :], pltpu.roll(dk_acc[2 * pair + 1, at, :], HEAD, 1))
                d_qkv_out[to, low : low + LANES] = (dq * cos_now - half_swap(dq) * sin_now).astype(BF16)
                d_qkv_out[to, proj + low : proj + low + LANES] = (dk * cos_now - half_swap(dk) * sin_now).astype(BF16)
                d_qkv_out[to, 2 * proj + low : 2 * proj + low + LANES] = dv_acc[pair, at, :].astype(BF16)
        part_rows = d_qkv_out[p * part : (p + 1) * part, :]
        back = nt_dot(part_rows, full[...])
        half = row_parts // 2
        if p == 0:
            keep_out[...] = back
        elif p < half:
            rest_out[(p - 1) * part : p * part, :] = back
        else:
            if p == half:
                send_own[...] = back.astype(BF16)
            else:
                send_rest[(p - half - 1) * part : (p - half) * part, :] = back.astype(BF16)


def attention_backward(tables, rows, weights, q_aug, k_aug, v_in, lse, cosine, sine, seg_row, seg_wide, hot_rows, heads, behind=()):
    proj = heads * HEAD
    length = cosine.shape[0]
    part, width = rows[0].shape
    shapes = (
        jax.ShapeDtypeStruct((part, width), F32),
        jax.ShapeDtypeStruct((length // 2 - part, width), F32),
        jax.ShapeDtypeStruct((part, width), BF16),
        jax.ShapeDtypeStruct((length // 2 - part, width), BF16),
        jax.ShapeDtypeStruct((length, 3 * proj), BF16),
        jax.ShapeDtypeStruct((heads, 16, QUERIES), F32),
    )
    count = len(rows) + len(weights) + 9
    operands = (tables, *rows, *weights, q_aug, k_aug, v_in, lse, cosine, sine, seg_row, seg_wide, hot_rows)
    return pl.pallas_call(
        without(functools.partial(bwd_kernel, len(rows), len(weights), heads), len(operands), len(behind)),
        out_shape=shapes,
        in_specs=[smem()] + [vmem()] * count + [anywhere()] * len(behind),
        out_specs=[vmem()] * 6,
        scratch_shapes=[
            pltpu.VMEM((width, 3 * proj), BF16),
            pltpu.VMEM((width, proj), BF16),
            pltpu.VMEM((length, proj), BF16),
            pltpu.VMEM((heads, LANES, length), BF16),
            pltpu.VMEM((length, proj), F32),
            pltpu.VMEM((heads, length, LANES), F32),
            pltpu.VMEM((heads // 2, length, LANES), F32),
        ],
        compiler_params=pltpu.CompilerParams(vmem_limit_bytes=VMEM_LIMIT),
        cost_estimate=pl.CostEstimate(
            flops=2 * length * width * 4 * proj, bytes_accessed=12 << 20, transcendentals=length * length * heads // 2
        ),
        name="attn_bwd",
    )(*operands, *behind)


def attention_tables(segments, variates, times, variate_bias, order, places):
    length = segments.shape[0]
    heads = variate_bias.shape[1]
    count = length // QUERIES
    half = HEAD // 2
    frequency = 10000.0 ** (-2.0 * jnp.arange(half, dtype=F32) / HEAD)
    angles = times.astype(F32)[:, None] * frequency
    cos_half, sin_half = jnp.cos(angles), jnp.sin(angles)
    wide = jax.ShapeDtypeStruct((length, LANES), F32)
    cosine, sine = rows_call(
        widen_kernel, "widen_angles", (wide, wide), jnp.concatenate([cos_half, sin_half], axis=1)
    )
    seg_row = segments.reshape(count, QUERIES)
    seg_wide = jnp.broadcast_to(segments[:, None], (length, QUERIES))
    lane = jnp.arange(LANES)
    live = (lane >= HEAD) & (lane < HEAD + 12)
    feature = ((variates[:, None] == (lane % 4)[None, :]) & live[None, :]).astype(BF16)
    gap = variate_bias[0] - variate_bias[1]
    high = lax.reduce_precision(gap, 8, 7)
    mid = lax.reduce_precision(gap - high, 8, 7)
    low = lax.reduce_precision(gap - high - mid, 8, 7)
    parts = jnp.repeat(jnp.stack([high, mid, low], axis=1), 4, axis=1)
    coef = jnp.pad(parts, ((0, -heads % 8), (HEAD, LANES - HEAD - 12)))
    kinds = jnp.arange(4)
    same = (variates[None, :] == kinds[:, None]).astype(F32)
    zeros = jnp.zeros_like(same)
    hot_rows = jnp.concatenate([same, zeros, 1.0 - same, zeros], axis=0)
    ends = segments.reshape(count, QUERIES)
    start = jnp.sum(segments[None, :] < ends[:, :1], axis=1)
    stop = jnp.sum(segments[None, :] <= ends[:, -1:], axis=1)
    first = start // LANES
    kind = (stop - first * LANES + STEP - 1) // STEP
    first = jnp.minimum(first, (length - kind * STEP) // LANES)
    size = max(count, order.shape[0], places.shape[0])
    pad = lambda a: jnp.pad(a.astype(jnp.int32), (0, size - a.shape[0]))
    tables = jnp.stack([pad(order), pad(first), pad(kind), pad(places)])
    return tables, cosine, sine, seg_row, seg_wide, feature, coef, hot_rows


def ffn_kernel(row_parts, flipped, which, *refs):
    rows, refs = refs[:row_parts], refs[row_parts:]
    near, refs = refs[:row_parts], refs[row_parts:]
    far, refs = refs[:row_parts], refs[row_parts:]
    weight, act_out, d_both_out, keep_out, rest_out, send_own, send_rest, grads, sems = refs
    part = rows[0].shape[0]
    share = part // 2
    cols = act_out.shape[1]
    half = row_parts // 2
    copies = []
    for p in range(row_parts):
        pair = (far[p], near[p]) if flipped else (near[p], far[p])
        for k in range(2):
            copy = pltpu.make_async_copy(pair[k].at[which[0]], grads.at[p, pl.ds(k * share, share)], sems.at[p, k])
            copy.start()
            copies.append(copy)
    for p in list(range(half, row_parts)) + list(range(half)):
        at = slice(p * part, (p + 1) * part)
        both = nn_dot(rows[p][...], weight[:, : 2 * cols])
        copies[2 * p].wait()
        copies[2 * p + 1].wait()
        d_act = nn_dot(grads[p], weight[:, 2 * cols :])
        gate, up = both[:, :cols], both[:, cols:]
        sig = 1.0 / (1.0 + jnp.exp(-gate))
        silu = gate * sig
        act_out[at, :] = (silu * up).astype(BF16)
        d_both_out[at, :cols] = (d_act * up * (sig + silu * (1.0 - sig))).astype(BF16)
        d_both_out[at, cols:] = (d_act * silu).astype(BF16)
        back = nt_dot(d_both_out[at, :], weight[:, : 2 * cols])
        if p == 0:
            keep_out[...] = back
        elif p < half:
            rest_out[(p - 1) * part : p * part, :] = back
        else:
            if p == half:
                send_own[...] = back.astype(BF16)
            else:
                send_rest[(p - half - 1) * part : (p - half) * part, :] = back.astype(BF16)


def ffn_middle(flipped, which, rows, near, far, weight, behind=()):
    part, width = rows[0].shape
    count = len(rows)
    length = part * count
    cols = weight.shape[1] // 3
    operands = (which, *rows, *near, *far, weight)
    return pl.pallas_call(
        without(functools.partial(ffn_kernel, count, flipped), len(operands), len(behind)),
        out_shape=(
            jax.ShapeDtypeStruct((length, cols), BF16),
            jax.ShapeDtypeStruct((length, 2 * cols), BF16),
            jax.ShapeDtypeStruct((part, width), F32),
            jax.ShapeDtypeStruct((length // 2 - part, width), F32),
            jax.ShapeDtypeStruct((part, width), BF16),
            jax.ShapeDtypeStruct((length // 2 - part, width), BF16),
        ),
        in_specs=[smem()] + [vmem()] * count + [anywhere()] * (2 * count) + [vmem()] + [anywhere()] * len(behind),
        out_specs=[vmem()] * 6,
        scratch_shapes=[pltpu.VMEM((count, part, width), BF16), pltpu.SemaphoreType.DMA((count, 2))],
        compiler_params=pltpu.CompilerParams(vmem_limit_bytes=VMEM_LIMIT),
        cost_estimate=pl.CostEstimate(
            flops=10 * length * width * cols, bytes_accessed=16 << 20, transcendentals=length * cols
        ),
        name="ffn_middle",
    )(*operands, *behind)


def ffn_grad_kernel(row_parts, which, *refs):
    own, refs = refs[:row_parts], refs[row_parts:]
    other, refs = refs[:row_parts], refs[row_parts:]
    near, refs = refs[:row_parts], refs[row_parts:]
    far, refs = refs[:row_parts], refs[row_parts:]
    act_own, act_other, d_own, d_other, out, left = refs
    part, width = own[0].shape
    share = part // 2
    length = part * row_parts
    cols = act_own.shape[1]
    ix = which[0]
    for what in range(2):
        for seq in range(2):
            for p in range(row_parts):
                at = seq * length + p * part
                for c in range(width // LANES):
                    lanes = slice(c * LANES, (c + 1) * LANES)
                    if what == 0:
                        now = ix if seq == 0 else 1 - ix
                        pair = (near[p], far[p]) if seq == 0 else (far[p], near[p])
                        tile = jnp.concatenate([ref[now, :, lanes] for ref in pair], axis=0)
                    else:
                        tile = (own, other)[seq][p][:, lanes]
                    left[lanes, at : at + part] = tile.astype(F32).T.astype(BF16)
        first, second = ((act_own, act_other), (d_own, d_other))[what]
        to = slice(2 * cols, 3 * cols) if what == 0 else slice(0, 2 * cols)
        step = width // 4
        for s in range(4):
            at = slice(s * step, (s + 1) * step)
            total = nn_dot(left[at, :length], first[...]) + nn_dot(left[at, length:], second[...])
            out[at, to] = total.astype(BF16)


def ffn_partials(which, own, other, near, far, act_own, act_other, d_own, d_other, behind=()):
    part, width = own[0].shape
    length = part * len(own)
    cols = act_own.shape[1]
    operands = (which, *own, *other, *near, *far, act_own, act_other, d_own, d_other)
    return pl.pallas_call(
        without(functools.partial(ffn_grad_kernel, len(own)), len(operands), len(behind)),
        out_shape=jax.ShapeDtypeStruct((width, 3 * cols), BF16),
        in_specs=[smem()] + [vmem()] * (4 * len(own) + 4) + [anywhere()] * len(behind),
        out_specs=vmem(),
        scratch_shapes=[pltpu.VMEM((width, 2 * length), BF16)],
        compiler_params=pltpu.CompilerParams(vmem_limit_bytes=VMEM_LIMIT),
        cost_estimate=pl.CostEstimate(
            flops=12 * length * width * cols, bytes_accessed=17 << 20, transcendentals=0
        ),
        name="ffn_partials",
    )(*operands, *behind)


def ffn_out_kernel(act_own, act_other, weight, *outs):
    length, cols = act_own.shape
    part = outs[0].shape[0]
    half = length // 2
    down = weight[:, 2 * cols :]
    for seq, act in enumerate((act_own, act_other)):
        both = nt_dot(act[:half, :], down)
        outs[4 * seq][...] = both[:part]
        outs[4 * seq + 1][...] = both[part:]
        both = nt_dot(act[half:, :], down).astype(BF16)
        outs[4 * seq + 2][...] = both[:part]
        outs[4 * seq + 3][...] = both[part:]


def ffn_result(act_own, act_other, weight, part, behind=()):
    length, cols = act_own.shape
    width = weight.shape[0]
    shapes = (
        jax.ShapeDtypeStruct((part, width), F32),
        jax.ShapeDtypeStruct((length // 2 - part, width), F32),
        jax.ShapeDtypeStruct((part, width), BF16),
        jax.ShapeDtypeStruct((length // 2 - part, width), BF16),
    )
    operands = (act_own, act_other, weight)
    return pl.pallas_call(
        without(ffn_out_kernel, len(operands), len(behind)),
        out_shape=shapes * 2,
        in_specs=[vmem()] * 3 + [anywhere()] * len(behind),
        out_specs=[vmem()] * 8,
        compiler_params=pltpu.CompilerParams(vmem_limit_bytes=VMEM_LIMIT),
        cost_estimate=pl.CostEstimate(
            flops=4 * length * width * cols, bytes_accessed=12 << 20, transcendentals=0
        ),
        name="ffn_result",
    )(*operands, *behind)


def without(kernel, start, count):
    return lambda *refs: kernel(*refs[:start], *refs[start + count :])


def rows_call(kernel, name, shapes, *operands, scalars=(), behind=()):
    single = not isinstance(shapes, (list, tuple))
    count = len(scalars) + len(operands)
    return pl.pallas_call(
        without(kernel, count, len(behind)),
        out_shape=shapes,
        in_specs=[smem()] * len(scalars) + [vmem()] * len(operands) + [anywhere()] * len(behind),
        out_specs=vmem() if single else [vmem()] * len(shapes),
        compiler_params=pltpu.CompilerParams(vmem_limit_bytes=VMEM_LIMIT),
        cost_estimate=pl.CostEstimate(
            flops=16 * operands[0].size, bytes_accessed=sum(o.size * o.dtype.itemsize for o in operands), transcendentals=0
        ),
        name=name,
    )(*scalars, *operands, *behind)


def pack_kernel(which, rows, query, key, value, out, gate, up, down, own, mine, packed):
    block, start = own.shape[0], 0
    for ref in (query, key, value, out):
        stop = start + ref.shape[1]
        own[:, start:stop] = ref[...]
        packed[:block, start:stop] = ref[...]
        start = stop
    width = rows.shape[2]
    packed[: rows.shape[1], start : start + width] = rows[1 - which[0]]
    start += width
    cols = gate.shape[1] // 2
    for k, ref in enumerate((gate, up, down)):
        for half in range(2):

            @pl.when(which[0] == half)
            def _(ref=ref, half=half, k=k):
                mine[:, k * cols : (k + 1) * cols] = ref[:, half * cols : (half + 1) * cols]
                packed[:block, start + k * cols : start + (k + 1) * cols] = ref[:, (1 - half) * cols : (2 - half) * cols]


def far_rows(near, packed, start):
    share, width = near.shape
    return packed[:share, start : start + width]


def stack_kernel(start, which, mine, theirs, out):
    block, width = mine.shape
    first = pl.multiple_of(which[0] * block, block)
    second = pl.multiple_of((1 - which[0]) * block, block)
    out[pl.ds(first, block), :] = mine[...]
    out[pl.ds(second, block), :] = theirs[:block, start : start + width]


def gains_kernel(place, gain_rows, gain, d_gain_two, bias_parts, out):
    blocks, _, block = gain_rows.shape
    for k in range(blocks):
        at = slice(k * block, (k + 1) * block)
        out[0:1, at] = gain_rows[k, 0:1, :] / gain[:, at].astype(F32)
    out[1:2, :] = d_gain_two[...]
    out[2:, :] = jnp.zeros(out[2:, :].shape, F32)
    lane = lane_of((1, LANES))
    lanes = pl.ds(pl.multiple_of(place[0] * LANES, LANES), LANES)
    for row in range(2):
        line = jnp.zeros((1, LANES), F32)
        for head in range(bias_parts.shape[0]):
            line = jnp.where(lane == head, jnp.sum(bias_parts[head, 8 * row : 8 * row + 8, :]), line)
        out[2 + row : 3 + row, lanes] = line


def gains_finish_kernel(place, mine, theirs, one, two, bias):
    total = mine[...] + theirs[...]
    one[...] = total[0:1]
    two[...] = total[1:2]
    lanes = pl.ds(pl.multiple_of(place[0] * LANES, LANES), LANES)
    bias[...] = mine[:, lanes] + theirs[:, lanes]


def widen_kernel(angles, cosine, sine):
    half = angles.shape[1] // 2
    cos_half, sin_half = angles[:, :half], angles[:, half:]
    cosine[...] = jnp.concatenate([cos_half] * (LANES // half), axis=1)
    sine[...] = jnp.concatenate([-sin_half, sin_half] * (LANES // half // 2), axis=1)


def pair_kernel(*refs):
    blocks = (len(refs) - 1) // 2
    keeps, other, outs = refs[:blocks], refs[blocks], refs[blocks + 1 :]
    rows = keeps[0].shape[0]
    for k in range(blocks):
        total = keeps[k][...].astype(F32) + other[k * rows : (k + 1) * rows, :].astype(F32)
        outs[k][...] = total.astype(outs[k].dtype)


def finish_kernel(count, own, *refs):
    total = own[...]
    for ref in refs[:-count]:
        total = total + ref[...].astype(F32)
    start = 0
    for out in refs[-count:]:
        stop = start + out.shape[1]
        out[...] = total[:, start:stop]
        start = stop


def pair_sums(partials, other):
    shape = partials[0].shape
    blocks = len(partials) - 1
    shapes = [jax.ShapeDtypeStruct(shape, F32 if k == 0 else BF16) for k in range(blocks)]
    return rows_call(pair_kernel, "pair_sums", shapes, *partials[:-1], other)


def weight_sums(own, arrived, pieces):
    outs = [jax.ShapeDtypeStruct((own.shape[0], own.shape[1] // pieces), F32)] * pieces
    return rows_call(functools.partial(finish_kernel, pieces), "weight_sums", outs, own, *arrived)


def ffn_finish_kernel(start, which, grads, far, *outs):
    cols = grads.shape[1] // 3
    rows = grads.shape[0] // 2
    mine = grads[pl.ds(pl.multiple_of(which[0] * rows, rows), rows), :].astype(F32)
    theirs = far[:rows, start:].astype(F32)
    for own in range(2):

        @pl.when(which[0] == own)
        def _(own=own):
            for k, out in enumerate(outs):
                out[:, own * cols : (own + 1) * cols] = mine[:, k * cols : (k + 1) * cols]
                out[:, (1 - own) * cols : (2 - own) * cols] = theirs[:, k * cols : (k + 1) * cols]


def quadrant(own, other, flip):
    share = own.shape[0] // 2
    return jnp.concatenate(
        [own[flip * share : (flip + 1) * share], other[(1 - flip) * share : (2 - flip) * share]], axis=0
    )


def out_split_kernel(hidden, keep, rest, twin, twin_rest, keep_next, rest_next, twin_next, twin_rest_next, *outs):
    first, cross, chips, chips_cross = outs
    part = hidden.shape[0]
    own = keep[...] + twin[...].astype(F32) + hidden[...]
    other = keep_next[...] + twin_next[...].astype(F32)
    first[...] = quadrant(own, other, 0)
    cross[...] = quadrant(own, other, 1).astype(BF16)
    own = rest[...] + twin_rest[...].astype(F32)
    other = rest_next[...] + twin_rest_next[...].astype(F32)
    for k in range(rest.shape[0] // part):
        at = slice(k * part, (k + 1) * part)
        chips[at, :] = quadrant(own[at], other[at], 0)
        chips_cross[at, :] = quadrant(own[at], other[at], 1).astype(BF16)


def swapped(values):
    half = values.shape[0] // 2
    return jnp.concatenate([values[half:], values[:half]], axis=0)


def add_kernel(part, values, arrived, out):
    for k in range(values.shape[0] // part):
        at = slice(k * part, (k + 1) * part)
        out[at, :] = (values[at, :] + swapped(arrived[at, :].astype(F32))).astype(BF16)


def out_finish_kernel(which, first, cross, *refs):
    arrived, out = refs[:-1], refs[-1]
    share = out.shape[1]
    total = first[...] + swapped(cross[...].astype(F32))
    for ref in arrived:
        total = total + ref[...].astype(F32)
    total = total.astype(BF16)
    out[pl.ds(which[0], 1)] = total[None, :share]
    out[pl.ds(1 - which[0], 1)] = total[None, share:]


def inverse_rms(values):
    return lax.rsqrt(jnp.mean(values * values, axis=-1, keepdims=True) + EPS)


def both_halves(start, first, second):
    return jnp.concatenate([first[...], far_rows(first, second, start)], axis=0).astype(F32)


def rows_sum(keep, twin, arrived):
    total = keep[...] + twin[...].astype(F32)
    for ref in arrived:
        total = total + ref[...].astype(F32)
    return total


def norm_kernel(start, near, far, gain, out):
    values = both_halves(start, near, far)
    out[...] = (values * inverse_rms(values) * gain[...].astype(F32)).astype(BF16)


def rest_kernel(rest, twin, out):
    out[...] = (rest[...] + twin[...].astype(F32)).astype(BF16)


def sum_kernel(keep, twin, *refs):
    refs[-1][...] = rows_sum(keep, twin, refs[:-1]).astype(BF16)


def middle_kernel(start, near, far, gain, keep, twin, *refs):
    arrived, (hidden, out) = refs[:-2], refs[-2:]
    values = both_halves(start, near, far) + rows_sum(keep, twin, arrived)
    hidden[...] = values
    out[...] = (values * inverse_rms(values) * gain[...].astype(F32)).astype(BF16)


def pull_norm(values, gain, grad):
    inv = inverse_rms(values)
    scaled = grad * gain
    normed = values * inv
    d_values = inv * (scaled - normed * jnp.mean(scaled * normed, axis=-1, keepdims=True))
    return d_values, jnp.sum(grad * normed, axis=0, keepdims=True)


def back_two_kernel(which, hidden, near, far, gain, across, keep, twin, *refs):
    arrived, (d_hidden, low, d_gain) = refs[:-3], refs[-3:]
    grad = rows_sum(keep, twin, arrived) + across[...].astype(F32)
    d_values, d_gain[...] = pull_norm(hidden[...], gain[...].astype(F32), grad)
    total = jnp.concatenate([near[which[0]], far[which[0]]], axis=0).astype(F32) + d_values
    d_hidden[...] = total
    low[...] = total.astype(BF16)


def back_one_kernel(start, which, near, far, gain, d_hidden, ffn_grad, keep, twin, *refs):
    arrived, (first, packed) = refs[:-2], refs[-2:]
    grad = rows_sum(keep, twin, arrived)
    d_values, _ = pull_norm(both_halves(start, near, far), gain[...].astype(F32), grad)
    total = (d_hidden[...] + d_values).astype(BF16)
    share, width = first.shape
    first[...] = total[:share]
    packed[:share, :width] = total[share:]
    rows = ffn_grad.shape[0] // 2
    packed[:rows, width:] = ffn_grad[pl.ds(pl.multiple_of((1 - which[0]) * rows, rows), rows), :]


def grad_kernel(row_parts, blocks, tables, *refs):
    rows, refs = refs[:row_parts], refs[row_parts:]
    right, refs = refs[0], refs[1:]
    keeps, send, left = refs[:blocks], refs[blocks], refs[blocks + 1]
    part, width = rows[0].shape
    block = keeps[0].shape[0]
    for p in range(row_parts):
        for c in range(width // LANES):
            tile = rows[p][:, c * LANES : (c + 1) * LANES].astype(F32)
            left[c * LANES : (c + 1) * LANES, p * part : (p + 1) * part] = tile.T.astype(BF16)
    for s in range(2 * blocks):
        at = pl.ds(pl.multiple_of(tables[3, s] * block, block), block)
        total = nn_dot(left[at, :], right[...]).astype(BF16)
        if s < blocks:
            keeps[s][...] = total
        else:
            send[(s - blocks) * block : (s - blocks + 1) * block, :] = total


def weight_partials(tables, rows, right, blocks):
    part, width = rows[0].shape
    length, cols = right.shape
    block = width // (2 * blocks)
    return pl.pallas_call(
        functools.partial(grad_kernel, len(rows), blocks),
        out_shape=(jax.ShapeDtypeStruct((block, cols), BF16),) * blocks
        + (jax.ShapeDtypeStruct((width // 2, cols), BF16),),
        in_specs=[smem()] + [vmem()] * (len(rows) + 1),
        out_specs=[vmem()] * (blocks + 1),
        scratch_shapes=[pltpu.VMEM((width, length), BF16)],
        compiler_params=pltpu.CompilerParams(vmem_limit_bytes=VMEM_LIMIT),
        cost_estimate=pl.CostEstimate(
            flops=2 * length * width * cols, bytes_accessed=8 << 20, transcendentals=0
        ),
        name="weight_partials",
    )(tables, *rows, right)


def qkv_grad_kernel(row_parts, blocks, tables, *refs):
    weights, refs = refs[: 2 * blocks], refs[2 * blocks :]
    gain_row, refs = refs[-2], refs[:-2] + refs[-1:]
    rows, right = refs[:row_parts], refs[row_parts]
    keeps, send, left = refs[row_parts + 1 : row_parts + 1 + blocks], refs[-2], refs[-1]
    part, width = rows[0].shape
    block = keeps[0].shape[0]
    cols = right.shape[1]
    for p in range(row_parts):
        for c in range(width // LANES):
            tile = rows[p][:, c * LANES : (c + 1) * LANES].astype(F32)
            left[c * LANES : (c + 1) * LANES, p * part : (p + 1) * part] = tile.T.astype(BF16)
    for s in range(2 * blocks):
        at = pl.ds(pl.multiple_of(tables[3, s] * block, block), block)
        total = nn_dot(left[at, :], right[...])
        product = total * weights[s][:block, :cols].astype(F32)
        product = sum(product[:, c * LANES : (c + 1) * LANES] for c in range(cols // LANES))
        high = product.astype(BF16)
        ones = jnp.ones((8, LANES), BF16)
        gain_row[pl.ds(tables[3, s], 1)] = (nt_dot(ones, high) + nt_dot(ones, (product - high.astype(F32)).astype(BF16)))[None]
        total = total.astype(BF16)
        if s < blocks:
            keeps[s][...] = total
        else:
            send[(s - blocks) * block : (s - blocks + 1) * block, :] = total


def qkv_partials(tables, weights, rows, right, blocks):
    part, width = rows[0].shape
    length, cols = right.shape
    block = width // (2 * blocks)
    return pl.pallas_call(
        functools.partial(qkv_grad_kernel, len(rows), blocks),
        out_shape=(jax.ShapeDtypeStruct((block, cols), BF16),) * blocks
        + (jax.ShapeDtypeStruct((width // 2, cols), BF16), jax.ShapeDtypeStruct((2 * blocks, 8, block), F32)),
        in_specs=[smem()] + [vmem()] * (len(weights) + len(rows) + 1),
        out_specs=[vmem()] * (blocks + 2),
        scratch_shapes=[pltpu.VMEM((width, length), BF16)],
        compiler_params=pltpu.CompilerParams(vmem_limit_bytes=VMEM_LIMIT),
        cost_estimate=pl.CostEstimate(
            flops=2 * length * width * cols, bytes_accessed=8 << 20, transcendentals=0
        ),
        name="qkv_partials",
    )(tables, *weights, *rows, right)


def hop(values, axis, flip):
    size = lax.axis_size(axis)
    return lax.ppermute(values, axis, [(i, i ^ flip) for i in range(size)])


def swap_blocks(values, axis, index, size):
    shape = values.shape
    bit = 1
    while bit < size:
        split = shape[:axis] + (size // (2 * bit), 2, bit) + shape[axis + 1 :]
        cut = values.reshape(split)
        cut = jnp.where((index & bit) != 0, jnp.flip(cut, axis + 1), cut)
        values = cut.reshape(shape)
        bit *= 2
    return values


def gather_chips(block):
    nt = lax.axis_size("tp")
    return [block] + [hop(block, "tp", 2 * k) for k in range(1, nt // 2)]


def with_twins(blocks):
    return blocks + [hop(block, "tp", 1) for block in blocks]


def gather_rows(block):
    return with_twins(gather_chips(block))


def region(ready, run):
    shapes = jax.eval_shape(run)
    return lax.cond(ready, run, lambda: jax.tree.map(lambda a: jnp.zeros(a.shape, a.dtype), shapes))


def chips_low(rest, twin, *behind):
    return rows_call(
        rest_kernel, "rest_rows", jax.ShapeDtypeStruct(rest.shape, BF16), rest, twin, behind=behind
    )


def chips_hop(low, nt):
    if nt == 4:
        return [hop(low, "tp", 2)]
    rows = low.shape[0] // (nt // 2 - 1)
    return [hop(low[(k - 1) * rows : k * rows], "tp", 2 * k) for k in range(1, nt // 2)]


def shards(
    layer_in,
    attn_gain,
    ffn_gain,
    query_weight,
    key_weight,
    value_weight,
    out_weight,
    variate_bias,
    gate_weight,
    up_weight,
    down_weight,
    segment_ids,
    variate_ids,
    time_ids,
    out_grad,
):
    seq_count, share, width = layer_in.shape
    nz, nx, nt = lax.axis_size("fsdp"), lax.axis_size("ctx"), lax.axis_size("tp")
    iz, ix, it = lax.axis_index("fsdp"), lax.axis_index("ctx"), lax.axis_index("tp")
    assert nx == 2 and seq_count == nx
    length = segment_ids.shape[1]
    heads = variate_bias.shape[1]
    proj = heads * HEAD

    def pick(table, which):
        return lax.dynamic_index_in_dim(table, which, 0, keepdims=False)

    def swap(mine, theirs):
        return jnp.where(ix == 0, mine, theirs), jnp.where(ix == 0, theirs, mine)

    gain_one, gain_two = attn_gain[None], ffn_gain[None]
    part = nx * share
    low_rows = jax.ShapeDtypeStruct((part, width), BF16)
    wide_rows = jax.ShapeDtypeStruct((part, width), F32)
    gain_row = jax.ShapeDtypeStruct((1, width), F32)
    half_rows = jax.ShapeDtypeStruct((share, width), BF16)
    which = ix.astype(jnp.int32).reshape(1)
    ready = ix >= 0
    cols = gate_weight.shape[1] // 2
    near, grad_own = pick(layer_in, ix), out_grad
    block = query_weight.shape[0]
    attn_shape = jax.ShapeDtypeStruct((block, 4 * proj), BF16)
    packed_shape = jax.ShapeDtypeStruct((max(block, share), 4 * proj + width + 3 * cols), BF16)
    ffn_shape = jax.ShapeDtypeStruct((gate_weight.shape[0], 3 * cols), BF16)
    attn_own, mine, packed = rows_call(
        pack_kernel, "pack_weights", (attn_shape, ffn_shape, packed_shape), layer_in, query_weight, key_weight,
        value_weight, out_weight, gate_weight, up_weight, down_weight, scalars=(which,),
    )
    start = 4 * proj

    def twin(block):
        return hop(block, "tp", 1)

    def across(block):
        return hop(block, "ctx", 1)

    def first_transfers():
        attn_z = [hop(attn_own, "fsdp", k) for k in range(1, nz)]
        far = across(packed)
        grad_y = gather_chips(grad_own)[1:]
        order = jnp.arange(nx * nt).reshape(nx, nt // 2, 2)
        order = swap_blocks(swap_blocks(swap_blocks(order, 0, ix, nx), 1, it // 2, nt // 2), 2, it % 2, 2)
        order = order.transpose(2, 1, 0).reshape(nx * nt)
        places = jnp.arange(nz * nx).reshape(nz, nx)
        places = swap_blocks(swap_blocks(places, 0, iz, nz), 1, ix, nx).transpose(1, 0).reshape(nz * nx)
        tables = attention_tables(
            pick(segment_ids, ix), pick(variate_ids, ix), pick(time_ids, ix), variate_bias, order, places
        )
        return attn_z, far, grad_y, tables

    attn_z, far, grad_y, made = region(ready, first_transfers)
    tables, cosine, sine, seg_row, seg_wide, feature, coef, hot_rows = made
    stack_shape = jax.ShapeDtypeStruct((2 * block, 3 * cols), BF16)
    ffn_w = rows_call(
        functools.partial(stack_kernel, start + width), "stack_weights", stack_shape, mine, far, scalars=(which,)
    )
    ffn_w = lax.all_gather(ffn_w, "fsdp", axis=0, tiled=True)

    rows_own = rows_call(functools.partial(norm_kernel, start), "norm_rows", low_rows, near, far, gain_one)

    def gather_one():
        return gather_chips(rows_own)[1:], [across(piece) for piece in attn_z]

    chips, rest_x = region(ready, gather_one)
    chips_one = [rows_own] + chips
    attn_w = [attn_own] + attn_z + [far] + rest_x

    def attend():
        twins = [twin(rows) for rows in chips_one]
        return across(grad_own), twins, attention_forward(
            tables, chips_one + twins, attn_w, cosine, sine, seg_row, seg_wide, feature, coef, heads
        )

    grad_far, twins, (q_aug, k_aug, v_rows, mixed, lse, keep, rest, send, send_rest) = region(ready, attend)

    def scatter_attn():
        low = chips_low(rest, twin(send_rest))
        return chips_hop(low, nt), twin(send), [across(piece) for piece in grad_y]

    rows_one = chips_one + twins
    chips, twins, grad_far_y = region(ready, scatter_attn)
    grad_near, grad_far = [grad_own] + grad_y, [grad_far] + grad_far_y
    hidden, rows_two = rows_call(
        functools.partial(middle_kernel, start), "middle_rows", (wide_rows, low_rows), near, far, gain_two, keep, twins,
        *chips,
    )

    def gather_two():
        return (
            gather_chips(rows_two)[1:],
            across(rows_two),
            [twin(rows) for rows in grad_near],
            [twin(rows) for rows in grad_far],
            twin(rows_two),
        )

    chips_two, next_own, near_twins, far_twins, rows_twin = region(ready, gather_two)
    grad_near, grad_far = grad_near + near_twins, grad_far + far_twins

    def ffn_own():
        twins = [twin(rows) for rows in chips_two]
        return [across(rows) for rows in chips_two], twins, ffn_middle(
            False, which, [rows_two] + chips_two + [rows_twin] + twins, grad_near, grad_far, ffn_w
        )

    next_y, twins, (act, d_both, keep, rest, send, send_rest) = region(ready, ffn_own)

    rows_two = [rows_two] + chips_two + [rows_twin] + twins
    rows_next = [next_own] + next_y

    def ffn_next():
        low = chips_low(rest, twin(send_rest))
        twins = [twin(rows) for rows in rows_next]
        return chips_hop(low, nt), twin(send), twins, ffn_middle(
            True, 1 - which, rows_next + twins, grad_near, grad_far, ffn_w
        )

    chips, twins, next_twins, made = region(ready, ffn_next)
    rows_next = rows_next + next_twins
    act_next, d_both_next, keep_next, rest_next, send_next, send_rest = made
    low_next = chips_low(rest_next, twin(send_rest))

    def scatter_next():
        return (
            chips_hop(low_next, nt),
            twin(send_next),
            ffn_partials(which, rows_two, rows_next, grad_near, grad_far, act, act_next, d_both, d_both_next),
            ffn_result(act, act_next, ffn_w, part),
        )

    chips_next, twins_next, ffn_grad, parts = region(ready, scatter_next)
    low_across = rows_call(sum_kernel, "sum_rows", low_rows, keep_next, twins_next, *chips_next)

    def cross_next():
        out_twins = [twin(parts[k]) for k in (2, 3, 6, 7)]
        rest_shape = (parts[1].shape[0], width)
        shapes = (
            wide_rows,
            low_rows,
            jax.ShapeDtypeStruct(rest_shape, F32),
            jax.ShapeDtypeStruct(rest_shape, BF16),
        )
        return across(low_across), rows_call(
            out_split_kernel, "out_split", shapes, hidden, parts[0], parts[1], out_twins[0], out_twins[1], parts[4],
            parts[5], out_twins[2], out_twins[3],
        )

    arrived, (out_first, out_cross, out_chips, out_chips_cross) = region(ready, cross_next)
    ffn_grad = lax.psum_scatter(ffn_grad, "fsdp", scatter_dimension=0, tiled=True)
    d_hidden, low, d_gain_two = rows_call(
        back_two_kernel,
        "back_two",
        (wide_rows, low_rows, gain_row),
        hidden,
        grad_near[0],
        grad_far[0],
        gain_two,
        arrived,
        keep,
        twins,
        *chips,
        scalars=(which,),
    )

    def gather_back():
        return gather_chips(low)[1:], twin(low), across(out_chips_cross)

    chips_back, twin_back, out_arrived = region(ready, gather_back)
    branch_rows = [low] + chips_back
    branch_rows = branch_rows + [twin_back] + [twin(rows) for rows in chips_back]
    low_out = rows_call(
        functools.partial(add_kernel, part), "add_rows", jax.ShapeDtypeStruct(out_chips.shape, BF16), out_chips, out_arrived
    )
    out_grads = weight_partials(tables, branch_rows, mixed, nz)

    def attend_back():
        return chips_hop(low_out, nt), across(out_cross), across(out_grads[-1]), attention_backward(
            tables, branch_rows, attn_w, q_aug, k_aug, v_rows, lse, cosine, sine, seg_row, seg_wide, hot_rows, heads
        )

    out_arrived, out_cross, out_other, made = region(ready, attend_back)
    keep, rest, send, send_rest, d_qkv, bias_parts = made

    place = it.astype(jnp.int32).reshape(1)
    gain_shape = jax.ShapeDtypeStruct((8, width), F32)

    def scatter_one():
        twins = twin(send)
        low = chips_low(rest, twin(send_rest), twins)
        grads = qkv_partials(tables, attn_w, rows_one, d_qkv, nz)
        sums = pair_sums(out_grads, out_other)
        arrived = [hop(piece, "fsdp", k) for k, piece in enumerate(sums) if k > 0]
        totals = rows_call(
            gains_kernel, "gain_rows", gain_shape, grads[-1], gain_one, d_gain_two, bias_parts, scalars=(place,)
        )
        totals = totals + twin(totals)
        totals = sum([hop(totals, "fsdp", k) for k in range(1, nz)], totals)
        return chips_hop(low, nt), twins, grads[:-1], across(grads[-2]), sums[0], arrived, totals

    chips, twins, qkv_grads, qkv_other, out_sum, out_z, totals = region(ready, scatter_one)
    packed_shape = jax.ShapeDtypeStruct((max(block, share), width + 3 * cols), BF16)
    d_near, packed = rows_call(
        functools.partial(back_one_kernel, start), "back_one", (half_rows, packed_shape), near, far, gain_one, d_hidden,
        ffn_grad, keep, twins, *chips, scalars=(which,),
    )
    qkv_sums = pair_sums(qkv_grads, qkv_other)

    def last_transfers():
        arrived = [hop(piece, "fsdp", k) for k, piece in enumerate(qkv_sums) if k > 0]
        (out_weight_grad,) = weight_sums(out_sum, out_z, 1)
        layer_out = rows_call(
            out_finish_kernel, "layer_out", jax.ShapeDtypeStruct(layer_in.shape, BF16), out_first, out_cross,
            *out_arrived, scalars=(which,),
        )
        chips = [hop(totals, "tp", 2 * k) for k in range(1, nt // 2)]
        return arrived, across(packed), chips, out_weight_grad, layer_out

    arrived, crossed, chips, out_weight_grad, layer_out = region(ready, last_transfers)
    totals = sum(chips, totals)

    def last_sums():
        ffn_grads = rows_call(
            functools.partial(ffn_finish_kernel, width), "ffn_sums",
            [jax.ShapeDtypeStruct(gate_weight.shape, F32)] * 3, ffn_grad, crossed, scalars=(which,),
        )
        in_shape = jax.ShapeDtypeStruct((nx * share, width), BF16)
        in_grad = rows_call(
            functools.partial(stack_kernel, 0), "in_rows", in_shape, d_near, crossed, scalars=(which,)
        )
        return across(totals), ffn_grads, in_grad.reshape(layer_in.shape), weight_sums(qkv_sums[0], arrived, 3)

    totals_x, (gate_grad, up_grad, down_grad), in_grad, qkv_grads = region(ready, last_sums)
    attn_gain_grad, ffn_gain_grad, bias_grad = rows_call(
        gains_finish_kernel, "gain_sums", (gain_row, gain_row, jax.ShapeDtypeStruct((8, LANES), F32)), totals, totals_x,
        scalars=(place,),
    )
    bias_grad = bias_grad[2:4, :heads]
    query_grad, key_grad, value_grad = qkv_grads
    return (
        layer_out,
        in_grad,
        attn_gain_grad.reshape(width),
        ffn_gain_grad.reshape(width),
        query_grad,
        key_grad,
        value_grad,
        out_weight_grad,
        bias_grad,
        gate_grad,
        up_grad,
        down_grad,
    )


def solution(mesh):
    rows = P("fsdp", ("ctx", "tp"), None)
    weight = P(("fsdp", "ctx"), "tp")
    ids = P("fsdp", None)
    bias = P(None, "tp")
    in_specs = (rows, P(), P()) + (weight,) * 4 + (bias,) + (weight,) * 3 + (ids,) * 3 + (rows,)
    out_specs = (rows, rows, P(), P()) + (weight,) * 4 + (bias,) + (weight,) * 3
    return jax.shard_map(shards, mesh=mesh, in_specs=in_specs, out_specs=out_specs, check_vma=False)
```

```python
import functools
import jax
import jax.numpy as jnp
from jax import lax
from jax.sharding import PartitionSpec as P
from jax.experimental import pallas as pl
from jax.experimental.pallas import tpu as pltpu

HEADS = 16
HEAD = 64
EPS = 1e-05
NEG = -1e30
F32 = jnp.float32
BF16 = jnp.bfloat16
LANES = 128
QUERIES = 256
STEP = 128
VMEM_LIMIT = 40 * 1024 * 1024
ROWS_LIMIT = 16 * 1024 * 1024
WIDE_LIMIT = 56 * 1024 * 1024


def nt_dot(left, right):
    return lax.dot_general(left, right, (((1,), (1,)), ((), ())), preferred_element_type=F32)


def nn_dot(left, right):
    return lax.dot_general(left, right, (((1,), (0,)), ((), ())), preferred_element_type=F32)


def tn_dot(left, right):
    return lax.dot_general(left, right, (((0,), (0,)), ((), ())), preferred_element_type=F32)


def lane_of(shape):
    return lax.broadcasted_iota(jnp.int32, shape, len(shape) - 1)


def half_swap(values):
    lane = lane_of(values.shape)
    forward = pltpu.roll(values, LANES - HEAD // 2, 1)
    back = pltpu.roll(values, HEAD // 2, 1)
    return jnp.where(lane % HEAD < HEAD // 2, forward, back)


def fwd_kernel(row_parts, weight_parts, heads, *refs):
    tables, refs = refs[0], refs[1:]
    rows, refs = refs[:row_parts], refs[row_parts:]
    weights, refs = refs[:weight_parts], refs[weight_parts:]
    cosine, sine, seg_row, seg_wide, feature, coef = refs[:6]
    q_aug, k_aug, v_out, mixed_out, lse_out, keep_out, rest_out, send_own, send_rest = refs[6:15]
    full, out_full, mixed_wide, v_turn = refs[15:]
    pairs = heads // 2
    proj = heads * HEAD
    length = q_aug.shape[1]
    block = weights[0].shape[0]
    part = rows[0].shape[0]
    share = part // 2
    for i in range(weight_parts):
        at = pl.ds(pl.multiple_of(tables[3, i] * block, block), block)
        full[at, :] = weights[i][:block, : 3 * proj]
        out_full[at, :] = weights[i][:block, 3 * proj : 4 * proj]
    for p in range(row_parts):
        raw = nn_dot(rows[p][...], full[...])
        for k in range(2):
            piece = raw[k * share : (k + 1) * share]
            start = pl.multiple_of(tables[0, 2 * p + k] * share, share)
            at = pl.ds(start, share)
            cos_now, sin_now, feat = cosine[at, :], sine[at, :], feature[at, :].astype(F32)
            lane = lane_of((share, LANES))
            for pair in range(pairs):
                low = pair * LANES
                q = piece[:, low : low + LANES]
                q = (q * cos_now + half_swap(q) * sin_now).astype(BF16).astype(F32) * HEAD**-0.5
                kk = piece[:, proj + low : proj + low + LANES]
                kk = kk * cos_now + half_swap(kk) * sin_now
                v_out[pair, at, :] = piece[:, 2 * proj + low : 2 * proj + low + LANES].astype(BF16)
                for odd in range(2):
                    head = 2 * pair + odd
                    q_now = pltpu.roll(q, HEAD, 1) if odd else q
                    k_now = pltpu.roll(kk, HEAD, 1) if odd else kk
                    q_feat = feat * coef[head : head + 1, :]
                    q_aug[head, at, :] = jnp.where(lane < HEAD, q_now, q_feat).astype(BF16)
                    k_aug[head, at, :] = jnp.where(lane < HEAD, k_now, feat).astype(BF16)
    for pair in range(pairs):
        for b in range(length // LANES):
            tile = v_out[pair, b * LANES : (b + 1) * LANES, :].astype(F32)
            v_turn[pair, :, b * LANES : (b + 1) * LANES] = tile.T.astype(BF16)

    def query_block(b, carry):
        at = pl.ds(pl.multiple_of(b * QUERIES, QUERIES), QUERIES)
        seg_q = seg_row[pl.ds(b, 1), :]
        first = pl.multiple_of(tables[1, b] * LANES, LANES)
        for kind in range(1, length // STEP + 1):

            @pl.when(tables[2, b] == kind)
            def _(kind=kind):
                win = pl.ds(first, kind * STEP)
                keep = seg_wide[win, :] == seg_q
                scores = [nt_dot(k_aug[h, win, :], q_aug[h, at, :]) for h in range(heads)]
                probs, totals = [], []
                for head in range(heads):
                    s = jnp.where(keep, scores[head], NEG)
                    top = jnp.max(s, axis=0, keepdims=True)
                    p = jnp.exp(s - top)
                    total = jnp.sum(p, axis=0, keepdims=True)
                    probs.append(p.astype(BF16))
                    totals.append(total)
                    lse_out[head, pl.ds(b, 1), :] = top + jnp.log(total)
                for pair in range(pairs):
                    outs = []
                    for odd in range(2):
                        head = 2 * pair + odd
                        turn = v_turn[pair, odd * HEAD : (odd + 1) * HEAD, win]
                        outs.append(nn_dot(turn, probs[head]) / totals[head])
                    mixed = jnp.concatenate(outs, axis=0).T
                    mixed_wide[at, pair * LANES : (pair + 1) * LANES] = mixed

        return carry

    lax.fori_loop(0, length // QUERIES, query_block, 0)
    for slot in range(2 * row_parts):
        start = pl.multiple_of(tables[0, slot] * share, share)
        piece = mixed_wide[pl.ds(start, share), :]
        mixed_out[slot * share : (slot + 1) * share, :] = piece.astype(BF16)
    half = row_parts // 2
    for p in range(row_parts):
        back = nt_dot(mixed_out[p * part : (p + 1) * part, :], out_full[...])
        if p == 0:
            keep_out[...] = back
        elif p < half:
            rest_out[(p - 1) * part : p * part, :] = back
        else:
            if p == half:
                send_own[...] = back.astype(BF16)
            else:
                send_rest[(p - half - 1) * part : (p - half) * part, :] = back.astype(BF16)


def vmem():
    return pl.BlockSpec(memory_space=pltpu.VMEM)


def anywhere():
    return pl.BlockSpec(memory_space=pl.ANY)


def smem():
    return pl.BlockSpec(memory_space=pltpu.SMEM)


def attention_forward(tables, rows, weights, cosine, sine, seg_row, seg_wide, feature, coef, heads, behind=()):
    proj = heads * HEAD
    length = cosine.shape[0]
    part, width = rows[0].shape
    shapes = (
        jax.ShapeDtypeStruct((heads, length, LANES), BF16),
        jax.ShapeDtypeStruct((heads, length, LANES), BF16),
        jax.ShapeDtypeStruct((heads // 2, length, LANES), BF16),
        jax.ShapeDtypeStruct((length, proj), BF16),
        jax.ShapeDtypeStruct((heads, length // QUERIES, QUERIES), F32),
        jax.ShapeDtypeStruct((part, width), F32),
        jax.ShapeDtypeStruct((length // 2 - part, width), F32),
        jax.ShapeDtypeStruct((part, width), BF16),
        jax.ShapeDtypeStruct((length // 2 - part, width), BF16),
    )
    count = len(rows) + len(weights) + 6
    operands = (tables, *rows, *weights, cosine, sine, seg_row, seg_wide, feature, coef)
    return pl.pallas_call(
        without(functools.partial(fwd_kernel, len(rows), len(weights), heads), len(operands), len(behind)),
        out_shape=shapes,
        in_specs=[smem()] + [vmem()] * count + [anywhere()] * len(behind),
        out_specs=[vmem()] * 9,
        scratch_shapes=[
            pltpu.VMEM((width, 3 * proj), BF16),
            pltpu.VMEM((width, proj), BF16),
            pltpu.VMEM((length, proj), F32),
            pltpu.VMEM((heads // 2, LANES, length), BF16),
        ],
        compiler_params=pltpu.CompilerParams(vmem_limit_bytes=VMEM_LIMIT),
        cost_estimate=pl.CostEstimate(
            flops=2 * length * width * 3 * proj, bytes_accessed=8 << 20, transcendentals=length * length * heads // 2
        ),
        name="attn_fwd",
    )(*operands, *behind)


def bwd_kernel(row_parts, weight_parts, heads, *refs):
    tables, refs = refs[0], refs[1:]
    rows, refs = refs[:row_parts], refs[row_parts:]
    weights, refs = refs[:weight_parts], refs[weight_parts:]
    q_aug, k_aug, v_in, lse, cosine, sine, seg_row, seg_wide, hot_rows = refs[:9]
    keep_out, rest_out, send_own, send_rest, d_qkv_out, bias_out = refs[9:15]
    full, out_full, d_out, k_turn, dq_acc, dk_acc, dv_acc = refs[15:]
    pairs = heads // 2
    proj = heads * HEAD
    length = q_aug.shape[1]
    block = weights[0].shape[0]
    part = rows[0].shape[0]
    share = part // 2
    for i in range(weight_parts):
        at = pl.ds(pl.multiple_of(tables[3, i] * block, block), block)
        full[at, :] = weights[i][:block, : 3 * proj]
        out_full[at, :] = weights[i][:block, 3 * proj : 4 * proj]
    for p in range(row_parts):
        raw = nn_dot(rows[p][...], out_full[...]).astype(BF16)
        for k in range(2):
            start = pl.multiple_of(tables[0, 2 * p + k] * share, share)
            d_out[pl.ds(start, share), :] = raw[k * share : (k + 1) * share]
    for head in range(heads):
        for b in range(length // LANES):
            tile = k_aug[head, b * LANES : (b + 1) * LANES, :].astype(F32)
            k_turn[head, :, b * LANES : (b + 1) * LANES] = tile.T.astype(BF16)
    dk_acc[...] = jnp.zeros(dk_acc.shape, F32)
    dv_acc[...] = jnp.zeros(dv_acc.shape, F32)
    bias_out[...] = jnp.zeros(bias_out.shape, F32)

    def query_block(b, carry):
        at = pl.ds(pl.multiple_of(b * QUERIES, QUERIES), QUERIES)
        seg_q = seg_row[pl.ds(b, 1), :]
        hot = hot_rows[:, at]
        first = pl.multiple_of(tables[1, b] * LANES, LANES)
        for kind in range(1, length // STEP + 1):

            @pl.when(tables[2, b] == kind)
            def _(kind=kind):
                win = pl.ds(first, kind * STEP)
                keep = seg_wide[win, :] == seg_q
                owns = []
                for head in range(heads):
                    chunk = slice(head // 2 * LANES, (head // 2 + 1) * LANES)
                    d_pair = d_out[at, chunk]
                    lane = lane_of(d_pair.shape)
                    owns.append(jnp.where((lane >= HEAD) == (head % 2 == 1), d_pair, jnp.zeros_like(d_pair)))
                turned = []
                for base in range(0, heads, 2):
                    group = range(base, base + 2)
                    s = [nt_dot(k_aug[h, win, :], q_aug[h, at, :]) for h in group]
                    dp = [nt_dot(v_in[h // 2, win, :], owns[h]) for h in group]
                    low, ds = [], []
                    for i, h in enumerate(group):
                        p = jnp.exp(jnp.where(keep, s[i] - lse[h, pl.ds(b, 1), :], NEG))
                        low.append(p.astype(BF16))
                        ds.append((p * (dp[i] - jnp.sum(p * dp[i], axis=0, keepdims=True))).astype(BF16))
                    for i, h in enumerate(group):
                        if i % 2 == 0:
                            both = jnp.concatenate(low[i : i + 2], axis=1)
                            dv_acc[h // 2, win, :] += nn_dot(both, jnp.concatenate(owns[h : h + 2], axis=0))
                        dk_acc[h, win, :] += nn_dot(ds[i], q_aug[h, at, :])
                        dq = nn_dot(k_turn[h, :, win], ds[i])
                        turned.append(dq[:HEAD])
                        sums = dq[HEAD : HEAD + 8]
                        bias_out[h] += jnp.concatenate([sums * hot[:8], sums * hot[8:]], axis=0)
                for pair in range(pairs):
                    chunk = slice(pair * LANES, (pair + 1) * LANES)
                    dq_acc[at, chunk] = jnp.concatenate(turned[2 * pair : 2 * pair + 2], axis=0).T * HEAD**-0.5

        return carry

    lax.fori_loop(0, length // QUERIES, query_block, 0)
    for p in range(row_parts):
        for k in range(2):
            slot = 2 * p + k
            at = pl.ds(pl.multiple_of(tables[0, slot] * share, share), share)
            to = slice(slot * share, (slot + 1) * share)
            cos_now, sin_now = cosine[at, :], sine[at, :]
            lane = lane_of((share, LANES))
            for pair in range(pairs):
                low = pair * LANES
                dq = dq_acc[at, low : low + LANES]
                dk = jnp.where(lane < HEAD, dk_acc[2 * pair, at, :], pltpu.roll(dk_acc[2 * pair + 1, at, :], HEAD, 1))
                d_qkv_out[to, low : low + LANES] = (dq * cos_now - half_swap(dq) * sin_now).astype(BF16)
                d_qkv_out[to, proj + low : proj + low + LANES] = (dk * cos_now - half_swap(dk) * sin_now).astype(BF16)
                d_qkv_out[to, 2 * proj + low : 2 * proj + low + LANES] = dv_acc[pair, at, :].astype(BF16)
        part_rows = d_qkv_out[p * part : (p + 1) * part, :]
        back = nt_dot(part_rows, full[...])
        half = row_parts // 2
        if p == 0:
            keep_out[...] = back
        elif p < half:
            rest_out[(p - 1) * part : p * part, :] = back
        else:
            if p == half:
                send_own[...] = back.astype(BF16)
            else:
                send_rest[(p - half - 1) * part : (p - half) * part, :] = back.astype(BF16)


def attention_backward(tables, rows, weights, q_aug, k_aug, v_in, lse, cosine, sine, seg_row, seg_wide, hot_rows, heads, behind=()):
    proj = heads * HEAD
    length = cosine.shape[0]
    part, width = rows[0].shape
    shapes = (
        jax.ShapeDtypeStruct((part, width), F32),
        jax.ShapeDtypeStruct((length // 2 - part, width), F32),
        jax.ShapeDtypeStruct((part, width), BF16),
        jax.ShapeDtypeStruct((length // 2 - part, width), BF16),
        jax.ShapeDtypeStruct((length, 3 * proj), BF16),
        jax.ShapeDtypeStruct((heads, 16, QUERIES), F32),
    )
    count = len(rows) + len(weights) + 9
    operands = (tables, *rows, *weights, q_aug, k_aug, v_in, lse, cosine, sine, seg_row, seg_wide, hot_rows)
    return pl.pallas_call(
        without(functools.partial(bwd_kernel, len(rows), len(weights), heads), len(operands), len(behind)),
        out_shape=shapes,
        in_specs=[smem()] + [vmem()] * count + [anywhere()] * len(behind),
        out_specs=[vmem()] * 6,
        scratch_shapes=[
            pltpu.VMEM((width, 3 * proj), BF16),
            pltpu.VMEM((width, proj), BF16),
            pltpu.VMEM((length, proj), BF16),
            pltpu.VMEM((heads, LANES, length), BF16),
            pltpu.VMEM((length, proj), F32),
            pltpu.VMEM((heads, length, LANES), F32),
            pltpu.VMEM((heads // 2, length, LANES), F32),
        ],
        compiler_params=pltpu.CompilerParams(vmem_limit_bytes=VMEM_LIMIT),
        cost_estimate=pl.CostEstimate(
            flops=2 * length * width * 4 * proj, bytes_accessed=12 << 20, transcendentals=length * length * heads // 2
        ),
        name="attn_bwd",
    )(*operands, *behind)


def attention_tables(segments, variates, times, variate_bias, order, places):
    length = segments.shape[0]
    heads = variate_bias.shape[1]
    count = length // QUERIES
    half = HEAD // 2
    frequency = 10000.0 ** (-2.0 * jnp.arange(half, dtype=F32) / HEAD)
    angles = times.astype(F32)[:, None] * frequency
    cos_half, sin_half = jnp.cos(angles), jnp.sin(angles)
    wide = jax.ShapeDtypeStruct((length, LANES), F32)
    cosine, sine = rows_call(
        widen_kernel, "widen_angles", (wide, wide), jnp.concatenate([cos_half, sin_half], axis=1)
    )
    seg_row = segments.reshape(count, QUERIES)
    seg_wide = jnp.broadcast_to(segments[:, None], (length, QUERIES))
    lane = jnp.arange(LANES)
    live = (lane >= HEAD) & (lane < HEAD + 12)
    feature = ((variates[:, None] == (lane % 4)[None, :]) & live[None, :]).astype(BF16)
    gap = variate_bias[0] - variate_bias[1]
    high = lax.reduce_precision(gap, 8, 7)
    mid = lax.reduce_precision(gap - high, 8, 7)
    low = lax.reduce_precision(gap - high - mid, 8, 7)
    parts = jnp.repeat(jnp.stack([high, mid, low], axis=1), 4, axis=1)
    coef = jnp.pad(parts, ((0, -heads % 8), (HEAD, LANES - HEAD - 12)))
    kinds = jnp.arange(4)
    same = (variates[None, :] == kinds[:, None]).astype(F32)
    zeros = jnp.zeros_like(same)
    hot_rows = jnp.concatenate([same, zeros, 1.0 - same, zeros], axis=0)
    ends = segments.reshape(count, QUERIES)
    start = jnp.sum(segments[None, :] < ends[:, :1], axis=1)
    stop = jnp.sum(segments[None, :] <= ends[:, -1:], axis=1)
    first = start // LANES
    kind = (stop - first * LANES + STEP - 1) // STEP
    first = jnp.minimum(first, (length - kind * STEP) // LANES)
    size = max(count, order.shape[0], places.shape[0])
    pad = lambda a: jnp.pad(a.astype(jnp.int32), (0, size - a.shape[0]))
    tables = jnp.stack([pad(order), pad(first), pad(kind), pad(places)])
    return tables, cosine, sine, seg_row, seg_wide, feature, coef, hot_rows


def ffn_kernel(row_parts, flipped, which, *refs):
    rows, refs = refs[:row_parts], refs[row_parts:]
    near, refs = refs[:row_parts], refs[row_parts:]
    far, refs = refs[:row_parts], refs[row_parts:]
    weight, act_out, d_both_out, keep_out, rest_out, send_own, send_rest, grads, sems = refs
    part = rows[0].shape[0]
    share = part // 2
    cols = act_out.shape[1]
    half = row_parts // 2
    copies = []
    for p in range(row_parts):
        pair = (far[p], near[p]) if flipped else (near[p], far[p])
        for k in range(2):
            copy = pltpu.make_async_copy(pair[k].at[which[0]], grads.at[p, pl.ds(k * share, share)], sems.at[p, k])
            copy.start()
            copies.append(copy)
    for p in list(range(half, row_parts)) + list(range(half)):
        at = slice(p * part, (p + 1) * part)
        both = nn_dot(rows[p][...], weight[:, : 2 * cols])
        copies[2 * p].wait()
        copies[2 * p + 1].wait()
        d_act = nn_dot(grads[p], weight[:, 2 * cols :])
        gate, up = both[:, :cols], both[:, cols:]
        sig = 1.0 / (1.0 + jnp.exp(-gate))
        silu = gate * sig
        act_out[at, :] = (silu * up).astype(BF16)
        d_both_out[at, :cols] = (d_act * up * (sig + silu * (1.0 - sig))).astype(BF16)
        d_both_out[at, cols:] = (d_act * silu).astype(BF16)
        back = nt_dot(d_both_out[at, :], weight[:, : 2 * cols])
        if p == 0:
            keep_out[...] = back
        elif p < half:
            rest_out[(p - 1) * part : p * part, :] = back
        else:
            if p == half:
                send_own[...] = back.astype(BF16)
            else:
                send_rest[(p - half - 1) * part : (p - half) * part, :] = back.astype(BF16)


def ffn_middle(flipped, which, rows, near, far, weight, behind=()):
    part, width = rows[0].shape
    count = len(rows)
    length = part * count
    cols = weight.shape[1] // 3
    operands = (which, *rows, *near, *far, weight)
    return pl.pallas_call(
        without(functools.partial(ffn_kernel, count, flipped), len(operands), len(behind)),
        out_shape=(
            jax.ShapeDtypeStruct((length, cols), BF16),
            jax.ShapeDtypeStruct((length, 2 * cols), BF16),
            jax.ShapeDtypeStruct((part, width), F32),
            jax.ShapeDtypeStruct((length // 2 - part, width), F32),
            jax.ShapeDtypeStruct((part, width), BF16),
            jax.ShapeDtypeStruct((length // 2 - part, width), BF16),
        ),
        in_specs=[smem()] + [vmem()] * count + [anywhere()] * (2 * count) + [vmem()] + [anywhere()] * len(behind),
        out_specs=[vmem()] * 6,
        scratch_shapes=[pltpu.VMEM((count, part, width), BF16), pltpu.SemaphoreType.DMA((count, 2))],
        compiler_params=pltpu.CompilerParams(vmem_limit_bytes=VMEM_LIMIT),
        cost_estimate=pl.CostEstimate(
            flops=10 * length * width * cols, bytes_accessed=16 << 20, transcendentals=length * cols
        ),
        name="ffn_middle",
    )(*operands, *behind)


def ffn_tail_kernel(row_parts, which, *refs):
    own, refs = refs[:row_parts], refs[row_parts:]
    other, refs = refs[:row_parts], refs[row_parts:]
    near, refs = refs[:row_parts], refs[row_parts:]
    far, refs = refs[:row_parts], refs[row_parts:]
    acts, boths, weight, refs = refs[:2], refs[2:4], refs[4], refs[5:]
    outs, grad_out, refs = refs[:8], refs[8], refs[9:]
    down_buf, act_buf, both_buf, grad_buf, row_buf, total, keeps, rests, twins, twin_rests = refs[:10]
    in_sems, grad_sems, row_sems, out_sems, total_sems = refs[10:]
    part, width = own[0].shape
    share = part // 2
    length = part * row_parts
    cols = acts[0].shape[1]
    half = length // 2

    def begin(source, target, sem):
        copy = pltpu.make_async_copy(source, target, sem)
        copy.start()
        return copy

    down_copy = begin(weight.at[:, pl.ds(2 * cols, cols)], down_buf, in_sems.at[0])
    act_copies = [begin(acts[seq], act_buf.at[seq], in_sems.at[1 + seq]) for seq in range(2)]
    grad_copies = []
    for seq in range(2):
        now = which[0] if seq == 0 else 1 - which[0]
        for p in range(row_parts):
            pair = (near[p], far[p]) if seq == 0 else (far[p], near[p])
            for k in range(2):
                to = grad_buf.at[seq, pl.ds(p * part + k * share, share)]
                grad_copies.append(begin(pair[k].at[now], to, grad_sems.at[seq, p, k]))
    row_copies = [
        begin((own, other)[seq][p], row_buf.at[seq, pl.ds(p * part, part)], row_sems.at[seq, p])
        for seq in range(2)
        for p in range(row_parts)
    ]
    both_copies = [begin(boths[seq], both_buf.at[seq], in_sems.at[3 + seq]) for seq in range(2)]
    down_copy.wait()
    out_copies = []
    for seq in range(2):
        act_copies[seq].wait()
        mine = nt_dot(act_buf[seq, :half, :], down_buf[...])
        keeps[seq] = mine[:part]
        rests[seq] = mine[part:]
        mine = nt_dot(act_buf[seq, half:, :], down_buf[...]).astype(BF16)
        twins[seq] = mine[:part]
        twin_rests[seq] = mine[part:]
        for k, buf in enumerate((keeps, rests, twins, twin_rests)):
            out_copies.append(begin(buf.at[seq], outs[4 * seq + k], out_sems.at[seq, k]))
    step = width // 4
    total_copies = []
    for what in range(2):
        for seq in range(2):
            for p in range(row_parts):
                if what == 0:
                    grad_copies[2 * (seq * row_parts + p)].wait()
                    grad_copies[2 * (seq * row_parts + p) + 1].wait()
                else:
                    row_copies[seq * row_parts + p].wait()
        if what == 1:
            both_copies[0].wait()
            both_copies[1].wait()
        right, source = (act_buf, both_buf)[what], (grad_buf, row_buf)[what]
        first, size = (2 * cols, cols) if what == 0 else (0, 2 * cols)
        for k in range(4):
            at = slice(k * step, (k + 1) * step)
            value = sum(tn_dot(source[seq, :, at], right[seq]) for seq in range(2))
            total[at, first : first + size] = value.astype(BF16)
            if what == 1:
                rows = pl.ds(k * step, step)
                total_copies.append(begin(total.at[rows], grad_out.at[rows], total_sems.at[k]))
    for copy in out_copies + total_copies:
        copy.wait()


def ffn_tail(which, own, other, near, far, act_own, act_other, d_own, d_other, weight):
    part, width = own[0].shape
    count = len(own)
    length = part * count
    cols = act_own.shape[1]
    rest = length // 2 - part
    shapes = (
        jax.ShapeDtypeStruct((part, width), F32),
        jax.ShapeDtypeStruct((rest, width), F32),
        jax.ShapeDtypeStruct((part, width), BF16),
        jax.ShapeDtypeStruct((rest, width), BF16),
    )
    made = pl.pallas_call(
        functools.partial(ffn_tail_kernel, count),
        out_shape=shapes * 2 + (jax.ShapeDtypeStruct((width, 3 * cols), BF16),),
        in_specs=[smem()] + [anywhere()] * (4 * count + 5),
        out_specs=[anywhere()] * 9,
        scratch_shapes=[
            pltpu.VMEM((width, cols), BF16),
            pltpu.VMEM((2, length, cols), BF16),
            pltpu.VMEM((2, length, 2 * cols), BF16),
            pltpu.VMEM((2, length, width), BF16),
            pltpu.VMEM((2, length, width), BF16),
            pltpu.VMEM((width, 3 * cols), BF16),
            pltpu.VMEM((2, part, width), F32),
            pltpu.VMEM((2, rest, width), F32),
            pltpu.VMEM((2, part, width), BF16),
            pltpu.VMEM((2, rest, width), BF16),
            pltpu.SemaphoreType.DMA((5,)),
            pltpu.SemaphoreType.DMA((2, count, 2)),
            pltpu.SemaphoreType.DMA((2, count)),
            pltpu.SemaphoreType.DMA((2, 4)),
            pltpu.SemaphoreType.DMA((4,)),
        ],
        compiler_params=pltpu.CompilerParams(vmem_limit_bytes=WIDE_LIMIT),
        name="ffn_tail",
    )(which, *own, *other, *near, *far, act_own, act_other, d_own, d_other, weight)
    return made[8], made[:8]


def without(kernel, start, count):
    return lambda *refs: kernel(*refs[:start], *refs[start + count :])


def rows_call(kernel, name, shapes, *operands, scalars=(), behind=(), limit=ROWS_LIMIT):
    single = not isinstance(shapes, (list, tuple))
    count = len(scalars) + len(operands)
    return pl.pallas_call(
        without(kernel, count, len(behind)),
        out_shape=shapes,
        in_specs=[smem()] * len(scalars) + [vmem()] * len(operands) + [anywhere()] * len(behind),
        out_specs=vmem() if single else [vmem()] * len(shapes),
        compiler_params=pltpu.CompilerParams(vmem_limit_bytes=limit),
        cost_estimate=pl.CostEstimate(
            flops=16 * operands[0].size, bytes_accessed=sum(o.size * o.dtype.itemsize for o in operands), transcendentals=0
        ),
        name=name,
    )(*scalars, *operands, *behind)


def pack_kernel(which, rows, query, key, value, out, gate, up, down, own, mine, packed):
    block, start = own.shape[0], 0
    for ref in (query, key, value, out):
        stop = start + ref.shape[1]
        own[:, start:stop] = ref[...]
        packed[:block, start:stop] = ref[...]
        start = stop
    width = rows.shape[2]
    packed[: rows.shape[1], start : start + width] = rows[1 - which[0]]
    start += width
    cols = gate.shape[1] // 2
    for k, ref in enumerate((gate, up, down)):
        for half in range(2):

            @pl.when(which[0] == half)
            def _(ref=ref, half=half, k=k):
                mine[:, k * cols : (k + 1) * cols] = ref[:, half * cols : (half + 1) * cols]
                packed[:block, start + k * cols : start + (k + 1) * cols] = ref[:, (1 - half) * cols : (2 - half) * cols]


def far_rows(near, packed, start):
    share, width = near.shape
    return packed[:share, start : start + width]


def stack_kernel(start, which, mine, theirs, out):
    block, width = mine.shape
    first = pl.multiple_of(which[0] * block, block)
    second = pl.multiple_of((1 - which[0]) * block, block)
    out[pl.ds(first, block), :] = mine[...]
    out[pl.ds(second, block), :] = theirs[:block, start : start + width]


def gains_kernel(place, gain_rows, gain, d_gain_two, bias_parts, out):
    blocks, _, block = gain_rows.shape
    for k in range(blocks):
        at = slice(k * block, (k + 1) * block)
        out[0:1, at] = gain_rows[k, 0:1, :] / gain[:, at].astype(F32)
    out[1:2, :] = d_gain_two[...]
    out[2:, :] = jnp.zeros(out[2:, :].shape, F32)
    lane = lane_of((1, LANES))
    lanes = pl.ds(pl.multiple_of(place[0] * LANES, LANES), LANES)
    for row in range(2):
        line = jnp.zeros((1, LANES), F32)
        for head in range(bias_parts.shape[0]):
            line = jnp.where(lane == head, jnp.sum(bias_parts[head, 8 * row : 8 * row + 8, :]), line)
        out[2 + row : 3 + row, lanes] = line


def gains_finish_kernel(place, mine, theirs, one, two, bias):
    total = mine[...] + theirs[...]
    one[...] = total[0:1]
    two[...] = total[1:2]
    lanes = pl.ds(pl.multiple_of(place[0] * LANES, LANES), LANES)
    bias[...] = (mine[:, lanes] + theirs[:, lanes])[2:4, : bias.shape[1]]


def widen_kernel(angles, cosine, sine):
    half = angles.shape[1] // 2
    cos_half, sin_half = angles[:, :half], angles[:, half:]
    cosine[...] = jnp.concatenate([cos_half] * (LANES // half), axis=1)
    sine[...] = jnp.concatenate([-sin_half, sin_half] * (LANES // half // 2), axis=1)


def pair_kernel(*refs):
    blocks = (len(refs) - 1) // 2
    keeps, other, outs = refs[:blocks], refs[blocks], refs[blocks + 1 :]
    rows = keeps[0].shape[0]
    for k in range(blocks):
        total = keeps[k][...].astype(F32) + other[k * rows : (k + 1) * rows, :].astype(F32)
        outs[k][...] = total.astype(outs[k].dtype)


def finish_kernel(count, own, *refs):
    total = own[...]
    for ref in refs[:-count]:
        total = total + ref[...].astype(F32)
    start = 0
    for out in refs[-count:]:
        stop = start + out.shape[1]
        out[...] = total[:, start:stop]
        start = stop


def pair_sums(partials, other):
    shape = partials[0].shape
    blocks = len(partials) - 1
    shapes = [jax.ShapeDtypeStruct(shape, F32 if k == 0 else BF16) for k in range(blocks)]
    return rows_call(pair_kernel, "pair_sums", shapes, *partials[:-1], other)


def weight_sums(own, arrived, pieces):
    outs = [jax.ShapeDtypeStruct((own.shape[0], own.shape[1] // pieces), F32)] * pieces
    return rows_call(functools.partial(finish_kernel, pieces), "weight_sums", outs, own, *arrived)


def last_kernel(start, count, which, grads, crossed, near, own, *refs):
    arrived, (gate, up, down, rows_out), outs = refs[:count], refs[count : count + 4], refs[count + 4 :]
    cols = grads.shape[1] // 3
    rows = grads.shape[0] // 2
    mine = grads[pl.ds(pl.multiple_of(which[0] * rows, rows), rows), :].astype(F32)
    theirs = crossed[:rows, start:].astype(F32)
    for half in range(2):

        @pl.when(which[0] == half)
        def _(half=half):
            for k, out in enumerate((gate, up, down)):
                out[:, half * cols : (half + 1) * cols] = mine[:, k * cols : (k + 1) * cols]
                out[:, (1 - half) * cols : (2 - half) * cols] = theirs[:, k * cols : (k + 1) * cols]

    stack_kernel(0, which, near, crossed, rows_out)
    finish_kernel(len(outs), own, *arrived, *outs)


def quadrant(own, other, flip):
    share = own.shape[0] // 2
    return jnp.concatenate(
        [own[flip * share : (flip + 1) * share], other[(1 - flip) * share : (2 - flip) * share]], axis=0
    )


def out_split_kernel(hidden, keep, rest, twin, twin_rest, keep_next, rest_next, twin_next, twin_rest_next, *outs):
    first, cross, chips, chips_cross = outs
    part = hidden.shape[0]
    own = keep[...] + twin[...].astype(F32) + hidden[...]
    other = keep_next[...] + twin_next[...].astype(F32)
    first[...] = quadrant(own, other, 0)
    cross[...] = quadrant(own, other, 1).astype(BF16)
    own = rest[...] + twin_rest[...].astype(F32)
    other = rest_next[...] + twin_rest_next[...].astype(F32)
    for k in range(rest.shape[0] // part):
        at = slice(k * part, (k + 1) * part)
        chips[at, :] = quadrant(own[at], other[at], 0)
        chips_cross[at, :] = quadrant(own[at], other[at], 1).astype(BF16)


def swapped(values):
    half = values.shape[0] // 2
    return jnp.concatenate([values[half:], values[:half]], axis=0)


def add_kernel(part, values, arrived, out):
    for k in range(values.shape[0] // part):
        at = slice(k * part, (k + 1) * part)
        out[at, :] = (values[at, :] + swapped(arrived[at, :].astype(F32))).astype(BF16)


def out_finish_kernel(which, first, cross, *refs):
    arrived, out = refs[:-1], refs[-1]
    share = out.shape[1]
    total = first[...] + swapped(cross[...].astype(F32))
    for ref in arrived:
        total = total + ref[...].astype(F32)
    total = total.astype(BF16)
    out[pl.ds(which[0], 1)] = total[None, :share]
    out[pl.ds(1 - which[0], 1)] = total[None, share:]


def inverse_rms(values):
    return lax.rsqrt(jnp.mean(values * values, axis=-1, keepdims=True) + EPS)


def both_halves(start, first, second):
    return jnp.concatenate([first[...], far_rows(first, second, start)], axis=0).astype(F32)


def rows_sum(keep, twin, arrived):
    total = keep[...] + twin[...].astype(F32)
    for ref in arrived:
        total = total + ref[...].astype(F32)
    return total


def norm_kernel(start, near, far, gain, out):
    values = both_halves(start, near, far)
    out[...] = (values * inverse_rms(values) * gain[...].astype(F32)).astype(BF16)


def rest_kernel(rest, twin, out):
    out[...] = (rest[...] + twin[...].astype(F32)).astype(BF16)


def sum_kernel(keep, twin, *refs):
    refs[-1][...] = rows_sum(keep, twin, refs[:-1]).astype(BF16)


def middle_kernel(start, near, far, gain, keep, twin, *refs):
    arrived, (hidden, out) = refs[:-2], refs[-2:]
    values = both_halves(start, near, far) + rows_sum(keep, twin, arrived)
    hidden[...] = values
    out[...] = (values * inverse_rms(values) * gain[...].astype(F32)).astype(BF16)


def pull_norm(values, gain, grad):
    inv = inverse_rms(values)
    scaled = grad * gain
    normed = values * inv
    d_values = inv * (scaled - normed * jnp.mean(scaled * normed, axis=-1, keepdims=True))
    return d_values, jnp.sum(grad * normed, axis=0, keepdims=True)


def back_two_kernel(which, hidden, near, far, gain, across, keep, twin, *refs):
    arrived, (d_hidden, low, d_gain) = refs[:-3], refs[-3:]
    grad = rows_sum(keep, twin, arrived) + across[...].astype(F32)
    d_values, d_gain[...] = pull_norm(hidden[...], gain[...].astype(F32), grad)
    total = jnp.concatenate([near[which[0]], far[which[0]]], axis=0).astype(F32) + d_values
    d_hidden[...] = total
    low[...] = total.astype(BF16)


def back_one_kernel(start, which, near, far, gain, d_hidden, ffn_grad, keep, twin, *refs):
    arrived, (first, packed) = refs[:-2], refs[-2:]
    grad = rows_sum(keep, twin, arrived)
    d_values, _ = pull_norm(both_halves(start, near, far), gain[...].astype(F32), grad)
    total = (d_hidden[...] + d_values).astype(BF16)
    share, width = first.shape
    first[...] = total[:share]
    packed[:share, :width] = total[share:]
    rows = ffn_grad.shape[0] // 2
    packed[:rows, width:] = ffn_grad[pl.ds(pl.multiple_of((1 - which[0]) * rows, rows), rows), :]


def grad_kernel(row_parts, blocks, tables, *refs):
    rows, refs = refs[:row_parts], refs[row_parts:]
    right, refs = refs[0], refs[1:]
    keeps, send, left = refs[:blocks], refs[blocks], refs[blocks + 1]
    block = keeps[0].shape[0]
    left_of(rows, right, left)
    for s in range(2 * blocks):
        at = pl.ds(pl.multiple_of(tables[3, s] * block, block), block)
        total = left[at, :].astype(BF16)
        if s < blocks:
            keeps[s][...] = total
        else:
            send[(s - blocks) * block : (s - blocks + 1) * block, :] = total


def weight_partials(tables, rows, right, blocks):
    part, width = rows[0].shape
    length, cols = right.shape
    block = width // (2 * blocks)
    return pl.pallas_call(
        functools.partial(grad_kernel, len(rows), blocks),
        out_shape=(jax.ShapeDtypeStruct((block, cols), BF16),) * blocks
        + (jax.ShapeDtypeStruct((width // 2, cols), BF16),),
        in_specs=[smem()] + [vmem()] * (len(rows) + 1),
        out_specs=[vmem()] * (blocks + 1),
        scratch_shapes=[pltpu.VMEM((width, cols), F32)],
        compiler_params=pltpu.CompilerParams(vmem_limit_bytes=VMEM_LIMIT),
        cost_estimate=pl.CostEstimate(
            flops=2 * length * width * cols, bytes_accessed=8 << 20, transcendentals=0
        ),
        name="weight_partials",
    )(tables, *rows, right)


def left_of(rows, right, total):
    part, width = rows[0].shape
    step = 2 * LANES
    for c in range(width // step):
        at = slice(c * step, (c + 1) * step)
        total[at, :] = sum(tn_dot(ref[:, at], right[p * part : (p + 1) * part, :]) for p, ref in enumerate(rows))


def send_kernel(row_parts, blocks, tables, *refs):
    rows, (right, send, left) = refs[:row_parts], refs[row_parts:]
    block = send.shape[0] // blocks
    left_of(rows, right, left)
    for s in range(blocks):
        at = pl.ds(pl.multiple_of(tables[3, blocks + s] * block, block), block)
        send[s * block : (s + 1) * block, :] = left[at, :].astype(BF16)


def keep_kernel(row_parts, blocks, tables, *refs):
    weights, refs = refs[: 2 * blocks], refs[2 * blocks :]
    rows, right, refs = refs[:row_parts], refs[row_parts], refs[row_parts + 1 :]
    keeps, (gain_row, left) = refs[:blocks], refs[blocks:]
    block = keeps[0].shape[0]
    cols = right.shape[1]
    left_of(rows, right, left)
    for s in range(2 * blocks):
        at = pl.ds(pl.multiple_of(tables[3, s] * block, block), block)
        total = left[at, :]
        product = total * weights[s][:block, :cols].astype(F32)
        product = sum(product[:, c * LANES : (c + 1) * LANES] for c in range(cols // LANES))
        high = product.astype(BF16)
        rest = (product - high.astype(F32)).astype(BF16)
        ones = jnp.ones((8, LANES), BF16)
        gain_row[pl.ds(tables[3, s], 1)] = (nt_dot(ones, high) + nt_dot(ones, rest))[None]
        if s < blocks:
            keeps[s][...] = total.astype(BF16)


def qkv_call(kernel, name, shapes, tables, operands, scratch):
    single = not isinstance(shapes, tuple)
    return pl.pallas_call(
        kernel,
        out_shape=shapes,
        in_specs=[smem()] + [vmem()] * len(operands),
        out_specs=vmem() if single else [vmem()] * len(shapes),
        scratch_shapes=[pltpu.VMEM(scratch, F32)],
        compiler_params=pltpu.CompilerParams(vmem_limit_bytes=VMEM_LIMIT),
        name=name,
    )(tables, *operands)


def qkv_partials(tables, weights, rows, right, blocks):
    part, width = rows[0].shape
    length, cols = right.shape
    block = width // (2 * blocks)
    send = qkv_call(
        functools.partial(send_kernel, len(rows), blocks),
        "qkv_send",
        jax.ShapeDtypeStruct((width // 2, cols), BF16),
        tables,
        [*rows, right],
        (width, cols),
    )
    keeps = qkv_call(
        functools.partial(keep_kernel, len(rows), blocks),
        "qkv_keep",
        (jax.ShapeDtypeStruct((block, cols), BF16),) * blocks + (jax.ShapeDtypeStruct((2 * blocks, 8, block), F32),),
        tables,
        [*weights, *rows, right],
        (width, cols),
    )
    return keeps[:-1], send, keeps[-1]


def hop(values, axis, flip):
    size = lax.axis_size(axis)
    return lax.ppermute(values, axis, [(i, i ^ flip) for i in range(size)])


def swap_blocks(values, axis, index, size):
    shape = values.shape
    bit = 1
    while bit < size:
        split = shape[:axis] + (size // (2 * bit), 2, bit) + shape[axis + 1 :]
        cut = values.reshape(split)
        cut = jnp.where((index & bit) != 0, jnp.flip(cut, axis + 1), cut)
        values = cut.reshape(shape)
        bit *= 2
    return values


def gather_chips(block):
    nt = lax.axis_size("tp")
    return [block] + [hop(block, "tp", 2 * k) for k in range(1, nt // 2)]


def with_twins(blocks):
    return blocks + [hop(block, "tp", 1) for block in blocks]


def gather_rows(block):
    return with_twins(gather_chips(block))


def region(ready, run):
    shapes = jax.eval_shape(run)
    return lax.cond(ready, run, lambda: jax.tree.map(lambda a: jnp.zeros(a.shape, a.dtype), shapes))


def chips_low(rest, twin, *behind):
    return rows_call(
        rest_kernel, "rest_rows", jax.ShapeDtypeStruct(rest.shape, BF16), rest, twin, behind=behind
    )


def chips_hop(low, nt):
    if nt == 4:
        return [hop(low, "tp", 2)]
    rows = low.shape[0] // (nt // 2 - 1)
    return [hop(low[(k - 1) * rows : k * rows], "tp", 2 * k) for k in range(1, nt // 2)]


def shards(
    layer_in,
    attn_gain,
    ffn_gain,
    query_weight,
    key_weight,
    value_weight,
    out_weight,
    variate_bias,
    gate_weight,
    up_weight,
    down_weight,
    segment_ids,
    variate_ids,
    time_ids,
    out_grad,
):
    seq_count, share, width = layer_in.shape
    nz, nx, nt = lax.axis_size("fsdp"), lax.axis_size("ctx"), lax.axis_size("tp")
    iz, ix, it = lax.axis_index("fsdp"), lax.axis_index("ctx"), lax.axis_index("tp")
    assert nx == 2 and seq_count == nx
    length = segment_ids.shape[1]
    heads = variate_bias.shape[1]
    proj = heads * HEAD

    def pick(table, which):
        return lax.dynamic_index_in_dim(table, which, 0, keepdims=False)

    def swap(mine, theirs):
        return jnp.where(ix == 0, mine, theirs), jnp.where(ix == 0, theirs, mine)

    gain_one, gain_two = attn_gain[None], ffn_gain[None]
    part = nx * share
    low_rows = jax.ShapeDtypeStruct((part, width), BF16)
    wide_rows = jax.ShapeDtypeStruct((part, width), F32)
    gain_row = jax.ShapeDtypeStruct((1, width), F32)
    half_rows = jax.ShapeDtypeStruct((share, width), BF16)
    which = ix.astype(jnp.int32).reshape(1)
    ready = ix >= 0
    cols = gate_weight.shape[1] // 2
    near, grad_own = pick(layer_in, ix), out_grad
    block = query_weight.shape[0]
    attn_shape = jax.ShapeDtypeStruct((block, 4 * proj), BF16)
    packed_shape = jax.ShapeDtypeStruct((max(block, share), 4 * proj + width + 3 * cols), BF16)
    ffn_shape = jax.ShapeDtypeStruct((gate_weight.shape[0], 3 * cols), BF16)
    attn_own, mine, packed = rows_call(
        pack_kernel, "pack_weights", (attn_shape, ffn_shape, packed_shape), layer_in, query_weight, key_weight,
        value_weight, out_weight, gate_weight, up_weight, down_weight, scalars=(which,), limit=WIDE_LIMIT,
    )
    start = 4 * proj

    def twin(block):
        return hop(block, "tp", 1)

    def across(block):
        return hop(block, "ctx", 1)

    def first_transfers():
        attn_z = [hop(attn_own, "fsdp", k) for k in range(1, nz)]
        far = across(packed)
        grad_y = gather_chips(grad_own)[1:]
        order = jnp.arange(nx * nt).reshape(nx, nt // 2, 2)
        order = swap_blocks(swap_blocks(swap_blocks(order, 0, ix, nx), 1, it // 2, nt // 2), 2, it % 2, 2)
        order = order.transpose(2, 1, 0).reshape(nx * nt)
        places = jnp.arange(nz * nx).reshape(nz, nx)
        places = swap_blocks(swap_blocks(places, 0, iz, nz), 1, ix, nx).transpose(1, 0).reshape(nz * nx)
        tables = attention_tables(
            pick(segment_ids, ix), pick(variate_ids, ix), pick(time_ids, ix), variate_bias, order, places
        )
        return attn_z, far, grad_y, tables

    attn_z, far, grad_y, made = region(ready, first_transfers)
    tables, cosine, sine, seg_row, seg_wide, feature, coef, hot_rows = made
    stack_shape = jax.ShapeDtypeStruct((2 * block, 3 * cols), BF16)
    ffn_w = rows_call(
        functools.partial(stack_kernel, start + width), "stack_weights", stack_shape, mine, far, scalars=(which,)
    )
    ffn_w = lax.all_gather(ffn_w, "fsdp", axis=0, tiled=True)

    rows_own = rows_call(functools.partial(norm_kernel, start), "norm_rows", low_rows, near, far, gain_one)

    def gather_one():
        return gather_chips(rows_own)[1:], [across(piece) for piece in attn_z]

    chips, rest_x = region(ready, gather_one)
    chips_one = [rows_own] + chips
    attn_w = [attn_own] + attn_z + [far] + rest_x

    def attend():
        twins = [twin(rows) for rows in chips_one]
        near_twins = [twin(rows) for rows in [grad_own] + grad_y]
        return across(grad_own), near_twins, twins, attention_forward(
            tables, chips_one + twins, attn_w, cosine, sine, seg_row, seg_wide, feature, coef, heads
        )

    grad_far, near_twins, twins, (q_aug, k_aug, v_rows, mixed, lse, keep, rest, send, send_rest) = region(ready, attend)

    def scatter_attn():
        low = chips_low(rest, twin(send_rest))
        return chips_hop(low, nt), twin(send), [across(piece) for piece in grad_y], twin(grad_far)

    rows_one = chips_one + twins
    chips, twins, grad_far_y, far_twin = region(ready, scatter_attn)
    grad_near, grad_far = [grad_own] + grad_y, [grad_far] + grad_far_y
    hidden, rows_two = rows_call(
        functools.partial(middle_kernel, start), "middle_rows", (wide_rows, low_rows), near, far, gain_two, keep, twins,
        *chips,
    )

    def gather_two():
        return (
            gather_chips(rows_two)[1:],
            across(rows_two),
            [twin(rows) for rows in grad_far[1:]],
            twin(rows_two),
        )

    chips_two, next_own, far_twins, rows_twin = region(ready, gather_two)
    grad_near, grad_far = grad_near + near_twins, grad_far + [far_twin] + far_twins

    def ffn_own():
        twins = [twin(rows) for rows in chips_two]
        return [across(rows) for rows in chips_two], twins, ffn_middle(
            False, which, [rows_two] + chips_two + [rows_twin] + twins, grad_near, grad_far, ffn_w
        )

    next_y, twins, (act, d_both, keep, rest, send, send_rest) = region(ready, ffn_own)

    rows_two = [rows_two] + chips_two + [rows_twin] + twins
    rows_next = [next_own] + next_y

    def ffn_next():
        low = chips_low(rest, twin(send_rest))
        twins = [twin(rows) for rows in rows_next]
        return chips_hop(low, nt), twin(send), twins, ffn_middle(
            True, 1 - which, rows_next + twins, grad_near, grad_far, ffn_w
        )

    chips, twins, next_twins, made = region(ready, ffn_next)
    rows_next = rows_next + next_twins
    act_next, d_both_next, keep_next, rest_next, send_next, send_rest = made
    low_next = chips_low(rest_next, twin(send_rest))

    def scatter_next():
        return (
            chips_hop(low_next, nt),
            twin(send_next),
            ffn_tail(which, rows_two, rows_next, grad_near, grad_far, act, act_next, d_both, d_both_next, ffn_w),
        )

    chips_next, twins_next, (ffn_grad, parts) = region(ready, scatter_next)
    low_across = rows_call(sum_kernel, "sum_rows", low_rows, keep_next, twins_next, *chips_next)

    def cross_next():
        out_twins = [twin(parts[k]) for k in (2, 3, 6, 7)]
        rest_shape = (parts[1].shape[0], width)
        shapes = (
            wide_rows,
            low_rows,
            jax.ShapeDtypeStruct(rest_shape, F32),
            jax.ShapeDtypeStruct(rest_shape, BF16),
        )
        return across(low_across), rows_call(
            out_split_kernel, "out_split", shapes, hidden, parts[0], parts[1], out_twins[0], out_twins[1], parts[4],
            parts[5], out_twins[2], out_twins[3],
        )

    arrived, (out_first, out_cross, out_chips, out_chips_cross) = region(ready, cross_next)
    ffn_grad = lax.psum_scatter(ffn_grad, "fsdp", scatter_dimension=0, tiled=True)
    d_hidden, low, d_gain_two = rows_call(
        back_two_kernel,
        "back_two",
        (wide_rows, low_rows, gain_row),
        hidden,
        grad_near[0],
        grad_far[0],
        gain_two,
        arrived,
        keep,
        twins,
        *chips,
        scalars=(which,),
    )

    def gather_back():
        return gather_chips(low)[1:], twin(low), across(out_chips_cross)

    chips_back, twin_back, out_arrived = region(ready, gather_back)
    branch_rows = [low] + chips_back
    branch_rows = branch_rows + [twin_back] + [twin(rows) for rows in chips_back]
    low_out = rows_call(
        functools.partial(add_kernel, part), "add_rows", jax.ShapeDtypeStruct(out_chips.shape, BF16), out_chips, out_arrived
    )
    out_grads = weight_partials(tables, branch_rows, mixed, nz)

    def attend_back():
        return chips_hop(low_out, nt), across(out_cross), across(out_grads[-1]), attention_backward(
            tables, branch_rows, attn_w, q_aug, k_aug, v_rows, lse, cosine, sine, seg_row, seg_wide, hot_rows, heads
        )

    out_arrived, out_cross, out_other, made = region(ready, attend_back)
    keep, rest, send, send_rest, d_qkv, bias_parts = made

    place = it.astype(jnp.int32).reshape(1)
    gain_shape = jax.ShapeDtypeStruct((8, width), F32)

    def scatter_one():
        twins = twin(send)
        low = chips_low(rest, twin(send_rest), twins)
        keeps, sent, gain_rows = qkv_partials(tables, attn_w, rows_one, d_qkv, nz)
        sums = pair_sums(out_grads, out_other)
        arrived = [hop(piece, "fsdp", k) for k, piece in enumerate(sums) if k > 0]
        totals = rows_call(
            gains_kernel, "gain_rows", gain_shape, gain_rows, gain_one, d_gain_two, bias_parts, scalars=(place,)
        )
        totals = totals + twin(totals)
        totals = sum([hop(totals, "fsdp", k) for k in range(1, nz)], totals)
        return chips_hop(low, nt), twins, keeps, across(sent), sums[0], arrived, totals

    chips, twins, qkv_keeps, qkv_other, out_sum, out_z, totals = region(ready, scatter_one)
    packed_shape = jax.ShapeDtypeStruct((max(block, share), width + 3 * cols), BF16)
    d_near, packed = rows_call(
        functools.partial(back_one_kernel, start), "back_one", (half_rows, packed_shape), near, far, gain_one, d_hidden,
        ffn_grad, keep, twins, *chips, scalars=(which,),
    )
    qkv_sums = pair_sums([*qkv_keeps, None], qkv_other)

    def last_transfers():
        arrived = [hop(piece, "fsdp", k) for k, piece in enumerate(qkv_sums) if k > 0]
        (out_weight_grad,) = weight_sums(out_sum, out_z, 1)
        layer_out = rows_call(
            out_finish_kernel, "layer_out", jax.ShapeDtypeStruct(layer_in.shape, BF16), out_first, out_cross,
            *out_arrived, scalars=(which,),
        )
        chips = [hop(totals, "tp", 2 * k) for k in range(1, nt // 2)]
        return arrived, across(packed), chips, out_weight_grad, layer_out

    arrived, crossed, chips, out_weight_grad, layer_out = region(ready, last_transfers)
    totals = sum(chips, totals)

    def last_sums():
        weight_shape = jax.ShapeDtypeStruct(gate_weight.shape, F32)
        in_shape = jax.ShapeDtypeStruct((nx * share, width), BF16)
        head_shape = jax.ShapeDtypeStruct(query_weight.shape, F32)
        return across(totals), rows_call(
            functools.partial(last_kernel, width, len(arrived)), "last_sums",
            [weight_shape] * 3 + [in_shape] + [head_shape] * 3,
            ffn_grad, crossed, d_near, qkv_sums[0], *arrived, scalars=(which,), limit=WIDE_LIMIT,
        )

    totals_x, made = region(ready, last_sums)
    gate_grad, up_grad, down_grad, in_grad, query_grad, key_grad, value_grad = made
    in_grad = in_grad.reshape(layer_in.shape)
    attn_gain_grad, ffn_gain_grad, bias_grad = rows_call(
        gains_finish_kernel, "gain_sums", (gain_row, gain_row, jax.ShapeDtypeStruct((2, heads), F32)), totals, totals_x,
        scalars=(place,),
    )
    return (
        layer_out,
        in_grad,
        attn_gain_grad.reshape(width),
        ffn_gain_grad.reshape(width),
        query_grad,
        key_grad,
        value_grad,
        out_weight_grad,
        bias_grad,
        gate_grad,
        up_grad,
        down_grad,
    )


def solution(mesh):
    rows = P("fsdp", ("ctx", "tp"), None)
    weight = P(("fsdp", "ctx"), "tp")
    ids = P("fsdp", None)
    bias = P(None, "tp")
    in_specs = (rows, P(), P()) + (weight,) * 4 + (bias,) + (weight,) * 3 + (ids,) * 3 + (rows,)
    out_specs = (rows, rows, P(), P()) + (weight,) * 4 + (bias,) + (weight,) * 3
    return jax.shard_map(shards, mesh=mesh, in_specs=in_specs, out_specs=out_specs, check_vma=False)
```

```python
import functools
import jax
import jax.numpy as jnp
from jax import lax
from jax.sharding import PartitionSpec as P
from jax.experimental import pallas as pl
from jax.experimental.pallas import tpu as pltpu

HEADS = 16
HEAD = 64
EPS = 1e-05
NEG = -1e30
F32 = jnp.float32
BF16 = jnp.bfloat16
LANES = 128
QUERIES = 256
STEP = 128
VMEM_LIMIT = 40 * 1024 * 1024
ROWS_LIMIT = 16 * 1024 * 1024
WIDE_LIMIT = 56 * 1024 * 1024


def nt_dot(left, right):
    return lax.dot_general(left, right, (((1,), (1,)), ((), ())), preferred_element_type=F32)


def nn_dot(left, right):
    return lax.dot_general(left, right, (((1,), (0,)), ((), ())), preferred_element_type=F32)


def tn_dot(left, right):
    return lax.dot_general(left, right, (((0,), (0,)), ((), ())), preferred_element_type=F32)


def lane_of(shape):
    return lax.broadcasted_iota(jnp.int32, shape, len(shape) - 1)


def half_swap(values):
    lane = lane_of(values.shape)
    forward = pltpu.roll(values, LANES - HEAD // 2, 1)
    back = pltpu.roll(values, HEAD // 2, 1)
    return jnp.where(lane % HEAD < HEAD // 2, forward, back)


def fwd_kernel(row_parts, weight_parts, heads, *refs):
    tables, refs = refs[0], refs[1:]
    rows, refs = refs[:row_parts], refs[row_parts:]
    weights, refs = refs[:weight_parts], refs[weight_parts:]
    cosine, sine, seg_row, seg_wide, feature, coef = refs[:6]
    q_aug, k_aug, v_out, mixed_out, lse_out, keep_out, rest_out, send_own, send_rest = refs[6:15]
    full, out_full, mixed_wide, v_turn = refs[15:]
    pairs = heads // 2
    proj = heads * HEAD
    length = q_aug.shape[1]
    block = weights[0].shape[0]
    part = rows[0].shape[0]
    share = part // 2
    for i in range(weight_parts):
        at = pl.ds(pl.multiple_of(tables[3, i] * block, block), block)
        full[at, :] = weights[i][:block, : 3 * proj]
        out_full[at, :] = weights[i][:block, 3 * proj : 4 * proj]
    for p in range(row_parts):
        raw = nn_dot(rows[p][...], full[...])
        for k in range(2):
            piece = raw[k * share : (k + 1) * share]
            start = pl.multiple_of(tables[0, 2 * p + k] * share, share)
            at = pl.ds(start, share)
            cos_now, sin_now, feat = cosine[at, :], sine[at, :], feature[at, :].astype(F32)
            lane = lane_of((share, LANES))
            for pair in range(pairs):
                low = pair * LANES
                q = piece[:, low : low + LANES]
                q = (q * cos_now + half_swap(q) * sin_now).astype(BF16).astype(F32) * HEAD**-0.5
                kk = piece[:, proj + low : proj + low + LANES]
                kk = kk * cos_now + half_swap(kk) * sin_now
                v_out[pair, at, :] = piece[:, 2 * proj + low : 2 * proj + low + LANES].astype(BF16)
                for odd in range(2):
                    head = 2 * pair + odd
                    q_now = pltpu.roll(q, HEAD, 1) if odd else q
                    k_now = pltpu.roll(kk, HEAD, 1) if odd else kk
                    q_feat = feat * coef[head : head + 1, :]
                    q_aug[head, at, :] = jnp.where(lane < HEAD, q_now, q_feat).astype(BF16)
                    k_aug[head, at, :] = jnp.where(lane < HEAD, k_now, feat).astype(BF16)
    for pair in range(pairs):
        for b in range(length // LANES):
            tile = v_out[pair, b * LANES : (b + 1) * LANES, :].astype(F32)
            v_turn[pair, :, b * LANES : (b + 1) * LANES] = tile.T.astype(BF16)

    def query_block(b, carry):
        at = pl.ds(pl.multiple_of(b * QUERIES, QUERIES), QUERIES)
        seg_q = seg_row[pl.ds(b, 1), :]
        first = pl.multiple_of(tables[1, b] * LANES, LANES)
        for kind in range(1, length // STEP + 1):

            @pl.when(tables[2, b] == kind)
            def _(kind=kind):
                win = pl.ds(first, kind * STEP)
                keep = seg_wide[win, :] == seg_q
                scores = [nt_dot(k_aug[h, win, :], q_aug[h, at, :]) for h in range(heads)]
                probs, totals = [], []
                for head in range(heads):
                    s = jnp.where(keep, scores[head], NEG)
                    top = jnp.max(s, axis=0, keepdims=True)
                    p = jnp.exp(s - top)
                    total = jnp.sum(p, axis=0, keepdims=True)
                    probs.append(p.astype(BF16))
                    totals.append(total)
                    lse_out[head, pl.ds(b, 1), :] = top + jnp.log(total)
                for pair in range(pairs):
                    outs = []
                    for odd in range(2):
                        head = 2 * pair + odd
                        turn = v_turn[pair, odd * HEAD : (odd + 1) * HEAD, win]
                        outs.append(nn_dot(turn, probs[head]) / totals[head])
                    mixed = jnp.concatenate(outs, axis=0).T
                    mixed_wide[at, pair * LANES : (pair + 1) * LANES] = mixed

        return carry

    lax.fori_loop(0, length // QUERIES, query_block, 0)
    for slot in range(2 * row_parts):
        start = pl.multiple_of(tables[0, slot] * share, share)
        piece = mixed_wide[pl.ds(start, share), :]
        mixed_out[slot * share : (slot + 1) * share, :] = piece.astype(BF16)
    half = row_parts // 2
    for p in range(row_parts):
        back = nt_dot(mixed_out[p * part : (p + 1) * part, :], out_full[...])
        if p == 0:
            keep_out[...] = back
        elif p < half:
            rest_out[(p - 1) * part : p * part, :] = back
        else:
            if p == half:
                send_own[...] = back.astype(BF16)
            else:
                send_rest[(p - half - 1) * part : (p - half) * part, :] = back.astype(BF16)


def vmem():
    return pl.BlockSpec(memory_space=pltpu.VMEM)


def anywhere():
    return pl.BlockSpec(memory_space=pl.ANY)


def smem():
    return pl.BlockSpec(memory_space=pltpu.SMEM)


def attention_forward(tables, rows, weights, cosine, sine, seg_row, seg_wide, feature, coef, heads, behind=()):
    proj = heads * HEAD
    length = cosine.shape[0]
    part, width = rows[0].shape
    shapes = (
        jax.ShapeDtypeStruct((heads, length, LANES), BF16),
        jax.ShapeDtypeStruct((heads, length, LANES), BF16),
        jax.ShapeDtypeStruct((heads // 2, length, LANES), BF16),
        jax.ShapeDtypeStruct((length, proj), BF16),
        jax.ShapeDtypeStruct((heads, length // QUERIES, QUERIES), F32),
        jax.ShapeDtypeStruct((part, width), F32),
        jax.ShapeDtypeStruct((length // 2 - part, width), F32),
        jax.ShapeDtypeStruct((part, width), BF16),
        jax.ShapeDtypeStruct((length // 2 - part, width), BF16),
    )
    count = len(rows) + len(weights) + 6
    operands = (tables, *rows, *weights, cosine, sine, seg_row, seg_wide, feature, coef)
    return pl.pallas_call(
        without(functools.partial(fwd_kernel, len(rows), len(weights), heads), len(operands), len(behind)),
        out_shape=shapes,
        in_specs=[smem()] + [vmem()] * count + [anywhere()] * len(behind),
        out_specs=[vmem()] * 9,
        scratch_shapes=[
            pltpu.VMEM((width, 3 * proj), BF16),
            pltpu.VMEM((width, proj), BF16),
            pltpu.VMEM((length, proj), F32),
            pltpu.VMEM((heads // 2, LANES, length), BF16),
        ],
        compiler_params=pltpu.CompilerParams(vmem_limit_bytes=VMEM_LIMIT),
        cost_estimate=pl.CostEstimate(
            flops=2 * length * width * 3 * proj, bytes_accessed=8 << 20, transcendentals=length * length * heads // 2
        ),
        name="attn_fwd",
    )(*operands, *behind)


def bwd_kernel(row_parts, weight_parts, heads, *refs):
    tables, refs = refs[0], refs[1:]
    rows, refs = refs[:row_parts], refs[row_parts:]
    weights, refs = refs[:weight_parts], refs[weight_parts:]
    q_aug, k_aug, v_in, lse, cosine, sine, seg_row, seg_wide, hot_rows = refs[:9]
    keep_out, rest_out, send_own, send_rest, d_qkv_out, bias_out = refs[9:15]
    full, out_full, d_out, k_turn, dq_acc, dk_acc, dv_acc = refs[15:]
    pairs = heads // 2
    proj = heads * HEAD
    length = q_aug.shape[1]
    block = weights[0].shape[0]
    part = rows[0].shape[0]
    share = part // 2
    for i in range(weight_parts):
        at = pl.ds(pl.multiple_of(tables[3, i] * block, block), block)
        full[at, :] = weights[i][:block, : 3 * proj]
        out_full[at, :] = weights[i][:block, 3 * proj : 4 * proj]
    for p in range(row_parts):
        raw = nn_dot(rows[p][...], out_full[...]).astype(BF16)
        for k in range(2):
            start = pl.multiple_of(tables[0, 2 * p + k] * share, share)
            d_out[pl.ds(start, share), :] = raw[k * share : (k + 1) * share]
    for head in range(heads):
        for b in range(length // LANES):
            tile = k_aug[head, b * LANES : (b + 1) * LANES, :].astype(F32)
            k_turn[head, :, b * LANES : (b + 1) * LANES] = tile.T.astype(BF16)
    dk_acc[...] = jnp.zeros(dk_acc.shape, F32)
    dv_acc[...] = jnp.zeros(dv_acc.shape, F32)
    bias_out[...] = jnp.zeros(bias_out.shape, F32)

    def query_block(b, carry):
        at = pl.ds(pl.multiple_of(b * QUERIES, QUERIES), QUERIES)
        seg_q = seg_row[pl.ds(b, 1), :]
        hot = hot_rows[:, at]
        first = pl.multiple_of(tables[1, b] * LANES, LANES)
        for kind in range(1, length // STEP + 1):

            @pl.when(tables[2, b] == kind)
            def _(kind=kind):
                win = pl.ds(first, kind * STEP)
                keep = seg_wide[win, :] == seg_q
                owns = []
                for head in range(heads):
                    chunk = slice(head // 2 * LANES, (head // 2 + 1) * LANES)
                    d_pair = d_out[at, chunk]
                    lane = lane_of(d_pair.shape)
                    owns.append(jnp.where((lane >= HEAD) == (head % 2 == 1), d_pair, jnp.zeros_like(d_pair)))
                turned = []
                for base in range(0, heads, 2):
                    group = range(base, base + 2)
                    s = [nt_dot(k_aug[h, win, :], q_aug[h, at, :]) for h in group]
                    dp = [nt_dot(v_in[h // 2, win, :], owns[h]) for h in group]
                    low, ds = [], []
                    for i, h in enumerate(group):
                        p = jnp.exp(jnp.where(keep, s[i] - lse[h, pl.ds(b, 1), :], NEG))
                        low.append(p.astype(BF16))
                        ds.append((p * (dp[i] - jnp.sum(p * dp[i], axis=0, keepdims=True))).astype(BF16))
                    for i, h in enumerate(group):
                        if i % 2 == 0:
                            both = jnp.concatenate(low[i : i + 2], axis=1)
                            dv_acc[h // 2, win, :] += nn_dot(both, jnp.concatenate(owns[h : h + 2], axis=0))
                        dk_acc[h, win, :] += nn_dot(ds[i], q_aug[h, at, :])
                        dq = nn_dot(k_turn[h, :, win], ds[i])
                        turned.append(dq[:HEAD])
                        sums = dq[HEAD : HEAD + 8]
                        bias_out[h] += jnp.concatenate([sums * hot[:8], sums * hot[8:]], axis=0)
                for pair in range(pairs):
                    chunk = slice(pair * LANES, (pair + 1) * LANES)
                    dq_acc[at, chunk] = jnp.concatenate(turned[2 * pair : 2 * pair + 2], axis=0).T * HEAD**-0.5

        return carry

    lax.fori_loop(0, length // QUERIES, query_block, 0)
    for p in range(row_parts):
        for k in range(2):
            slot = 2 * p + k
            at = pl.ds(pl.multiple_of(tables[0, slot] * share, share), share)
            to = slice(slot * share, (slot + 1) * share)
            cos_now, sin_now = cosine[at, :], sine[at, :]
            lane = lane_of((share, LANES))
            for pair in range(pairs):
                low = pair * LANES
                dq = dq_acc[at, low : low + LANES]
                dk = jnp.where(lane < HEAD, dk_acc[2 * pair, at, :], pltpu.roll(dk_acc[2 * pair + 1, at, :], HEAD, 1))
                d_qkv_out[to, low : low + LANES] = (dq * cos_now - half_swap(dq) * sin_now).astype(BF16)
                d_qkv_out[to, proj + low : proj + low + LANES] = (dk * cos_now - half_swap(dk) * sin_now).astype(BF16)
                d_qkv_out[to, 2 * proj + low : 2 * proj + low + LANES] = dv_acc[pair, at, :].astype(BF16)
        part_rows = d_qkv_out[p * part : (p + 1) * part, :]
        back = nt_dot(part_rows, full[...])
        half = row_parts // 2
        if p == 0:
            keep_out[...] = back
        elif p < half:
            rest_out[(p - 1) * part : p * part, :] = back
        else:
            if p == half:
                send_own[...] = back.astype(BF16)
            else:
                send_rest[(p - half - 1) * part : (p - half) * part, :] = back.astype(BF16)


def attention_backward(tables, rows, weights, q_aug, k_aug, v_in, lse, cosine, sine, seg_row, seg_wide, hot_rows, heads, behind=()):
    proj = heads * HEAD
    length = cosine.shape[0]
    part, width = rows[0].shape
    shapes = (
        jax.ShapeDtypeStruct((part, width), F32),
        jax.ShapeDtypeStruct((length // 2 - part, width), F32),
        jax.ShapeDtypeStruct((part, width), BF16),
        jax.ShapeDtypeStruct((length // 2 - part, width), BF16),
        jax.ShapeDtypeStruct((length, 3 * proj), BF16),
        jax.ShapeDtypeStruct((heads, 16, QUERIES), F32),
    )
    count = len(rows) + len(weights) + 9
    operands = (tables, *rows, *weights, q_aug, k_aug, v_in, lse, cosine, sine, seg_row, seg_wide, hot_rows)
    return pl.pallas_call(
        without(functools.partial(bwd_kernel, len(rows), len(weights), heads), len(operands), len(behind)),
        out_shape=shapes,
        in_specs=[smem()] + [vmem()] * count + [anywhere()] * len(behind),
        out_specs=[vmem()] * 6,
        scratch_shapes=[
            pltpu.VMEM((width, 3 * proj), BF16),
            pltpu.VMEM((width, proj), BF16),
            pltpu.VMEM((length, proj), BF16),
            pltpu.VMEM((heads, LANES, length), BF16),
            pltpu.VMEM((length, proj), F32),
            pltpu.VMEM((heads, length, LANES), F32),
            pltpu.VMEM((heads // 2, length, LANES), F32),
        ],
        compiler_params=pltpu.CompilerParams(vmem_limit_bytes=VMEM_LIMIT),
        cost_estimate=pl.CostEstimate(
            flops=2 * length * width * 4 * proj, bytes_accessed=12 << 20, transcendentals=length * length * heads // 2
        ),
        name="attn_bwd",
    )(*operands, *behind)


def attention_tables(segments, variates, times, variate_bias, order, places):
    length = segments.shape[0]
    heads = variate_bias.shape[1]
    count = length // QUERIES
    half = HEAD // 2
    frequency = 10000.0 ** (-2.0 * jnp.arange(half, dtype=F32) / HEAD)
    angles = times.astype(F32)[:, None] * frequency
    cos_half, sin_half = jnp.cos(angles), jnp.sin(angles)
    wide = jax.ShapeDtypeStruct((length, LANES), F32)
    cosine, sine = rows_call(
        widen_kernel, "widen_angles", (wide, wide), jnp.concatenate([cos_half, sin_half], axis=1)
    )
    seg_row = segments.reshape(count, QUERIES)
    seg_wide = jnp.broadcast_to(segments[:, None], (length, QUERIES))
    lane = jnp.arange(LANES)
    live = (lane >= HEAD) & (lane < HEAD + 12)
    feature = ((variates[:, None] == (lane % 4)[None, :]) & live[None, :]).astype(BF16)
    gap = variate_bias[0] - variate_bias[1]
    high = lax.reduce_precision(gap, 8, 7)
    mid = lax.reduce_precision(gap - high, 8, 7)
    low = lax.reduce_precision(gap - high - mid, 8, 7)
    parts = jnp.repeat(jnp.stack([high, mid, low], axis=1), 4, axis=1)
    coef = jnp.pad(parts, ((0, -heads % 8), (HEAD, LANES - HEAD - 12)))
    kinds = jnp.arange(4)
    same = (variates[None, :] == kinds[:, None]).astype(F32)
    zeros = jnp.zeros_like(same)
    hot_rows = jnp.concatenate([same, zeros, 1.0 - same, zeros], axis=0)
    ends = segments.reshape(count, QUERIES)
    start = jnp.sum(segments[None, :] < ends[:, :1], axis=1)
    stop = jnp.sum(segments[None, :] <= ends[:, -1:], axis=1)
    first = start // LANES
    kind = (stop - first * LANES + STEP - 1) // STEP
    first = jnp.minimum(first, (length - kind * STEP) // LANES)
    size = max(count, order.shape[0], places.shape[0])
    pad = lambda a: jnp.pad(a.astype(jnp.int32), (0, size - a.shape[0]))
    tables = jnp.stack([pad(order), pad(first), pad(kind), pad(places)])
    return tables, cosine, sine, seg_row, seg_wide, feature, coef, hot_rows


def ffn_kernel(row_parts, flipped, which, *refs):
    rows, refs = refs[:row_parts], refs[row_parts:]
    near, refs = refs[:row_parts], refs[row_parts:]
    far, refs = refs[:row_parts], refs[row_parts:]
    weight, act_out, d_both_out, keep_out, rest_out, send_own, send_rest, grads, sems = refs
    part = rows[0].shape[0]
    share = part // 2
    cols = act_out.shape[1]
    half = row_parts // 2
    copies = []
    for p in range(row_parts):
        pair = (far[p], near[p]) if flipped else (near[p], far[p])
        for k in range(2):
            copy = pltpu.make_async_copy(pair[k].at[which[0]], grads.at[p, pl.ds(k * share, share)], sems.at[p, k])
            copy.start()
            copies.append(copy)
    for p in list(range(half, row_parts)) + list(range(half)):
        at = slice(p * part, (p + 1) * part)
        both = nn_dot(rows[p][...], weight[:, : 2 * cols])
        copies[2 * p].wait()
        copies[2 * p + 1].wait()
        d_act = nn_dot(grads[p], weight[:, 2 * cols :])
        gate, up = both[:, :cols], both[:, cols:]
        sig = 1.0 / (1.0 + jnp.exp(-gate))
        silu = gate * sig
        act_out[at, :] = (silu * up).astype(BF16)
        d_both_out[at, :cols] = (d_act * up * (sig + silu * (1.0 - sig))).astype(BF16)
        d_both_out[at, cols:] = (d_act * silu).astype(BF16)
        back = nt_dot(d_both_out[at, :], weight[:, : 2 * cols])
        if p == 0:
            keep_out[...] = back
        elif p < half:
            rest_out[(p - 1) * part : p * part, :] = back
        else:
            if p == half:
                send_own[...] = back.astype(BF16)
            else:
                send_rest[(p - half - 1) * part : (p - half) * part, :] = back.astype(BF16)


def ffn_middle(flipped, which, rows, near, far, weight, behind=()):
    part, width = rows[0].shape
    count = len(rows)
    length = part * count
    cols = weight.shape[1] // 3
    operands = (which, *rows, *near, *far, weight)
    return pl.pallas_call(
        without(functools.partial(ffn_kernel, count, flipped), len(operands), len(behind)),
        out_shape=(
            jax.ShapeDtypeStruct((length, cols), BF16),
            jax.ShapeDtypeStruct((length, 2 * cols), BF16),
            jax.ShapeDtypeStruct((part, width), F32),
            jax.ShapeDtypeStruct((length // 2 - part, width), F32),
            jax.ShapeDtypeStruct((part, width), BF16),
            jax.ShapeDtypeStruct((length // 2 - part, width), BF16),
        ),
        in_specs=[smem()] + [vmem()] * count + [anywhere()] * (2 * count) + [vmem()] + [anywhere()] * len(behind),
        out_specs=[vmem()] * 6,
        scratch_shapes=[pltpu.VMEM((count, part, width), BF16), pltpu.SemaphoreType.DMA((count, 2))],
        compiler_params=pltpu.CompilerParams(vmem_limit_bytes=VMEM_LIMIT),
        cost_estimate=pl.CostEstimate(
            flops=10 * length * width * cols, bytes_accessed=16 << 20, transcendentals=length * cols
        ),
        name="ffn_middle",
    )(*operands, *behind)


def ffn_tail_kernel(row_parts, which, *refs):
    own, refs = refs[:row_parts], refs[row_parts:]
    other, refs = refs[:row_parts], refs[row_parts:]
    near, refs = refs[:row_parts], refs[row_parts:]
    far, refs = refs[:row_parts], refs[row_parts:]
    acts, boths, weight, refs = refs[:2], refs[2:4], refs[4], refs[5:]
    outs, grad_out, refs = refs[:8], refs[8], refs[9:]
    down_buf, act_buf, both_buf, grad_buf, row_buf, total, keeps, rests, twins, twin_rests = refs[:10]
    in_sems, grad_sems, row_sems, out_sems, total_sems = refs[10:]
    part, width = own[0].shape
    share = part // 2
    length = part * row_parts
    cols = acts[0].shape[1]
    half = length // 2

    def begin(source, target, sem):
        copy = pltpu.make_async_copy(source, target, sem)
        copy.start()
        return copy

    down_copy = begin(weight.at[:, pl.ds(2 * cols, cols)], down_buf, in_sems.at[0])
    act_copies = [begin(acts[seq], act_buf.at[seq], in_sems.at[1 + seq]) for seq in range(2)]
    grad_copies = []
    for seq in range(2):
        now = which[0] if seq == 0 else 1 - which[0]
        for p in range(row_parts):
            pair = (near[p], far[p]) if seq == 0 else (far[p], near[p])
            for k in range(2):
                to = grad_buf.at[seq, pl.ds(p * part + k * share, share)]
                grad_copies.append(begin(pair[k].at[now], to, grad_sems.at[seq, p, k]))
    row_copies = [
        begin((own, other)[seq][p], row_buf.at[seq, pl.ds(p * part, part)], row_sems.at[seq, p])
        for seq in range(2)
        for p in range(row_parts)
    ]
    both_copies = [begin(boths[seq], both_buf.at[seq], in_sems.at[3 + seq]) for seq in range(2)]
    down_copy.wait()
    out_copies = []
    for seq in range(2):
        act_copies[seq].wait()
        mine = nt_dot(act_buf[seq, :half, :], down_buf[...])
        keeps[seq] = mine[:part]
        rests[seq] = mine[part:]
        mine = nt_dot(act_buf[seq, half:, :], down_buf[...]).astype(BF16)
        twins[seq] = mine[:part]
        twin_rests[seq] = mine[part:]
        for k, buf in enumerate((keeps, rests, twins, twin_rests)):
            out_copies.append(begin(buf.at[seq], outs[4 * seq + k], out_sems.at[seq, k]))
    step = width // 4
    total_copies = []
    for what in range(2):
        for seq in range(2):
            for p in range(row_parts):
                if what == 0:
                    grad_copies[2 * (seq * row_parts + p)].wait()
                    grad_copies[2 * (seq * row_parts + p) + 1].wait()
                else:
                    row_copies[seq * row_parts + p].wait()
        if what == 1:
            both_copies[0].wait()
            both_copies[1].wait()
        right, source = (act_buf, both_buf)[what], (grad_buf, row_buf)[what]
        first, size = (2 * cols, cols) if what == 0 else (0, 2 * cols)
        for k in range(4):
            at = slice(k * step, (k + 1) * step)
            value = sum(tn_dot(source[seq, :, at], right[seq]) for seq in range(2))
            total[at, first : first + size] = value.astype(BF16)
            if what == 1:
                rows = pl.ds(k * step, step)
                total_copies.append(begin(total.at[rows], grad_out.at[rows], total_sems.at[k]))
    for copy in out_copies + total_copies:
        copy.wait()


def ffn_tail(which, own, other, near, far, act_own, act_other, d_own, d_other, weight):
    part, width = own[0].shape
    count = len(own)
    length = part * count
    cols = act_own.shape[1]
    rest = length // 2 - part
    shapes = (
        jax.ShapeDtypeStruct((part, width), F32),
        jax.ShapeDtypeStruct((rest, width), F32),
        jax.ShapeDtypeStruct((part, width), BF16),
        jax.ShapeDtypeStruct((rest, width), BF16),
    )
    made = pl.pallas_call(
        functools.partial(ffn_tail_kernel, count),
        out_shape=shapes * 2 + (jax.ShapeDtypeStruct((width, 3 * cols), BF16),),
        in_specs=[smem()] + [anywhere()] * (4 * count + 5),
        out_specs=[anywhere()] * 8 + [pl.BlockSpec(memory_space=pltpu.HBM)],
        scratch_shapes=[
            pltpu.VMEM((width, cols), BF16),
            pltpu.VMEM((2, length, cols), BF16),
            pltpu.VMEM((2, length, 2 * cols), BF16),
            pltpu.VMEM((2, length, width), BF16),
            pltpu.VMEM((2, length, width), BF16),
            pltpu.VMEM((width, 3 * cols), BF16),
            pltpu.VMEM((2, part, width), F32),
            pltpu.VMEM((2, rest, width), F32),
            pltpu.VMEM((2, part, width), BF16),
            pltpu.VMEM((2, rest, width), BF16),
            pltpu.SemaphoreType.DMA((5,)),
            pltpu.SemaphoreType.DMA((2, count, 2)),
            pltpu.SemaphoreType.DMA((2, count)),
            pltpu.SemaphoreType.DMA((2, 4)),
            pltpu.SemaphoreType.DMA((4,)),
        ],
        compiler_params=pltpu.CompilerParams(vmem_limit_bytes=WIDE_LIMIT),
        name="ffn_tail",
    )(which, *own, *other, *near, *far, act_own, act_other, d_own, d_other, weight)
    return made[8], made[:8]


def without(kernel, start, count):
    return lambda *refs: kernel(*refs[:start], *refs[start + count :])


def rows_call(kernel, name, shapes, *operands, scalars=(), behind=(), limit=ROWS_LIMIT):
    single = not isinstance(shapes, (list, tuple))
    count = len(scalars) + len(operands)
    return pl.pallas_call(
        without(kernel, count, len(behind)),
        out_shape=shapes,
        in_specs=[smem()] * len(scalars) + [vmem()] * len(operands) + [anywhere()] * len(behind),
        out_specs=vmem() if single else [vmem()] * len(shapes),
        compiler_params=pltpu.CompilerParams(vmem_limit_bytes=limit),
        cost_estimate=pl.CostEstimate(
            flops=16 * operands[0].size, bytes_accessed=sum(o.size * o.dtype.itemsize for o in operands), transcendentals=0
        ),
        name=name,
    )(*scalars, *operands, *behind)


def pack_kernel(which, rows, query, key, value, out, gate, up, down, own, mine, packed):
    block, start = own.shape[0], 0
    for ref in (query, key, value, out):
        stop = start + ref.shape[1]
        own[:, start:stop] = ref[...]
        packed[:block, start:stop] = ref[...]
        start = stop
    width = rows.shape[2]
    packed[: rows.shape[1], start : start + width] = rows[1 - which[0]]
    start += width
    cols = gate.shape[1] // 2
    for k, ref in enumerate((gate, up, down)):
        for half in range(2):

            @pl.when(which[0] == half)
            def _(ref=ref, half=half, k=k):
                mine[:, k * cols : (k + 1) * cols] = ref[:, half * cols : (half + 1) * cols]
                packed[:block, start + k * cols : start + (k + 1) * cols] = ref[:, (1 - half) * cols : (2 - half) * cols]


def stack_kernel(start, which, mine, theirs, out):
    block, width = mine.shape
    first = pl.multiple_of(which[0] * block, block)
    second = pl.multiple_of((1 - which[0]) * block, block)
    out[pl.ds(first, block), :] = mine[...]
    out[pl.ds(second, block), :] = theirs[:block, start : start + width]


def gains_kernel(place, gain_rows, gain, d_gain_two, bias_parts, out):
    blocks, _, block = gain_rows.shape
    for k in range(blocks):
        at = slice(k * block, (k + 1) * block)
        out[0:1, at] = gain_rows[k, 0:1, :] / gain[:, at].astype(F32)
    out[1:2, :] = d_gain_two[...]
    out[2:, :] = jnp.zeros(out[2:, :].shape, F32)
    lane = lane_of((1, LANES))
    lanes = pl.ds(pl.multiple_of(place[0] * LANES, LANES), LANES)
    for row in range(2):
        line = jnp.zeros((1, LANES), F32)
        for head in range(bias_parts.shape[0]):
            line = jnp.where(lane == head, jnp.sum(bias_parts[head, 8 * row : 8 * row + 8, :]), line)
        out[2 + row : 3 + row, lanes] = line


def ride_kernel(totals, twin, *refs):
    lows, (own, *outs) = refs[: len(refs) // 2], refs[len(refs) // 2 :]
    total = totals[...] + twin[...]
    own[...] = total
    high = total.astype(BF16).astype(F32)
    parts = (high, total - high)
    block, cols = lows[0].shape
    for low, out in zip(lows, outs):
        out[:block, :] = low[...]
        row = block
        for part in parts:
            for c in range(part.shape[1] // cols):
                out[row : row + part.shape[0], :] = part[:, c * cols : (c + 1) * cols].astype(BF16)
                row += part.shape[0]


def arrive_kernel(own, totals, *refs):
    arrived, (grad, total) = refs[:-2], refs[-2:]
    block, cols = own.shape
    rows, width = totals.shape
    value = own[...]
    sums = [totals[:, c * cols : (c + 1) * cols] for c in range(width // cols)]
    for ref in arrived:
        value = value + ref[:block, :].astype(F32)
        for k in range(2 * len(sums)):
            at = block + k * rows
            sums[k % len(sums)] = sums[k % len(sums)] + ref[at : at + rows, :].astype(F32)
    grad[...] = value
    for c, part in enumerate(sums):
        total[:, c * cols : (c + 1) * cols] = part


def gains_finish_kernel(place, mine, *refs):
    theirs, (one, two, bias) = refs[:-3], refs[-3:]
    lanes = pl.ds(pl.multiple_of(place[0] * LANES, LANES), LANES)
    total, line = mine[...], mine[:, lanes]
    for ref in theirs:
        total = total + ref[...]
        line = line + ref[:, lanes]
    one[...] = total[0:1]
    two[...] = total[1:2]
    bias[...] = line[2:4, : bias.shape[1]]


def widen_kernel(angles, cosine, sine):
    half = angles.shape[1] // 2
    cos_half, sin_half = angles[:, :half], angles[:, half:]
    cosine[...] = jnp.concatenate([cos_half] * (LANES // half), axis=1)
    sine[...] = jnp.concatenate([-sin_half, sin_half] * (LANES // half // 2), axis=1)


def pair_kernel(*refs):
    blocks = (len(refs) - 1) // 2
    keeps, other, outs = refs[:blocks], refs[blocks], refs[blocks + 1 :]
    rows = keeps[0].shape[0]
    for k in range(blocks):
        total = keeps[k][...].astype(F32) + other[k * rows : (k + 1) * rows, :].astype(F32)
        outs[k][...] = total.astype(outs[k].dtype)


def finish_kernel(count, own, *refs):
    total = own[...]
    for ref in refs[:-count]:
        total = total + ref[...].astype(F32)
    start = 0
    for out in refs[-count:]:
        stop = start + out.shape[1]
        out[...] = total[:, start:stop]
        start = stop


def pair_sums(partials, other):
    shape = partials[0].shape
    blocks = len(partials) - 1
    shapes = [jax.ShapeDtypeStruct(shape, F32 if k == 0 else BF16) for k in range(blocks)]
    return rows_call(pair_kernel, "pair_sums", shapes, *partials[:-1], other)


def weight_sums(own, arrived, pieces):
    outs = [jax.ShapeDtypeStruct((own.shape[0], own.shape[1] // pieces), F32)] * pieces
    return rows_call(functools.partial(finish_kernel, pieces), "weight_sums", outs, own, *arrived)


def last_kernel(start, count, which, grads, crossed, near, own, *refs):
    arrived, (gate, up, down, rows_out), outs = refs[:count], refs[count : count + 4], refs[count + 4 :]
    cols = grads.shape[1] // 3
    rows = grads.shape[0] // 2
    mine = grads[pl.ds(pl.multiple_of(which[0] * rows, rows), rows), :].astype(F32)
    theirs = crossed[:rows, start:].astype(F32)
    for half in range(2):

        @pl.when(which[0] == half)
        def _(half=half):
            for k, out in enumerate((gate, up, down)):
                out[:, half * cols : (half + 1) * cols] = mine[:, k * cols : (k + 1) * cols]
                out[:, (1 - half) * cols : (2 - half) * cols] = theirs[:, k * cols : (k + 1) * cols]

    stack_kernel(0, which, near, crossed, rows_out)
    finish_kernel(len(outs), own, *arrived, *outs)


def quadrant(own, other, flip):
    share = own.shape[0] // 2
    return jnp.concatenate(
        [own[flip * share : (flip + 1) * share], other[(1 - flip) * share : (2 - flip) * share]], axis=0
    )


def out_split_kernel(hidden, keep, rest, twin, twin_rest, keep_next, rest_next, twin_next, twin_rest_next, *outs):
    first, cross, chips, chips_cross = outs
    part = hidden.shape[0]
    own = keep[...] + twin[...].astype(F32) + hidden[...]
    other = keep_next[...] + twin_next[...].astype(F32)
    first[...] = quadrant(own, other, 0)
    cross[...] = quadrant(own, other, 1).astype(BF16)
    own = rest[...] + twin_rest[...].astype(F32)
    other = rest_next[...] + twin_rest_next[...].astype(F32)
    for k in range(rest.shape[0] // part):
        at = slice(k * part, (k + 1) * part)
        chips[at, :] = quadrant(own[at], other[at], 0)
        chips_cross[at, :] = quadrant(own[at], other[at], 1).astype(BF16)


def swapped(values):
    half = values.shape[0] // 2
    return jnp.concatenate([values[half:], values[:half]], axis=0)


def add_kernel(part, values, arrived, out):
    for k in range(values.shape[0] // part):
        at = slice(k * part, (k + 1) * part)
        out[at, :] = (values[at, :] + swapped(arrived[at, :].astype(F32))).astype(BF16)


def out_finish_kernel(which, first, cross, *refs):
    arrived, out = refs[:-1], refs[-1]
    share = out.shape[1]
    total = first[...] + swapped(cross[...].astype(F32))
    for ref in arrived:
        total = total + ref[...].astype(F32)
    total = total.astype(BF16)
    out[pl.ds(which[0], 1)] = total[None, :share]
    out[pl.ds(1 - which[0], 1)] = total[None, share:]


def inverse_rms(values):
    return lax.rsqrt(jnp.mean(values * values, axis=-1, keepdims=True) + EPS)


def both_halves(start, rows, packed, which):
    share, width = rows.shape[1:]
    return jnp.concatenate([rows[which[0]], packed[:share, start : start + width]], axis=0).astype(F32)


def rows_sum(keep, twin, arrived):
    total = keep[...] + twin[...].astype(F32)
    for ref in arrived:
        total = total + ref[...].astype(F32)
    return total


def norm_kernel(start, which, rows, far, gain, out, far_attn):
    far_attn[...] = far[: far_attn.shape[0], :start]
    values = both_halves(start, rows, far, which)
    out[...] = (values * inverse_rms(values) * gain[...].astype(F32)).astype(BF16)


def rest_kernel(rest, twin, out):
    out[...] = (rest[...] + twin[...].astype(F32)).astype(BF16)


def sum_kernel(keep, twin, *refs):
    refs[-1][...] = rows_sum(keep, twin, refs[:-1]).astype(BF16)


def middle_kernel(start, which, rows, far, gain, keep, twin, *refs):
    arrived, (hidden, out) = refs[:-2], refs[-2:]
    values = both_halves(start, rows, far, which) + rows_sum(keep, twin, arrived)
    hidden[...] = values
    out[...] = (values * inverse_rms(values) * gain[...].astype(F32)).astype(BF16)


def pull_norm(values, gain, grad):
    inv = inverse_rms(values)
    scaled = grad * gain
    normed = values * inv
    d_values = inv * (scaled - normed * jnp.mean(scaled * normed, axis=-1, keepdims=True))
    return d_values, jnp.sum(grad * normed, axis=0, keepdims=True)


def back_two_kernel(which, hidden, near, far, gain, across, keep, twin, *refs):
    arrived, (d_hidden, low, d_gain) = refs[:-3], refs[-3:]
    grad = rows_sum(keep, twin, arrived) + across[...].astype(F32)
    d_values, d_gain[...] = pull_norm(hidden[...], gain[...].astype(F32), grad)
    total = jnp.concatenate([near[which[0]], far[which[0]]], axis=0).astype(F32) + d_values
    d_hidden[...] = total
    low[...] = total.astype(BF16)


def back_one_kernel(start, which, rows, far, gain, d_hidden, ffn_grad, keep, twin, *refs):
    arrived, (first, packed) = refs[:-2], refs[-2:]
    grad = rows_sum(keep, twin, arrived)
    d_values, _ = pull_norm(both_halves(start, rows, far, which), gain[...].astype(F32), grad)
    total = (d_hidden[...] + d_values).astype(BF16)
    share, width = first.shape
    first[...] = total[:share]
    packed[:share, :width] = total[share:]
    block = ffn_grad.shape[0] // 2
    packed[:block, width:] = ffn_grad[pl.ds(pl.multiple_of((1 - which[0]) * block, block), block), :]


def grad_kernel(row_parts, blocks, tables, *refs):
    rows, refs = refs[:row_parts], refs[row_parts:]
    right, refs = refs[0], refs[1:]
    keeps, send, left = refs[:blocks], refs[blocks], refs[blocks + 1]
    block = keeps[0].shape[0]
    left_of(rows, right, left)
    for s in range(2 * blocks):
        at = pl.ds(pl.multiple_of(tables[3, s] * block, block), block)
        total = left[at, :].astype(BF16)
        if s < blocks:
            keeps[s][...] = total
        else:
            send[(s - blocks) * block : (s - blocks + 1) * block, :] = total


def weight_partials(tables, rows, right, blocks):
    part, width = rows[0].shape
    length, cols = right.shape
    block = width // (2 * blocks)
    return pl.pallas_call(
        functools.partial(grad_kernel, len(rows), blocks),
        out_shape=(jax.ShapeDtypeStruct((block, cols), BF16),) * blocks
        + (jax.ShapeDtypeStruct((width // 2, cols), BF16),),
        in_specs=[smem()] + [vmem()] * (len(rows) + 1),
        out_specs=[vmem()] * (blocks + 1),
        scratch_shapes=[pltpu.VMEM((width, cols), F32)],
        compiler_params=pltpu.CompilerParams(vmem_limit_bytes=VMEM_LIMIT),
        cost_estimate=pl.CostEstimate(
            flops=2 * length * width * cols, bytes_accessed=8 << 20, transcendentals=0
        ),
        name="weight_partials",
    )(tables, *rows, right)


def left_of(rows, right, total):
    part, width = rows[0].shape
    step = 2 * LANES
    for c in range(width // step):
        at = slice(c * step, (c + 1) * step)
        total[at, :] = sum(tn_dot(ref[:, at], right[p * part : (p + 1) * part, :]) for p, ref in enumerate(rows))


def send_kernel(row_parts, blocks, tables, *refs):
    rows, (right, send, left) = refs[:row_parts], refs[row_parts:]
    block = send.shape[0] // blocks
    left_of(rows, right, left)
    for s in range(blocks):
        at = pl.ds(pl.multiple_of(tables[3, blocks + s] * block, block), block)
        send[s * block : (s + 1) * block, :] = left[at, :].astype(BF16)


def keep_kernel(row_parts, blocks, tables, *refs):
    weights, refs = refs[: 2 * blocks], refs[2 * blocks :]
    rows, right, refs = refs[:row_parts], refs[row_parts], refs[row_parts + 1 :]
    keeps, (gain_row, left) = refs[:blocks], refs[blocks:]
    block = keeps[0].shape[0]
    cols = right.shape[1]
    left_of(rows, right, left)
    for s in range(2 * blocks):
        at = pl.ds(pl.multiple_of(tables[3, s] * block, block), block)
        total = left[at, :]
        product = total * weights[s][:block, :cols].astype(F32)
        product = sum(product[:, c * LANES : (c + 1) * LANES] for c in range(cols // LANES))
        high = product.astype(BF16)
        rest = (product - high.astype(F32)).astype(BF16)
        ones = jnp.ones((8, LANES), BF16)
        gain_row[pl.ds(tables[3, s], 1)] = (nt_dot(ones, high) + nt_dot(ones, rest))[None]
        if s < blocks:
            keeps[s][...] = total.astype(BF16)


def qkv_call(kernel, name, shapes, tables, operands, scratch):
    single = not isinstance(shapes, tuple)
    return pl.pallas_call(
        kernel,
        out_shape=shapes,
        in_specs=[smem()] + [vmem()] * len(operands),
        out_specs=vmem() if single else [vmem()] * len(shapes),
        scratch_shapes=[pltpu.VMEM(scratch, F32)],
        compiler_params=pltpu.CompilerParams(vmem_limit_bytes=VMEM_LIMIT),
        name=name,
    )(tables, *operands)


def qkv_partials(tables, weights, rows, right, blocks):
    part, width = rows[0].shape
    length, cols = right.shape
    block = width // (2 * blocks)
    send = qkv_call(
        functools.partial(send_kernel, len(rows), blocks),
        "qkv_send",
        jax.ShapeDtypeStruct((width // 2, cols), BF16),
        tables,
        [*rows, right],
        (width, cols),
    )
    keeps = qkv_call(
        functools.partial(keep_kernel, len(rows), blocks),
        "qkv_keep",
        (jax.ShapeDtypeStruct((block, cols), BF16),) * blocks + (jax.ShapeDtypeStruct((2 * blocks, 8, block), F32),),
        tables,
        [*weights, *rows, right],
        (width, cols),
    )
    return keeps[:-1], send, keeps[-1]


def hop(values, axis, flip):
    size = lax.axis_size(axis)
    return lax.ppermute(values, axis, [(i, i ^ flip) for i in range(size)])


def swap_blocks(values, axis, index, size):
    shape = values.shape
    bit = 1
    while bit < size:
        split = shape[:axis] + (size // (2 * bit), 2, bit) + shape[axis + 1 :]
        cut = values.reshape(split)
        cut = jnp.where((index & bit) != 0, jnp.flip(cut, axis + 1), cut)
        values = cut.reshape(shape)
        bit *= 2
    return values


def gather_chips(block):
    nt = lax.axis_size("tp")
    return [block] + [hop(block, "tp", 2 * k) for k in range(1, nt // 2)]


def with_twins(blocks):
    return blocks + [hop(block, "tp", 1) for block in blocks]


def gather_rows(block):
    return with_twins(gather_chips(block))


def region(ready, run):
    shapes = jax.eval_shape(run)
    return lax.cond(ready, run, lambda: jax.tree.map(lambda a: jnp.zeros(a.shape, a.dtype), shapes))


def chips_low(rest, twin, *behind):
    return rows_call(
        rest_kernel, "rest_rows", jax.ShapeDtypeStruct(rest.shape, BF16), rest, twin, behind=behind
    )


def chips_hop(low, nt):
    if nt == 4:
        return [hop(low, "tp", 2)]
    rows = low.shape[0] // (nt // 2 - 1)
    return [hop(low[(k - 1) * rows : k * rows], "tp", 2 * k) for k in range(1, nt // 2)]


def shards(
    layer_in,
    attn_gain,
    ffn_gain,
    query_weight,
    key_weight,
    value_weight,
    out_weight,
    variate_bias,
    gate_weight,
    up_weight,
    down_weight,
    segment_ids,
    variate_ids,
    time_ids,
    out_grad,
):
    seq_count, share, width = layer_in.shape
    nz, nx, nt = lax.axis_size("fsdp"), lax.axis_size("ctx"), lax.axis_size("tp")
    iz, ix, it = lax.axis_index("fsdp"), lax.axis_index("ctx"), lax.axis_index("tp")
    assert nx == 2 and seq_count == nx
    length = segment_ids.shape[1]
    heads = variate_bias.shape[1]
    proj = heads * HEAD

    def pick(table, which):
        return lax.dynamic_index_in_dim(table, which, 0, keepdims=False)

    def swap(mine, theirs):
        return jnp.where(ix == 0, mine, theirs), jnp.where(ix == 0, theirs, mine)

    gain_one, gain_two = attn_gain[None], ffn_gain[None]
    part = nx * share
    low_rows = jax.ShapeDtypeStruct((part, width), BF16)
    wide_rows = jax.ShapeDtypeStruct((part, width), F32)
    gain_row = jax.ShapeDtypeStruct((1, width), F32)
    half_rows = jax.ShapeDtypeStruct((share, width), BF16)
    which = ix.astype(jnp.int32).reshape(1)
    ready = ix >= 0
    cols = gate_weight.shape[1] // 2
    grad_own = out_grad
    block = query_weight.shape[0]
    attn_shape = jax.ShapeDtypeStruct((block, 4 * proj), BF16)
    packed_shape = jax.ShapeDtypeStruct((max(block, share), 4 * proj + width + 3 * cols), BF16)
    ffn_shape = jax.ShapeDtypeStruct((gate_weight.shape[0], 3 * cols), BF16)
    attn_own, mine, packed = rows_call(
        pack_kernel, "pack_weights", (attn_shape, ffn_shape, packed_shape), layer_in, query_weight, key_weight,
        value_weight, out_weight, gate_weight, up_weight, down_weight, scalars=(which,), limit=WIDE_LIMIT,
    )
    start = 4 * proj

    def twin(block):
        return hop(block, "tp", 1)

    def across(block):
        return hop(block, "ctx", 1)

    def first_transfers():
        attn_z = [hop(attn_own, "fsdp", k) for k in range(1, nz)]
        far = across(packed)
        grad_y = gather_chips(grad_own)[1:]
        order = jnp.arange(nx * nt).reshape(nx, nt // 2, 2)
        order = swap_blocks(swap_blocks(swap_blocks(order, 0, ix, nx), 1, it // 2, nt // 2), 2, it % 2, 2)
        order = order.transpose(2, 1, 0).reshape(nx * nt)
        places = jnp.arange(nz * nx).reshape(nz, nx)
        places = swap_blocks(swap_blocks(places, 0, iz, nz), 1, ix, nx).transpose(1, 0).reshape(nz * nx)
        tables = attention_tables(
            pick(segment_ids, ix), pick(variate_ids, ix), pick(time_ids, ix), variate_bias, order, places
        )
        return attn_z, far, grad_y, tables

    attn_z, far, grad_y, made = region(ready, first_transfers)
    tables, cosine, sine, seg_row, seg_wide, feature, coef, hot_rows = made
    stack_shape = jax.ShapeDtypeStruct((2 * block, 3 * cols), BF16)
    ffn_w = rows_call(
        functools.partial(stack_kernel, start + width), "stack_weights", stack_shape, mine, far, scalars=(which,)
    )
    ffn_w = lax.all_gather(ffn_w, "fsdp", axis=0, tiled=True)

    rows_own, far_attn = rows_call(
        functools.partial(norm_kernel, start), "norm_rows", (low_rows, attn_shape), layer_in, far, gain_one,
        scalars=(which,),
    )

    def gather_one():
        rest = [hop(far_attn, "fsdp", 1)] + [across(piece) for piece in attn_z[1:]]
        return gather_chips(rows_own)[1:], rest

    chips, rest_x = region(ready, gather_one)
    chips_one = [rows_own] + chips
    attn_w = [attn_own] + attn_z + [far] + rest_x

    def attend():
        twins = [twin(rows) for rows in chips_one]
        near_twins = [twin(rows) for rows in [grad_own] + grad_y]
        return across(grad_own), near_twins, twins, attention_forward(
            tables, chips_one + twins, attn_w, cosine, sine, seg_row, seg_wide, feature, coef, heads
        )

    grad_far, near_twins, twins, (q_aug, k_aug, v_rows, mixed, lse, keep, rest, send, send_rest) = region(ready, attend)

    def scatter_attn():
        low = chips_low(rest, twin(send_rest))
        return chips_hop(low, nt), twin(send), [across(piece) for piece in grad_y], twin(grad_far)

    rows_one = chips_one + twins
    chips, twins, grad_far_y, far_twin = region(ready, scatter_attn)
    grad_near, grad_far = [grad_own] + grad_y, [grad_far] + grad_far_y
    hidden, rows_two = rows_call(
        functools.partial(middle_kernel, start), "middle_rows", (wide_rows, low_rows), layer_in, far, gain_two, keep,
        twins, *chips, scalars=(which,),
    )

    def gather_two():
        return (
            gather_chips(rows_two)[1:],
            across(rows_two),
            [twin(rows) for rows in grad_far[1:]],
            twin(rows_two),
        )

    chips_two, next_own, far_twins, rows_twin = region(ready, gather_two)
    grad_near, grad_far = grad_near + near_twins, grad_far + [far_twin] + far_twins

    def ffn_own():
        twins = [twin(rows) for rows in chips_two]
        return [across(rows) for rows in chips_two], twins, ffn_middle(
            False, which, [rows_two] + chips_two + [rows_twin] + twins, grad_near, grad_far, ffn_w
        )

    next_y, twins, (act, d_both, keep, rest, send, send_rest) = region(ready, ffn_own)

    rows_two = [rows_two] + chips_two + [rows_twin] + twins
    rows_next = [next_own] + next_y

    def ffn_next():
        low = chips_low(rest, twin(send_rest))
        twins = [twin(rows) for rows in rows_next]
        return chips_hop(low, nt), twin(send), twins, ffn_middle(
            True, 1 - which, rows_next + twins, grad_near, grad_far, ffn_w
        )

    chips, twins, next_twins, made = region(ready, ffn_next)
    rows_next = rows_next + next_twins
    act_next, d_both_next, keep_next, rest_next, send_next, send_rest = made
    low_next = chips_low(rest_next, twin(send_rest))

    def scatter_next():
        return (
            chips_hop(low_next, nt),
            twin(send_next),
            ffn_tail(which, rows_two, rows_next, grad_near, grad_far, act, act_next, d_both, d_both_next, ffn_w),
        )

    chips_next, twins_next, (ffn_grad, parts) = region(ready, scatter_next)
    low_across = rows_call(sum_kernel, "sum_rows", low_rows, keep_next, twins_next, *chips_next)

    def cross_next():
        out_twins = [twin(parts[k]) for k in (2, 3, 6, 7)]
        rest_shape = (parts[1].shape[0], width)
        shapes = (
            wide_rows,
            low_rows,
            jax.ShapeDtypeStruct(rest_shape, F32),
            jax.ShapeDtypeStruct(rest_shape, BF16),
        )
        return across(low_across), rows_call(
            out_split_kernel, "out_split", shapes, hidden, parts[0], parts[1], out_twins[0], out_twins[1], parts[4],
            parts[5], out_twins[2], out_twins[3],
        )

    arrived, (out_first, out_cross, out_chips, out_chips_cross) = region(ready, cross_next)
    ffn_grad = lax.psum_scatter(ffn_grad, "fsdp", scatter_dimension=0, tiled=True)
    d_hidden, low, d_gain_two = rows_call(
        back_two_kernel,
        "back_two",
        (wide_rows, low_rows, gain_row),
        hidden,
        grad_near[0],
        grad_far[0],
        gain_two,
        arrived,
        keep,
        twins,
        *chips,
        scalars=(which,),
    )

    def gather_back():
        return gather_chips(low)[1:], twin(low), across(out_chips_cross)

    chips_back, twin_back, out_arrived = region(ready, gather_back)
    def attend_back():
        rows = [low] + chips_back + [twin_back] + [twin(rows) for rows in chips_back]
        cross = across(out_cross)
        low_shape = jax.ShapeDtypeStruct(out_chips.shape, BF16)
        low_out = rows_call(functools.partial(add_kernel, part), "add_rows", low_shape, out_chips, out_arrived)
        grads = weight_partials(tables, rows, mixed, nz)
        return chips_hop(low_out, nt), cross, across(grads[-1]), grads, attention_backward(
            tables, rows, attn_w, q_aug, k_aug, v_rows, lse, cosine, sine, seg_row, seg_wide, hot_rows, heads
        )

    out_arrived, out_cross, out_other, out_grads, made = region(ready, attend_back)
    keep, rest, send, send_rest, d_qkv, bias_parts = made

    place = it.astype(jnp.int32).reshape(1)
    gain_shape = jax.ShapeDtypeStruct((8, width), F32)

    def scatter_one():
        twins = twin(send)
        low = chips_low(rest, twin(send_rest), twins)
        keeps, sent, gain_rows = qkv_partials(tables, attn_w, rows_one, d_qkv, nz)
        sums = pair_sums(out_grads, out_other)
        totals = rows_call(
            gains_kernel, "gain_rows", gain_shape, gain_rows, gain_one, d_gain_two, bias_parts, scalars=(place,)
        )
        lows = sums[1:]
        ride_shape = jax.ShapeDtypeStruct((block + 16 * (width // proj), proj), BF16)
        totals, *lows = rows_call(
            ride_kernel, "ride_rows", [gain_shape] + [ride_shape] * len(lows), totals, twin(totals), *lows
        )
        arrived = [hop(low_out, "fsdp", 1 + k) for k, low_out in enumerate(lows)]
        out_weight_grad, totals = rows_call(
            arrive_kernel, "out_sums", (jax.ShapeDtypeStruct((block, proj), F32), gain_shape), sums[0], totals, *arrived
        )
        totals = totals + across(totals)
        return chips_hop(low, nt), twins, keeps, across(sent), out_weight_grad, totals

    chips, twins, qkv_keeps, qkv_other, out_weight_grad, totals = region(ready, scatter_one)
    packed_shape = jax.ShapeDtypeStruct((max(block, share), width + 3 * cols), BF16)
    d_near, packed = rows_call(
        functools.partial(back_one_kernel, start), "back_one", (half_rows, packed_shape), layer_in, far, gain_one, d_hidden,
        ffn_grad, keep, twins, *chips, scalars=(which,),
    )
    qkv_sums = pair_sums([*qkv_keeps, None], qkv_other)

    def last_transfers():
        arrived = [hop(piece, "fsdp", k) for k, piece in enumerate(qkv_sums) if k > 0]
        layer_out = rows_call(
            out_finish_kernel, "layer_out", jax.ShapeDtypeStruct(layer_in.shape, BF16), out_first, out_cross,
            *out_arrived, scalars=(which,),
        )
        summed = rows_call(
            gains_finish_kernel, "gain_sums", (gain_row, gain_row, jax.ShapeDtypeStruct((2, heads), F32)), totals,
            *[hop(totals, "tp", 2 * k) for k in range(1, nt // 2)], scalars=(place,),
        )
        return arrived, across(packed), summed, layer_out

    arrived, crossed, summed, layer_out = region(ready, last_transfers)
    attn_gain_grad, ffn_gain_grad, bias_grad = summed
    weight_shape = jax.ShapeDtypeStruct(gate_weight.shape, F32)
    in_shape = jax.ShapeDtypeStruct((nx * share, width), BF16)
    head_shape = jax.ShapeDtypeStruct(query_weight.shape, F32)
    gate_grad, up_grad, down_grad, in_grad, query_grad, key_grad, value_grad = rows_call(
        functools.partial(last_kernel, width, len(arrived)), "last_sums",
        [weight_shape] * 3 + [in_shape] + [head_shape] * 3,
        ffn_grad, crossed, d_near, qkv_sums[0], *arrived, scalars=(which,), limit=WIDE_LIMIT,
    )
    in_grad = in_grad.reshape(layer_in.shape)
    return (
        layer_out,
        in_grad,
        attn_gain_grad.reshape(width),
        ffn_gain_grad.reshape(width),
        query_grad,
        key_grad,
        value_grad,
        out_weight_grad,
        bias_grad,
        gate_grad,
        up_grad,
        down_grad,
    )


def solution(mesh):
    rows = P("fsdp", ("ctx", "tp"), None)
    weight = P(("fsdp", "ctx"), "tp")
    ids = P("fsdp", None)
    bias = P(None, "tp")
    in_specs = (rows, P(), P()) + (weight,) * 4 + (bias,) + (weight,) * 3 + (ids,) * 3 + (rows,)
    out_specs = (rows, rows, P(), P()) + (weight,) * 4 + (bias,) + (weight,) * 3
    return jax.shard_map(shards, mesh=mesh, in_specs=in_specs, out_specs=out_specs, check_vma=False)
```

```python
import functools
import jax
import jax.numpy as jnp
from jax import lax
from jax.sharding import PartitionSpec as P
from jax.experimental import pallas as pl
from jax.experimental.pallas import tpu as pltpu

HEADS = 16
HEAD = 64
EPS = 1e-05
NEG = -1e30
F32 = jnp.float32
BF16 = jnp.bfloat16
LANES = 128
QUERIES = 256
STEP = 128
VMEM_LIMIT = 40 * 1024 * 1024
ROWS_LIMIT = 16 * 1024 * 1024
WIDE_LIMIT = 56 * 1024 * 1024


def nt_dot(left, right):
    return lax.dot_general(left, right, (((1,), (1,)), ((), ())), preferred_element_type=F32)


def nn_dot(left, right):
    return lax.dot_general(left, right, (((1,), (0,)), ((), ())), preferred_element_type=F32)


def tn_dot(left, right):
    return lax.dot_general(left, right, (((0,), (0,)), ((), ())), preferred_element_type=F32)


def lane_of(shape):
    return lax.broadcasted_iota(jnp.int32, shape, len(shape) - 1)


def half_swap(values):
    lane = lane_of(values.shape)
    forward = pltpu.roll(values, LANES - HEAD // 2, 1)
    back = pltpu.roll(values, HEAD // 2, 1)
    return jnp.where(lane % HEAD < HEAD // 2, forward, back)


def fwd_kernel(row_parts, weight_parts, heads, *refs):
    tables, refs = refs[0], refs[1:]
    rows, refs = refs[:row_parts], refs[row_parts:]
    weights, refs = refs[:weight_parts], refs[weight_parts:]
    cosine, sine, seg_row, seg_wide, feature, coef = refs[:6]
    q_aug, k_aug, v_out, mixed_out, lse_out, keep_out, rest_out, send_own, send_rest = refs[6:15]
    full, out_full, mixed_wide, v_turn = refs[15:]
    pairs = heads // 2
    proj = heads * HEAD
    length = q_aug.shape[1]
    block = weights[0].shape[0]
    part = rows[0].shape[0]
    share = part // 2
    for i in range(weight_parts):
        at = pl.ds(pl.multiple_of(tables[3, i] * block, block), block)
        full[at, :] = weights[i][:block, : 3 * proj]
        out_full[at, :] = weights[i][:block, 3 * proj : 4 * proj]
    for p in range(row_parts):
        raw = nn_dot(rows[p][...], full[...])
        for k in range(2):
            piece = raw[k * share : (k + 1) * share]
            start = pl.multiple_of(tables[0, 2 * p + k] * share, share)
            at = pl.ds(start, share)
            cos_now, sin_now, feat = cosine[at, :], sine[at, :], feature[at, :].astype(F32)
            lane = lane_of((share, LANES))
            for pair in range(pairs):
                low = pair * LANES
                q = piece[:, low : low + LANES]
                q = (q * cos_now + half_swap(q) * sin_now).astype(BF16).astype(F32) * HEAD**-0.5
                kk = piece[:, proj + low : proj + low + LANES]
                kk = kk * cos_now + half_swap(kk) * sin_now
                v_out[pair, at, :] = piece[:, 2 * proj + low : 2 * proj + low + LANES].astype(BF16)
                for odd in range(2):
                    head = 2 * pair + odd
                    q_now = pltpu.roll(q, HEAD, 1) if odd else q
                    k_now = pltpu.roll(kk, HEAD, 1) if odd else kk
                    q_feat = feat * coef[head : head + 1, :]
                    q_aug[head, at, :] = jnp.where(lane < HEAD, q_now, q_feat).astype(BF16)
                    k_aug[head, at, :] = jnp.where(lane < HEAD, k_now, feat).astype(BF16)
    for pair in range(pairs):
        for b in range(length // LANES):
            tile = v_out[pair, b * LANES : (b + 1) * LANES, :].astype(F32)
            v_turn[pair, :, b * LANES : (b + 1) * LANES] = tile.T.astype(BF16)

    def query_block(b, carry):
        at = pl.ds(pl.multiple_of(b * QUERIES, QUERIES), QUERIES)
        seg_q = seg_row[pl.ds(b, 1), :]
        first = pl.multiple_of(tables[1, b] * LANES, LANES)
        for kind in range(1, length // STEP + 1):

            @pl.when(tables[2, b] == kind)
            def _(kind=kind):
                win = pl.ds(first, kind * STEP)
                keep = seg_wide[win, :] == seg_q
                scores = [nt_dot(k_aug[h, win, :], q_aug[h, at, :]) for h in range(heads)]
                probs, totals = [], []
                for head in range(heads):
                    s = jnp.where(keep, scores[head], NEG)
                    top = jnp.max(s, axis=0, keepdims=True)
                    p = jnp.exp(s - top)
                    total = jnp.sum(p, axis=0, keepdims=True)
                    probs.append(p.astype(BF16))
                    totals.append(total)
                    lse_out[head, pl.ds(b, 1), :] = top + jnp.log(total)
                for pair in range(pairs):
                    outs = []
                    for odd in range(2):
                        head = 2 * pair + odd
                        turn = v_turn[pair, odd * HEAD : (odd + 1) * HEAD, win]
                        outs.append(nn_dot(turn, probs[head]) / totals[head])
                    mixed = jnp.concatenate(outs, axis=0).T
                    mixed_wide[at, pair * LANES : (pair + 1) * LANES] = mixed

        return carry

    lax.fori_loop(0, length // QUERIES, query_block, 0)
    for slot in range(2 * row_parts):
        start = pl.multiple_of(tables[0, slot] * share, share)
        piece = mixed_wide[pl.ds(start, share), :]
        mixed_out[slot * share : (slot + 1) * share, :] = piece.astype(BF16)
    half = row_parts // 2
    for p in range(row_parts):
        back = nt_dot(mixed_out[p * part : (p + 1) * part, :], out_full[...])
        if p == 0:
            keep_out[...] = back
        elif p < half:
            rest_out[(p - 1) * part : p * part, :] = back
        else:
            if p == half:
                send_own[...] = back.astype(BF16)
            else:
                send_rest[(p - half - 1) * part : (p - half) * part, :] = back.astype(BF16)


def vmem():
    return pl.BlockSpec(memory_space=pltpu.VMEM)


def anywhere():
    return pl.BlockSpec(memory_space=pl.ANY)


def smem():
    return pl.BlockSpec(memory_space=pltpu.SMEM)


def attention_forward(tables, rows, weights, cosine, sine, seg_row, seg_wide, feature, coef, heads, behind=()):
    proj = heads * HEAD
    length = cosine.shape[0]
    part, width = rows[0].shape
    shapes = (
        jax.ShapeDtypeStruct((heads, length, LANES), BF16),
        jax.ShapeDtypeStruct((heads, length, LANES), BF16),
        jax.ShapeDtypeStruct((heads // 2, length, LANES), BF16),
        jax.ShapeDtypeStruct((length, proj), BF16),
        jax.ShapeDtypeStruct((heads, length // QUERIES, QUERIES), F32),
        jax.ShapeDtypeStruct((part, width), F32),
        jax.ShapeDtypeStruct((length // 2 - part, width), F32),
        jax.ShapeDtypeStruct((part, width), BF16),
        jax.ShapeDtypeStruct((length // 2 - part, width), BF16),
    )
    count = len(rows) + len(weights) + 6
    operands = (tables, *rows, *weights, cosine, sine, seg_row, seg_wide, feature, coef)
    return pl.pallas_call(
        without(functools.partial(fwd_kernel, len(rows), len(weights), heads), len(operands), len(behind)),
        out_shape=shapes,
        in_specs=[smem()] + [vmem()] * count + [anywhere()] * len(behind),
        out_specs=[vmem()] * 9,
        scratch_shapes=[
            pltpu.VMEM((width, 3 * proj), BF16),
            pltpu.VMEM((width, proj), BF16),
            pltpu.VMEM((length, proj), F32),
            pltpu.VMEM((heads // 2, LANES, length), BF16),
        ],
        compiler_params=pltpu.CompilerParams(vmem_limit_bytes=VMEM_LIMIT),
        cost_estimate=pl.CostEstimate(
            flops=2 * length * width * 3 * proj, bytes_accessed=8 << 20, transcendentals=length * length * heads // 2
        ),
        name="attn_fwd",
    )(*operands, *behind)


def bwd_kernel(row_parts, weight_parts, heads, *refs):
    tables, refs = refs[0], refs[1:]
    rows, refs = refs[:row_parts], refs[row_parts:]
    weights, refs = refs[:weight_parts], refs[weight_parts:]
    q_aug, k_aug, v_in, lse, cosine, sine, seg_row, seg_wide, hot_rows = refs[:9]
    keep_out, rest_out, send_own, send_rest, d_qkv_out, bias_out = refs[9:15]
    full, out_full, d_out, k_turn, dq_acc, dk_acc, dv_acc = refs[15:]
    pairs = heads // 2
    proj = heads * HEAD
    length = q_aug.shape[1]
    block = weights[0].shape[0]
    part = rows[0].shape[0]
    share = part // 2
    for i in range(weight_parts):
        at = pl.ds(pl.multiple_of(tables[3, i] * block, block), block)
        full[at, :] = weights[i][:block, : 3 * proj]
        out_full[at, :] = weights[i][:block, 3 * proj : 4 * proj]
    for p in range(row_parts):
        raw = nn_dot(rows[p][...], out_full[...]).astype(BF16)
        for k in range(2):
            start = pl.multiple_of(tables[0, 2 * p + k] * share, share)
            d_out[pl.ds(start, share), :] = raw[k * share : (k + 1) * share]
    for head in range(heads):
        for b in range(length // LANES):
            tile = k_aug[head, b * LANES : (b + 1) * LANES, :].astype(F32)
            k_turn[head, :, b * LANES : (b + 1) * LANES] = tile.T.astype(BF16)
    dk_acc[...] = jnp.zeros(dk_acc.shape, F32)
    dv_acc[...] = jnp.zeros(dv_acc.shape, F32)
    bias_out[...] = jnp.zeros(bias_out.shape, F32)

    def query_block(b, carry):
        at = pl.ds(pl.multiple_of(b * QUERIES, QUERIES), QUERIES)
        seg_q = seg_row[pl.ds(b, 1), :]
        hot = hot_rows[:, at]
        first = pl.multiple_of(tables[1, b] * LANES, LANES)
        for kind in range(1, length // STEP + 1):

            @pl.when(tables[2, b] == kind)
            def _(kind=kind):
                win = pl.ds(first, kind * STEP)
                keep = seg_wide[win, :] == seg_q
                owns = []
                for head in range(heads):
                    chunk = slice(head // 2 * LANES, (head // 2 + 1) * LANES)
                    d_pair = d_out[at, chunk]
                    lane = lane_of(d_pair.shape)
                    owns.append(jnp.where((lane >= HEAD) == (head % 2 == 1), d_pair, jnp.zeros_like(d_pair)))
                turned = []
                for base in range(0, heads, 2):
                    group = range(base, base + 2)
                    s = [nt_dot(k_aug[h, win, :], q_aug[h, at, :]) for h in group]
                    dp = [nt_dot(v_in[h // 2, win, :], owns[h]) for h in group]
                    low, ds = [], []
                    for i, h in enumerate(group):
                        p = jnp.exp(jnp.where(keep, s[i] - lse[h, pl.ds(b, 1), :], NEG))
                        low.append(p.astype(BF16))
                        ds.append((p * (dp[i] - jnp.sum(p * dp[i], axis=0, keepdims=True))).astype(BF16))
                    for i, h in enumerate(group):
                        if i % 2 == 0:
                            both = jnp.concatenate(low[i : i + 2], axis=1)
                            dv_acc[h // 2, win, :] += nn_dot(both, jnp.concatenate(owns[h : h + 2], axis=0))
                        dk_acc[h, win, :] += nn_dot(ds[i], q_aug[h, at, :])
                        dq = nn_dot(k_turn[h, :, win], ds[i])
                        turned.append(dq[:HEAD])
                        sums = dq[HEAD : HEAD + 8]
                        bias_out[h] += jnp.concatenate([sums * hot[:8], sums * hot[8:]], axis=0)
                for pair in range(pairs):
                    chunk = slice(pair * LANES, (pair + 1) * LANES)
                    dq_acc[at, chunk] = jnp.concatenate(turned[2 * pair : 2 * pair + 2], axis=0).T * HEAD**-0.5

        return carry

    lax.fori_loop(0, length // QUERIES, query_block, 0)
    for p in range(row_parts):
        for k in range(2):
            slot = 2 * p + k
            at = pl.ds(pl.multiple_of(tables[0, slot] * share, share), share)
            to = slice(slot * share, (slot + 1) * share)
            cos_now, sin_now = cosine[at, :], sine[at, :]
            lane = lane_of((share, LANES))
            for pair in range(pairs):
                low = pair * LANES
                dq = dq_acc[at, low : low + LANES]
                dk = jnp.where(lane < HEAD, dk_acc[2 * pair, at, :], pltpu.roll(dk_acc[2 * pair + 1, at, :], HEAD, 1))
                d_qkv_out[to, low : low + LANES] = (dq * cos_now - half_swap(dq) * sin_now).astype(BF16)
                d_qkv_out[to, proj + low : proj + low + LANES] = (dk * cos_now - half_swap(dk) * sin_now).astype(BF16)
                d_qkv_out[to, 2 * proj + low : 2 * proj + low + LANES] = dv_acc[pair, at, :].astype(BF16)
        part_rows = d_qkv_out[p * part : (p + 1) * part, :]
        back = nt_dot(part_rows, full[...])
        half = row_parts // 2
        if p == 0:
            keep_out[...] = back
        elif p < half:
            rest_out[(p - 1) * part : p * part, :] = back
        else:
            if p == half:
                send_own[...] = back.astype(BF16)
            else:
                send_rest[(p - half - 1) * part : (p - half) * part, :] = back.astype(BF16)


def attention_backward(tables, rows, weights, q_aug, k_aug, v_in, lse, cosine, sine, seg_row, seg_wide, hot_rows, heads, behind=()):
    proj = heads * HEAD
    length = cosine.shape[0]
    part, width = rows[0].shape
    shapes = (
        jax.ShapeDtypeStruct((part, width), F32),
        jax.ShapeDtypeStruct((length // 2 - part, width), F32),
        jax.ShapeDtypeStruct((part, width), BF16),
        jax.ShapeDtypeStruct((length // 2 - part, width), BF16),
        jax.ShapeDtypeStruct((length, 3 * proj), BF16),
        jax.ShapeDtypeStruct((heads, 16, QUERIES), F32),
    )
    count = len(rows) + len(weights) + 9
    operands = (tables, *rows, *weights, q_aug, k_aug, v_in, lse, cosine, sine, seg_row, seg_wide, hot_rows)
    return pl.pallas_call(
        without(functools.partial(bwd_kernel, len(rows), len(weights), heads), len(operands), len(behind)),
        out_shape=shapes,
        in_specs=[smem()] + [vmem()] * count + [anywhere()] * len(behind),
        out_specs=[vmem()] * 6,
        scratch_shapes=[
            pltpu.VMEM((width, 3 * proj), BF16),
            pltpu.VMEM((width, proj), BF16),
            pltpu.VMEM((length, proj), BF16),
            pltpu.VMEM((heads, LANES, length), BF16),
            pltpu.VMEM((length, proj), F32),
            pltpu.VMEM((heads, length, LANES), F32),
            pltpu.VMEM((heads // 2, length, LANES), F32),
        ],
        compiler_params=pltpu.CompilerParams(vmem_limit_bytes=VMEM_LIMIT),
        cost_estimate=pl.CostEstimate(
            flops=2 * length * width * 4 * proj, bytes_accessed=12 << 20, transcendentals=length * length * heads // 2
        ),
        name="attn_bwd",
    )(*operands, *behind)


def attention_tables(segments, variates, times, variate_bias, order, places):
    length = segments.shape[0]
    heads = variate_bias.shape[1]
    count = length // QUERIES
    half = HEAD // 2
    frequency = 10000.0 ** (-2.0 * jnp.arange(half, dtype=F32) / HEAD)
    angles = times.astype(F32)[:, None] * frequency
    cos_half, sin_half = jnp.cos(angles), jnp.sin(angles)
    wide = jax.ShapeDtypeStruct((length, LANES), F32)
    cosine, sine = rows_call(
        widen_kernel, "widen_angles", (wide, wide), jnp.concatenate([cos_half, sin_half], axis=1)
    )
    seg_row = segments.reshape(count, QUERIES)
    seg_wide = jnp.broadcast_to(segments[:, None], (length, QUERIES))
    lane = jnp.arange(LANES)
    live = (lane >= HEAD) & (lane < HEAD + 12)
    feature = ((variates[:, None] == (lane % 4)[None, :]) & live[None, :]).astype(BF16)
    gap = variate_bias[0] - variate_bias[1]
    high = lax.reduce_precision(gap, 8, 7)
    mid = lax.reduce_precision(gap - high, 8, 7)
    low = lax.reduce_precision(gap - high - mid, 8, 7)
    parts = jnp.repeat(jnp.stack([high, mid, low], axis=1), 4, axis=1)
    coef = jnp.pad(parts, ((0, -heads % 8), (HEAD, LANES - HEAD - 12)))
    kinds = jnp.arange(4)
    same = (variates[None, :] == kinds[:, None]).astype(F32)
    zeros = jnp.zeros_like(same)
    hot_rows = jnp.concatenate([same, zeros, 1.0 - same, zeros], axis=0)
    ends = segments.reshape(count, QUERIES)
    start = jnp.sum(segments[None, :] < ends[:, :1], axis=1)
    stop = jnp.sum(segments[None, :] <= ends[:, -1:], axis=1)
    first = start // LANES
    kind = (stop - first * LANES + STEP - 1) // STEP
    first = jnp.minimum(first, (length - kind * STEP) // LANES)
    size = max(count, order.shape[0], places.shape[0])
    pad = lambda a: jnp.pad(a.astype(jnp.int32), (0, size - a.shape[0]))
    tables = jnp.stack([pad(order), pad(first), pad(kind), pad(places)])
    return tables, cosine, sine, seg_row, seg_wide, feature, coef, hot_rows


def ffn_kernel(row_parts, flipped, which, *refs):
    rows, refs = refs[:row_parts], refs[row_parts:]
    near, refs = refs[:row_parts], refs[row_parts:]
    far, refs = refs[:row_parts], refs[row_parts:]
    weight, act_out, d_both_out, keep_out, rest_out, send_own, send_rest, grads, sems = refs
    part = rows[0].shape[0]
    share = part // 2
    cols = act_out.shape[1]
    half = row_parts // 2
    copies = []
    for p in range(row_parts):
        pair = (far[p], near[p]) if flipped else (near[p], far[p])
        for k in range(2):
            copy = pltpu.make_async_copy(pair[k].at[which[0]], grads.at[p, pl.ds(k * share, share)], sems.at[p, k])
            copy.start()
            copies.append(copy)
    for p in list(range(half, row_parts)) + list(range(half)):
        at = slice(p * part, (p + 1) * part)
        both = nn_dot(rows[p][...], weight[:, : 2 * cols])
        copies[2 * p].wait()
        copies[2 * p + 1].wait()
        d_act = nn_dot(grads[p], weight[:, 2 * cols :])
        gate, up = both[:, :cols], both[:, cols:]
        sig = 1.0 / (1.0 + jnp.exp(-gate))
        silu = gate * sig
        act_out[at, :] = (silu * up).astype(BF16)
        d_both_out[at, :cols] = (d_act * up * (sig + silu * (1.0 - sig))).astype(BF16)
        d_both_out[at, cols:] = (d_act * silu).astype(BF16)
        back = nt_dot(d_both_out[at, :], weight[:, : 2 * cols])
        if p == 0:
            keep_out[...] = back
        elif p < half:
            rest_out[(p - 1) * part : p * part, :] = back
        else:
            if p == half:
                send_own[...] = back.astype(BF16)
            else:
                send_rest[(p - half - 1) * part : (p - half) * part, :] = back.astype(BF16)


def ffn_middle(flipped, which, rows, near, far, weight, behind=()):
    part, width = rows[0].shape
    count = len(rows)
    length = part * count
    cols = weight.shape[1] // 3
    operands = (which, *rows, *near, *far, weight)
    return pl.pallas_call(
        without(functools.partial(ffn_kernel, count, flipped), len(operands), len(behind)),
        out_shape=(
            jax.ShapeDtypeStruct((length, cols), BF16),
            jax.ShapeDtypeStruct((length, 2 * cols), BF16),
            jax.ShapeDtypeStruct((part, width), F32),
            jax.ShapeDtypeStruct((length // 2 - part, width), F32),
            jax.ShapeDtypeStruct((part, width), BF16),
            jax.ShapeDtypeStruct((length // 2 - part, width), BF16),
        ),
        in_specs=[smem()] + [vmem()] * count + [anywhere()] * (2 * count) + [vmem()] + [anywhere()] * len(behind),
        out_specs=[vmem()] * 6,
        scratch_shapes=[pltpu.VMEM((count, part, width), BF16), pltpu.SemaphoreType.DMA((count, 2))],
        compiler_params=pltpu.CompilerParams(vmem_limit_bytes=VMEM_LIMIT),
        cost_estimate=pl.CostEstimate(
            flops=10 * length * width * cols, bytes_accessed=16 << 20, transcendentals=length * cols
        ),
        name="ffn_middle",
    )(*operands, *behind)


def ffn_tail_kernel(row_parts, which, *refs):
    own, refs = refs[:row_parts], refs[row_parts:]
    other, refs = refs[:row_parts], refs[row_parts:]
    near, refs = refs[:row_parts], refs[row_parts:]
    far, refs = refs[:row_parts], refs[row_parts:]
    acts, boths, weight, refs = refs[:2], refs[2:4], refs[4], refs[5:]
    outs, grad_out, refs = refs[:8], refs[8], refs[9:]
    down_buf, act_buf, both_buf, grad_buf, row_buf, total, keeps, rests, twins, twin_rests = refs[:10]
    in_sems, grad_sems, row_sems, out_sems, total_sems = refs[10:]
    part, width = own[0].shape
    share = part // 2
    length = part * row_parts
    cols = acts[0].shape[1]
    half = length // 2

    def begin(source, target, sem):
        copy = pltpu.make_async_copy(source, target, sem)
        copy.start()
        return copy

    down_copy = begin(weight.at[:, pl.ds(2 * cols, cols)], down_buf, in_sems.at[0])
    act_copies = [begin(acts[seq], act_buf.at[seq], in_sems.at[1 + seq]) for seq in range(2)]
    grad_copies = []
    for seq in range(2):
        now = which[0] if seq == 0 else 1 - which[0]
        for p in range(row_parts):
            pair = (near[p], far[p]) if seq == 0 else (far[p], near[p])
            for k in range(2):
                to = grad_buf.at[seq, pl.ds(p * part + k * share, share)]
                grad_copies.append(begin(pair[k].at[now], to, grad_sems.at[seq, p, k]))
    row_copies = [
        begin((own, other)[seq][p], row_buf.at[seq, pl.ds(p * part, part)], row_sems.at[seq, p])
        for seq in range(2)
        for p in range(row_parts)
    ]
    both_copies = [begin(boths[seq], both_buf.at[seq], in_sems.at[3 + seq]) for seq in range(2)]
    down_copy.wait()
    out_copies = []
    for seq in range(2):
        act_copies[seq].wait()
        mine = nt_dot(act_buf[seq, :half, :], down_buf[...])
        keeps[seq] = mine[:part]
        rests[seq] = mine[part:]
        mine = nt_dot(act_buf[seq, half:, :], down_buf[...]).astype(BF16)
        twins[seq] = mine[:part]
        twin_rests[seq] = mine[part:]
        for k, buf in enumerate((keeps, rests, twins, twin_rests)):
            out_copies.append(begin(buf.at[seq], outs[4 * seq + k], out_sems.at[seq, k]))
    step = width // 4
    total_copies = []
    for what in range(2):
        for seq in range(2):
            for p in range(row_parts):
                if what == 0:
                    grad_copies[2 * (seq * row_parts + p)].wait()
                    grad_copies[2 * (seq * row_parts + p) + 1].wait()
                else:
                    row_copies[seq * row_parts + p].wait()
        if what == 1:
            both_copies[0].wait()
            both_copies[1].wait()
        right, source = (act_buf, both_buf)[what], (grad_buf, row_buf)[what]
        first, size = (2 * cols, cols) if what == 0 else (0, 2 * cols)
        for k in range(4):
            at = slice(k * step, (k + 1) * step)
            value = sum(tn_dot(source[seq, :, at], right[seq]) for seq in range(2))
            total[at, first : first + size] = value.astype(BF16)
            if what == 1:
                rows = pl.ds(k * step, step)
                total_copies.append(begin(total.at[rows], grad_out.at[rows], total_sems.at[k]))
    for copy in out_copies + total_copies:
        copy.wait()


def ffn_tail(which, own, other, near, far, act_own, act_other, d_own, d_other, weight):
    part, width = own[0].shape
    count = len(own)
    length = part * count
    cols = act_own.shape[1]
    rest = length // 2 - part
    shapes = (
        jax.ShapeDtypeStruct((part, width), F32),
        jax.ShapeDtypeStruct((rest, width), F32),
        jax.ShapeDtypeStruct((part, width), BF16),
        jax.ShapeDtypeStruct((rest, width), BF16),
    )
    made = pl.pallas_call(
        functools.partial(ffn_tail_kernel, count),
        out_shape=shapes * 2 + (jax.ShapeDtypeStruct((width, 3 * cols), BF16),),
        in_specs=[smem()] + [anywhere()] * (4 * count + 5),
        out_specs=[anywhere()] * 8 + [pl.BlockSpec(memory_space=pltpu.HBM)],
        scratch_shapes=[
            pltpu.VMEM((width, cols), BF16),
            pltpu.VMEM((2, length, cols), BF16),
            pltpu.VMEM((2, length, 2 * cols), BF16),
            pltpu.VMEM((2, length, width), BF16),
            pltpu.VMEM((2, length, width), BF16),
            pltpu.VMEM((width, 3 * cols), BF16),
            pltpu.VMEM((2, part, width), F32),
            pltpu.VMEM((2, rest, width), F32),
            pltpu.VMEM((2, part, width), BF16),
            pltpu.VMEM((2, rest, width), BF16),
            pltpu.SemaphoreType.DMA((5,)),
            pltpu.SemaphoreType.DMA((2, count, 2)),
            pltpu.SemaphoreType.DMA((2, count)),
            pltpu.SemaphoreType.DMA((2, 4)),
            pltpu.SemaphoreType.DMA((4,)),
        ],
        compiler_params=pltpu.CompilerParams(vmem_limit_bytes=WIDE_LIMIT),
        name="ffn_tail",
    )(which, *own, *other, *near, *far, act_own, act_other, d_own, d_other, weight)
    return made[8], made[:8]


def without(kernel, start, count):
    return lambda *refs: kernel(*refs[:start], *refs[start + count :])


def rows_call(kernel, name, shapes, *operands, scalars=(), behind=(), limit=ROWS_LIMIT):
    single = not isinstance(shapes, (list, tuple))
    count = len(scalars) + len(operands)
    return pl.pallas_call(
        without(kernel, count, len(behind)),
        out_shape=shapes,
        in_specs=[smem()] * len(scalars) + [vmem()] * len(operands) + [anywhere()] * len(behind),
        out_specs=vmem() if single else [vmem()] * len(shapes),
        compiler_params=pltpu.CompilerParams(vmem_limit_bytes=limit),
        cost_estimate=pl.CostEstimate(
            flops=16 * operands[0].size, bytes_accessed=sum(o.size * o.dtype.itemsize for o in operands), transcendentals=0
        ),
        name=name,
    )(*scalars, *operands, *behind)


def pack_kernel(which, rows, query, key, value, out, gate, up, down, own, mine, packed):
    block, start = own.shape[0], 0
    for ref in (query, key, value, out):
        stop = start + ref.shape[1]
        own[:, start:stop] = ref[...]
        packed[:block, start:stop] = ref[...]
        start = stop
    width = rows.shape[2]
    packed[: rows.shape[1], start : start + width] = rows[1 - which[0]]
    start += width
    cols = gate.shape[1] // 2
    for k, ref in enumerate((gate, up, down)):
        for half in range(2):

            @pl.when(which[0] == half)
            def _(ref=ref, half=half, k=k):
                mine[:, k * cols : (k + 1) * cols] = ref[:, half * cols : (half + 1) * cols]
                packed[:block, start + k * cols : start + (k + 1) * cols] = ref[:, (1 - half) * cols : (2 - half) * cols]


def stack_kernel(start, which, mine, theirs, out):
    block, width = mine.shape
    first = pl.multiple_of(which[0] * block, block)
    second = pl.multiple_of((1 - which[0]) * block, block)
    out[pl.ds(first, block), :] = mine[...]
    out[pl.ds(second, block), :] = theirs[:block, start : start + width]


def turn_kernel(start, blocks, chips, which, *refs):
    back, refs = refs[: 7 + chips], refs[7 + chips :]
    pairs, outs = refs[: blocks + 1], refs[blocks + 1 :]
    pair_kernel(*pairs, *outs[2:])
    back_one_kernel(start, which, *back, *outs[:2])


def gains_kernel(place, gain_rows, gain, d_gain_two, bias_parts, out):
    blocks, _, block = gain_rows.shape
    for k in range(blocks):
        at = slice(k * block, (k + 1) * block)
        out[0:1, at] = gain_rows[k, 0:1, :] / gain[:, at].astype(F32)
    out[1:2, :] = d_gain_two[...]
    out[2:, :] = jnp.zeros(out[2:, :].shape, F32)
    lane = lane_of((1, LANES))
    lanes = pl.ds(pl.multiple_of(place[0] * LANES, LANES), LANES)
    for row in range(2):
        line = jnp.zeros((1, LANES), F32)
        for head in range(bias_parts.shape[0]):
            line = jnp.where(lane == head, jnp.sum(bias_parts[head, 8 * row : 8 * row + 8, :]), line)
        out[2 + row : 3 + row, lanes] = line


def ride_kernel(totals, twin, *refs):
    lows, (own, *outs) = refs[: len(refs) // 2], refs[len(refs) // 2 :]
    total = totals[...] + twin[...]
    own[...] = total
    high = total.astype(BF16).astype(F32)
    parts = (high, total - high)
    block, cols = lows[0].shape
    for low, out in zip(lows, outs):
        out[:block, :] = low[...]
        row = block
        for part in parts:
            for c in range(part.shape[1] // cols):
                out[row : row + part.shape[0], :] = part[:, c * cols : (c + 1) * cols].astype(BF16)
                row += part.shape[0]


def arrive_kernel(own, totals, *refs):
    arrived, (grad, total) = refs[:-2], refs[-2:]
    block, cols = own.shape
    rows, width = totals.shape
    value = own[...]
    sums = [totals[:, c * cols : (c + 1) * cols] for c in range(width // cols)]
    for ref in arrived:
        value = value + ref[:block, :].astype(F32)
        for k in range(2 * len(sums)):
            at = block + k * rows
            sums[k % len(sums)] = sums[k % len(sums)] + ref[at : at + rows, :].astype(F32)
    grad[...] = value
    for c, part in enumerate(sums):
        total[:, c * cols : (c + 1) * cols] = part


def gains_finish_kernel(place, mine, *refs):
    theirs, (one, two, bias) = refs[:-3], refs[-3:]
    lanes = pl.ds(pl.multiple_of(place[0] * LANES, LANES), LANES)
    total, line = mine[...], mine[:, lanes]
    for ref in theirs:
        total = total + ref[...]
        line = line + ref[:, lanes]
    one[...] = total[0:1]
    two[...] = total[1:2]
    bias[...] = line[2:4, : bias.shape[1]]


def first_kernel(start, which, mine, rows, far, gain, stack, out, far_attn):
    width = rows.shape[2]
    stack_kernel(start + width, which, mine, far, stack)
    norm_kernel(start, which, rows, far, gain, out, far_attn)


def widen_kernel(angles, cosine, sine):
    half = angles.shape[1] // 2
    cos_half, sin_half = angles[:, :half], angles[:, half:]
    cosine[...] = jnp.concatenate([cos_half] * (LANES // half), axis=1)
    sine[...] = jnp.concatenate([-sin_half, sin_half] * (LANES // half // 2), axis=1)


def pair_kernel(*refs):
    blocks = (len(refs) - 1) // 2
    keeps, other, outs = refs[:blocks], refs[blocks], refs[blocks + 1 :]
    rows = keeps[0].shape[0]
    for k in range(blocks):
        total = keeps[k][...].astype(F32) + other[k * rows : (k + 1) * rows, :].astype(F32)
        outs[k][...] = total.astype(outs[k].dtype)


def finish_kernel(count, own, *refs):
    total = own[...]
    for ref in refs[:-count]:
        total = total + ref[...].astype(F32)
    start = 0
    for out in refs[-count:]:
        stop = start + out.shape[1]
        out[...] = total[:, start:stop]
        start = stop


def pair_sums(partials, other):
    shape = partials[0].shape
    blocks = len(partials) - 1
    shapes = [jax.ShapeDtypeStruct(shape, F32 if k == 0 else BF16) for k in range(blocks)]
    return rows_call(pair_kernel, "pair_sums", shapes, *partials[:-1], other)


def weight_sums(own, arrived, pieces):
    outs = [jax.ShapeDtypeStruct((own.shape[0], own.shape[1] // pieces), F32)] * pieces
    return rows_call(functools.partial(finish_kernel, pieces), "weight_sums", outs, own, *arrived)


def last_kernel(start, count, which, grads, crossed, near, own, *refs):
    arrived, (gate, up, down, rows_out), outs = refs[:count], refs[count : count + 4], refs[count + 4 :]
    cols = grads.shape[1] // 3
    rows = grads.shape[0] // 2
    mine = grads[pl.ds(pl.multiple_of(which[0] * rows, rows), rows), :].astype(F32)
    theirs = crossed[:rows, start:].astype(F32)
    for half in range(2):

        @pl.when(which[0] == half)
        def _(half=half):
            for k, out in enumerate((gate, up, down)):
                out[:, half * cols : (half + 1) * cols] = mine[:, k * cols : (k + 1) * cols]
                out[:, (1 - half) * cols : (2 - half) * cols] = theirs[:, k * cols : (k + 1) * cols]

    stack_kernel(0, which, near, crossed, rows_out)
    finish_kernel(len(outs), own, *arrived, *outs)


def quadrant(own, other, flip):
    share = own.shape[0] // 2
    return jnp.concatenate(
        [own[flip * share : (flip + 1) * share], other[(1 - flip) * share : (2 - flip) * share]], axis=0
    )


def out_split_kernel(hidden, keep, rest, twin, twin_rest, keep_next, rest_next, twin_next, twin_rest_next, *outs):
    first, cross, chips, chips_cross = outs
    part = hidden.shape[0]
    own = keep[...] + twin[...].astype(F32) + hidden[...]
    other = keep_next[...] + twin_next[...].astype(F32)
    first[...] = quadrant(own, other, 0)
    cross[...] = quadrant(own, other, 1).astype(BF16)
    own = rest[...] + twin_rest[...].astype(F32)
    other = rest_next[...] + twin_rest_next[...].astype(F32)
    for k in range(rest.shape[0] // part):
        at = slice(k * part, (k + 1) * part)
        chips[at, :] = quadrant(own[at], other[at], 0)
        chips_cross[at, :] = quadrant(own[at], other[at], 1).astype(BF16)


def swapped(values):
    half = values.shape[0] // 2
    return jnp.concatenate([values[half:], values[:half]], axis=0)


def add_kernel(part, values, arrived, out):
    for k in range(values.shape[0] // part):
        at = slice(k * part, (k + 1) * part)
        out[at, :] = (values[at, :] + swapped(arrived[at, :].astype(F32))).astype(BF16)


def out_finish_kernel(which, first, cross, *refs):
    arrived, out = refs[:-1], refs[-1]
    share = out.shape[1]
    total = first[...] + swapped(cross[...].astype(F32))
    for ref in arrived:
        total = total + ref[...].astype(F32)
    total = total.astype(BF16)
    out[pl.ds(which[0], 1)] = total[None, :share]
    out[pl.ds(1 - which[0], 1)] = total[None, share:]


def inverse_rms(values):
    return lax.rsqrt(jnp.mean(values * values, axis=-1, keepdims=True) + EPS)


def both_halves(start, rows, packed, which):
    share, width = rows.shape[1:]
    return jnp.concatenate([rows[which[0]], packed[:share, start : start + width]], axis=0).astype(F32)


def rows_sum(keep, twin, arrived):
    total = keep[...] + twin[...].astype(F32)
    for ref in arrived:
        total = total + ref[...].astype(F32)
    return total


def norm_kernel(start, which, rows, far, gain, out, far_attn):
    far_attn[...] = far[: far_attn.shape[0], :start]
    values = both_halves(start, rows, far, which)
    out[...] = (values * inverse_rms(values) * gain[...].astype(F32)).astype(BF16)


def rest_kernel(rest, twin, out):
    out[...] = (rest[...] + twin[...].astype(F32)).astype(BF16)


def sum_kernel(keep, twin, *refs):
    refs[-1][...] = rows_sum(keep, twin, refs[:-1]).astype(BF16)


def middle_kernel(start, which, rows, far, gain, keep, twin, *refs):
    arrived, (hidden, out) = refs[:-2], refs[-2:]
    values = both_halves(start, rows, far, which) + rows_sum(keep, twin, arrived)
    hidden[...] = values
    out[...] = (values * inverse_rms(values) * gain[...].astype(F32)).astype(BF16)


def pull_norm(values, gain, grad):
    inv = inverse_rms(values)
    scaled = grad * gain
    normed = values * inv
    d_values = inv * (scaled - normed * jnp.mean(scaled * normed, axis=-1, keepdims=True))
    return d_values, jnp.sum(grad * normed, axis=0, keepdims=True)


def back_two_kernel(which, hidden, near, far, gain, across, keep, twin, *refs):
    arrived, (d_hidden, low, d_gain) = refs[:-3], refs[-3:]
    grad = rows_sum(keep, twin, arrived) + across[...].astype(F32)
    d_values, d_gain[...] = pull_norm(hidden[...], gain[...].astype(F32), grad)
    total = jnp.concatenate([near[which[0]], far[which[0]]], axis=0).astype(F32) + d_values
    d_hidden[...] = total
    low[...] = total.astype(BF16)


def back_one_kernel(start, which, rows, far, gain, d_hidden, ffn_grad, keep, twin, *refs):
    arrived, (first, packed) = refs[:-2], refs[-2:]
    grad = rows_sum(keep, twin, arrived)
    d_values, _ = pull_norm(both_halves(start, rows, far, which), gain[...].astype(F32), grad)
    total = (d_hidden[...] + d_values).astype(BF16)
    share, width = first.shape
    first[...] = total[:share]
    packed[:share, :width] = total[share:]
    block = ffn_grad.shape[0] // 2
    packed[:block, width:] = ffn_grad[pl.ds(pl.multiple_of((1 - which[0]) * block, block), block), :]


def grad_kernel(row_parts, blocks, tables, *refs):
    rows, refs = refs[:row_parts], refs[row_parts:]
    right, refs = refs[0], refs[1:]
    keeps, send, left = refs[:blocks], refs[blocks], refs[blocks + 1]
    block = keeps[0].shape[0]
    left_of(rows, right, left)
    for s in range(2 * blocks):
        at = pl.ds(pl.multiple_of(tables[3, s] * block, block), block)
        total = left[at, :].astype(BF16)
        if s < blocks:
            keeps[s][...] = total
        else:
            send[(s - blocks) * block : (s - blocks + 1) * block, :] = total


def weight_partials(tables, rows, right, blocks):
    part, width = rows[0].shape
    length, cols = right.shape
    block = width // (2 * blocks)
    return pl.pallas_call(
        functools.partial(grad_kernel, len(rows), blocks),
        out_shape=(jax.ShapeDtypeStruct((block, cols), BF16),) * blocks
        + (jax.ShapeDtypeStruct((width // 2, cols), BF16),),
        in_specs=[smem()] + [vmem()] * (len(rows) + 1),
        out_specs=[vmem()] * (blocks + 1),
        scratch_shapes=[pltpu.VMEM((width, cols), F32)],
        compiler_params=pltpu.CompilerParams(vmem_limit_bytes=VMEM_LIMIT),
        cost_estimate=pl.CostEstimate(
            flops=2 * length * width * cols, bytes_accessed=8 << 20, transcendentals=0
        ),
        name="weight_partials",
    )(tables, *rows, right)


def left_of(rows, right, total):
    part, width = rows[0].shape
    step = 2 * LANES
    for c in range(width // step):
        at = slice(c * step, (c + 1) * step)
        total[at, :] = sum(tn_dot(ref[:, at], right[p * part : (p + 1) * part, :]) for p, ref in enumerate(rows))


def send_kernel(row_parts, blocks, tables, *refs):
    rows, (right, send, left) = refs[:row_parts], refs[row_parts:]
    block = send.shape[0] // blocks
    left_of(rows, right, left)
    for s in range(blocks):
        at = pl.ds(pl.multiple_of(tables[3, blocks + s] * block, block), block)
        send[s * block : (s + 1) * block, :] = left[at, :].astype(BF16)


def keep_kernel(row_parts, blocks, tables, *refs):
    weights, refs = refs[: 2 * blocks], refs[2 * blocks :]
    rows, right, refs = refs[:row_parts], refs[row_parts], refs[row_parts + 1 :]
    keeps, (gain_row, left) = refs[:blocks], refs[blocks:]
    block = keeps[0].shape[0]
    cols = right.shape[1]
    left_of(rows, right, left)
    for s in range(2 * blocks):
        at = pl.ds(pl.multiple_of(tables[3, s] * block, block), block)
        total = left[at, :]
        product = total * weights[s][:block, :cols].astype(F32)
        product = sum(product[:, c * LANES : (c + 1) * LANES] for c in range(cols // LANES))
        high = product.astype(BF16)
        rest = (product - high.astype(F32)).astype(BF16)
        ones = jnp.ones((8, LANES), BF16)
        gain_row[pl.ds(tables[3, s], 1)] = (nt_dot(ones, high) + nt_dot(ones, rest))[None]
        if s < blocks:
            keeps[s][...] = total.astype(BF16)


def qkv_call(kernel, name, shapes, tables, operands, scratch):
    single = not isinstance(shapes, tuple)
    return pl.pallas_call(
        kernel,
        out_shape=shapes,
        in_specs=[smem()] + [vmem()] * len(operands),
        out_specs=vmem() if single else [vmem()] * len(shapes),
        scratch_shapes=[pltpu.VMEM(scratch, F32)],
        compiler_params=pltpu.CompilerParams(vmem_limit_bytes=VMEM_LIMIT),
        name=name,
    )(tables, *operands)


def qkv_partials(tables, weights, rows, right, blocks):
    part, width = rows[0].shape
    length, cols = right.shape
    block = width // (2 * blocks)
    send = qkv_call(
        functools.partial(send_kernel, len(rows), blocks),
        "qkv_send",
        jax.ShapeDtypeStruct((width // 2, cols), BF16),
        tables,
        [*rows, right],
        (width, cols),
    )
    keeps = qkv_call(
        functools.partial(keep_kernel, len(rows), blocks),
        "qkv_keep",
        (jax.ShapeDtypeStruct((block, cols), BF16),) * blocks + (jax.ShapeDtypeStruct((2 * blocks, 8, block), F32),),
        tables,
        [*weights, *rows, right],
        (width, cols),
    )
    return keeps[:-1], send, keeps[-1]


def hop(values, axis, flip):
    size = lax.axis_size(axis)
    return lax.ppermute(values, axis, [(i, i ^ flip) for i in range(size)])


def swap_blocks(values, axis, index, size):
    shape = values.shape
    bit = 1
    while bit < size:
        split = shape[:axis] + (size // (2 * bit), 2, bit) + shape[axis + 1 :]
        cut = values.reshape(split)
        cut = jnp.where((index & bit) != 0, jnp.flip(cut, axis + 1), cut)
        values = cut.reshape(shape)
        bit *= 2
    return values


def gather_chips(block):
    nt = lax.axis_size("tp")
    return [block] + [hop(block, "tp", 2 * k) for k in range(1, nt // 2)]


def with_twins(blocks):
    return blocks + [hop(block, "tp", 1) for block in blocks]


def gather_rows(block):
    return with_twins(gather_chips(block))


def region(ready, run):
    shapes = jax.eval_shape(run)
    return lax.cond(ready, run, lambda: jax.tree.map(lambda a: jnp.zeros(a.shape, a.dtype), shapes))


def chips_low(rest, twin, *behind):
    return rows_call(
        rest_kernel, "rest_rows", jax.ShapeDtypeStruct(rest.shape, BF16), rest, twin, behind=behind
    )


def chips_hop(low, nt):
    if nt == 4:
        return [hop(low, "tp", 2)]
    rows = low.shape[0] // (nt // 2 - 1)
    return [hop(low[(k - 1) * rows : k * rows], "tp", 2 * k) for k in range(1, nt // 2)]


def shards(
    layer_in,
    attn_gain,
    ffn_gain,
    query_weight,
    key_weight,
    value_weight,
    out_weight,
    variate_bias,
    gate_weight,
    up_weight,
    down_weight,
    segment_ids,
    variate_ids,
    time_ids,
    out_grad,
):
    seq_count, share, width = layer_in.shape
    nz, nx, nt = lax.axis_size("fsdp"), lax.axis_size("ctx"), lax.axis_size("tp")
    iz, ix, it = lax.axis_index("fsdp"), lax.axis_index("ctx"), lax.axis_index("tp")
    assert nx == 2 and seq_count == nx
    length = segment_ids.shape[1]
    heads = variate_bias.shape[1]
    proj = heads * HEAD

    def pick(table, which):
        return lax.dynamic_index_in_dim(table, which, 0, keepdims=False)

    def swap(mine, theirs):
        return jnp.where(ix == 0, mine, theirs), jnp.where(ix == 0, theirs, mine)

    gain_one, gain_two = attn_gain[None], ffn_gain[None]
    part = nx * share
    low_rows = jax.ShapeDtypeStruct((part, width), BF16)
    wide_rows = jax.ShapeDtypeStruct((part, width), F32)
    gain_row = jax.ShapeDtypeStruct((1, width), F32)
    half_rows = jax.ShapeDtypeStruct((share, width), BF16)
    which = ix.astype(jnp.int32).reshape(1)
    ready = ix >= 0
    cols = gate_weight.shape[1] // 2
    grad_own = out_grad
    block = query_weight.shape[0]
    attn_shape = jax.ShapeDtypeStruct((block, 4 * proj), BF16)
    packed_shape = jax.ShapeDtypeStruct((max(block, share), 4 * proj + width + 3 * cols), BF16)
    ffn_shape = jax.ShapeDtypeStruct((gate_weight.shape[0], 3 * cols), BF16)
    attn_own, mine, packed = rows_call(
        pack_kernel, "pack_weights", (attn_shape, ffn_shape, packed_shape), layer_in, query_weight, key_weight,
        value_weight, out_weight, gate_weight, up_weight, down_weight, scalars=(which,), limit=WIDE_LIMIT,
    )
    start = 4 * proj

    def twin(block):
        return hop(block, "tp", 1)

    def across(block):
        return hop(block, "ctx", 1)

    def first_transfers():
        attn_z = [hop(attn_own, "fsdp", k) for k in range(1, nz)]
        far = across(packed)
        grad_y = gather_chips(grad_own)[1:]
        order = jnp.arange(nx * nt).reshape(nx, nt // 2, 2)
        order = swap_blocks(swap_blocks(swap_blocks(order, 0, ix, nx), 1, it // 2, nt // 2), 2, it % 2, 2)
        order = order.transpose(2, 1, 0).reshape(nx * nt)
        places = jnp.arange(nz * nx).reshape(nz, nx)
        places = swap_blocks(swap_blocks(places, 0, iz, nz), 1, ix, nx).transpose(1, 0).reshape(nz * nx)
        tables = attention_tables(
            pick(segment_ids, ix), pick(variate_ids, ix), pick(time_ids, ix), variate_bias, order, places
        )
        return attn_z, far, grad_y, tables

    attn_z, far, grad_y, made = region(ready, first_transfers)
    tables, cosine, sine, seg_row, seg_wide, feature, coef, hot_rows = made
    stack_shape = jax.ShapeDtypeStruct((2 * block, 3 * cols), BF16)
    ffn_w, rows_own, far_attn = rows_call(
        functools.partial(first_kernel, start), "first_rows", (stack_shape, low_rows, attn_shape), mine, layer_in, far,
        gain_one, scalars=(which,), limit=WIDE_LIMIT,
    )
    ffn_w = lax.all_gather(ffn_w, "fsdp", axis=0, tiled=True)

    def gather_one():
        rest = [hop(far_attn, "fsdp", 1)] + [across(piece) for piece in attn_z[1:]]
        return gather_chips(rows_own)[1:], rest

    chips, rest_x = region(ready, gather_one)
    chips_one = [rows_own] + chips
    attn_w = [attn_own] + attn_z + [far_attn] + rest_x

    def attend():
        twins = [twin(rows) for rows in chips_one]
        near_twins = [twin(rows) for rows in [grad_own] + grad_y]
        return across(grad_own), near_twins, twins, attention_forward(
            tables, chips_one + twins, attn_w, cosine, sine, seg_row, seg_wide, feature, coef, heads
        )

    grad_far, near_twins, twins, (q_aug, k_aug, v_rows, mixed, lse, keep, rest, send, send_rest) = region(ready, attend)

    def scatter_attn():
        low = chips_low(rest, twin(send_rest))
        return chips_hop(low, nt), twin(send), [across(piece) for piece in grad_y], twin(grad_far)

    rows_one = chips_one + twins
    chips, twins, grad_far_y, far_twin = region(ready, scatter_attn)
    grad_near, grad_far = [grad_own] + grad_y, [grad_far] + grad_far_y
    hidden, rows_two = rows_call(
        functools.partial(middle_kernel, start), "middle_rows", (wide_rows, low_rows), layer_in, far, gain_two, keep,
        twins, *chips, scalars=(which,),
    )

    def gather_two():
        return (
            gather_chips(rows_two)[1:],
            across(rows_two),
            [twin(rows) for rows in grad_far[1:]],
            twin(rows_two),
        )

    chips_two, next_own, far_twins, rows_twin = region(ready, gather_two)
    grad_near, grad_far = grad_near + near_twins, grad_far + [far_twin] + far_twins

    def ffn_own():
        twins = [twin(rows) for rows in chips_two]
        return [across(rows) for rows in chips_two], twins, ffn_middle(
            False, which, [rows_two] + chips_two + [rows_twin] + twins, grad_near, grad_far, ffn_w
        )

    next_y, twins, (act, d_both, keep, rest, send, send_rest) = region(ready, ffn_own)

    rows_two = [rows_two] + chips_two + [rows_twin] + twins
    rows_next = [next_own] + next_y

    def ffn_next():
        low = chips_low(rest, twin(send_rest))
        twins = [twin(rows) for rows in rows_next]
        return chips_hop(low, nt), twin(send), twins, ffn_middle(
            True, 1 - which, rows_next + twins, grad_near, grad_far, ffn_w
        )

    chips, twins, next_twins, made = region(ready, ffn_next)
    rows_next = rows_next + next_twins
    act_next, d_both_next, keep_next, rest_next, send_next, send_rest = made
    low_next = chips_low(rest_next, twin(send_rest))

    def scatter_next():
        return (
            chips_hop(low_next, nt),
            twin(send_next),
            ffn_tail(which, rows_two, rows_next, grad_near, grad_far, act, act_next, d_both, d_both_next, ffn_w),
        )

    chips_next, twins_next, (ffn_grad, parts) = region(ready, scatter_next)
    low_across = rows_call(sum_kernel, "sum_rows", low_rows, keep_next, twins_next, *chips_next)

    def cross_next():
        out_twins = [twin(parts[k]) for k in (2, 3, 6, 7)]
        rest_shape = (parts[1].shape[0], width)
        shapes = (
            wide_rows,
            low_rows,
            jax.ShapeDtypeStruct(rest_shape, F32),
            jax.ShapeDtypeStruct(rest_shape, BF16),
        )
        return across(low_across), rows_call(
            out_split_kernel, "out_split", shapes, hidden, parts[0], parts[1], out_twins[0], out_twins[1], parts[4],
            parts[5], out_twins[2], out_twins[3],
        )

    arrived, (out_first, out_cross, out_chips, out_chips_cross) = region(ready, cross_next)
    ffn_grad = lax.psum_scatter(ffn_grad, "fsdp", scatter_dimension=0, tiled=True)
    d_hidden, low, d_gain_two = rows_call(
        back_two_kernel,
        "back_two",
        (wide_rows, low_rows, gain_row),
        hidden,
        grad_near[0],
        grad_far[0],
        gain_two,
        arrived,
        keep,
        twins,
        *chips,
        scalars=(which,),
    )

    def gather_back():
        return gather_chips(low)[1:], twin(low), across(out_chips_cross)

    chips_back, twin_back, out_arrived = region(ready, gather_back)
    def attend_back():
        rows = [low] + chips_back + [twin_back] + [twin(rows) for rows in chips_back]
        cross = across(out_cross)
        low_shape = jax.ShapeDtypeStruct(out_chips.shape, BF16)
        low_out = rows_call(functools.partial(add_kernel, part), "add_rows", low_shape, out_chips, out_arrived)
        grads = weight_partials(tables, rows, mixed, nz)
        return chips_hop(low_out, nt), cross, across(grads[-1]), grads, attention_backward(
            tables, rows, attn_w, q_aug, k_aug, v_rows, lse, cosine, sine, seg_row, seg_wide, hot_rows, heads
        )

    out_arrived, out_cross, out_other, out_grads, made = region(ready, attend_back)
    keep, rest, send, send_rest, d_qkv, bias_parts = made

    place = it.astype(jnp.int32).reshape(1)
    gain_shape = jax.ShapeDtypeStruct((8, width), F32)

    def scatter_one():
        twins = twin(send)
        low = chips_low(rest, twin(send_rest), twins)
        keeps, sent, gain_rows = qkv_partials(tables, attn_w, rows_one, d_qkv, nz)
        sums = pair_sums(out_grads, out_other)
        totals = rows_call(
            gains_kernel, "gain_rows", gain_shape, gain_rows, gain_one, d_gain_two, bias_parts, scalars=(place,)
        )
        lows = sums[1:]
        ride_shape = jax.ShapeDtypeStruct((block + 16 * (width // proj), proj), BF16)
        totals, *lows = rows_call(
            ride_kernel, "ride_rows", [gain_shape] + [ride_shape] * len(lows), totals, twin(totals), *lows
        )
        arrived = [hop(low_out, "fsdp", 1 + k) for k, low_out in enumerate(lows)]
        out_weight_grad, totals = rows_call(
            arrive_kernel, "out_sums", (jax.ShapeDtypeStruct((block, proj), F32), gain_shape), sums[0], totals, *arrived
        )
        return chips_hop(low, nt), twins, keeps, across(sent), out_weight_grad, totals

    chips, twins, qkv_keeps, qkv_other, out_weight_grad, totals = region(ready, scatter_one)
    packed_shape = jax.ShapeDtypeStruct((max(block, share), width + 3 * cols), BF16)
    pair_shapes = [jax.ShapeDtypeStruct((block, 3 * proj), F32 if k == 0 else BF16) for k in range(nz)]
    d_near, packed, *qkv_sums = rows_call(
        functools.partial(turn_kernel, start, nz, len(chips)), "turn_rows", [half_rows, packed_shape] + pair_shapes,
        layer_in, far, gain_one, d_hidden, ffn_grad, keep, twins, *chips, *qkv_keeps, qkv_other,
        scalars=(which,), limit=WIDE_LIMIT,
    )

    def last_transfers():
        arrived = [hop(piece, "fsdp", k) for k, piece in enumerate(qkv_sums) if k > 0]
        layer_out = rows_call(
            out_finish_kernel, "layer_out", jax.ShapeDtypeStruct(layer_in.shape, BF16), out_first, out_cross,
            *out_arrived, scalars=(which,),
        )
        chips = sum([hop(totals, "tp", 2 * k) for k in range(1, nt // 2)], totals)
        summed = rows_call(
            gains_finish_kernel, "gain_sums", (gain_row, gain_row, jax.ShapeDtypeStruct((2, heads), F32)), chips,
            across(chips), scalars=(place,),
        )
        return arrived, across(packed), summed, layer_out

    arrived, crossed, summed, layer_out = region(ready, last_transfers)
    attn_gain_grad, ffn_gain_grad, bias_grad = summed
    weight_shape = jax.ShapeDtypeStruct(gate_weight.shape, F32)
    in_shape = jax.ShapeDtypeStruct((nx * share, width), BF16)
    head_shape = jax.ShapeDtypeStruct(query_weight.shape, F32)
    gate_grad, up_grad, down_grad, in_grad, query_grad, key_grad, value_grad = rows_call(
        functools.partial(last_kernel, width, len(arrived)), "last_sums",
        [weight_shape] * 3 + [in_shape] + [head_shape] * 3,
        ffn_grad, crossed, d_near, qkv_sums[0], *arrived, scalars=(which,), limit=WIDE_LIMIT,
    )
    in_grad = in_grad.reshape(layer_in.shape)
    return (
        layer_out,
        in_grad,
        attn_gain_grad.reshape(width),
        ffn_gain_grad.reshape(width),
        query_grad,
        key_grad,
        value_grad,
        out_weight_grad,
        bias_grad,
        gate_grad,
        up_grad,
        down_grad,
    )


def solution(mesh):
    rows = P("fsdp", ("ctx", "tp"), None)
    weight = P(("fsdp", "ctx"), "tp")
    ids = P("fsdp", None)
    bias = P(None, "tp")
    in_specs = (rows, P(), P()) + (weight,) * 4 + (bias,) + (weight,) * 3 + (ids,) * 3 + (rows,)
    out_specs = (rows, rows, P(), P()) + (weight,) * 4 + (bias,) + (weight,) * 3
    return jax.shard_map(shards, mesh=mesh, in_specs=in_specs, out_specs=out_specs, check_vma=False)
```

```python
import functools
import jax
import jax.numpy as jnp
from jax import lax
from jax.sharding import PartitionSpec as P
from jax.experimental import pallas as pl
from jax.experimental.pallas import tpu as pltpu

HEADS = 16
HEAD = 64
EPS = 1e-05
NEG = -1e30
F32 = jnp.float32
BF16 = jnp.bfloat16
LANES = 128
QUERIES = 256
STEP = 128
VMEM_LIMIT = 40 * 1024 * 1024
ROWS_LIMIT = 16 * 1024 * 1024
WIDE_LIMIT = 56 * 1024 * 1024


def nt_dot(left, right):
    return lax.dot_general(left, right, (((1,), (1,)), ((), ())), preferred_element_type=F32)


def nn_dot(left, right):
    return lax.dot_general(left, right, (((1,), (0,)), ((), ())), preferred_element_type=F32)


def tn_dot(left, right):
    return lax.dot_general(left, right, (((0,), (0,)), ((), ())), preferred_element_type=F32)


def lane_of(shape):
    return lax.broadcasted_iota(jnp.int32, shape, len(shape) - 1)


def half_swap(values):
    lane = lane_of(values.shape)
    forward = pltpu.roll(values, LANES - HEAD // 2, 1)
    back = pltpu.roll(values, HEAD // 2, 1)
    return jnp.where(lane % HEAD < HEAD // 2, forward, back)


def fwd_kernel(row_parts, weight_parts, heads, *refs):
    tables, refs = refs[0], refs[1:]
    rows, refs = refs[:row_parts], refs[row_parts:]
    weights, refs = refs[:weight_parts], refs[weight_parts:]
    cosine, sine, seg_row, seg_wide, feature, coef = refs[:6]
    q_aug, k_aug, v_out, mixed_out, lse_out, keep_out, rest_out, send_own, send_rest = refs[6:15]
    full, out_full, mixed_wide, v_turn = refs[15:]
    pairs = heads // 2
    proj = heads * HEAD
    length = q_aug.shape[1]
    block = weights[0].shape[0]
    part = rows[0].shape[0]
    share = part // 2
    for i in range(weight_parts):
        at = pl.ds(pl.multiple_of(tables[3, i] * block, block), block)
        full[at, :] = weights[i][:block, : 3 * proj]
        out_full[at, :] = weights[i][:block, 3 * proj : 4 * proj]
    for p in range(row_parts):
        raw = nn_dot(rows[p][...], full[...])
        for k in range(2):
            piece = raw[k * share : (k + 1) * share]
            start = pl.multiple_of(tables[0, 2 * p + k] * share, share)
            at = pl.ds(start, share)
            cos_now, sin_now, feat = cosine[at, :], sine[at, :], feature[at, :].astype(F32)
            lane = lane_of((share, LANES))
            for pair in range(pairs):
                low = pair * LANES
                q = piece[:, low : low + LANES]
                q = (q * cos_now + half_swap(q) * sin_now).astype(BF16).astype(F32) * HEAD**-0.5
                kk = piece[:, proj + low : proj + low + LANES]
                kk = kk * cos_now + half_swap(kk) * sin_now
                v_out[pair, at, :] = piece[:, 2 * proj + low : 2 * proj + low + LANES].astype(BF16)
                for odd in range(2):
                    head = 2 * pair + odd
                    q_now = pltpu.roll(q, HEAD, 1) if odd else q
                    k_now = pltpu.roll(kk, HEAD, 1) if odd else kk
                    q_feat = feat * coef[head : head + 1, :]
                    q_aug[head, at, :] = jnp.where(lane < HEAD, q_now, q_feat).astype(BF16)
                    k_aug[head, at, :] = jnp.where(lane < HEAD, k_now, feat).astype(BF16)
    for pair in range(pairs):
        for b in range(length // LANES):
            tile = v_out[pair, b * LANES : (b + 1) * LANES, :].astype(F32)
            v_turn[pair, :, b * LANES : (b + 1) * LANES] = tile.T.astype(BF16)

    def query_block(b, carry):
        at = pl.ds(pl.multiple_of(b * QUERIES, QUERIES), QUERIES)
        seg_q = seg_row[pl.ds(b, 1), :]
        first = pl.multiple_of(tables[1, b] * LANES, LANES)
        for kind in range(1, length // STEP + 1):

            @pl.when(tables[2, b] == kind)
            def _(kind=kind):
                win = pl.ds(first, kind * STEP)
                keep = seg_wide[win, :] == seg_q
                scores = [nt_dot(k_aug[h, win, :], q_aug[h, at, :]) for h in range(heads)]
                probs, totals = [], []
                for head in range(heads):
                    s = jnp.where(keep, scores[head], NEG)
                    top = jnp.max(s, axis=0, keepdims=True)
                    p = jnp.exp(s - top)
                    total = jnp.sum(p, axis=0, keepdims=True)
                    probs.append(p.astype(BF16))
                    totals.append(total)
                    lse_out[head, pl.ds(b, 1), :] = top + jnp.log(total)
                for pair in range(pairs):
                    outs = []
                    for odd in range(2):
                        head = 2 * pair + odd
                        turn = v_turn[pair, odd * HEAD : (odd + 1) * HEAD, win]
                        outs.append(nn_dot(turn, probs[head]) / totals[head])
                    mixed = jnp.concatenate(outs, axis=0).T
                    mixed_wide[at, pair * LANES : (pair + 1) * LANES] = mixed

        return carry

    lax.fori_loop(0, length // QUERIES, query_block, 0)
    for slot in range(2 * row_parts):
        start = pl.multiple_of(tables[0, slot] * share, share)
        piece = mixed_wide[pl.ds(start, share), :]
        mixed_out[slot * share : (slot + 1) * share, :] = piece.astype(BF16)
    half = row_parts // 2
    for p in range(row_parts):
        back = nt_dot(mixed_out[p * part : (p + 1) * part, :], out_full[...])
        if p == 0:
            keep_out[...] = back
        elif p < half:
            rest_out[(p - 1) * part : p * part, :] = back
        else:
            if p == half:
                send_own[...] = back.astype(BF16)
            else:
                send_rest[(p - half - 1) * part : (p - half) * part, :] = back.astype(BF16)


def vmem():
    return pl.BlockSpec(memory_space=pltpu.VMEM)


def anywhere():
    return pl.BlockSpec(memory_space=pl.ANY)


def smem():
    return pl.BlockSpec(memory_space=pltpu.SMEM)


def attention_forward(tables, rows, weights, cosine, sine, seg_row, seg_wide, feature, coef, heads, behind=()):
    proj = heads * HEAD
    length = cosine.shape[0]
    part, width = rows[0].shape
    shapes = (
        jax.ShapeDtypeStruct((heads, length, LANES), BF16),
        jax.ShapeDtypeStruct((heads, length, LANES), BF16),
        jax.ShapeDtypeStruct((heads // 2, length, LANES), BF16),
        jax.ShapeDtypeStruct((length, proj), BF16),
        jax.ShapeDtypeStruct((heads, length // QUERIES, QUERIES), F32),
        jax.ShapeDtypeStruct((part, width), F32),
        jax.ShapeDtypeStruct((length // 2 - part, width), F32),
        jax.ShapeDtypeStruct((part, width), BF16),
        jax.ShapeDtypeStruct((length // 2 - part, width), BF16),
    )
    count = len(rows) + len(weights) + 6
    operands = (tables, *rows, *weights, cosine, sine, seg_row, seg_wide, feature, coef)
    return pl.pallas_call(
        without(functools.partial(fwd_kernel, len(rows), len(weights), heads), len(operands), len(behind)),
        out_shape=shapes,
        in_specs=[smem()] + [vmem()] * count + [anywhere()] * len(behind),
        out_specs=[vmem()] * 9,
        scratch_shapes=[
            pltpu.VMEM((width, 3 * proj), BF16),
            pltpu.VMEM((width, proj), BF16),
            pltpu.VMEM((length, proj), F32),
            pltpu.VMEM((heads // 2, LANES, length), BF16),
        ],
        compiler_params=pltpu.CompilerParams(vmem_limit_bytes=VMEM_LIMIT),
        cost_estimate=pl.CostEstimate(
            flops=2 * length * width * 3 * proj, bytes_accessed=8 << 20, transcendentals=length * length * heads // 2
        ),
        name="attn_fwd",
    )(*operands, *behind)


def bwd_kernel(row_parts, weight_parts, heads, *refs):
    tables, refs = refs[0], refs[1:]
    rows, refs = refs[:row_parts], refs[row_parts:]
    weights, refs = refs[:weight_parts], refs[weight_parts:]
    q_aug, k_aug, v_in, lse, cosine, sine, seg_row, seg_wide, hot_rows = refs[:9]
    keep_out, rest_out, send_own, send_rest, d_qkv_out, bias_out = refs[9:15]
    full, out_full, d_out, k_turn, dq_acc, dk_acc, dv_acc = refs[15:]
    pairs = heads // 2
    proj = heads * HEAD
    length = q_aug.shape[1]
    block = weights[0].shape[0]
    part = rows[0].shape[0]
    share = part // 2
    for i in range(weight_parts):
        at = pl.ds(pl.multiple_of(tables[3, i] * block, block), block)
        full[at, :] = weights[i][:block, : 3 * proj]
        out_full[at, :] = weights[i][:block, 3 * proj : 4 * proj]
    for p in range(row_parts):
        raw = nn_dot(rows[p][...], out_full[...]).astype(BF16)
        for k in range(2):
            start = pl.multiple_of(tables[0, 2 * p + k] * share, share)
            d_out[pl.ds(start, share), :] = raw[k * share : (k + 1) * share]
    for head in range(heads):
        for b in range(length // LANES):
            tile = k_aug[head, b * LANES : (b + 1) * LANES, :].astype(F32)
            k_turn[head, :, b * LANES : (b + 1) * LANES] = tile.T.astype(BF16)
    dk_acc[...] = jnp.zeros(dk_acc.shape, F32)
    dv_acc[...] = jnp.zeros(dv_acc.shape, F32)
    bias_out[...] = jnp.zeros(bias_out.shape, F32)

    def query_block(b, carry):
        at = pl.ds(pl.multiple_of(b * QUERIES, QUERIES), QUERIES)
        seg_q = seg_row[pl.ds(b, 1), :]
        hot = hot_rows[:, at]
        first = pl.multiple_of(tables[1, b] * LANES, LANES)
        for kind in range(1, length // STEP + 1):

            @pl.when(tables[2, b] == kind)
            def _(kind=kind):
                win = pl.ds(first, kind * STEP)
                keep = seg_wide[win, :] == seg_q
                owns = []
                for head in range(heads):
                    chunk = slice(head // 2 * LANES, (head // 2 + 1) * LANES)
                    d_pair = d_out[at, chunk]
                    lane = lane_of(d_pair.shape)
                    owns.append(jnp.where((lane >= HEAD) == (head % 2 == 1), d_pair, jnp.zeros_like(d_pair)))
                turned = []
                for base in range(0, heads, 2):
                    group = range(base, base + 2)
                    s = [nt_dot(k_aug[h, win, :], q_aug[h, at, :]) for h in group]
                    dp = [nt_dot(v_in[h // 2, win, :], owns[h]) for h in group]
                    low, ds = [], []
                    for i, h in enumerate(group):
                        p = jnp.exp(jnp.where(keep, s[i] - lse[h, pl.ds(b, 1), :], NEG))
                        low.append(p.astype(BF16))
                        ds.append((p * (dp[i] - jnp.sum(p * dp[i], axis=0, keepdims=True))).astype(BF16))
                    for i, h in enumerate(group):
                        if i % 2 == 0:
                            both = jnp.concatenate(low[i : i + 2], axis=1)
                            dv_acc[h // 2, win, :] += nn_dot(both, jnp.concatenate(owns[h : h + 2], axis=0))
                        dk_acc[h, win, :] += nn_dot(ds[i], q_aug[h, at, :])
                        dq = nn_dot(k_turn[h, :, win], ds[i])
                        turned.append(dq[:HEAD])
                        sums = dq[HEAD : HEAD + 8]
                        bias_out[h] += jnp.concatenate([sums * hot[:8], sums * hot[8:]], axis=0)
                for pair in range(pairs):
                    chunk = slice(pair * LANES, (pair + 1) * LANES)
                    dq_acc[at, chunk] = jnp.concatenate(turned[2 * pair : 2 * pair + 2], axis=0).T * HEAD**-0.5

        return carry

    lax.fori_loop(0, length // QUERIES, query_block, 0)
    for p in range(row_parts):
        for k in range(2):
            slot = 2 * p + k
            at = pl.ds(pl.multiple_of(tables[0, slot] * share, share), share)
            to = slice(slot * share, (slot + 1) * share)
            cos_now, sin_now = cosine[at, :], sine[at, :]
            lane = lane_of((share, LANES))
            for pair in range(pairs):
                low = pair * LANES
                dq = dq_acc[at, low : low + LANES]
                dk = jnp.where(lane < HEAD, dk_acc[2 * pair, at, :], pltpu.roll(dk_acc[2 * pair + 1, at, :], HEAD, 1))
                d_qkv_out[to, low : low + LANES] = (dq * cos_now - half_swap(dq) * sin_now).astype(BF16)
                d_qkv_out[to, proj + low : proj + low + LANES] = (dk * cos_now - half_swap(dk) * sin_now).astype(BF16)
                d_qkv_out[to, 2 * proj + low : 2 * proj + low + LANES] = dv_acc[pair, at, :].astype(BF16)
        part_rows = d_qkv_out[p * part : (p + 1) * part, :]
        back = nt_dot(part_rows, full[...])
        half = row_parts // 2
        if p == 0:
            keep_out[...] = back
        elif p < half:
            rest_out[(p - 1) * part : p * part, :] = back
        else:
            if p == half:
                send_own[...] = back.astype(BF16)
            else:
                send_rest[(p - half - 1) * part : (p - half) * part, :] = back.astype(BF16)


def attention_backward(tables, rows, weights, q_aug, k_aug, v_in, lse, cosine, sine, seg_row, seg_wide, hot_rows, heads, behind=()):
    proj = heads * HEAD
    length = cosine.shape[0]
    part, width = rows[0].shape
    shapes = (
        jax.ShapeDtypeStruct((part, width), F32),
        jax.ShapeDtypeStruct((length // 2 - part, width), F32),
        jax.ShapeDtypeStruct((part, width), BF16),
        jax.ShapeDtypeStruct((length // 2 - part, width), BF16),
        jax.ShapeDtypeStruct((length, 3 * proj), BF16),
        jax.ShapeDtypeStruct((heads, 16, QUERIES), F32),
    )
    count = len(rows) + len(weights) + 9
    operands = (tables, *rows, *weights, q_aug, k_aug, v_in, lse, cosine, sine, seg_row, seg_wide, hot_rows)
    return pl.pallas_call(
        without(functools.partial(bwd_kernel, len(rows), len(weights), heads), len(operands), len(behind)),
        out_shape=shapes,
        in_specs=[smem()] + [vmem()] * count + [anywhere()] * len(behind),
        out_specs=[vmem()] * 6,
        scratch_shapes=[
            pltpu.VMEM((width, 3 * proj), BF16),
            pltpu.VMEM((width, proj), BF16),
            pltpu.VMEM((length, proj), BF16),
            pltpu.VMEM((heads, LANES, length), BF16),
            pltpu.VMEM((length, proj), F32),
            pltpu.VMEM((heads, length, LANES), F32),
            pltpu.VMEM((heads // 2, length, LANES), F32),
        ],
        compiler_params=pltpu.CompilerParams(vmem_limit_bytes=VMEM_LIMIT),
        cost_estimate=pl.CostEstimate(
            flops=2 * length * width * 4 * proj, bytes_accessed=12 << 20, transcendentals=length * length * heads // 2
        ),
        name="attn_bwd",
    )(*operands, *behind)


def attention_tables(segments, variates, times, variate_bias, order, places):
    length = segments.shape[0]
    heads = variate_bias.shape[1]
    count = length // QUERIES
    half = HEAD // 2
    frequency = 10000.0 ** (-2.0 * jnp.arange(half, dtype=F32) / HEAD)
    angles = times.astype(F32)[:, None] * frequency
    cos_half, sin_half = jnp.cos(angles), jnp.sin(angles)
    wide = jax.ShapeDtypeStruct((length, LANES), F32)
    cosine, sine = rows_call(
        widen_kernel, "widen_angles", (wide, wide), jnp.concatenate([cos_half, sin_half], axis=1)
    )
    seg_row = segments.reshape(count, QUERIES)
    seg_wide = jnp.broadcast_to(segments[:, None], (length, QUERIES))
    lane = jnp.arange(LANES)
    live = (lane >= HEAD) & (lane < HEAD + 12)
    feature = ((variates[:, None] == (lane % 4)[None, :]) & live[None, :]).astype(BF16)
    gap = variate_bias[0] - variate_bias[1]
    high = lax.reduce_precision(gap, 8, 7)
    mid = lax.reduce_precision(gap - high, 8, 7)
    low = lax.reduce_precision(gap - high - mid, 8, 7)
    parts = jnp.repeat(jnp.stack([high, mid, low], axis=1), 4, axis=1)
    coef = jnp.pad(parts, ((0, -heads % 8), (HEAD, LANES - HEAD - 12)))
    kinds = jnp.arange(4)
    same = (variates[None, :] == kinds[:, None]).astype(F32)
    zeros = jnp.zeros_like(same)
    hot_rows = jnp.concatenate([same, zeros, 1.0 - same, zeros], axis=0)
    ends = segments.reshape(count, QUERIES)
    start = jnp.sum(segments[None, :] < ends[:, :1], axis=1)
    stop = jnp.sum(segments[None, :] <= ends[:, -1:], axis=1)
    first = start // LANES
    kind = (stop - first * LANES + STEP - 1) // STEP
    first = jnp.minimum(first, (length - kind * STEP) // LANES)
    size = max(count, order.shape[0], places.shape[0])
    pad = lambda a: jnp.pad(a.astype(jnp.int32), (0, size - a.shape[0]))
    tables = jnp.stack([pad(order), pad(first), pad(kind), pad(places)])
    return tables, cosine, sine, seg_row, seg_wide, feature, coef, hot_rows


def ffn_kernel(row_parts, flipped, which, *refs):
    rows, refs = refs[:row_parts], refs[row_parts:]
    near, refs = refs[:row_parts], refs[row_parts:]
    far, refs = refs[:row_parts], refs[row_parts:]
    weight, act_out, d_both_out, keep_out, rest_out, send_own, send_rest, grads, sems = refs
    part = rows[0].shape[0]
    share = part // 2
    cols = act_out.shape[1]
    half = row_parts // 2
    copies = []
    for p in range(row_parts):
        pair = (far[p], near[p]) if flipped else (near[p], far[p])
        for k in range(2):
            copy = pltpu.make_async_copy(pair[k].at[which[0]], grads.at[p, pl.ds(k * share, share)], sems.at[p, k])
            copy.start()
            copies.append(copy)
    for p in list(range(half, row_parts)) + list(range(half)):
        at = slice(p * part, (p + 1) * part)
        both = nn_dot(rows[p][...], weight[:, : 2 * cols])
        copies[2 * p].wait()
        copies[2 * p + 1].wait()
        d_act = nn_dot(grads[p], weight[:, 2 * cols :])
        gate, up = both[:, :cols], both[:, cols:]
        sig = 1.0 / (1.0 + jnp.exp(-gate))
        silu = gate * sig
        act_out[at, :] = (silu * up).astype(BF16)
        d_both_out[at, :cols] = (d_act * up * (sig + silu * (1.0 - sig))).astype(BF16)
        d_both_out[at, cols:] = (d_act * silu).astype(BF16)
        back = nt_dot(d_both_out[at, :], weight[:, : 2 * cols])
        if p == 0:
            keep_out[...] = back
        elif p < half:
            rest_out[(p - 1) * part : p * part, :] = back
        else:
            if p == half:
                send_own[...] = back.astype(BF16)
            else:
                send_rest[(p - half - 1) * part : (p - half) * part, :] = back.astype(BF16)


def ffn_middle(flipped, which, rows, near, far, weight, behind=()):
    part, width = rows[0].shape
    count = len(rows)
    length = part * count
    cols = weight.shape[1] // 3
    operands = (which, *rows, *near, *far, weight)
    return pl.pallas_call(
        without(functools.partial(ffn_kernel, count, flipped), len(operands), len(behind)),
        out_shape=(
            jax.ShapeDtypeStruct((length, cols), BF16),
            jax.ShapeDtypeStruct((length, 2 * cols), BF16),
            jax.ShapeDtypeStruct((part, width), F32),
            jax.ShapeDtypeStruct((length // 2 - part, width), F32),
            jax.ShapeDtypeStruct((part, width), BF16),
            jax.ShapeDtypeStruct((length // 2 - part, width), BF16),
        ),
        in_specs=[smem()] + [vmem()] * count + [anywhere()] * (2 * count) + [vmem()] + [anywhere()] * len(behind),
        out_specs=[vmem()] * 6,
        scratch_shapes=[pltpu.VMEM((count, part, width), BF16), pltpu.SemaphoreType.DMA((count, 2))],
        compiler_params=pltpu.CompilerParams(vmem_limit_bytes=VMEM_LIMIT),
        cost_estimate=pl.CostEstimate(
            flops=10 * length * width * cols, bytes_accessed=16 << 20, transcendentals=length * cols
        ),
        name="ffn_middle",
    )(*operands, *behind)


def ffn_tail_kernel(row_parts, which, *refs):
    own, refs = refs[:row_parts], refs[row_parts:]
    other, refs = refs[:row_parts], refs[row_parts:]
    near, refs = refs[:row_parts], refs[row_parts:]
    far, refs = refs[:row_parts], refs[row_parts:]
    acts, boths, weight, refs = refs[:2], refs[2:4], refs[4], refs[5:]
    outs, stacks, grad_out, refs = refs[:4], refs[4:6], refs[6], refs[7:]
    down_buf, act_buf, both_buf, grad_buf, row_buf, total, keeps, rests, twins, twin_rests = refs[:10]
    in_sems, grad_sems, row_sems, out_sems, total_sems = refs[10:]
    part, width = own[0].shape
    share = part // 2
    length = part * row_parts
    cols = acts[0].shape[1]
    half = length // 2

    def begin(source, target, sem):
        copy = pltpu.make_async_copy(source, target, sem)
        copy.start()
        return copy

    down_copy = begin(weight.at[:, pl.ds(2 * cols, cols)], down_buf, in_sems.at[0])
    act_copies = [begin(acts[seq], act_buf.at[seq], in_sems.at[1 + seq]) for seq in range(2)]
    grad_copies = []
    for seq in range(2):
        now = which[0] if seq == 0 else 1 - which[0]
        for p in range(row_parts):
            pair = (near[p], far[p]) if seq == 0 else (far[p], near[p])
            for k in range(2):
                to = grad_buf.at[seq, pl.ds(p * part + k * share, share)]
                grad_copies.append(begin(pair[k].at[now], to, grad_sems.at[seq, p, k]))
    row_copies = [
        begin((own, other)[seq][p], row_buf.at[seq, pl.ds(p * part, part)], row_sems.at[seq, p])
        for seq in range(2)
        for p in range(row_parts)
    ]
    both_copies = [begin(boths[seq], both_buf.at[seq], in_sems.at[3 + seq]) for seq in range(2)]
    down_copy.wait()
    out_copies = []
    for seq in range(2):
        act_copies[seq].wait()
        mine = nt_dot(act_buf[seq, :half, :], down_buf[...])
        keeps[seq] = mine[:part]
        rests[seq] = mine[part:]
        mine = nt_dot(act_buf[seq, half:, :], down_buf[...]).astype(BF16)
        twins[seq] = mine[:part]
        twin_rests[seq] = mine[part:]
        for k, buf in enumerate((keeps, rests, twins, twin_rests)):
            to = outs[2 * seq + k] if k < 2 else stacks[k - 2].at[seq]
            out_copies.append(begin(buf.at[seq], to, out_sems.at[seq, k]))
    step = width // 4
    total_copies = []
    for what in range(2):
        for seq in range(2):
            for p in range(row_parts):
                if what == 0:
                    grad_copies[2 * (seq * row_parts + p)].wait()
                    grad_copies[2 * (seq * row_parts + p) + 1].wait()
                else:
                    row_copies[seq * row_parts + p].wait()
        if what == 1:
            both_copies[0].wait()
            both_copies[1].wait()
        right, source = (act_buf, both_buf)[what], (grad_buf, row_buf)[what]
        first, size = (2 * cols, cols) if what == 0 else (0, 2 * cols)
        for k in range(4):
            at = slice(k * step, (k + 1) * step)
            value = sum(tn_dot(source[seq, :, at], right[seq]) for seq in range(2))
            total[at, first : first + size] = value.astype(BF16)
            if what == 1:
                rows = pl.ds(k * step, step)
                total_copies.append(begin(total.at[rows], grad_out.at[rows], total_sems.at[k]))
    for copy in out_copies + total_copies:
        copy.wait()


def ffn_tail(which, own, other, near, far, act_own, act_other, d_own, d_other, weight):
    part, width = own[0].shape
    count = len(own)
    length = part * count
    cols = act_own.shape[1]
    rest = length // 2 - part
    shapes = (
        jax.ShapeDtypeStruct((part, width), F32),
        jax.ShapeDtypeStruct((rest, width), F32),
    )
    stacks = (
        jax.ShapeDtypeStruct((2, part, width), BF16),
        jax.ShapeDtypeStruct((2, rest, width), BF16),
    )
    made = pl.pallas_call(
        functools.partial(ffn_tail_kernel, count),
        out_shape=shapes * 2 + stacks + (jax.ShapeDtypeStruct((width, 3 * cols), BF16),),
        in_specs=[smem()] + [anywhere()] * (4 * count + 5),
        out_specs=[anywhere()] * 6 + [pl.BlockSpec(memory_space=pltpu.HBM)],
        scratch_shapes=[
            pltpu.VMEM((width, cols), BF16),
            pltpu.VMEM((2, length, cols), BF16),
            pltpu.VMEM((2, length, 2 * cols), BF16),
            pltpu.VMEM((2, length, width), BF16),
            pltpu.VMEM((2, length, width), BF16),
            pltpu.VMEM((width, 3 * cols), BF16),
            pltpu.VMEM((2, part, width), F32),
            pltpu.VMEM((2, rest, width), F32),
            pltpu.VMEM((2, part, width), BF16),
            pltpu.VMEM((2, rest, width), BF16),
            pltpu.SemaphoreType.DMA((5,)),
            pltpu.SemaphoreType.DMA((2, count, 2)),
            pltpu.SemaphoreType.DMA((2, count)),
            pltpu.SemaphoreType.DMA((2, 4)),
            pltpu.SemaphoreType.DMA((4,)),
        ],
        compiler_params=pltpu.CompilerParams(vmem_limit_bytes=WIDE_LIMIT),
        name="ffn_tail",
    )(which, *own, *other, *near, *far, act_own, act_other, d_own, d_other, weight)
    return made[6], made[:6]


def without(kernel, start, count):
    return lambda *refs: kernel(*refs[:start], *refs[start + count :])


def rows_call(kernel, name, shapes, *operands, scalars=(), behind=(), limit=ROWS_LIMIT):
    single = not isinstance(shapes, (list, tuple))
    count = len(scalars) + len(operands)
    return pl.pallas_call(
        without(kernel, count, len(behind)),
        out_shape=shapes,
        in_specs=[smem()] * len(scalars) + [vmem()] * len(operands) + [anywhere()] * len(behind),
        out_specs=vmem() if single else [vmem()] * len(shapes),
        compiler_params=pltpu.CompilerParams(vmem_limit_bytes=limit),
        cost_estimate=pl.CostEstimate(
            flops=16 * operands[0].size, bytes_accessed=sum(o.size * o.dtype.itemsize for o in operands), transcendentals=0
        ),
        name=name,
    )(*scalars, *operands, *behind)


def pack_kernel(which, rows, query, key, value, out, gate, up, down, own, mine, packed):
    block, start = own.shape[0], 0
    for ref in (query, key, value, out):
        stop = start + ref.shape[1]
        own[:, start:stop] = ref[...]
        packed[:block, start:stop] = ref[...]
        start = stop
    width = rows.shape[2]
    packed[: rows.shape[1], start : start + width] = rows[1 - which[0]]
    start += width
    cols = gate.shape[1] // 2
    for k, ref in enumerate((gate, up, down)):
        for half in range(2):

            @pl.when(which[0] == half)
            def _(ref=ref, half=half, k=k):
                mine[:, k * cols : (k + 1) * cols] = ref[:, half * cols : (half + 1) * cols]
                packed[:block, start + k * cols : start + (k + 1) * cols] = ref[:, (1 - half) * cols : (2 - half) * cols]


def stack_kernel(start, which, mine, theirs, out):
    block, width = mine.shape
    first = pl.multiple_of(which[0] * block, block)
    second = pl.multiple_of((1 - which[0]) * block, block)
    out[pl.ds(first, block), :] = mine[...]
    out[pl.ds(second, block), :] = theirs[:block, start : start + width]


def turn_kernel(start, blocks, chips, which, *refs):
    back, refs = refs[: 7 + chips], refs[7 + chips :]
    pairs, outs = refs[: blocks + 1], refs[blocks + 1 :]
    pair_kernel(*pairs, *outs[2:])
    back_one_kernel(start, which, *back, *outs[:2])


def gains_kernel(place, gain_rows, gain, d_gain_two, bias_parts, out):
    blocks, _, block = gain_rows.shape
    for k in range(blocks):
        at = slice(k * block, (k + 1) * block)
        out[0:1, at] = gain_rows[k, 0:1, :] / gain[:, at].astype(F32)
    out[1:2, :] = d_gain_two[...]
    out[2:, :] = jnp.zeros(out[2:, :].shape, F32)
    lane = lane_of((1, LANES))
    lanes = pl.ds(pl.multiple_of(place[0] * LANES, LANES), LANES)
    for row in range(2):
        line = jnp.zeros((1, LANES), F32)
        for head in range(bias_parts.shape[0]):
            line = jnp.where(lane == head, jnp.sum(bias_parts[head, 8 * row : 8 * row + 8, :]), line)
        out[2 + row : 3 + row, lanes] = line


def ride_kernel(totals, twin, *refs):
    lows, (own, *outs) = refs[: len(refs) // 2], refs[len(refs) // 2 :]
    total = totals[...] + twin[...]
    own[...] = total
    high = total.astype(BF16).astype(F32)
    parts = (high, total - high)
    block, cols = lows[0].shape
    for low, out in zip(lows, outs):
        out[:block, :] = low[...]
        row = block
        for part in parts:
            for c in range(part.shape[1] // cols):
                out[row : row + part.shape[0], :] = part[:, c * cols : (c + 1) * cols].astype(BF16)
                row += part.shape[0]


def arrive_kernel(own, totals, *refs):
    arrived, (grad, total) = refs[:-2], refs[-2:]
    block, cols = own.shape
    rows, width = totals.shape
    value = own[...]
    sums = [totals[:, c * cols : (c + 1) * cols] for c in range(width // cols)]
    for ref in arrived:
        value = value + ref[:block, :].astype(F32)
        for k in range(2 * len(sums)):
            at = block + k * rows
            sums[k % len(sums)] = sums[k % len(sums)] + ref[at : at + rows, :].astype(F32)
    grad[...] = value
    for c, part in enumerate(sums):
        total[:, c * cols : (c + 1) * cols] = part


def gains_finish_kernel(place, mine, *refs):
    theirs, (one, two, bias) = refs[:-3], refs[-3:]
    lanes = pl.ds(pl.multiple_of(place[0] * LANES, LANES), LANES)
    total, line = mine[...], mine[:, lanes]
    for ref in theirs:
        total = total + ref[...]
        line = line + ref[:, lanes]
    one[...] = total[0:1]
    two[...] = total[1:2]
    bias[...] = line[2:4, : bias.shape[1]]


def first_kernel(start, which, mine, rows, far, gain, stack, out, far_attn):
    width = rows.shape[2]
    stack_kernel(start + width, which, mine, far, stack)
    norm_kernel(start, which, rows, far, gain, out, far_attn)


def widen_kernel(angles, cosine, sine):
    half = angles.shape[1] // 2
    cos_half, sin_half = angles[:, :half], angles[:, half:]
    cosine[...] = jnp.concatenate([cos_half] * (LANES // half), axis=1)
    sine[...] = jnp.concatenate([-sin_half, sin_half] * (LANES // half // 2), axis=1)


def pair_kernel(*refs):
    blocks = (len(refs) - 1) // 2
    keeps, other, outs = refs[:blocks], refs[blocks], refs[blocks + 1 :]
    rows = keeps[0].shape[0]
    for k in range(blocks):
        total = keeps[k][...].astype(F32) + other[k * rows : (k + 1) * rows, :].astype(F32)
        outs[k][...] = total.astype(outs[k].dtype)


def finish_kernel(count, own, *refs):
    total = own[...]
    for ref in refs[:-count]:
        total = total + ref[...].astype(F32)
    start = 0
    for out in refs[-count:]:
        stop = start + out.shape[1]
        out[...] = total[:, start:stop]
        start = stop


def pair_sums(partials, other):
    shape = partials[0].shape
    blocks = len(partials) - 1
    shapes = [jax.ShapeDtypeStruct(shape, F32 if k == 0 else BF16) for k in range(blocks)]
    return rows_call(pair_kernel, "pair_sums", shapes, *partials[:-1], other)


def weight_sums(own, arrived, pieces):
    outs = [jax.ShapeDtypeStruct((own.shape[0], own.shape[1] // pieces), F32)] * pieces
    return rows_call(functools.partial(finish_kernel, pieces), "weight_sums", outs, own, *arrived)


def last_kernel(start, count, which, grads, crossed, near, own, *refs):
    arrived, (gate, up, down, rows_out), outs = refs[:count], refs[count : count + 4], refs[count + 4 :]
    cols = grads.shape[1] // 3
    rows = grads.shape[0] // 2
    mine = grads[pl.ds(pl.multiple_of(which[0] * rows, rows), rows), :].astype(F32)
    theirs = crossed[:rows, start:].astype(F32)
    for half in range(2):

        @pl.when(which[0] == half)
        def _(half=half):
            for k, out in enumerate((gate, up, down)):
                out[:, half * cols : (half + 1) * cols] = mine[:, k * cols : (k + 1) * cols]
                out[:, (1 - half) * cols : (2 - half) * cols] = theirs[:, k * cols : (k + 1) * cols]

    stack_kernel(0, which, near, crossed, rows_out)
    finish_kernel(len(outs), own, *arrived, *outs)


def quadrant(own, other, flip):
    share = own.shape[0] // 2
    return jnp.concatenate(
        [own[flip * share : (flip + 1) * share], other[(1 - flip) * share : (2 - flip) * share]], axis=0
    )


def out_split_kernel(hidden, keep, rest, keep_next, rest_next, twins, twin_rests, *outs):
    first, cross, chips, chips_cross = outs
    part = hidden.shape[0]
    own = keep[...] + twins[0].astype(F32) + hidden[...]
    other = keep_next[...] + twins[1].astype(F32)
    first[...] = quadrant(own, other, 0)
    cross[...] = quadrant(own, other, 1).astype(BF16)
    own = rest[...] + twin_rests[0].astype(F32)
    other = rest_next[...] + twin_rests[1].astype(F32)
    for k in range(rest.shape[0] // part):
        at = slice(k * part, (k + 1) * part)
        chips[at, :] = quadrant(own[at], other[at], 0)
        chips_cross[at, :] = quadrant(own[at], other[at], 1).astype(BF16)


def swapped(values):
    half = values.shape[0] // 2
    return jnp.concatenate([values[half:], values[:half]], axis=0)


def add_kernel(part, values, arrived, out):
    for k in range(values.shape[0] // part):
        at = slice(k * part, (k + 1) * part)
        out[at, :] = (values[at, :] + swapped(arrived[at, :].astype(F32))).astype(BF16)


def out_finish_kernel(which, first, cross, *refs):
    arrived, out = refs[:-1], refs[-1]
    share = out.shape[1]
    total = first[...] + swapped(cross[...].astype(F32))
    for ref in arrived:
        total = total + ref[...].astype(F32)
    total = total.astype(BF16)
    out[pl.ds(which[0], 1)] = total[None, :share]
    out[pl.ds(1 - which[0], 1)] = total[None, share:]


def inverse_rms(values):
    return lax.rsqrt(jnp.mean(values * values, axis=-1, keepdims=True) + EPS)


def both_halves(start, rows, packed, which):
    share, width = rows.shape[1:]
    return jnp.concatenate([rows[which[0]], packed[:share, start : start + width]], axis=0).astype(F32)


def rows_sum(keep, twin, arrived):
    total = keep[...] + twin[...].astype(F32)
    for ref in arrived:
        total = total + ref[...].astype(F32)
    return total


def norm_kernel(start, which, rows, far, gain, out, far_attn):
    far_attn[...] = far[: far_attn.shape[0], :start]
    values = both_halves(start, rows, far, which)
    out[...] = (values * inverse_rms(values) * gain[...].astype(F32)).astype(BF16)


def rest_kernel(rest, twin, out):
    out[...] = (rest[...] + twin[...].astype(F32)).astype(BF16)


def sum_kernel(keep, twin, *refs):
    refs[-1][...] = rows_sum(keep, twin, refs[:-1]).astype(BF16)


def middle_kernel(start, which, rows, far, gain, keep, twin, *refs):
    arrived, (hidden, out) = refs[:-2], refs[-2:]
    values = both_halves(start, rows, far, which) + rows_sum(keep, twin, arrived)
    hidden[...] = values
    out[...] = (values * inverse_rms(values) * gain[...].astype(F32)).astype(BF16)


def pull_norm(values, gain, grad):
    inv = inverse_rms(values)
    scaled = grad * gain
    normed = values * inv
    d_values = inv * (scaled - normed * jnp.mean(scaled * normed, axis=-1, keepdims=True))
    return d_values, jnp.sum(grad * normed, axis=0, keepdims=True)


def back_two_kernel(which, hidden, near, far, gain, across, keep, twin, *refs):
    arrived, (d_hidden, low, d_gain) = refs[:-3], refs[-3:]
    grad = rows_sum(keep, twin, arrived) + across[...].astype(F32)
    d_values, d_gain[...] = pull_norm(hidden[...], gain[...].astype(F32), grad)
    total = jnp.concatenate([near[which[0]], far[which[0]]], axis=0).astype(F32) + d_values
    d_hidden[...] = total
    low[...] = total.astype(BF16)


def back_one_kernel(start, which, rows, far, gain, d_hidden, ffn_grad, keep, twin, *refs):
    arrived, (first, packed) = refs[:-2], refs[-2:]
    grad = rows_sum(keep, twin, arrived)
    d_values, _ = pull_norm(both_halves(start, rows, far, which), gain[...].astype(F32), grad)
    total = (d_hidden[...] + d_values).astype(BF16)
    share, width = first.shape
    first[...] = total[:share]
    packed[:share, :width] = total[share:]
    block = ffn_grad.shape[0] // 2
    packed[:block, width:] = ffn_grad[pl.ds(pl.multiple_of((1 - which[0]) * block, block), block), :]


def grad_kernel(row_parts, blocks, tables, *refs):
    rows, refs = refs[:row_parts], refs[row_parts:]
    right, refs = refs[0], refs[1:]
    keeps, send, left = refs[:blocks], refs[blocks], refs[blocks + 1]
    block = keeps[0].shape[0]
    left_of(rows, right, left)
    for s in range(2 * blocks):
        at = pl.ds(pl.multiple_of(tables[3, s] * block, block), block)
        total = left[at, :].astype(BF16)
        if s < blocks:
            keeps[s][...] = total
        else:
            send[(s - blocks) * block : (s - blocks + 1) * block, :] = total


def weight_partials(tables, rows, right, blocks):
    part, width = rows[0].shape
    length, cols = right.shape
    block = width // (2 * blocks)
    return pl.pallas_call(
        functools.partial(grad_kernel, len(rows), blocks),
        out_shape=(jax.ShapeDtypeStruct((block, cols), BF16),) * blocks
        + (jax.ShapeDtypeStruct((width // 2, cols), BF16),),
        in_specs=[smem()] + [vmem()] * (len(rows) + 1),
        out_specs=[vmem()] * (blocks + 1),
        scratch_shapes=[pltpu.VMEM((width, cols), F32)],
        compiler_params=pltpu.CompilerParams(vmem_limit_bytes=VMEM_LIMIT),
        cost_estimate=pl.CostEstimate(
            flops=2 * length * width * cols, bytes_accessed=8 << 20, transcendentals=0
        ),
        name="weight_partials",
    )(tables, *rows, right)


def left_of(rows, right, total):
    part, width = rows[0].shape
    step = 2 * LANES
    for c in range(width // step):
        at = slice(c * step, (c + 1) * step)
        total[at, :] = sum(tn_dot(ref[:, at], right[p * part : (p + 1) * part, :]) for p, ref in enumerate(rows))


def send_kernel(row_parts, blocks, tables, *refs):
    rows, (right, send, left) = refs[:row_parts], refs[row_parts:]
    block = send.shape[0] // blocks
    left_of(rows, right, left)
    for s in range(blocks):
        at = pl.ds(pl.multiple_of(tables[3, blocks + s] * block, block), block)
        send[s * block : (s + 1) * block, :] = left[at, :].astype(BF16)


def keep_kernel(row_parts, blocks, tables, *refs):
    weights, refs = refs[: 2 * blocks], refs[2 * blocks :]
    rows, right, refs = refs[:row_parts], refs[row_parts], refs[row_parts + 1 :]
    keeps, (gain_row, left) = refs[:blocks], refs[blocks:]
    block = keeps[0].shape[0]
    cols = right.shape[1]
    left_of(rows, right, left)
    for s in range(2 * blocks):
        at = pl.ds(pl.multiple_of(tables[3, s] * block, block), block)
        total = left[at, :]
        product = total * weights[s][:block, :cols].astype(F32)
        product = sum(product[:, c * LANES : (c + 1) * LANES] for c in range(cols // LANES))
        high = product.astype(BF16)
        rest = (product - high.astype(F32)).astype(BF16)
        ones = jnp.ones((8, LANES), BF16)
        gain_row[pl.ds(tables[3, s], 1)] = (nt_dot(ones, high) + nt_dot(ones, rest))[None]
        if s < blocks:
            keeps[s][...] = total.astype(BF16)


def qkv_call(kernel, name, shapes, tables, operands, scratch):
    single = not isinstance(shapes, tuple)
    return pl.pallas_call(
        kernel,
        out_shape=shapes,
        in_specs=[smem()] + [vmem()] * len(operands),
        out_specs=vmem() if single else [vmem()] * len(shapes),
        scratch_shapes=[pltpu.VMEM(scratch, F32)],
        compiler_params=pltpu.CompilerParams(vmem_limit_bytes=VMEM_LIMIT),
        name=name,
    )(tables, *operands)


def qkv_partials(tables, weights, rows, right, blocks):
    part, width = rows[0].shape
    length, cols = right.shape
    block = width // (2 * blocks)
    send = qkv_call(
        functools.partial(send_kernel, len(rows), blocks),
        "qkv_send",
        jax.ShapeDtypeStruct((width // 2, cols), BF16),
        tables,
        [*rows, right],
        (width, cols),
    )
    keeps = qkv_call(
        functools.partial(keep_kernel, len(rows), blocks),
        "qkv_keep",
        (jax.ShapeDtypeStruct((block, cols), BF16),) * blocks + (jax.ShapeDtypeStruct((2 * blocks, 8, block), F32),),
        tables,
        [*weights, *rows, right],
        (width, cols),
    )
    return keeps[:-1], send, keeps[-1]


def hop(values, axis, flip):
    size = lax.axis_size(axis)
    return lax.ppermute(values, axis, [(i, i ^ flip) for i in range(size)])


def swap_blocks(values, axis, index, size):
    shape = values.shape
    bit = 1
    while bit < size:
        split = shape[:axis] + (size // (2 * bit), 2, bit) + shape[axis + 1 :]
        cut = values.reshape(split)
        cut = jnp.where((index & bit) != 0, jnp.flip(cut, axis + 1), cut)
        values = cut.reshape(shape)
        bit *= 2
    return values


def gather_chips(block):
    nt = lax.axis_size("tp")
    return [block] + [hop(block, "tp", 2 * k) for k in range(1, nt // 2)]


def with_twins(blocks):
    return blocks + [hop(block, "tp", 1) for block in blocks]


def gather_rows(block):
    return with_twins(gather_chips(block))


def region(ready, run):
    shapes = jax.eval_shape(run)
    return lax.cond(ready, run, lambda: jax.tree.map(lambda a: jnp.zeros(a.shape, a.dtype), shapes))


def chips_low(rest, twin, *behind):
    return rows_call(
        rest_kernel, "rest_rows", jax.ShapeDtypeStruct(rest.shape, BF16), rest, twin, behind=behind
    )


def chips_hop(low, nt):
    if nt == 4:
        return [hop(low, "tp", 2)]
    rows = low.shape[0] // (nt // 2 - 1)
    return [hop(low[(k - 1) * rows : k * rows], "tp", 2 * k) for k in range(1, nt // 2)]


def shards(
    layer_in,
    attn_gain,
    ffn_gain,
    query_weight,
    key_weight,
    value_weight,
    out_weight,
    variate_bias,
    gate_weight,
    up_weight,
    down_weight,
    segment_ids,
    variate_ids,
    time_ids,
    out_grad,
):
    seq_count, share, width = layer_in.shape
    nz, nx, nt = lax.axis_size("fsdp"), lax.axis_size("ctx"), lax.axis_size("tp")
    iz, ix, it = lax.axis_index("fsdp"), lax.axis_index("ctx"), lax.axis_index("tp")
    assert nx == 2 and seq_count == nx
    length = segment_ids.shape[1]
    heads = variate_bias.shape[1]
    proj = heads * HEAD

    def pick(table, which):
        return lax.dynamic_index_in_dim(table, which, 0, keepdims=False)

    def swap(mine, theirs):
        return jnp.where(ix == 0, mine, theirs), jnp.where(ix == 0, theirs, mine)

    gain_one, gain_two = attn_gain[None], ffn_gain[None]
    part = nx * share
    low_rows = jax.ShapeDtypeStruct((part, width), BF16)
    wide_rows = jax.ShapeDtypeStruct((part, width), F32)
    gain_row = jax.ShapeDtypeStruct((1, width), F32)
    half_rows = jax.ShapeDtypeStruct((share, width), BF16)
    which = ix.astype(jnp.int32).reshape(1)
    ready = ix >= 0
    cols = gate_weight.shape[1] // 2
    grad_own = out_grad
    block = query_weight.shape[0]
    attn_shape = jax.ShapeDtypeStruct((block, 4 * proj), BF16)
    packed_shape = jax.ShapeDtypeStruct((max(block, share), 4 * proj + width + 3 * cols), BF16)
    ffn_shape = jax.ShapeDtypeStruct((gate_weight.shape[0], 3 * cols), BF16)
    attn_own, mine, packed = rows_call(
        pack_kernel, "pack_weights", (attn_shape, ffn_shape, packed_shape), layer_in, query_weight, key_weight,
        value_weight, out_weight, gate_weight, up_weight, down_weight, scalars=(which,), limit=WIDE_LIMIT,
    )
    start = 4 * proj

    def twin(block):
        return hop(block, "tp", 1)

    def across(block):
        return hop(block, "ctx", 1)

    def first_transfers():
        attn_z = [hop(attn_own, "fsdp", k) for k in range(1, nz)]
        far = across(packed)
        grad_y = gather_chips(grad_own)[1:]
        order = jnp.arange(nx * nt).reshape(nx, nt // 2, 2)
        order = swap_blocks(swap_blocks(swap_blocks(order, 0, ix, nx), 1, it // 2, nt // 2), 2, it % 2, 2)
        order = order.transpose(2, 1, 0).reshape(nx * nt)
        places = jnp.arange(nz * nx).reshape(nz, nx)
        places = swap_blocks(swap_blocks(places, 0, iz, nz), 1, ix, nx).transpose(1, 0).reshape(nz * nx)
        tables = attention_tables(
            pick(segment_ids, ix), pick(variate_ids, ix), pick(time_ids, ix), variate_bias, order, places
        )
        return attn_z, far, grad_y, tables

    attn_z, far, grad_y, made = region(ready, first_transfers)
    tables, cosine, sine, seg_row, seg_wide, feature, coef, hot_rows = made
    stack_shape = jax.ShapeDtypeStruct((2 * block, 3 * cols), BF16)
    ffn_w, rows_own, far_attn = rows_call(
        functools.partial(first_kernel, start), "first_rows", (stack_shape, low_rows, attn_shape), mine, layer_in, far,
        gain_one, scalars=(which,), limit=WIDE_LIMIT,
    )
    ffn_w = lax.all_gather(ffn_w, "fsdp", axis=0, tiled=True)

    def gather_one():
        rest = [hop(far_attn, "fsdp", 1)] + [across(piece) for piece in attn_z[1:]]
        return gather_chips(rows_own)[1:], rest

    chips, rest_x = region(ready, gather_one)
    chips_one = [rows_own] + chips
    attn_w = [attn_own] + attn_z + [far_attn] + rest_x

    def attend():
        twins = [twin(rows) for rows in chips_one]
        near_twins = [twin(rows) for rows in [grad_own] + grad_y]
        return across(grad_own), near_twins, twins, attention_forward(
            tables, chips_one + twins, attn_w, cosine, sine, seg_row, seg_wide, feature, coef, heads
        )

    grad_far, near_twins, twins, (q_aug, k_aug, v_rows, mixed, lse, keep, rest, send, send_rest) = region(ready, attend)

    def scatter_attn():
        low = chips_low(rest, twin(send_rest))
        return chips_hop(low, nt), twin(send), [across(piece) for piece in grad_y], twin(grad_far)

    rows_one = chips_one + twins
    chips, twins, grad_far_y, far_twin = region(ready, scatter_attn)
    grad_near, grad_far = [grad_own] + grad_y, [grad_far] + grad_far_y
    hidden, rows_two = rows_call(
        functools.partial(middle_kernel, start), "middle_rows", (wide_rows, low_rows), layer_in, far, gain_two, keep,
        twins, *chips, scalars=(which,),
    )

    def gather_two():
        return (
            gather_chips(rows_two)[1:],
            across(rows_two),
            [twin(rows) for rows in grad_far[1:]],
            twin(rows_two),
        )

    chips_two, next_own, far_twins, rows_twin = region(ready, gather_two)
    grad_near, grad_far = grad_near + near_twins, grad_far + [far_twin] + far_twins

    def ffn_own():
        twins = [twin(rows) for rows in chips_two]
        return [across(rows) for rows in chips_two], twins, ffn_middle(
            False, which, [rows_two] + chips_two + [rows_twin] + twins, grad_near, grad_far, ffn_w
        )

    next_y, twins, (act, d_both, keep, rest, send, send_rest) = region(ready, ffn_own)

    rows_two = [rows_two] + chips_two + [rows_twin] + twins
    rows_next = [next_own] + next_y

    def ffn_next():
        low = chips_low(rest, twin(send_rest))
        twins = [twin(rows) for rows in rows_next]
        return chips_hop(low, nt), twin(send), twins, ffn_middle(
            True, 1 - which, rows_next + twins, grad_near, grad_far, ffn_w
        )

    chips, twins, next_twins, made = region(ready, ffn_next)
    rows_next = rows_next + next_twins
    act_next, d_both_next, keep_next, rest_next, send_next, send_rest = made
    low_next = chips_low(rest_next, twin(send_rest))

    def scatter_next():
        return (
            chips_hop(low_next, nt),
            twin(send_next),
            ffn_tail(which, rows_two, rows_next, grad_near, grad_far, act, act_next, d_both, d_both_next, ffn_w),
        )

    chips_next, twins_next, (ffn_grad, parts) = region(ready, scatter_next)
    low_across = rows_call(sum_kernel, "sum_rows", low_rows, keep_next, twins_next, *chips_next)

    def cross_next():
        out_twins = [twin(parts[k]) for k in (4, 5)]
        rest_shape = (parts[1].shape[0], width)
        shapes = (
            wide_rows,
            low_rows,
            jax.ShapeDtypeStruct(rest_shape, F32),
            jax.ShapeDtypeStruct(rest_shape, BF16),
        )
        return across(low_across), rows_call(
            out_split_kernel, "out_split", shapes, hidden, *parts[:4], *out_twins,
        )

    arrived, (out_first, out_cross, out_chips, out_chips_cross) = region(ready, cross_next)
    ffn_grad = lax.psum_scatter(ffn_grad, "fsdp", scatter_dimension=0, tiled=True)
    d_hidden, low, d_gain_two = rows_call(
        back_two_kernel,
        "back_two",
        (wide_rows, low_rows, gain_row),
        hidden,
        grad_near[0],
        grad_far[0],
        gain_two,
        arrived,
        keep,
        twins,
        *chips,
        scalars=(which,),
    )

    def gather_back():
        return gather_chips(low)[1:], twin(low), across(out_chips_cross)

    chips_back, twin_back, out_arrived = region(ready, gather_back)
    def attend_back():
        rows = [low] + chips_back + [twin_back] + [twin(rows) for rows in chips_back]
        cross = across(out_cross)
        low_shape = jax.ShapeDtypeStruct(out_chips.shape, BF16)
        low_out = rows_call(functools.partial(add_kernel, part), "add_rows", low_shape, out_chips, out_arrived)
        grads = weight_partials(tables, rows, mixed, nz)
        return chips_hop(low_out, nt), cross, across(grads[-1]), grads, attention_backward(
            tables, rows, attn_w, q_aug, k_aug, v_rows, lse, cosine, sine, seg_row, seg_wide, hot_rows, heads
        )

    out_arrived, out_cross, out_other, out_grads, made = region(ready, attend_back)
    keep, rest, send, send_rest, d_qkv, bias_parts = made

    place = it.astype(jnp.int32).reshape(1)
    gain_shape = jax.ShapeDtypeStruct((8, width), F32)

    def scatter_one():
        twins = twin(send)
        low = chips_low(rest, twin(send_rest), twins)
        keeps, sent, gain_rows = qkv_partials(tables, attn_w, rows_one, d_qkv, nz)
        sums = pair_sums(out_grads, out_other)
        totals = rows_call(
            gains_kernel, "gain_rows", gain_shape, gain_rows, gain_one, d_gain_two, bias_parts, scalars=(place,)
        )
        lows = sums[1:]
        ride_shape = jax.ShapeDtypeStruct((block + 16 * (width // proj), proj), BF16)
        totals, *lows = rows_call(
            ride_kernel, "ride_rows", [gain_shape] + [ride_shape] * len(lows), totals, twin(totals), *lows
        )
        arrived = [hop(low_out, "fsdp", 1 + k) for k, low_out in enumerate(lows)]
        out_weight_grad, totals = rows_call(
            arrive_kernel, "out_sums", (jax.ShapeDtypeStruct((block, proj), F32), gain_shape), sums[0], totals, *arrived
        )
        return chips_hop(low, nt), twins, keeps, across(sent), out_weight_grad, totals

    chips, twins, qkv_keeps, qkv_other, out_weight_grad, totals = region(ready, scatter_one)
    packed_shape = jax.ShapeDtypeStruct((max(block, share), width + 3 * cols), BF16)
    pair_shapes = [jax.ShapeDtypeStruct((block, 3 * proj), F32 if k == 0 else BF16) for k in range(nz)]
    d_near, packed, *qkv_sums = rows_call(
        functools.partial(turn_kernel, start, nz, len(chips)), "turn_rows", [half_rows, packed_shape] + pair_shapes,
        layer_in, far, gain_one, d_hidden, ffn_grad, keep, twins, *chips, *qkv_keeps, qkv_other,
        scalars=(which,), limit=WIDE_LIMIT,
    )

    def last_transfers():
        arrived = [hop(piece, "fsdp", k) for k, piece in enumerate(qkv_sums) if k > 0]
        layer_out = rows_call(
            out_finish_kernel, "layer_out", jax.ShapeDtypeStruct(layer_in.shape, BF16), out_first, out_cross,
            *out_arrived, scalars=(which,),
        )
        chips = sum([hop(totals, "tp", 2 * k) for k in range(1, nt // 2)], totals)
        summed = rows_call(
            gains_finish_kernel, "gain_sums", (gain_row, gain_row, jax.ShapeDtypeStruct((2, heads), F32)), chips,
            across(chips), scalars=(place,),
        )
        return arrived, across(packed), summed, layer_out

    arrived, crossed, summed, layer_out = region(ready, last_transfers)
    attn_gain_grad, ffn_gain_grad, bias_grad = summed
    weight_shape = jax.ShapeDtypeStruct(gate_weight.shape, F32)
    in_shape = jax.ShapeDtypeStruct((nx * share, width), BF16)
    head_shape = jax.ShapeDtypeStruct(query_weight.shape, F32)
    gate_grad, up_grad, down_grad, in_grad, query_grad, key_grad, value_grad = rows_call(
        functools.partial(last_kernel, width, len(arrived)), "last_sums",
        [weight_shape] * 3 + [in_shape] + [head_shape] * 3,
        ffn_grad, crossed, d_near, qkv_sums[0], *arrived, scalars=(which,), limit=WIDE_LIMIT,
    )
    in_grad = in_grad.reshape(layer_in.shape)
    return (
        layer_out,
        in_grad,
        attn_gain_grad.reshape(width),
        ffn_gain_grad.reshape(width),
        query_grad,
        key_grad,
        value_grad,
        out_weight_grad,
        bias_grad,
        gate_grad,
        up_grad,
        down_grad,
    )


def solution(mesh):
    rows = P("fsdp", ("ctx", "tp"), None)
    weight = P(("fsdp", "ctx"), "tp")
    ids = P("fsdp", None)
    bias = P(None, "tp")
    in_specs = (rows, P(), P()) + (weight,) * 4 + (bias,) + (weight,) * 3 + (ids,) * 3 + (rows,)
    out_specs = (rows, rows, P(), P()) + (weight,) * 4 + (bias,) + (weight,) * 3
    return jax.shard_map(shards, mesh=mesh, in_specs=in_specs, out_specs=out_specs, check_vma=False)
```
